32 devices in a mesh: dp: 16 (over z, y, core), mp: 2 (over x).
Axes of the slice: x: 2, y: 2, z: 4, core: 2. Of those that a mesh axis runs over, the one named last changes fastest.
Arguments:
- tokens: bfloat16 [8976, 1024], P('dp'), may hold values from -6 to 6
- query_weight: bfloat16 [1024, 1024], P(None, 'mp'), may hold values from -0.1875 to 0.1875
- key_weight: bfloat16 [1024, 1024], P(None, 'mp'), may hold values from -0.1875 to 0.1875
- value_weight: bfloat16 [1024, 1024], P(None, 'mp'), may hold values from -0.1875 to 0.1875
- output_weight: bfloat16 [1024, 1024], P('mp'), may hold values from -1.5 to 1.5
- query_position: bfloat16 [1024, 1024], P(None, 'mp'), may hold values from -0.1875 to 0.1875
- key_position: bfloat16 [1024, 1024], P(None, 'mp'), may hold values from -0.1875 to 0.1875
- position_tables: bfloat16 [3, 128, 1024], replicated, may hold values from -6 to 6
- gain_one: float32 [1024], replicated, may hold values from 0.5 to 1.5
- shift_one: float32 [1024], replicated, may hold values from -2 to 2
- up_weight: bfloat16 [1024, 4096], P(None, 'mp'), may hold values from -0.1875 to 0.1875
- down_weight: bfloat16 [4096, 1024], P('mp'), may hold values from -0.09375 to 0.09375
- gain_two: float32 [1024], replicated, may hold values from 0.5 to 1.5
- shift_two: float32 [1024], replicated, may hold values from -2 to 2
- buckets: int32 [16, 3, 561, 561], P('dp'), may hold values from 0 to 127
- text_length: int32 [16], P('dp'), may hold values from 1 to 512, as said below
- cotangent: bfloat16 [8976, 1024], P('dp'), may hold values from -6 to 6
Outputs:
- layer_output: bfloat16 [8976, 1024], P('dp')
- input_gradient: bfloat16 [8976, 1024], P('dp')
- query_gradient: float32 [1024, 1024], P('dp', 'mp')
- key_gradient: float32 [1024, 1024], P('dp', 'mp')
- value_gradient: float32 [1024, 1024], P('dp', 'mp')
- output_gradient: float32 [1024, 1024], P('mp', 'dp')
- query_position_gradient: float32 [1024, 1024], P('dp', 'mp')
- key_position_gradient: float32 [1024, 1024], P('dp', 'mp')
- table_gradient: float32 [3, 128, 1024], P(None, None, ('dp', 'mp'))
- gain_one_gradient: float32 [1024], P('dp')
- shift_one_gradient: float32 [1024], P('dp')
- up_gradient: float32 [1024, 4096], P('dp', 'mp')
- down_gradient: float32 [4096, 1024], P('mp', 'dp')
- gain_two_gradient: float32 [1024], P('dp')
- shift_two_gradient: float32 [1024], P('dp')
The draws below stay inside these ranges and needn't reach their ends.
Inputs may be any that keep to these rules, and one draw needn't show every extreme that they name: `text_length`: some page uses all 512 text tokens and some page uses exactly one.
All inputs are finite; a program needn't handle non-finite values.
Results may differ from the reference program's by a relative error of at most 0.015.
Values sent between devices are 32-bit elements; how exact they have to be, the bound alone decides.
No kernel may reach another device: no remote copies, remote signals or barrier semaphores. Data moves between devices by JAX's collectives and lax.ppermute only.
A program may use at most 384 MiB of HBM per device.

```python
import jax
import jax.numpy as jnp
from jax import lax

D = 1024
HEADS = 16
HEAD = 64
FF = 4096
REL = 128
TEXT = 512
PAGE = 561
PAGES = 16
TOKENS = 8976


def draw_text_length(key, part):
    lengths = jax.random.randint(jax.random.fold_in(key, 11), (PAGES,), 1, TEXT + 1)
    chosen = jax.random.randint(jax.random.fold_in(key, 12), (), 0, PAGES)
    offset = jax.random.randint(jax.random.fold_in(key, 13), (), 0, PAGES - 1)
    second = (chosen + 1 + offset) % PAGES
    lengths = lengths.at[chosen].set(TEXT)
    return lengths.at[second].set(1).astype(jnp.int32)


def touch_ends(entries, rng, low, top_value):
    longest = entries.shape.index(max(entries.shape))
    spots = []
    for shift in (0, 1):
        where = [jax.random.randint(jax.random.fold_in(rng, axis), (), 0, length) for axis, length in enumerate(entries.shape)]
        where[longest] = (where[longest] + shift) % entries.shape[longest]
        spots.append(tuple(where))
    return entries.at[spots[0]].set(low).at[spots[1]].set(top_value)


def level_of(rng, extent, split, low, high):
    level, own = 1.0, jax.random.fold_in(rng, 6)
    for dim, parts in split:
        heights = jnp.exp(jax.random.uniform(jax.random.fold_in(own, dim), (parts,), jnp.float32, low / len(split), high / len(split)))
        level = level * jnp.repeat(heights, extent[dim] // parts).reshape([-1 if axis == dim else 1 for axis in range(len(extent))])
    return level


def scatter_about(rng, extent, scale, reach, cuts=(), held_as=jnp.bfloat16):
    values = jax.random.normal(rng, extent, jnp.float32) * scale
    if len(cuts) > 0:
        values = level_of(rng, extent, cuts, -0.22, 0.18) * values
    return jnp.clip(values, min=-reach, max=reach).astype(held_as)


def setup_inputs(seed: int = 0) -> dict:
    keys = jax.random.split(jax.random.key(seed), 18)
    tokens = scatter_about(keys[0], (TOKENS, D), 1.0, 6.0, ((0, 16),))
    query_weight = scatter_about(keys[1], (D, D), D ** -0.5, 0.1875, ((1, 2),))
    key_weight = scatter_about(keys[2], (D, D), D ** -0.5, 0.1875, ((1, 2),))
    value_weight = scatter_about(keys[3], (D, D), D ** -0.5, 0.1875, ((1, 2),))
    output_weight = scatter_about(keys[4], (D, D), (D * 8 // PAGE) ** -0.5, 1.5, ((0, 2),))
    query_position = scatter_about(keys[5], (D, D), D ** -0.5, 0.1875, ((1, 2),))
    key_position = scatter_about(keys[6], (D, D), D ** -0.5, 0.1875, ((1, 2),))
    position_tables = scatter_about(keys[7], (3, REL, D), 1.0, 6.0)
    gain_one = jnp.clip(1.0 + 0.1 * jax.random.normal(keys[8], (D,), jnp.float32), 0.5, 1.5)
    shift_one = scatter_about(keys[9], (D,), 0.3, 2.0, (), jnp.float32)
    up_weight = scatter_about(keys[10], (D, FF), D ** -0.5, 0.1875, ((1, 2),))
    down_weight = scatter_about(keys[11], (FF, D), FF ** -0.5, 0.09375, ((0, 2),))
    gain_two = jnp.clip(1.0 + 0.1 * jax.random.normal(keys[12], (D,), jnp.float32), 0.5, 1.5)
    shift_two = scatter_about(keys[13], (D,), 0.3, 2.0, (), jnp.float32)
    buckets = touch_ends(jax.random.randint(keys[14], (PAGES, 3, PAGE, PAGE), 0, REL), jax.random.fold_in(keys[14], 1), 0, REL - 1).astype(jnp.int32)
    text_length = draw_text_length(jax.random.fold_in(keys[17], 71), 0)
    cotangent = scatter_about(keys[16], (TOKENS, D), 1.0, 6.0, ((0, 16),))
    return {"tokens": tokens, "query_weight": query_weight, "key_weight": key_weight, "value_weight": value_weight, "output_weight": output_weight, "query_position": query_position, "key_position": key_position, "position_tables": position_tables, "gain_one": gain_one, "shift_one": shift_one, "up_weight": up_weight, "down_weight": down_weight, "gain_two": gain_two, "shift_two": shift_two, "buckets": buckets, "text_length": text_length, "cotangent": cotangent}


@jax.custom_vjp
def low(v):
    return lax.optimization_barrier(v.astype(jnp.bfloat16)).astype(jnp.float32)

@jax.custom_vjp
def low_back(v):
    return v

def low_keep(v):
    return (low(v), None)

def low_pass(kept, grad):
    return (grad,)

def back_keep(v):
    return (v, None)

def back_low(kept, grad):
    return (low(grad),)
low.defvjp(low_keep, low_pass)
low_back.defvjp(back_keep, back_low)
highest = lax.Precision.HIGHEST
epsilon = 1e-05

def matmul(left, right):
    return jnp.dot(left, right, precision=highest, preferred_element_type=jnp.float32)

def layer_norm(summed, gain, shift):
    centred = summed - lax.optimization_barrier(jnp.mean(summed, axis=1, keepdims=True))
    inverse = lax.rsqrt(lax.optimization_barrier(jnp.mean(centred * centred, axis=1, keepdims=True)) + epsilon)
    return centred * inverse * gain + shift

def forward(tokens, query_weight, key_weight, value_weight, output_weight, query_position, key_position, position_tables, gain_one, shift_one, up_weight, down_weight, gain_two, shift_two, buckets, text_length):
    page_count = buckets.shape[0]
    score_scale = (7.0 * HEAD) ** (-0.5)

    def heads_of(flat):
        return flat.reshape(page_count, PAGE, HEADS, HEAD).transpose(0, 2, 1, 3)
    query_rows = heads_of(low(low_back(matmul(tokens, query_weight))))
    key_rows = heads_of(low(low_back(matmul(tokens, key_weight))))
    value_rows = heads_of(low(low_back(matmul(tokens, value_weight))))
    tables_flat = position_tables.reshape(3 * REL, D)
    pos_key = low(matmul(tables_flat, key_position)).reshape(3, REL, HEADS, HEAD).transpose(0, 2, 1, 3)
    pos_query = low(matmul(tables_flat, query_position)).reshape(3, REL, HEADS, HEAD).transpose(0, 2, 1, 3)

    def page_attention(items):
        queries, keys_page, values_page, bucket, used = items
        raw = jnp.einsum('hse,hte->hst', queries, keys_page, precision=highest)
        for relation in range(3):
            picked = jnp.broadcast_to(bucket[relation][None], raw.shape)
            near_table = low(low_back(jnp.einsum('hse,hbe->hsb', queries, pos_key[relation], precision=highest)))
            raw = raw + jnp.take_along_axis(near_table, picked, axis=2)
            far_table = low(low_back(jnp.einsum('hte,hbe->hbt', keys_page, pos_query[relation], precision=highest)))
            raw = raw + jnp.take_along_axis(far_table, picked, axis=1)
        raw = low_back(raw)
        position = jnp.arange(PAGE)
        key_valid = (position >= TEXT) | (position < used)
        scores = jnp.where(key_valid[None, None, :], raw * score_scale, -1e+30)
        probability = jax.nn.softmax(scores, axis=2)
        return jnp.einsum('hst,hte->hse', low(probability), values_page, precision=highest)
    context = lax.map(jax.checkpoint(page_attention), (query_rows, key_rows, value_rows, buckets, text_length))
    context = low(low_back(context.transpose(0, 2, 1, 3).reshape(-1, D)))
    attended = low_back(matmul(context, output_weight))
    first = layer_norm(tokens + attended, gain_one, shift_one)
    hidden = low(jax.nn.gelu(low_back(matmul(low(first), up_weight)), approximate=False))
    feed = low_back(matmul(hidden, down_weight))
    return layer_norm(first + feed, gain_two, shift_two)

def reference(tokens, query_weight, key_weight, value_weight, output_weight, query_position, key_position, position_tables, gain_one, shift_one, up_weight, down_weight, gain_two, shift_two, buckets, text_length, cotangent):
    floats = tuple((array.astype(jnp.float32) for array in (tokens, query_weight, key_weight, value_weight, output_weight, query_position, key_position, position_tables, gain_one, shift_one, up_weight, down_weight, gain_two, shift_two)))

    def run_layer(*weights):
        return forward(*weights, buckets, text_length)
    layer_output, pullback = jax.vjp(run_layer, *floats)
    gradients = pullback(cotangent.astype(jnp.float32))
    return (layer_output.astype(jnp.bfloat16), gradients[0].astype(jnp.bfloat16), gradients[1], gradients[2], gradients[3], gradients[4], gradients[5], gradients[6], gradients[7], gradients[8], gradients[9], gradients[10], gradients[11], gradients[12], gradients[13])
```

```python
import functools

import jax
import jax.numpy as jnp
from jax import lax
from jax.experimental import pallas as pl
from jax.experimental.pallas import tpu as pltpu
from jax.sharding import PartitionSpec as P

D = 1024
epsilon = 1e-05
highest = lax.Precision.HIGHEST
HEAD = 64
REL = 128
TEXT = 512
bf16 = jnp.bfloat16
f32 = jnp.float32
LIMIT = 10900.0
VMEM_CAP = 62 * 2**20


def lane_gather(table, index):
    numbers = lax.GatherDimensionNumbers(
        offset_dims=(),
        collapsed_slice_dims=(1,),
        start_index_map=(1,),
        operand_batching_dims=(0,),
        start_indices_batching_dims=(0,),
    )
    return lax.gather(
        table, index[..., None], numbers, (1, 1), mode=lax.GatherScatterMode.PROMISE_IN_BOUNDS
    )


def nt(left, right):
    return lax.dot_general(left, right, (((1,), (1,)), ((), ())), preferred_element_type=f32)


def nn(left, right):
    return jnp.dot(left, right, preferred_element_type=f32)


def tn(left, right):
    return lax.dot_general(left, right, (((0,), (0,)), ((), ())), preferred_element_type=f32)


def lane_half(shape):
    return lax.broadcasted_iota(jnp.int32, shape, len(shape) - 1) < HEAD


def unpack_pair(packed):
    low = (packed << 16) >> 16
    high = (packed - low) >> 16
    return high.astype(f32), low.astype(f32)


def forward_kernel(
    used_ref, q_ref, k_ref, v_ref, pk_ref, pq_ref, b_ref,
    p_ref, ctx_ref, bp_ref, bt_ref,
    near_tab, far_tab, near_inv, far_inv, far_sum, near_sum, score, *, span, rows, cols, pairs, scale,
):
    for r in range(3):
        bp_ref[r, span - span % 8:rows, :] = jnp.zeros((rows - span + span % 8, cols), jnp.int32)
        bp_ref[r, :, span - span % 128:cols] = jnp.zeros((rows, cols - span + span % 128), jnp.int32)
        bp_ref[r, 0:span, 0:span] = b_ref[0, r]
    for r in range(3):
        for jb in range(cols // 128):
            high = min(128, rows - jb * 128)
            for ib in range(cols // 128):
                tall = min(128, rows - ib * 128)
                block = bp_ref[r, ib * 128:ib * 128 + tall, jb * 128:(jb + 1) * 128]
                if tall < 128:
                    block = jnp.concatenate([block, jnp.zeros((128 - tall, 128), jnp.int32)], axis=0)
                bt_ref[r, jb * 128:jb * 128 + high, ib * 128:(ib + 1) * 128] = block.T[:high]

    half = lane_half((64, 128))

    def make_tables(src_ref, pos_ref, tab, inv, p):
        cut = slice(p * 128, (p + 1) * 128)

        def body(step, carry):
            at = pl.ds(pl.multiple_of(step * 64, 64), 64)
            block = src_ref[at, cut]
            zero = jnp.zeros_like(block)
            first = nt(jnp.where(half, block, zero), pos_ref[:, cut]).astype(bf16).astype(f32)
            second = nt(jnp.where(half, zero, block), pos_ref[:, cut]).astype(bf16).astype(f32)
            top0 = jnp.maximum(jnp.max(jnp.abs(first), axis=1, keepdims=True), 1e-30)
            top1 = jnp.maximum(jnp.max(jnp.abs(second), axis=1, keepdims=True), 1e-30)
            whole0 = jnp.round(first * (LIMIT / top0)).astype(jnp.int32)
            whole1 = jnp.round(second * (LIMIT / top1)).astype(jnp.int32)
            tab[p, at, :] = whole0 * 65536 + whole1
            inv[2 * p, at, :] = jnp.broadcast_to(top0 * (1.0 / LIMIT), (64, 128))
            inv[2 * p + 1, at, :] = jnp.broadcast_to(top1 * (1.0 / LIMIT), (64, 128))
            return carry

        lax.fori_loop(0, rows // 64, body, 0)

    for p in range(pairs):
        make_tables(q_ref, pk_ref, near_tab, near_inv, p)
        make_tables(k_ref, pq_ref, far_tab, far_inv, p)

    def look_up(tab, index_ref, at, out, out_at):
        for c in range(cols // 128):
            total = [None] * pairs
            for r in range(3):
                index = index_ref[r, at, c * 128:(c + 1) * 128]
                for p in range(pairs):
                    got = lane_gather(tab[p, at, r * 128:(r + 1) * 128], index)
                    total[p] = got if total[p] is None else total[p] + got
            for p in range(pairs):
                out[p, out_at, c * 128:(c + 1) * 128] = total[p]

    def far_body(step, carry):
        at = pl.ds(pl.multiple_of(step * 8, 8), 8)
        look_up(far_tab, bt_ref, at, far_sum, at)
        return carry

    lax.fori_loop(0, rows // 8, far_body, 0)
    for p in range(pairs):
        far_sum[p, rows:, :] = jnp.zeros((cols - rows, cols), jnp.int32)

    used = used_ref[0]
    place = lax.broadcasted_iota(jnp.int32, (1, cols), 1)
    valid = ((place >= TEXT) & (place < span)) | (place < used)
    inv_rows = []
    for h in range(2 * pairs):
        inv_rows.append(jnp.concatenate(
            [far_inv[h, j * 128:min(rows, (j + 1) * 128), :].T[0:1] for j in range(cols // 128 - 1)]
            + [jnp.concatenate([far_inv[h, cols - 128:rows, :],
                                jnp.zeros((cols - rows, 128), f32)], axis=0).T[0:1]], axis=1))

    def block_body(start, tall):
        def near_body(step, carry):
            at = pl.ds(pl.multiple_of(start + step * 8, 8), 8)
            look_up(near_tab, bp_ref, at, near_sum, pl.ds(pl.multiple_of(step * 8, 8), 8))
            return carry

        lax.fori_loop(0, tall // 8, near_body, 0)
        at = pl.ds(start, tall)
        for p in range(pairs):
            cut = slice(p * 128, (p + 1) * 128)
            block = q_ref[at, cut]
            zero = jnp.zeros_like(block)
            mask = lane_half((tall, 128))
            score[0, 0:tall, :] = nt(jnp.where(mask, block, zero), k_ref[:, cut])
            score[1, 0:tall, :] = nt(jnp.where(mask, zero, block), k_ref[:, cut])
            for c in range(cols // 128):
                turned = far_sum[p, c * 128:(c + 1) * 128, pl.ds(start, 128)].T[0:tall]
                here = slice(c * 128, (c + 1) * 128)
                f0, f1 = unpack_pair(turned)
                n0, n1 = unpack_pair(near_sum[p, 0:tall, here])
                score[0, 0:tall, here] += (
                    f0 * inv_rows[2 * p][:, here] + n0 * near_inv[2 * p, at, :]
                )
                score[1, 0:tall, here] += (
                    f1 * inv_rows[2 * p + 1][:, here] + n1 * near_inv[2 * p + 1, at, :]
                )
            for h in range(2):
                for s in range(tall // 16):
                    raw = score[h, s * 16:(s + 1) * 16, :]
                    logits = jnp.where(valid, raw * scale, -1e30)
                    top = jnp.max(logits, axis=1, keepdims=True)
                    grown = jnp.exp(logits - top)
                    share = grown * (1.0 / jnp.sum(grown, axis=1, keepdims=True))
                    p_ref[2 * p + h, pl.ds(pl.multiple_of(start + s * 16, 16), 16), :] = share.astype(bf16)
            c0 = nn(p_ref[2 * p, at, :], v_ref[:, cut])
            c1 = nn(p_ref[2 * p + 1, at, :], v_ref[:, cut])
            ctx_ref[at, cut] = jnp.where(mask, c0, c1).astype(bf16)

    def outer(step, carry):
        block_body(pl.multiple_of(step * 128, 128), 128)
        return carry

    lax.fori_loop(0, rows // 128, outer, 0)
    if rows % 128:
        block_body(rows - rows % 128, rows % 128)


def project_kernel(x_ref, wq_ref, wk_ref, wv_ref, t_ref, kp_ref, qp_ref, qkv_ref, pk_ref, pq_ref, *, span, cols, width):
    tail = span - span % 128
    qkv_ref[span - span % 16:cols, :] = jnp.zeros((cols - span + span % 16, 3 * width), bf16)
    for n, w_ref in enumerate((wq_ref, wk_ref, wv_ref)):
        cut = slice(n * width, (n + 1) * width)

        def body(step, carry, cut=cut, w_ref=w_ref):
            at = pl.ds(pl.multiple_of(step * 128, 128), 128)
            qkv_ref[at, cut] = nn(x_ref[at, :], w_ref[...]).astype(bf16)
            return carry

        lax.fori_loop(0, span // 128, body, 0)
        if tail < span:
            qkv_ref[tail:span, cut] = nn(x_ref[tail:span, :], w_ref[...]).astype(bf16)
    for r in range(3):
        at = slice(r * REL, (r + 1) * REL)
        pk_ref[at, :] = nn(t_ref[r], kp_ref[...]).astype(bf16)
        pq_ref[at, :] = nn(t_ref[r], qp_ref[...]).astype(bf16)


def project(tokens, query_weight, key_weight, value_weight, tables, key_position, query_position, span):
    width = query_weight.shape[1]
    rows, cols = sizes(span)
    whole = pl.BlockSpec(memory_space=pltpu.VMEM)
    return pl.pallas_call(
        functools.partial(project_kernel, span=span, cols=cols, width=width),
        out_shape=(
            jax.ShapeDtypeStruct((cols, 3 * width), bf16),
            jax.ShapeDtypeStruct((3 * REL, width), bf16),
            jax.ShapeDtypeStruct((3 * REL, width), bf16),
        ),
        in_specs=[whole] * 7,
        out_specs=(whole,) * 3,
        compiler_params=pltpu.CompilerParams(vmem_limit_bytes=VMEM_CAP),
        cost_estimate=pl.CostEstimate(flops=4 * 10**9, bytes_accessed=9 * 10**6, transcendentals=0),
        name="project",
    )(tokens, query_weight, key_weight, value_weight, tables, key_position, query_position)


def pick(half, block, h):
    zero = jnp.zeros_like(block)
    return jnp.where(half, block, zero) if h == 0 else jnp.where(half, zero, block)


def draw_kernel(
    p_ref, up_ref, q_ref, k_ref, v_ref,
    d_ref, dt_ref, dq_ref, dk_ref, dv_ref, wide, flat, turned, *, rows, cols, scale,
):
    half = lane_half((64, 128))
    rows_half = lane_half((rows, 128))
    cols_half = lane_half((cols, 128))

    def body(step, carry):
        at = pl.ds(pl.multiple_of(step * 64, 64), 64)
        pair = []
        for h in range(2):
            reach = nt(pick(half, up_ref[at, :], h), v_ref[...])
            share = p_ref[h, at, :].astype(f32)
            inner = jnp.sum(reach * share, axis=1, keepdims=True)
            back = share * (reach - inner) * scale
            wide[h, at, :] = back
            flat[h, at, :] = back.astype(bf16)
            pair.append(back.reshape(8, 8, cols))
        d_ref[pl.ds(pl.multiple_of(step * 8, 8), 8), :, :] = jnp.concatenate(pair, axis=1).astype(bf16)
        return carry

    lax.fori_loop(0, rows // 64, body, 0)
    for jb in range(cols // 128):
        tall = min(128, rows - jb * 128)
        for ib in range(cols // 128):
            wide_rows = min(128, rows - ib * 128)
            pair = []
            for h in range(2):
                block = wide[h, ib * 128:ib * 128 + wide_rows, jb * 128:(jb + 1) * 128]
                if wide_rows < 128:
                    block = jnp.concatenate([block, jnp.zeros((128 - wide_rows, 128), f32)], axis=0)
                other = block.T[:tall]
                turned[h, jb * 128:jb * 128 + tall, ib * 128:(ib + 1) * 128] = other.astype(bf16)
                pair.append(other.reshape(tall // 8, 8, 128))
            dt_ref[jb * 16:jb * 16 + tall // 8, :, ib * 128:(ib + 1) * 128] = jnp.concatenate(
                pair, axis=1
            ).astype(bf16)
    dq_ref[...] = nn(flat[0], pick(cols_half, k_ref[...], 0)) + nn(flat[1], pick(cols_half, k_ref[...], 1))
    dk_ref[...] = nn(turned[0], pick(cols_half, q_ref[...], 0)) + nn(turned[1], pick(cols_half, q_ref[...], 1))
    dv = tn(p_ref[0], pick(rows_half, up_ref[...], 0)) + tn(p_ref[1], pick(rows_half, up_ref[...], 1))
    dv_ref[...] = dv[:rows].astype(bf16)


def scatter_kernel(d_ref, b_ref, merge_ref, out_ref, *, groups, cols):
    base = jnp.where(lax.broadcasted_iota(jnp.int32, (16, cols), 0) >= 8, 1.0, 0.0).astype(bf16)
    own = (lax.broadcasted_iota(jnp.int32, (256, 256), 0) % 8) == (
        lax.broadcasted_iota(jnp.int32, (256, 256), 1) % 8
    )
    zero = jnp.asarray(0.0, bf16)
    one = jnp.asarray(1.0, bf16)

    def body(g, carry):
        back = d_ref[g]
        for r in range(3):
            bucket = b_ref[r, pl.ds(pl.multiple_of(g * 8, 8), 8), :]
            low = (bucket & 31).astype(f32)
            high = (bucket >> 5).astype(f32)
            low = jnp.concatenate([low, low], axis=0).astype(bf16) - base
            high = jnp.concatenate([high, high], axis=0).astype(bf16)
            hot = jnp.concatenate(
                [jnp.where(low == jnp.asarray(2.0 * k, bf16), one, zero) for k in range(16)], axis=0
            )
            sieved = []
            for l in range(4):
                mask = high == jnp.asarray(float(l), bf16)
                for p in range(4):
                    sieved.append(jnp.where(mask, back[p * 16:(p + 1) * 16], zero))
            sums = nt(jnp.concatenate(sieved, axis=0), hot)
            sums = jnp.where(own, sums, 0.0).astype(bf16)
            total = None
            for l in range(4):
                term = nn(sums[l * 64:(l + 1) * 64], merge_ref[l])
                total = term if total is None else total + term
            out_ref[g, :, r * 128:(r + 1) * 128] = total.astype(bf16)
        return carry

    lax.fori_loop(0, groups, body, 0)


def close_kernel(s_ref, base_ref, pos_ref, side_ref, out_ref, table_ref, *, rows):
    rows2 = 2 * rows
    half3 = lane_half((rows // 8, 8, 128))
    flat = s_ref[...].reshape(rows2, 3 * REL)
    both = nn(flat, pos_ref[...]).reshape(rows // 8, 16, 128)
    mine = jnp.where(half3, both[:, 0:8, :], both[:, 8:16, :]).reshape(rows, 128)
    out_ref[...] = (base_ref[...] + mine).astype(bf16)
    side = side_ref[0:rows, :].astype(f32).reshape(rows // 8, 8, 128)
    zero = jnp.zeros_like(side)
    spread = jnp.concatenate([jnp.where(half3, side, zero), jnp.where(half3, zero, side)], axis=1)
    table_ref[...] = tn(flat, spread.reshape(rows2, 128).astype(bf16))


def merge_table():
    l = lax.broadcasted_iota(jnp.int32, (4, 256, 128), 0)
    a = lax.broadcasted_iota(jnp.int32, (4, 256, 128), 1) // 8
    c = lax.broadcasted_iota(jnp.int32, (4, 256, 128), 2)
    return (c == l * 32 + a).astype(bf16)


def sizes(span):
    return -(-span // 64) * 64, -(-span // 128) * 128


def attention_forward(qkv, pos_key, pos_query, buckets, used, scale):
    span = buckets.shape[2]
    rows, cols = sizes(span)
    width = pos_key.shape[1]
    pairs = width // 128
    whole = pl.BlockSpec(memory_space=pltpu.VMEM)
    i32 = jnp.int32

    def kernel(used_ref, qkv_ref, *rest):
        forward_kernel(
            used_ref, qkv_ref.at[:, 0:width], qkv_ref.at[:, width:2 * width],
            qkv_ref.at[:, 2 * width:3 * width], *rest,
            span=span, rows=rows, cols=cols, pairs=pairs, scale=scale,
        )

    return pl.pallas_call(
        kernel,
        out_shape=(
            jax.ShapeDtypeStruct((2 * pairs, rows, cols), bf16),
            jax.ShapeDtypeStruct((rows, width), bf16),
            jax.ShapeDtypeStruct((3, rows, cols), i32),
            jax.ShapeDtypeStruct((3, rows, cols), i32),
        ),
        in_specs=[pl.BlockSpec(memory_space=pltpu.SMEM)] + [whole] * 4,
        out_specs=(whole,) * 4,
        scratch_shapes=[
            pltpu.VMEM((pairs, rows, 3 * REL), i32),
            pltpu.VMEM((pairs, rows, 3 * REL), i32),
            pltpu.VMEM((2 * pairs, rows, 128), f32),
            pltpu.VMEM((2 * pairs, rows, 128), f32),
            pltpu.VMEM((pairs, cols, cols), i32),
            pltpu.VMEM((pairs, 128, cols), i32),
            pltpu.VMEM((2, 128, cols), f32),
        ],
        compiler_params=pltpu.CompilerParams(vmem_limit_bytes=VMEM_CAP),
        cost_estimate=pl.CostEstimate(flops=60000000000, bytes_accessed=25000000, transcendentals=0),
        name="attention_forward",
    )(used, qkv, pos_key, pos_query, buckets)


def attention_draw(share, upstream, qkv, scale):
    heads, rows, cols = share.shape
    width = upstream.shape[1]
    pairs = heads // 2
    groups = rows // 8
    return pl.pallas_call(
        functools.partial(draw_kernel, rows=rows, cols=cols, scale=scale),
        grid=(pairs,),
        in_specs=[
            pl.BlockSpec((2, rows, cols), lambda p: (p, 0, 0)),
            pl.BlockSpec((rows, 128), lambda p: (0, p)),
            pl.BlockSpec((cols, 128), lambda p: (0, p)),
            pl.BlockSpec((cols, 128), lambda p: (0, p + pairs)),
            pl.BlockSpec((cols, 128), lambda p: (0, p + 2 * pairs)),
        ],
        out_specs=(
            pl.BlockSpec((groups, 16, cols), lambda p: (0, p, 0)),
            pl.BlockSpec((groups, 16, cols), lambda p: (0, p, 0)),
            pl.BlockSpec((rows, 128), lambda p: (0, p)),
            pl.BlockSpec((rows, 128), lambda p: (0, p)),
            pl.BlockSpec((rows, 128), lambda p: (0, p)),
        ),
        out_shape=(
            jax.ShapeDtypeStruct((groups, 8 * heads, cols), bf16),
            jax.ShapeDtypeStruct((groups, 8 * heads, cols), bf16),
            jax.ShapeDtypeStruct((rows, width), f32),
            jax.ShapeDtypeStruct((rows, width), f32),
            jax.ShapeDtypeStruct((rows, width), bf16),
        ),
        scratch_shapes=[
            pltpu.VMEM((2, rows, cols), f32),
            pltpu.VMEM((2, rows, cols), bf16),
            pltpu.VMEM((2, rows, cols), bf16),
        ],
        compiler_params=pltpu.CompilerParams(vmem_limit_bytes=VMEM_CAP),
        cost_estimate=pl.CostEstimate(flops=20000000000, bytes_accessed=25000000, transcendentals=0),
        name="attention_draw",
    )(share, upstream, qkv, qkv, qkv)


def attention_scatter(back, buckets, merge):
    groups, _, cols = back.shape
    whole = pl.BlockSpec(memory_space=pltpu.VMEM)
    return pl.pallas_call(
        functools.partial(scatter_kernel, groups=groups, cols=cols),
        out_shape=jax.ShapeDtypeStruct((groups, back.shape[1], 3 * REL), bf16),
        in_specs=[whole] * 3,
        out_specs=whole,
        compiler_params=pltpu.CompilerParams(vmem_limit_bytes=VMEM_CAP),
        cost_estimate=pl.CostEstimate(flops=70000000000, bytes_accessed=12000000, transcendentals=0),
        name="attention_scatter",
    )(back, buckets, merge)


def attention_close(sums, base, pos, qkv, side):
    rows, width = base.shape
    pairs = width // 128
    groups = rows // 8
    return pl.pallas_call(
        functools.partial(close_kernel, rows=rows),
        grid=(pairs,),
        in_specs=[
            pl.BlockSpec((groups, 16, 3 * REL), lambda p: (0, p, 0)),
            pl.BlockSpec((rows, 128), lambda p: (0, p)),
            pl.BlockSpec((3 * REL, 128), lambda p: (0, p)),
            pl.BlockSpec((qkv.shape[0], 128), lambda p: (0, p + side * pairs)),
        ],
        out_specs=(
            pl.BlockSpec((rows, 128), lambda p: (0, p)),
            pl.BlockSpec((3 * REL, 128), lambda p: (0, p)),
        ),
        out_shape=(
            jax.ShapeDtypeStruct((rows, width), bf16),
            jax.ShapeDtypeStruct((3 * REL, width), f32),
        ),
        compiler_params=pltpu.CompilerParams(vmem_limit_bytes=VMEM_CAP),
        cost_estimate=pl.CostEstimate(flops=5000000000, bytes_accessed=10000000, transcendentals=0),
        name="attention_close",
    )(sums, base, pos, qkv)

def exact_left(left, right):
    return lax.dot_general(
        left, right, (((0,), (0,)), ((), ())), precision=highest, preferred_element_type=jnp.float32
    )


def exact_right(left, right):
    return lax.dot_general(
        left, right, (((1,), (1,)), ((), ())), precision=highest, preferred_element_type=jnp.float32
    )


def norm_forward(summed, gain, shift):
    centred = summed - jnp.mean(summed, axis=1, keepdims=True)
    inverse = lax.rsqrt(jnp.mean(centred * centred, axis=1, keepdims=True) + epsilon)
    normal = centred * inverse
    return (normal * gain + shift, normal, inverse)


def norm_backward(upstream, normal, inverse, gain):
    scaled = upstream * gain
    inner = jnp.mean(scaled, axis=1, keepdims=True)
    aligned = jnp.mean(scaled * normal, axis=1, keepdims=True)
    return (
        inverse * (scaled - inner - normal * aligned),
        jnp.sum(upstream * normal, axis=0),
        jnp.sum(upstream, axis=0),
    )


def shards(
    tokens,
    query_weight,
    key_weight,
    value_weight,
    output_weight,
    query_position,
    key_position,
    position_tables,
    gain_one,
    shift_one,
    up_weight,
    down_weight,
    gain_two,
    shift_two,
    buckets,
    text_length,
    cotangent,
):
    span = buckets.shape[2]
    rows, cols = sizes(span)
    score_scale = (7.0 * HEAD) ** (-0.5)
    tables_flat = position_tables.reshape(3 * REL, D)
    qkv, pos_key, pos_query = project(
        tokens, query_weight, key_weight, value_weight, position_tables, key_position, query_position, span
    )
    share, context, bucket_rows, bucket_cols = attention_forward(
        qkv, pos_key, pos_query, buckets, text_length, score_scale
    )
    context = context[:span]
    attended = lax.psum(nn(context, output_weight), "mp")
    first, normal_one, inverse_one = norm_forward(
        tokens.astype(f32) + attended, gain_one, shift_one
    )
    first_low = first.astype(bf16)
    upward = nn(first_low, up_weight)
    hidden = jax.nn.gelu(upward, approximate=False).astype(bf16)
    feed = lax.psum(nn(hidden, down_weight), "mp")
    final, normal_two, inverse_two = norm_forward(first + feed, gain_two, shift_two)
    layer_output = final.astype(bf16)
    second_back, gain_two_grad, shift_two_grad = norm_backward(
        cotangent.astype(f32), normal_two, inverse_two, gain_two
    )
    second_low = second_back.astype(bf16)
    down_grad = tn(hidden, second_low)
    hidden_back = nt(second_low, down_weight)
    gelu_back = jax.vjp(lambda inner_value: jax.nn.gelu(inner_value, approximate=False), upward)[1]
    upward_back = gelu_back(hidden_back)[0].astype(bf16)
    up_grad = tn(first_low, upward_back)
    first_back = second_back + lax.psum(nt(upward_back, up_weight), "mp")
    residual_back, gain_one_grad, shift_one_grad = norm_backward(
        first_back, normal_one, inverse_one, gain_one
    )
    residual_low = residual_back.astype(bf16)
    output_grad = tn(context, residual_low)
    context_back = jnp.pad(nt(residual_low, output_weight).astype(bf16), ((0, rows - span), (0, 0)))

    merge = merge_table()
    back, back_turned, query_base, key_base, value_back = attention_draw(
        share, context_back, qkv, score_scale
    )
    near_sums = attention_scatter(back, bucket_rows, merge)
    query_back, key_table_sum = attention_close(near_sums, query_base, pos_key, qkv, 0)
    far_sums = attention_scatter(back_turned, bucket_cols, merge)
    key_back, query_table_sum = attention_close(far_sums, key_base, pos_query, qkv, 1)
    query_flat, key_flat, value_flat = query_back[:span], key_back[:span], value_back[:span]
    query_grad = tn(tokens, query_flat)
    key_grad = tn(tokens, key_flat)
    value_grad = tn(tokens, value_flat)
    input_part = (
        nt(query_flat, query_weight) + nt(key_flat, key_weight) + nt(value_flat, value_weight)
    )
    input_gradient = (residual_back + lax.psum(input_part, "mp")).astype(bf16)
    tables_wide = tables_flat.astype(f32)
    key_position_grad = exact_left(tables_wide, key_table_sum)
    query_position_grad = exact_left(tables_wide, query_table_sum)
    table_part = exact_right(key_table_sum, key_position.astype(f32)) + exact_right(
        query_table_sum, query_position.astype(f32)
    )
    table_gradient = lax.psum_scatter(
        table_part.reshape(3, REL, D), ("dp", "mp"), scatter_dimension=2, tiled=True
    )
    summed = (
        lax.psum_scatter(query_grad, "dp", scatter_dimension=0, tiled=True),
        lax.psum_scatter(key_grad, "dp", scatter_dimension=0, tiled=True),
        lax.psum_scatter(value_grad, "dp", scatter_dimension=0, tiled=True),
        lax.psum_scatter(output_grad, "dp", scatter_dimension=1, tiled=True),
        lax.psum_scatter(query_position_grad, "dp", scatter_dimension=0, tiled=True),
        lax.psum_scatter(key_position_grad, "dp", scatter_dimension=0, tiled=True),
        lax.psum_scatter(up_grad, "dp", scatter_dimension=0, tiled=True),
        lax.psum_scatter(down_grad, "dp", scatter_dimension=1, tiled=True),
        lax.psum_scatter(gain_one_grad, "dp", scatter_dimension=0, tiled=True),
        lax.psum_scatter(shift_one_grad, "dp", scatter_dimension=0, tiled=True),
        lax.psum_scatter(gain_two_grad, "dp", scatter_dimension=0, tiled=True),
        lax.psum_scatter(shift_two_grad, "dp", scatter_dimension=0, tiled=True),
    )
    return (
        layer_output,
        input_gradient,
        summed[0],
        summed[1],
        summed[2],
        summed[3],
        summed[4],
        summed[5],
        table_gradient,
        summed[8],
        summed[9],
        summed[6],
        summed[7],
        summed[10],
        summed[11],
    )


def solution(mesh):
    return jax.shard_map(
        shards,
        mesh=mesh,
        in_specs=(
            P("dp", None),
            P(None, "mp"),
            P(None, "mp"),
            P(None, "mp"),
            P("mp", None),
            P(None, "mp"),
            P(None, "mp"),
            P(),
            P(),
            P(),
            P(None, "mp"),
            P("mp", None),
            P(),
            P(),
            P("dp", None, None, None),
            P("dp"),
            P("dp", None),
        ),
        out_specs=(
            P("dp", None),
            P("dp", None),
            P("dp", "mp"),
            P("dp", "mp"),
            P("dp", "mp"),
            P("mp", "dp"),
            P("dp", "mp"),
            P("dp", "mp"),
            P(None, None, ("dp", "mp")),
            P("dp"),
            P("dp"),
            P("dp", "mp"),
            P("mp", "dp"),
            P("dp"),
            P("dp"),
        ),
        check_vma=False,
    )
```

```python
import functools

import jax
import jax.numpy as jnp
from jax import lax
from jax.experimental import pallas as pl
from jax.experimental.pallas import tpu as pltpu
from jax.sharding import PartitionSpec as P

D = 1024
epsilon = 1e-05
HEAD = 64
REL = 128
TEXT = 512
bf16 = jnp.bfloat16
f32 = jnp.float32
LIMIT = 10900.0
VMEM_CAP = 62 * 2**20


def lane_gather(table, index):
    numbers = lax.GatherDimensionNumbers(
        offset_dims=(),
        collapsed_slice_dims=(1,),
        start_index_map=(1,),
        operand_batching_dims=(0,),
        start_indices_batching_dims=(0,),
    )
    return lax.gather(
        table, index[..., None], numbers, (1, 1), mode=lax.GatherScatterMode.PROMISE_IN_BOUNDS
    )


def nt(left, right):
    return lax.dot_general(left, right, (((1,), (1,)), ((), ())), preferred_element_type=f32)


def nn(left, right):
    return jnp.dot(left, right, preferred_element_type=f32)


def tn(left, right):
    return lax.dot_general(left, right, (((0,), (0,)), ((), ())), preferred_element_type=f32)


def lane_half(shape):
    return lax.broadcasted_iota(jnp.int32, shape, len(shape) - 1) < HEAD


def unpack_pair(packed):
    low = (packed << 16) >> 16
    high = (packed - low) >> 16
    return high.astype(f32), low.astype(f32)


def forward_kernel(
    used_ref, q_ref, k_ref, v_ref, pk_ref, pq_ref, b_ref,
    p_ref, ctx_ref, bp_ref, bt_ref,
    near_tab, far_tab, near_inv, far_inv, far_sum, near_sum, score, *, span, rows, cols, pairs, scale,
):
    for r in range(3):
        bp_ref[r, span - span % 8:rows, :] = jnp.zeros((rows - span + span % 8, cols), jnp.int32)
        bp_ref[r, :, span - span % 128:cols] = jnp.zeros((rows, cols - span + span % 128), jnp.int32)
        bp_ref[r, 0:span, 0:span] = b_ref[0, r]
    for r in range(3):
        for jb in range(cols // 128):
            high = min(128, rows - jb * 128)
            for ib in range(cols // 128):
                tall = min(128, rows - ib * 128)
                block = bp_ref[r, ib * 128:ib * 128 + tall, jb * 128:(jb + 1) * 128]
                if tall < 128:
                    block = jnp.concatenate([block, jnp.zeros((128 - tall, 128), jnp.int32)], axis=0)
                bt_ref[r, jb * 128:jb * 128 + high, ib * 128:(ib + 1) * 128] = block.T[:high]

    half = lane_half((64, 128))

    def make_tables(src_ref, pos_ref, tab, inv, p):
        cut = slice(p * 128, (p + 1) * 128)

        def body(step, carry):
            at = pl.ds(pl.multiple_of(step * 64, 64), 64)
            block = src_ref[at, cut]
            zero = jnp.zeros_like(block)
            first = nt(jnp.where(half, block, zero), pos_ref[:, cut]).astype(bf16).astype(f32)
            second = nt(jnp.where(half, zero, block), pos_ref[:, cut]).astype(bf16).astype(f32)
            top0 = jnp.maximum(jnp.max(jnp.abs(first), axis=1, keepdims=True), 1e-30)
            top1 = jnp.maximum(jnp.max(jnp.abs(second), axis=1, keepdims=True), 1e-30)
            whole0 = jnp.round(first * (LIMIT / top0)).astype(jnp.int32)
            whole1 = jnp.round(second * (LIMIT / top1)).astype(jnp.int32)
            tab[p, at, :] = whole0 * 65536 + whole1
            inv[2 * p, at, :] = jnp.broadcast_to(top0 * (1.0 / LIMIT), (64, 128))
            inv[2 * p + 1, at, :] = jnp.broadcast_to(top1 * (1.0 / LIMIT), (64, 128))
            return carry

        lax.fori_loop(0, rows // 64, body, 0)

    for p in range(pairs):
        make_tables(q_ref, pk_ref, near_tab, near_inv, p)
        make_tables(k_ref, pq_ref, far_tab, far_inv, p)

    def look_up(tab, index_ref, at, out, out_at):
        for c in range(cols // 128):
            total = [None] * pairs
            for r in range(3):
                index = index_ref[r, at, c * 128:(c + 1) * 128]
                for p in range(pairs):
                    got = lane_gather(tab[p, at, r * 128:(r + 1) * 128], index)
                    total[p] = got if total[p] is None else total[p] + got
            for p in range(pairs):
                out[p, out_at, c * 128:(c + 1) * 128] = total[p]

    def far_body(step, carry):
        at = pl.ds(pl.multiple_of(step * 8, 8), 8)
        look_up(far_tab, bt_ref, at, far_sum, at)
        return carry

    lax.fori_loop(0, rows // 8, far_body, 0)
    for p in range(pairs):
        far_sum[p, rows:, :] = jnp.zeros((cols - rows, cols), jnp.int32)

    used = used_ref[0]
    place = lax.broadcasted_iota(jnp.int32, (1, cols), 1)
    valid = ((place >= TEXT) & (place < span)) | (place < used)
    inv_rows = []
    for h in range(2 * pairs):
        inv_rows.append(jnp.concatenate(
            [far_inv[h, j * 128:min(rows, (j + 1) * 128), :].T[0:1] for j in range(cols // 128 - 1)]
            + [jnp.concatenate([far_inv[h, cols - 128:rows, :],
                                jnp.zeros((cols - rows, 128), f32)], axis=0).T[0:1]], axis=1))

    def block_body(start, tall):
        def near_body(step, carry):
            at = pl.ds(pl.multiple_of(start + step * 8, 8), 8)
            look_up(near_tab, bp_ref, at, near_sum, pl.ds(pl.multiple_of(step * 8, 8), 8))
            return carry

        lax.fori_loop(0, tall // 8, near_body, 0)
        at = pl.ds(start, tall)
        for p in range(pairs):
            cut = slice(p * 128, (p + 1) * 128)
            block = q_ref[at, cut]
            zero = jnp.zeros_like(block)
            mask = lane_half((tall, 128))
            score[0, 0:tall, :] = nt(jnp.where(mask, block, zero), k_ref[:, cut])
            score[1, 0:tall, :] = nt(jnp.where(mask, zero, block), k_ref[:, cut])
            for c in range(cols // 128):
                turned = far_sum[p, c * 128:(c + 1) * 128, pl.ds(start, 128)].T[0:tall]
                here = slice(c * 128, (c + 1) * 128)
                f0, f1 = unpack_pair(turned)
                n0, n1 = unpack_pair(near_sum[p, 0:tall, here])
                score[0, 0:tall, here] += (
                    f0 * inv_rows[2 * p][:, here] + n0 * near_inv[2 * p, at, :]
                )
                score[1, 0:tall, here] += (
                    f1 * inv_rows[2 * p + 1][:, here] + n1 * near_inv[2 * p + 1, at, :]
                )
            for h in range(2):
                for s in range(tall // 16):
                    raw = score[h, s * 16:(s + 1) * 16, :]
                    logits = jnp.where(valid, raw * scale, -1e30)
                    top = jnp.max(logits, axis=1, keepdims=True)
                    grown = jnp.exp(logits - top)
                    share = grown * (1.0 / jnp.sum(grown, axis=1, keepdims=True))
                    p_ref[2 * p + h, pl.ds(pl.multiple_of(start + s * 16, 16), 16), :] = share.astype(bf16)
            c0 = nn(p_ref[2 * p, at, :], v_ref[:, cut])
            c1 = nn(p_ref[2 * p + 1, at, :], v_ref[:, cut])
            ctx_ref[at, cut] = jnp.where(mask, c0, c1).astype(bf16)

    def outer(step, carry):
        block_body(pl.multiple_of(step * 128, 128), 128)
        return carry

    lax.fori_loop(0, rows // 128, outer, 0)
    if rows % 128:
        block_body(rows - rows % 128, rows % 128)


def project_kernel(x_ref, wq_ref, wk_ref, wv_ref, t_ref, kp_ref, qp_ref, qkv_ref, pk_ref, pq_ref, *, span, cols, width):
    tail = span - span % 128
    qkv_ref[span - span % 16:cols, :] = jnp.zeros((cols - span + span % 16, 3 * width), bf16)
    for n, w_ref in enumerate((wq_ref, wk_ref, wv_ref)):
        cut = slice(n * width, (n + 1) * width)

        def body(step, carry, cut=cut, w_ref=w_ref):
            at = pl.ds(pl.multiple_of(step * 128, 128), 128)
            qkv_ref[at, cut] = nn(x_ref[at, :], w_ref[...]).astype(bf16)
            return carry

        lax.fori_loop(0, span // 128, body, 0)
        if tail < span:
            qkv_ref[tail:span, cut] = nn(x_ref[tail:span, :], w_ref[...]).astype(bf16)
    for r in range(3):
        at = slice(r * REL, (r + 1) * REL)
        pk_ref[at, :] = nn(t_ref[r], kp_ref[...]).astype(bf16)
        pq_ref[at, :] = nn(t_ref[r], qp_ref[...]).astype(bf16)


def project(tokens, query_weight, key_weight, value_weight, tables, key_position, query_position, span):
    width = query_weight.shape[1]
    rows, cols = sizes(span)
    whole = pl.BlockSpec(memory_space=pltpu.VMEM)
    return pl.pallas_call(
        functools.partial(project_kernel, span=span, cols=cols, width=width),
        out_shape=(
            jax.ShapeDtypeStruct((cols, 3 * width), bf16),
            jax.ShapeDtypeStruct((3 * REL, width), bf16),
            jax.ShapeDtypeStruct((3 * REL, width), bf16),
        ),
        in_specs=[whole] * 7,
        out_specs=(whole,) * 3,
        compiler_params=pltpu.CompilerParams(vmem_limit_bytes=VMEM_CAP),
        cost_estimate=pl.CostEstimate(flops=4 * 10**9, bytes_accessed=9 * 10**6, transcendentals=0),
        name="project",
    )(tokens, query_weight, key_weight, value_weight, tables, key_position, query_position)


def pick(half, block, h):
    zero = jnp.zeros_like(block)
    return jnp.where(half, block, zero) if h == 0 else jnp.where(half, zero, block)


def draw_kernel(
    p_ref, up_ref, q_ref, k_ref, v_ref,
    d_ref, dt_ref, dq_ref, dk_ref, dv_ref, wide, flat, turned, *, rows, cols, scale,
):
    half = lane_half((64, 128))
    rows_half = lane_half((rows, 128))
    cols_half = lane_half((cols, 128))

    def body(step, carry):
        at = pl.ds(pl.multiple_of(step * 64, 64), 64)
        pair = []
        for h in range(2):
            reach = nt(pick(half, up_ref[at, :], h), v_ref[...])
            share = p_ref[h, at, :].astype(f32)
            inner = jnp.sum(reach * share, axis=1, keepdims=True)
            back = share * (reach - inner) * scale
            wide[h, at, :] = back
            flat[h, at, :] = back.astype(bf16)
            pair.append(back.reshape(8, 8, cols))
        d_ref[pl.ds(pl.multiple_of(step * 8, 8), 8), :, :] = jnp.concatenate(pair, axis=1).astype(bf16)
        return carry

    lax.fori_loop(0, rows // 64, body, 0)
    for jb in range(cols // 128):
        tall = min(128, rows - jb * 128)
        for ib in range(cols // 128):
            wide_rows = min(128, rows - ib * 128)
            pair = []
            for h in range(2):
                block = wide[h, ib * 128:ib * 128 + wide_rows, jb * 128:(jb + 1) * 128]
                if wide_rows < 128:
                    block = jnp.concatenate([block, jnp.zeros((128 - wide_rows, 128), f32)], axis=0)
                other = block.T[:tall]
                turned[h, jb * 128:jb * 128 + tall, ib * 128:(ib + 1) * 128] = other.astype(bf16)
                pair.append(other.reshape(tall // 8, 8, 128))
            dt_ref[jb * 16:jb * 16 + tall // 8, :, ib * 128:(ib + 1) * 128] = jnp.concatenate(
                pair, axis=1
            ).astype(bf16)
    dq_ref[...] = nn(flat[0], pick(cols_half, k_ref[...], 0)) + nn(flat[1], pick(cols_half, k_ref[...], 1))
    dk_ref[...] = nn(turned[0], pick(cols_half, q_ref[...], 0)) + nn(turned[1], pick(cols_half, q_ref[...], 1))
    dv = tn(p_ref[0], pick(rows_half, up_ref[...], 0)) + tn(p_ref[1], pick(rows_half, up_ref[...], 1))
    dv_ref[...] = dv[:rows].astype(bf16)


def scatter_kernel(d_ref, b_ref, merge_ref, out_ref, *, groups, cols):
    base = jnp.where(lax.broadcasted_iota(jnp.int32, (16, cols), 0) >= 8, 1.0, 0.0).astype(bf16)
    own = (lax.broadcasted_iota(jnp.int32, (256, 256), 0) % 8) == (
        lax.broadcasted_iota(jnp.int32, (256, 256), 1) % 8
    )
    zero = jnp.asarray(0.0, bf16)
    one = jnp.asarray(1.0, bf16)

    def body(g, carry):
        back = d_ref[g]
        for r in range(3):
            bucket = b_ref[r, pl.ds(pl.multiple_of(g * 8, 8), 8), :]
            low = (bucket & 31).astype(f32)
            high = (bucket >> 5).astype(f32)
            low = jnp.concatenate([low, low], axis=0).astype(bf16) - base
            high = jnp.concatenate([high, high], axis=0).astype(bf16)
            hot = jnp.concatenate(
                [jnp.where(low == jnp.asarray(2.0 * k, bf16), one, zero) for k in range(16)], axis=0
            )
            sieved = []
            for l in range(4):
                mask = high == jnp.asarray(float(l), bf16)
                for p in range(4):
                    sieved.append(jnp.where(mask, back[p * 16:(p + 1) * 16], zero))
            sums = nt(jnp.concatenate(sieved, axis=0), hot)
            sums = jnp.where(own, sums, 0.0).astype(bf16)
            total = None
            for l in range(4):
                term = nn(sums[l * 64:(l + 1) * 64], merge_ref[l])
                total = term if total is None else total + term
            out_ref[g, :, r * 128:(r + 1) * 128] = total.astype(bf16)
        return carry

    lax.fori_loop(0, groups, body, 0)


def close_kernel(*refs, rows, count):
    base_ref, pos_ref, side_ref, out_ref, table_ref = refs[count:]
    rows2 = 2 * rows
    half3 = lane_half((rows // 8, 8, 128))
    flat = jnp.concatenate([ref[...] for ref in refs[:count]], axis=0).reshape(rows2, 3 * REL)
    both = nn(flat, pos_ref[...]).reshape(rows // 8, 16, 128)
    mine = jnp.where(half3, both[:, 0:8, :], both[:, 8:16, :]).reshape(rows, 128)
    out_ref[...] = base_ref[...] + mine
    side = side_ref[0:rows, :].astype(f32).reshape(rows // 8, 8, 128)
    zero = jnp.zeros_like(side)
    spread = jnp.concatenate([jnp.where(half3, side, zero), jnp.where(half3, zero, side)], axis=1)
    table_ref[...] = tn(flat, spread.reshape(rows2, 128).astype(bf16)).astype(bf16)


def merge_table():
    l = lax.broadcasted_iota(jnp.int32, (4, 256, 128), 0)
    a = lax.broadcasted_iota(jnp.int32, (4, 256, 128), 1) // 8
    c = lax.broadcasted_iota(jnp.int32, (4, 256, 128), 2)
    return (c == l * 32 + a).astype(bf16)


def sizes(span):
    return -(-span // 64) * 64, -(-span // 128) * 128


def attention_forward(qkv, pos_key, pos_query, buckets, used, scale):
    span = buckets.shape[2]
    rows, cols = sizes(span)
    width = pos_key.shape[1]
    pairs = width // 128
    whole = pl.BlockSpec(memory_space=pltpu.VMEM)
    i32 = jnp.int32

    def kernel(used_ref, qkv_ref, *rest):
        forward_kernel(
            used_ref, qkv_ref.at[:, 0:width], qkv_ref.at[:, width:2 * width],
            qkv_ref.at[:, 2 * width:3 * width], *rest,
            span=span, rows=rows, cols=cols, pairs=pairs, scale=scale,
        )

    return pl.pallas_call(
        kernel,
        out_shape=(
            jax.ShapeDtypeStruct((2 * pairs, rows, cols), bf16),
            jax.ShapeDtypeStruct((rows, width), bf16),
            jax.ShapeDtypeStruct((3, rows, cols), i32),
            jax.ShapeDtypeStruct((3, rows, cols), i32),
        ),
        in_specs=[pl.BlockSpec(memory_space=pltpu.SMEM)] + [whole] * 4,
        out_specs=(whole,) * 4,
        scratch_shapes=[
            pltpu.VMEM((pairs, rows, 3 * REL), i32),
            pltpu.VMEM((pairs, rows, 3 * REL), i32),
            pltpu.VMEM((2 * pairs, rows, 128), f32),
            pltpu.VMEM((2 * pairs, rows, 128), f32),
            pltpu.VMEM((pairs, cols, cols), i32),
            pltpu.VMEM((pairs, 128, cols), i32),
            pltpu.VMEM((2, 128, cols), f32),
        ],
        compiler_params=pltpu.CompilerParams(vmem_limit_bytes=VMEM_CAP),
        cost_estimate=pl.CostEstimate(flops=60000000000, bytes_accessed=25000000, transcendentals=0),
        name="attention_forward",
    )(used, qkv, pos_key, pos_query, buckets)


def attention_draw(share, upstream, qkv, scale):
    heads, rows, cols = share.shape
    width = upstream.shape[1]
    pairs = heads // 2
    groups = rows // 8
    return pl.pallas_call(
        functools.partial(draw_kernel, rows=rows, cols=cols, scale=scale),
        grid=(pairs,),
        in_specs=[
            pl.BlockSpec((2, rows, cols), lambda p: (p, 0, 0)),
            pl.BlockSpec((rows, 128), lambda p: (0, p)),
            pl.BlockSpec((cols, 128), lambda p: (0, p)),
            pl.BlockSpec((cols, 128), lambda p: (0, p + pairs)),
            pl.BlockSpec((cols, 128), lambda p: (0, p + 2 * pairs)),
        ],
        out_specs=(
            pl.BlockSpec((groups, 16, cols), lambda p: (0, p, 0)),
            pl.BlockSpec((groups, 16, cols), lambda p: (0, p, 0)),
            pl.BlockSpec((rows, 128), lambda p: (0, p)),
            pl.BlockSpec((rows, 128), lambda p: (0, p)),
            pl.BlockSpec((rows, 128), lambda p: (0, p)),
        ),
        out_shape=(
            jax.ShapeDtypeStruct((groups, 8 * heads, cols), bf16),
            jax.ShapeDtypeStruct((groups, 8 * heads, cols), bf16),
            jax.ShapeDtypeStruct((rows, width), f32),
            jax.ShapeDtypeStruct((rows, width), f32),
            jax.ShapeDtypeStruct((rows, width), bf16),
        ),
        scratch_shapes=[
            pltpu.VMEM((2, rows, cols), f32),
            pltpu.VMEM((2, rows, cols), bf16),
            pltpu.VMEM((2, rows, cols), bf16),
        ],
        compiler_params=pltpu.CompilerParams(vmem_limit_bytes=VMEM_CAP),
        cost_estimate=pl.CostEstimate(flops=20000000000, bytes_accessed=25000000, transcendentals=0),
        name="attention_draw",
    )(share, upstream, qkv, qkv, qkv)


def attention_scatter(back, buckets, merge, part, count):
    groups, high, cols = back.shape
    groups = groups // count
    whole = pl.BlockSpec(memory_space=pltpu.VMEM)
    return pl.pallas_call(
        functools.partial(scatter_kernel, groups=groups, cols=cols),
        grid=(1,),
        out_shape=jax.ShapeDtypeStruct((groups, high, 3 * REL), bf16),
        in_specs=[
            pl.BlockSpec((groups, high, cols), lambda g: (part, 0, 0)),
            pl.BlockSpec((3, groups * 8, cols), lambda g: (0, part, 0)),
            whole,
        ],
        out_specs=pl.BlockSpec((groups, high, 3 * REL), lambda g: (0, 0, 0)),
        compiler_params=pltpu.CompilerParams(vmem_limit_bytes=VMEM_CAP),
        cost_estimate=pl.CostEstimate(flops=7 * 10**10 // count, bytes_accessed=12 * 10**6 // count, transcendentals=0),
        name="attention_scatter",
    )(back, buckets, merge)


def attention_close(sums, base, pos, qkv, side):
    rows, width = base.shape
    pairs = width // 128
    groups = rows // 8
    return pl.pallas_call(
        functools.partial(close_kernel, rows=rows, count=len(sums)),
        grid=(pairs,),
        in_specs=[
            pl.BlockSpec((groups // len(sums), 16, 3 * REL), lambda p: (0, p, 0))
        ] * len(sums) + [
            pl.BlockSpec((rows, 128), lambda p: (0, p)),
            pl.BlockSpec((3 * REL, 128), lambda p: (0, p)),
            pl.BlockSpec((qkv.shape[0], 128), lambda p: (0, p + side * pairs)),
        ],
        out_specs=(
            pl.BlockSpec((rows, 128), lambda p: (0, p)),
            pl.BlockSpec((3 * REL, 128), lambda p: (0, p)),
        ),
        out_shape=(
            jax.ShapeDtypeStruct((rows, width), f32),
            jax.ShapeDtypeStruct((3 * REL, width), bf16),
        ),
        compiler_params=pltpu.CompilerParams(vmem_limit_bytes=VMEM_CAP),
        cost_estimate=pl.CostEstimate(flops=5000000000, bytes_accessed=10000000, transcendentals=0),
        name="attention_close",
    )(*sums, base, pos, qkv)


def fill_turned(x_ref, turned, rows):
    depth = x_ref.shape[1]
    for a in range(0, rows, 128):
        tall = min(128, rows - a)
        for b in range(0, depth, 128):
            block = x_ref[a:a + tall, b:b + 128]
            if tall < 128:
                block = jnp.concatenate([block, jnp.zeros((128 - tall, 128), block.dtype)], axis=0)
            turned[b:b + 128, a:a + tall] = block.T[:, :tall]


def each_block(pick_ref, blocks, keeps, bit, slot):
    if not keeps:
        return [(0, d, d) for d in range(blocks)]
    shift = bit - 1
    listed = []
    for out in range(2):
        value = pick_ref[slot] if out == 1 else 1 - pick_ref[slot]
        for e in range(blocks // 2):
            low = e & ((1 << shift) - 1)
            listed.append((out, e, ((e >> shift) << (shift + 1)) + low + value * (1 << shift)))
    return listed


def weight_kernel(pick_ref, x_ref, y_ref, *rest, rows, blocks, deep, keeps, bit):
    add_ref = rest[0] if keeps else None
    outs = rest[1:3] if keeps else rest[0:1]
    turned = rest[-1]

    @pl.when(pl.program_id(0) == 0)
    def _():
        fill_turned(x_ref, turned, rows)

    for out, place, d in each_block(pick_ref, blocks, keeps, bit, 1):
        at = pl.ds(pl.multiple_of((2 * d + pick_ref[0]) * deep, deep), deep)
        part = nn(turned[at, :], y_ref[...])
        outs[out][place] = part + add_ref[d] if keeps else part


def weight_half(pick, x, y, add=None, *, parts, bits, tile=512):
    rows, depth = x.shape
    wide = y.shape[1]
    deep = depth // parts
    blocks = parts // 2
    keeps = add is not None

    def tiled(n):
        return pl.BlockSpec((n, deep, tile), lambda c: (0, 0, c))

    ins = [
        pl.BlockSpec(memory_space=pltpu.SMEM),
        pl.BlockSpec((rows, depth), lambda c: (0, 0)),
        pl.BlockSpec((rows, tile), lambda c: (0, c)),
    ]
    args = [pick, x, y]
    shape = (jax.ShapeDtypeStruct((blocks, deep, wide), f32),)
    specs = (tiled(blocks),)
    if keeps:
        ins.append(tiled(blocks))
        args += add
        shape = (jax.ShapeDtypeStruct((blocks // 2, deep, wide), f32),) * 2
        specs = (tiled(blocks // 2),) * 2
    return pl.pallas_call(
        functools.partial(weight_kernel, rows=rows, blocks=blocks, deep=deep, keeps=keeps, bit=bits[0]),
        grid=(wide // tile,),
        in_specs=ins,
        out_specs=specs,
        out_shape=shape,
        scratch_shapes=[pltpu.VMEM((depth, rows), bf16)],
        compiler_params=pltpu.CompilerParams(vmem_limit_bytes=VMEM_CAP),
        cost_estimate=pl.CostEstimate(
            flops=rows * depth * wide, bytes_accessed=4 * depth * wide, transcendentals=0
        ),
        name="weight_half",
    )(*args)


def many_kernel(pick_ref, *refs, plan, widths, turns, blocks, deep, keeps, bits):
    n_in = 2 * len(plan)
    ins = refs[:n_in]
    n_out = len(widths)
    adds = refs[n_in:n_in + n_out] if keeps else None
    outs = refs[n_in + n_out:n_in + 3 * n_out] if keeps else refs[n_in:n_in + n_out]
    scratch = refs[len(refs) - sum(turns):]
    left = []
    used = 0
    for n, turn in enumerate(turns):
        if turn:
            fill_turned(ins[2 * n], scratch[used], ins[2 * n].shape[0])
            left.append(scratch[used])
            used += 1
        else:
            left.append(ins[2 * n])
    right = [ins[2 * n + 1][...] for n in range(len(plan))]
    for group in range(n_out):
        for out, place, d in each_block(pick_ref, blocks, keeps, bits[group], 1 + group):
            at = pl.ds(pl.multiple_of((2 * d + pick_ref[0]) * deep, deep), deep)
            target = outs[2 * group + out] if keeps else outs[group]
            for n, (kind, own, start, wide) in enumerate(plan):
                if own != group:
                    continue
                rows = left[n][at, :]
                if kind == "copy":
                    part = rows
                elif kind == "nt":
                    part = nt(rows, right[n])
                else:
                    part = nn(rows, right[n])
                cut = slice(start, start + wide)
                if keeps:
                    part = part + adds[group][d, :, cut]
                target[place, :, cut] = part


def many_half(pick, pairs, plan, widths, add=None, *, parts, bits):
    whole = pl.BlockSpec(memory_space=pltpu.VMEM)
    turns = [kind != "nt" for kind, *_ in plan]
    depth = max(left.shape[1] for (left, _), turn in zip(pairs, turns) if turn)
    deep = depth // parts
    blocks = parts // 2
    keeps = add is not None
    args = [pick] + [operand for pair in pairs for operand in pair] + (list(add) if keeps else [])
    if keeps:
        shape = [jax.ShapeDtypeStruct((blocks // 2, deep, w), f32) for w in widths for _ in range(2)]
    else:
        shape = [jax.ShapeDtypeStruct((blocks, deep, w), f32) for w in widths]
    return pl.pallas_call(
        functools.partial(
            many_kernel, plan=plan, widths=widths, turns=turns, blocks=blocks, deep=deep,
            keeps=keeps, bits=[b[0] for b in bits],
        ),
        in_specs=[pl.BlockSpec(memory_space=pltpu.SMEM)] + [whole] * (len(args) - 1),
        out_specs=[whole] * len(shape),
        out_shape=shape,
        scratch_shapes=[
            pltpu.VMEM((left.shape[1], left.shape[0]), left.dtype)
            for (left, _), turn in zip(pairs, turns) if turn
        ],
        compiler_params=pltpu.CompilerParams(vmem_limit_bytes=VMEM_CAP),
        cost_estimate=pl.CostEstimate(
            flops=600 * depth * sum(widths), bytes_accessed=6 * depth * sum(widths), transcendentals=0
        ),
        name="many_half",
    )(*args)


def flipped(value, bit, size):
    return lax.ppermute(value, "dp", [(i, i ^ (1 << bit)) for i in range(size)])


def bit_of(index, bit):
    return (index >> bit) & 1


class Halving:
    def __init__(self, make, index, size, orders):
        self.make, self.index, self.size, self.orders = make, index, size, orders
        mine = bit_of(index, 0).astype(jnp.int32)
        self.pick = jnp.stack([mine] + [bit_of(index, bits[0]).astype(jnp.int32) for bits in orders])
        self.other = self.pick.at[0].set(1 - mine)
        self.stage = 0

    def work(self):
        if self.stage == 0:
            self.pending = [(sent, None) for sent in self.make(self.other, None)]
        elif self.stage == 1:
            outs = self.make(self.pick, self.extra)
            self.pending = [(outs[2 * g], outs[2 * g + 1]) for g in range(len(self.orders))]
            self.axes = [
                [b for b in range(self.size.bit_length() - 1, 0, -1) if b != bits[0] and b < self.size.bit_length() - 1]
                for bits in self.orders
            ]
        else:
            self.pending = [
                self.split(g, held, extra) for g, (held, extra) in enumerate(zip(self.held, self.extra))
            ]
        return [part for pair in self.pending for part in pair if part is not None]

    def split(self, g, held, extra):
        bits = self.orders[g]
        if self.stage > len(bits):
            return held + extra, None
        bit = bits[self.stage - 1]
        axis = self.axes[g].index(bit)
        shape = (2,) * len(self.axes[g]) + held.shape[-2:]
        self.axes[g].remove(bit)
        own = bit_of(self.index, bit)
        held, extra = held.reshape(shape), extra.reshape(shape)

        def half(value, at):
            return lax.dynamic_index_in_dim(value, at, axis, keepdims=False)

        return half(held, 1 - own) + half(extra, 1 - own), half(held, own) + half(extra, own)

    def go(self, parts):
        parts = list(parts)
        pairs = [
            tuple(None if part is None else parts.pop(0) for part in pair) for pair in self.pending
        ]
        self.held = [home for _, home in pairs]
        last = self.stage > len(self.orders[0])
        if last:
            self.result = [away for away, _ in pairs]
        else:
            bit = lambda g: 0 if self.stage == 0 else self.orders[g][self.stage - 1]
            self.extra = [flipped(away, bit(g), self.size) for g, (away, _) in enumerate(pairs)]
        self.stage += 1

    def step(self):
        self.go(self.work())

    def finish(self):
        while self.stage <= len(self.orders[0]) + 1:
            self.step()
        return self.result


def tie(values, *chains):
    works = [chain.work() for chain in chains]
    values, works = lax.optimization_barrier((values, works))
    for chain, parts in zip(chains, works):
        chain.go(parts)
    return values


def across(value):
    return value + lax.ppermute(value, "mp", [(0, 1), (1, 0)])


def join_kernel(base_ref, early_ref, mine_ref, w_ref, other_ref, ow_ref, out_ref, *, span):
    weight = ow_ref[...].astype(bf16)
    for start in range(0, span, 64):
        tall = min(64, span - start)
        at = slice(start, start + 64)
        total = base_ref[at, :] + early_ref[at, :] + nt(mine_ref[at, :], w_ref[...])
        total = total + nt(other_ref[at, :].astype(bf16), weight)
        out_ref[start:start + tall, :] = total.astype(bf16)[:tall]


def join(base, early, mine, weight, other, other_weight, span):
    whole = pl.BlockSpec(memory_space=pltpu.VMEM)
    return pl.pallas_call(
        functools.partial(join_kernel, span=span),
        in_specs=[whole] * 6,
        out_specs=whole,
        out_shape=jax.ShapeDtypeStruct((span, base.shape[1]), bf16),
        compiler_params=pltpu.CompilerParams(vmem_limit_bytes=VMEM_CAP),
        cost_estimate=pl.CostEstimate(flops=3 * 10**9, bytes_accessed=12 * 10**6, transcendentals=0),
        name="join",
    )(base, early, mine, weight, other, other_weight)


def norm_forward(summed, gain, shift):
    centred = summed - jnp.mean(summed, axis=1, keepdims=True)
    inverse = lax.rsqrt(jnp.mean(centred * centred, axis=1, keepdims=True) + epsilon)
    normal = centred * inverse
    return (normal * gain + shift, normal, inverse)


def norm_backward(upstream, normal, inverse, gain):
    scaled = upstream * gain
    inner = jnp.mean(scaled, axis=1, keepdims=True)
    aligned = jnp.mean(scaled * normal, axis=1, keepdims=True)
    return (
        inverse * (scaled - inner - normal * aligned),
        jnp.sum(upstream * normal, axis=0),
        jnp.sum(upstream, axis=0),
    )


def shards(
    tokens,
    query_weight,
    key_weight,
    value_weight,
    output_weight,
    query_position,
    key_position,
    position_tables,
    gain_one,
    shift_one,
    up_weight,
    down_weight,
    gain_two,
    shift_two,
    buckets,
    text_length,
    cotangent,
):
    span = buckets.shape[2]
    rows, cols = sizes(span)
    size = lax.axis_size("dp")
    index = lax.axis_index("dp")
    bits = list(range(1, size.bit_length() - 1))
    low_first, high_first = bits, bits[1:] + bits[:1]
    score_scale = (7.0 * HEAD) ** (-0.5)
    tables_flat = position_tables.reshape(3 * REL, D)
    width = query_weight.shape[1]
    spare = ((0, rows - span), (0, 0))

    def chain(make, *orders):
        return Halving(make, index, size, list(orders))

    other_key_weight = lax.ppermute(key_weight.astype(f32), "mp", [(0, 1), (1, 0)])
    qkv, pos_key, pos_query = project(
        tokens, query_weight, key_weight, value_weight, position_tables, key_position, query_position, span
    )
    tokens = jnp.pad(tokens, spare)
    cotangent = jnp.pad(cotangent, spare)
    share, context, bucket_rows, bucket_cols = attention_forward(
        qkv, pos_key, pos_query, buckets, text_length, score_scale
    )
    attended = across(nn(context, output_weight))
    first, normal_one, inverse_one = norm_forward(
        tokens.astype(f32) + attended, gain_one, shift_one
    )
    first_low = first.astype(bf16)
    upward = nn(first_low, up_weight)
    hidden = jax.nn.gelu(upward, approximate=False).astype(bf16)
    feed = across(nn(hidden, down_weight))
    final, normal_two, inverse_two = norm_forward(first + feed, gain_two, shift_two)
    layer_output = final[:span].astype(bf16)
    second_back, gain_two_grad, shift_two_grad = norm_backward(
        cotangent.astype(f32), normal_two, inverse_two, gain_two
    )
    second_low = second_back.astype(bf16)
    hidden_back = nt(second_low, down_weight)
    gelu_back = jax.vjp(lambda inner_value: jax.nn.gelu(inner_value, approximate=False), upward)[1]
    upward_back = gelu_back(hidden_back)[0].astype(bf16)

    back_part = nt(upward_back, up_weight)
    back_other = lax.ppermute(back_part, "mp", [(0, 1), (1, 0)])
    down_chain = chain(
        lambda pick, add: weight_half(pick, second_low, hidden, add, parts=size, bits=high_first), high_first
    )
    up_chain = chain(
        lambda pick, add: weight_half(pick, first_low, upward_back, add, parts=size, bits=low_first), low_first
    )
    down_chain.step()
    up_chain.step()
    down_chain.step()
    back_other = tie(back_other, up_chain)
    first_back = second_back + back_part + back_other
    residual_back, gain_one_grad, shift_one_grad = norm_backward(
        first_back, normal_one, inverse_one, gain_one
    )
    residual_low = residual_back.astype(bf16)
    context_back = nt(residual_low, output_weight).astype(bf16)

    merge = merge_table()
    back, back_turned, query_base, key_base, value_back = attention_draw(
        share, context_back, qkv, score_scale
    )
    nothing = jnp.zeros_like(gain_one)
    gains = jnp.stack(
        [gain_one_grad, shift_one_grad, gain_two_grad, shift_two_grad] + [nothing] * 4
    )
    gains = jnp.concatenate([gains, jnp.zeros((120, gains.shape[1]), f32)], axis=0)
    dummy = jnp.zeros((8, 128), bf16)
    outer_chain = chain(
        lambda pick, add: many_half(
            pick,
            [(residual_low, context), (tokens, value_back), (gains, dummy)],
            [("nn", 0, 0, width), ("nn", 0, width, width), ("copy", 0, 2 * width, 128)],
            [2 * width + 128],
            add, parts=size, bits=[low_first],
        ),
        low_first,
    )
    outer_chain.step()

    def tail(rows_back, sums, position, orders):
        return chain(
            lambda pick, add: many_half(
                pick,
                [(tokens, rows_back), (tables_flat, sums), (position, sums)],
                [("nn", 0, 0, width), ("nn", 1, 0, width), ("nt", 0, width, 3 * REL)],
                [width + 3 * REL, width],
                add, parts=size, bits=orders,
            ),
            *orders,
        )

    near = []
    near.append(attention_scatter(back, bucket_rows, merge, 0, 2))
    back, near = tie((back, near), outer_chain, down_chain)
    near.append(attention_scatter(back, bucket_rows, merge, 1, 2))
    near, back_turned = tie((near, back_turned), up_chain)
    query_back, key_table_sum = attention_close(near, query_base, pos_key, qkv, 0)
    query_low = query_back.astype(bf16)
    early_part = nt(query_low, query_weight) + nt(value_back, value_weight)
    early = across(early_part)
    near_chain = tail(query_low, key_table_sum, key_position, [high_first, low_first])
    back_turned = tie(back_turned, near_chain, down_chain)
    far = []
    far.append(attention_scatter(back_turned, bucket_cols, merge, 0, 2))
    back_turned, far = tie((back_turned, far), near_chain, up_chain, outer_chain)
    far.append(attention_scatter(back_turned, bucket_cols, merge, 1, 2))
    far = tie(far, near_chain, outer_chain, up_chain, down_chain)
    key_back, query_table_sum = attention_close(far, key_base, pos_query, qkv, 1)
    key_other = lax.ppermute(key_back, "mp", [(0, 1), (1, 0)])
    key_low = key_back.astype(bf16)
    far_chain = tail(key_low, query_table_sum, query_position, [low_first, high_first])
    far_chain.step()
    far_chain.step()
    input_gradient = join(
        residual_back, early, key_low, key_weight, key_other, other_key_weight, span
    )
    (down_share,) = down_chain.finish()
    (up_share,) = up_chain.finish()
    (outer_share,) = outer_chain.finish()
    near_main, key_position_grad = near_chain.finish()
    far_main, query_position_grad = far_chain.finish()

    table_rows = near_main[:, width:] + far_main[:, width:]
    table_rows = table_rows.reshape(2, table_rows.shape[0] // 2, 3 * REL)
    side = lax.axis_index("mp")
    table_mine = lax.dynamic_index_in_dim(table_rows, side, 0, keepdims=False) + lax.ppermute(
        lax.dynamic_index_in_dim(table_rows, 1 - side, 0, keepdims=False), "mp", [(0, 1), (1, 0)]
    )
    table_gradient = table_mine.T.reshape(3, REL, table_mine.shape[0])
    gains_mine = outer_share[:, 2 * width:]
    return (
        layer_output,
        input_gradient,
        near_main[:, 0:width],
        far_main[:, 0:width],
        outer_share[:, width:2 * width],
        outer_share[:, 0:width].T,
        query_position_grad,
        key_position_grad,
        table_gradient,
        gains_mine[:, 0],
        gains_mine[:, 1],
        up_share,
        down_share.T,
        gains_mine[:, 2],
        gains_mine[:, 3],
    )


def solution(mesh):
    return jax.shard_map(
        shards,
        mesh=mesh,
        in_specs=(
            P("dp", None),
            P(None, "mp"),
            P(None, "mp"),
            P(None, "mp"),
            P("mp", None),
            P(None, "mp"),
            P(None, "mp"),
            P(),
            P(),
            P(),
            P(None, "mp"),
            P("mp", None),
            P(),
            P(),
            P("dp", None, None, None),
            P("dp"),
            P("dp", None),
        ),
        out_specs=(
            P("dp", None),
            P("dp", None),
            P("dp", "mp"),
            P("dp", "mp"),
            P("dp", "mp"),
            P("mp", "dp"),
            P("dp", "mp"),
            P("dp", "mp"),
            P(None, None, ("dp", "mp")),
            P("dp"),
            P("dp"),
            P("dp", "mp"),
            P("mp", "dp"),
            P("dp"),
            P("dp"),
        ),
        check_vma=False,
    )
```

```python
import functools

import jax
import jax.numpy as jnp
from jax import lax
from jax.experimental import pallas as pl
from jax.experimental.pallas import tpu as pltpu
from jax.sharding import PartitionSpec as P

D = 1024
epsilon = 1e-05
HEAD = 64
REL = 128
TEXT = 512
bf16 = jnp.bfloat16
f32 = jnp.float32
LIMIT = 10900.0
VMEM_CAP = 62 * 2**20


def lane_gather(table, index):
    numbers = lax.GatherDimensionNumbers(
        offset_dims=(),
        collapsed_slice_dims=(1,),
        start_index_map=(1,),
        operand_batching_dims=(0,),
        start_indices_batching_dims=(0,),
    )
    return lax.gather(
        table, index[..., None], numbers, (1, 1), mode=lax.GatherScatterMode.PROMISE_IN_BOUNDS
    )


def nt(left, right):
    return lax.dot_general(left, right, (((1,), (1,)), ((), ())), preferred_element_type=f32)


def nn(left, right):
    return jnp.dot(left, right, preferred_element_type=f32)


def tn(left, right):
    return lax.dot_general(left, right, (((0,), (0,)), ((), ())), preferred_element_type=f32)


def lane_half(shape):
    return lax.broadcasted_iota(jnp.int32, shape, len(shape) - 1) < HEAD


def unpack_pair(packed):
    low = (packed << 16) >> 16
    high = (packed - low) >> 16
    return high.astype(f32), low.astype(f32)


def fill_tables(src_ref, first, tall, pos_ref, tab, inv, p):
    half = lane_half((64, 128))
    cut = slice(p * 128, (p + 1) * 128)

    def body(step, carry):
        at = pl.ds(pl.multiple_of(step * 64, 64), 64)
        block = src_ref[pl.ds(pl.multiple_of(first + step * 64, 64), 64), cut]
        zero = jnp.zeros_like(block)
        first_head = nt(jnp.where(half, block, zero), pos_ref[:, cut]).astype(bf16).astype(f32)
        second_head = nt(jnp.where(half, zero, block), pos_ref[:, cut]).astype(bf16).astype(f32)
        top0 = jnp.maximum(jnp.max(jnp.abs(first_head), axis=1, keepdims=True), 1e-30)
        top1 = jnp.maximum(jnp.max(jnp.abs(second_head), axis=1, keepdims=True), 1e-30)
        whole0 = jnp.round(first_head * (LIMIT / top0)).astype(jnp.int32)
        whole1 = jnp.round(second_head * (LIMIT / top1)).astype(jnp.int32)
        tab[p, at, :] = whole0 * 65536 + whole1
        inv[2 * p, at, :] = jnp.broadcast_to(top0 * (1.0 / LIMIT), (64, 128))
        inv[2 * p + 1, at, :] = jnp.broadcast_to(top1 * (1.0 / LIMIT), (64, 128))
        return carry

    lax.fori_loop(0, tall // 64, body, 0)


def look_up(tab, index_ref, at, store, *, pairs, cols):
    for c in range(cols // 128):
        total = [None] * pairs
        for r in range(3):
            index = index_ref[r, at, c * 128:(c + 1) * 128]
            for p in range(pairs):
                got = lane_gather(tab[p, at, r * 128:(r + 1) * 128], index)
                total[p] = got if total[p] is None else total[p] + got
        for p in range(pairs):
            store(p, c, total[p])


def prepare_rows(
    k_ref, pq_ref, b_ref, head_ref, rest_ref, bt_ref, far_head, far_rest, inv_ref,
    far_tab, far_inv, *, span, rows, cols, pairs, split,
):
    edge = span - span % 8 - split
    for r in range(3):
        head_ref[r, :, span - span % 128:cols] = jnp.zeros((split, cols - span + span % 128), jnp.int32)
        rest_ref[r, edge:rows - split, :] = jnp.zeros((rows - split - edge, cols), jnp.int32)
        rest_ref[r, :, span - span % 128:cols] = jnp.zeros((rows - split, cols - span + span % 128), jnp.int32)
        head_ref[r, :, 0:span] = b_ref[0, r, 0:split]
        rest_ref[r, 0:span - split, 0:span] = b_ref[0, r, split:span]
    for r in range(3):
        for jb in range(cols // 128):
            high = min(128, rows - jb * 128)
            for ib in range(cols // 128):
                tall = min(128, rows - ib * 128)
                here = slice(jb * 128, (jb + 1) * 128)
                if ib * 128 < split:
                    block = head_ref[r, ib * 128:ib * 128 + tall, here]
                else:
                    block = rest_ref[r, ib * 128 - split:ib * 128 - split + tall, here]
                if tall < 128:
                    block = jnp.concatenate([block, jnp.zeros((128 - tall, 128), jnp.int32)], axis=0)
                bt_ref[r, jb * 128:jb * 128 + high, ib * 128:(ib + 1) * 128] = block.T[:high]
    for p in range(pairs):
        fill_tables(k_ref, 0, rows, pq_ref, far_tab, far_inv, p)

    def far_body(step, carry):
        at = pl.ds(pl.multiple_of(step * 8, 8), 8)

        def store(p, c, total):
            if c * 128 < split:
                far_head[p, at, c * 128:(c + 1) * 128] = total
            else:
                far_rest[p, at, c * 128 - split:(c + 1) * 128 - split] = total

        look_up(far_tab, bt_ref, at, store, pairs=pairs, cols=cols)
        return carry

    lax.fori_loop(0, rows // 8, far_body, 0)
    for p in range(pairs):
        far_head[p, rows:, :] = jnp.zeros((cols - rows, split), jnp.int32)
        far_rest[p, rows:, :] = jnp.zeros((cols - rows, cols - split), jnp.int32)
    for h in range(2 * pairs):
        inv_ref[h:h + 1, :] = jnp.concatenate(
            [far_inv[h, j * 128:min(rows, (j + 1) * 128), :].T[0:1] for j in range(cols // 128 - 1)]
            + [jnp.concatenate([far_inv[h, cols - 128:rows, :],
                                jnp.zeros((cols - rows, 128), f32)], axis=0).T[0:1]], axis=1)


def forward_rows(
    used_ref, q_ref, k_ref, v_ref, pk_ref, b_ref, far_sum, inv_ref, p_ref, ctx_ref,
    near_tab, near_inv, near_sum, score, *, first, rows, span, cols, pairs, scale,
):
    for p in range(pairs):
        fill_tables(q_ref, first, rows, pk_ref, near_tab, near_inv, p)
    used = used_ref[0]
    place = lax.broadcasted_iota(jnp.int32, (1, cols), 1)
    valid = ((place >= TEXT) & (place < span)) | (place < used)

    def block_body(start, tall):
        def near_body(step, carry):
            at = pl.ds(pl.multiple_of(start + step * 8, 8), 8)
            out_at = pl.ds(pl.multiple_of(step * 8, 8), 8)

            def store(p, c, total):
                near_sum[p, out_at, c * 128:(c + 1) * 128] = total

            look_up(near_tab, b_ref, at, store, pairs=pairs, cols=cols)
            return carry

        lax.fori_loop(0, tall // 8, near_body, 0)
        at = pl.ds(start, tall)
        for p in range(pairs):
            cut = slice(p * 128, (p + 1) * 128)
            block = q_ref[pl.ds(pl.multiple_of(first + start, 64), tall), cut]
            zero = jnp.zeros_like(block)
            mask = lane_half((tall, 128))
            score[0, 0:tall, :] = nt(jnp.where(mask, block, zero), k_ref[:, cut])
            score[1, 0:tall, :] = nt(jnp.where(mask, zero, block), k_ref[:, cut])
            for c in range(cols // 128):
                turned = far_sum[p, c * 128:(c + 1) * 128, pl.ds(start, 128)].T[0:tall]
                here = slice(c * 128, (c + 1) * 128)
                f0, f1 = unpack_pair(turned)
                n0, n1 = unpack_pair(near_sum[p, 0:tall, here])
                score[0, 0:tall, here] += (
                    f0 * inv_ref[2 * p:2 * p + 1, here] + n0 * near_inv[2 * p, at, :]
                )
                score[1, 0:tall, here] += (
                    f1 * inv_ref[2 * p + 1:2 * p + 2, here] + n1 * near_inv[2 * p + 1, at, :]
                )
            for h in range(2):
                for s in range(tall // 16):
                    raw = score[h, s * 16:(s + 1) * 16, :]
                    logits = jnp.where(valid, raw * scale, -1e30)
                    top = jnp.max(logits, axis=1, keepdims=True)
                    grown = jnp.exp(logits - top)
                    share = grown * (1.0 / jnp.sum(grown, axis=1, keepdims=True))
                    p_ref[2 * p + h, pl.ds(pl.multiple_of(start + s * 16, 16), 16), :] = share.astype(bf16)
            c0 = nn(p_ref[2 * p, at, :], v_ref[:, cut])
            c1 = nn(p_ref[2 * p + 1, at, :], v_ref[:, cut])
            ctx_ref[at, cut] = jnp.where(mask, c0, c1).astype(bf16)

    def outer(step, carry):
        block_body(pl.multiple_of(step * 128, 128), 128)
        return carry

    lax.fori_loop(0, rows // 128, outer, 0)
    if rows % 128:
        block_body(rows - rows % 128, rows % 128)


def project_kernel(x_ref, wq_ref, wk_ref, wv_ref, t_ref, kp_ref, qp_ref, qkv_ref, pk_ref, pq_ref, *, span, cols, width):
    tail = span - span % 128
    qkv_ref[span - span % 16:cols, :] = jnp.zeros((cols - span + span % 16, 3 * width), bf16)
    for n, w_ref in enumerate((wq_ref, wk_ref, wv_ref)):
        cut = slice(n * width, (n + 1) * width)

        def body(step, carry, cut=cut, w_ref=w_ref):
            at = pl.ds(pl.multiple_of(step * 128, 128), 128)
            qkv_ref[at, cut] = nn(x_ref[at, :], w_ref[...]).astype(bf16)
            return carry

        lax.fori_loop(0, span // 128, body, 0)
        if tail < span:
            qkv_ref[tail:span, cut] = nn(x_ref[tail:span, :], w_ref[...]).astype(bf16)
    for r in range(3):
        at = slice(r * REL, (r + 1) * REL)
        pk_ref[at, :] = nn(t_ref[r], kp_ref[...]).astype(bf16)
        pq_ref[at, :] = nn(t_ref[r], qp_ref[...]).astype(bf16)


def project(tokens, query_weight, key_weight, value_weight, tables, key_position, query_position, span):
    width = query_weight.shape[1]
    rows, cols = sizes(span)
    whole = pl.BlockSpec(memory_space=pltpu.VMEM)
    return pl.pallas_call(
        functools.partial(project_kernel, span=span, cols=cols, width=width),
        out_shape=(
            jax.ShapeDtypeStruct((cols, 3 * width), bf16),
            jax.ShapeDtypeStruct((3 * REL, width), bf16),
            jax.ShapeDtypeStruct((3 * REL, width), bf16),
        ),
        in_specs=[whole] * 7,
        out_specs=(whole,) * 3,
        compiler_params=pltpu.CompilerParams(vmem_limit_bytes=VMEM_CAP),
        cost_estimate=pl.CostEstimate(flops=4 * 10**9, bytes_accessed=9 * 10**6, transcendentals=0),
        name="project",
    )(tokens, query_weight, key_weight, value_weight, tables, key_position, query_position)


def pick(half, block, h):
    zero = jnp.zeros_like(block)
    return jnp.where(half, block, zero) if h == 0 else jnp.where(half, zero, block)


def draw_kernel(
    p_ref, up_ref, q_ref, k_ref, v_ref, *refs, first, tall, rows, cols, scale, adds,
):
    extra = refs[:adds]
    d_ref, dt_ref, dq_ref, dk_ref, dv_ref, wide, flat, turned = refs[adds:]
    lanes = turned.shape[2]
    half = lane_half((64, 128))

    def body(step, carry):
        at = pl.ds(pl.multiple_of(step * 64, 64), 64)
        pair = []
        for h in range(2):
            reach = nt(pick(half, up_ref[at, :], h), v_ref[...])
            share = p_ref[h, at, :].astype(f32)
            inner = jnp.sum(reach * share, axis=1, keepdims=True)
            back = share * (reach - inner) * scale
            wide[h, at, :] = back
            flat[h, at, :] = back.astype(bf16)
            pair.append(back.reshape(8, 8, cols))
        d_ref[pl.ds(pl.multiple_of(step * 8, 8), 8), :, :] = jnp.concatenate(pair, axis=1).astype(bf16)
        return carry

    lax.fori_loop(0, tall // 64, body, 0)
    for jb in range(cols // 128):
        high = min(128, rows - jb * 128)
        for ib in range(lanes // 128):
            wide_rows = min(128, tall - ib * 128)
            pair = []
            for h in range(2):
                block = wide[h, ib * 128:ib * 128 + wide_rows, jb * 128:(jb + 1) * 128]
                if wide_rows < 128:
                    block = jnp.concatenate([block, jnp.zeros((128 - wide_rows, 128), f32)], axis=0)
                other = block.T[:high]
                turned[h, jb * 128:jb * 128 + high, ib * 128:(ib + 1) * 128] = other.astype(bf16)
                pair.append(other.reshape(high // 8, 8, 128))
            dt_ref[jb * 16:jb * 16 + high // 8, :, ib * 128:(ib + 1) * 128] = jnp.concatenate(
                pair, axis=1
            ).astype(bf16)
    keys, queries, ups = k_ref[...], q_ref[first:first + lanes, :], up_ref[...]
    cols_half, lanes_half, tall_half = (lane_half((n, 128)) for n in (cols, lanes, tall))
    dq_ref[...] = nn(flat[0], pick(cols_half, keys, 0)) + nn(flat[1], pick(cols_half, keys, 1))
    dk = nn(turned[0], pick(lanes_half, queries, 0)) + nn(turned[1], pick(lanes_half, queries, 1))
    dv = tn(p_ref[0], pick(tall_half, ups, 0)) + tn(p_ref[1], pick(tall_half, ups, 1))
    dv = dv[:rows]
    if adds:
        dk, dv = dk + extra[0][...], dv + extra[1][...]
    dk_ref[...] = dk
    dv_ref[...] = dv.astype(dv_ref.dtype)


def scatter_kernel(*refs, groups, cols):
    *d_refs, b_ref, merge_ref, out_ref = refs
    base = jnp.where(lax.broadcasted_iota(jnp.int32, (16, cols), 0) >= 8, 1.0, 0.0).astype(bf16)
    own = (lax.broadcasted_iota(jnp.int32, (256, 256), 0) % 8) == (
        lax.broadcasted_iota(jnp.int32, (256, 256), 1) % 8
    )
    zero = jnp.asarray(0.0, bf16)
    one = jnp.asarray(1.0, bf16)

    def body(g, carry):
        back = jnp.concatenate([d_ref[g] for d_ref in d_refs], axis=1) if len(d_refs) > 1 else d_refs[0][g]
        for r in range(3):
            bucket = b_ref[r, pl.ds(pl.multiple_of(g * 8, 8), 8), :]
            low = (bucket & 31).astype(f32)
            high = (bucket >> 5).astype(f32)
            low = jnp.concatenate([low, low], axis=0).astype(bf16) - base
            high = jnp.concatenate([high, high], axis=0).astype(bf16)
            hot = jnp.concatenate(
                [jnp.where(low == jnp.asarray(2.0 * k, bf16), one, zero) for k in range(16)], axis=0
            )
            sieved = []
            for l in range(4):
                mask = high == jnp.asarray(float(l), bf16)
                for p in range(4):
                    sieved.append(jnp.where(mask, back[p * 16:(p + 1) * 16], zero))
            sums = nt(jnp.concatenate(sieved, axis=0), hot)
            sums = jnp.where(own, sums, 0.0).astype(bf16)
            total = None
            for l in range(4):
                term = nn(sums[l * 64:(l + 1) * 64], merge_ref[l])
                total = term if total is None else total + term
            out_ref[g, :, r * 128:(r + 1) * 128] = total.astype(bf16)
        return carry

    lax.fori_loop(0, groups, body, 0)


def close_kernel(*refs, rows, count):
    base_ref, pos_ref, side_ref, out_ref, table_ref = refs[count:]
    rows2 = 2 * rows
    half3 = lane_half((rows // 8, 8, 128))
    flat = jnp.concatenate([ref[...] for ref in refs[:count]], axis=0).reshape(rows2, 3 * REL)
    both = nn(flat, pos_ref[...]).reshape(rows // 8, 16, 128)
    mine = jnp.where(half3, both[:, 0:8, :], both[:, 8:16, :]).reshape(rows, 128)
    out_ref[...] = base_ref[...] + mine
    side = side_ref[0:rows, :].astype(f32).reshape(rows // 8, 8, 128)
    zero = jnp.zeros_like(side)
    spread = jnp.concatenate([jnp.where(half3, side, zero), jnp.where(half3, zero, side)], axis=1)
    table_ref[...] = tn(flat, spread.reshape(rows2, 128).astype(bf16)).astype(bf16)


def merge_table():
    l = lax.broadcasted_iota(jnp.int32, (4, 256, 128), 0)
    a = lax.broadcasted_iota(jnp.int32, (4, 256, 128), 1) // 8
    c = lax.broadcasted_iota(jnp.int32, (4, 256, 128), 2)
    return (c == l * 32 + a).astype(bf16)


def sizes(span):
    return -(-span // 64) * 64, -(-span // 128) * 128


def forward_scratch(pairs, tall, cols):
    return [
        pltpu.VMEM((pairs, tall, 3 * REL), jnp.int32),
        pltpu.VMEM((2 * pairs, tall, 128), f32),
        pltpu.VMEM((pairs, 128, cols), jnp.int32),
        pltpu.VMEM((2, 128, cols), f32),
    ]


def attention_head(qkv, pos_key, pos_query, buckets, used, scale, split):
    span = buckets.shape[2]
    rows, cols = sizes(span)
    width = pos_key.shape[1]
    pairs = width // 128
    whole = pl.BlockSpec(memory_space=pltpu.VMEM)
    i32 = jnp.int32

    def kernel(
        used_ref, qkv_ref, pk_ref, pq_ref, b_ref, p_ref, ctx_ref, head_ref, rest_ref, bt_ref, far_rest, inv_ref,
        far_tab, far_inv, far_head, *scratch,
    ):
        k_ref = qkv_ref.at[:, width:2 * width]
        prepare_rows(
            k_ref, pq_ref, b_ref, head_ref, rest_ref, bt_ref, far_head, far_rest, inv_ref, far_tab, far_inv,
            span=span, rows=rows, cols=cols, pairs=pairs, split=split,
        )
        forward_rows(
            used_ref, qkv_ref.at[:, 0:width], k_ref, qkv_ref.at[:, 2 * width:3 * width], pk_ref, head_ref,
            far_head, inv_ref, p_ref, ctx_ref, *scratch,
            first=0, rows=split, span=span, cols=cols, pairs=pairs, scale=scale,
        )

    return pl.pallas_call(
        kernel,
        out_shape=(
            jax.ShapeDtypeStruct((2 * pairs, split, cols), bf16),
            jax.ShapeDtypeStruct((split, width), bf16),
            jax.ShapeDtypeStruct((3, split, cols), i32),
            jax.ShapeDtypeStruct((3, rows - split, cols), i32),
            jax.ShapeDtypeStruct((3, rows, cols), i32),
            jax.ShapeDtypeStruct((pairs, cols, cols - split), i32),
            jax.ShapeDtypeStruct((2 * pairs, cols), f32),
        ),
        in_specs=[pl.BlockSpec(memory_space=pltpu.SMEM)] + [whole] * 4,
        out_specs=(whole,) * 7,
        scratch_shapes=[
            pltpu.VMEM((pairs, rows, 3 * REL), i32),
            pltpu.VMEM((2 * pairs, rows, 128), f32),
            pltpu.VMEM((pairs, cols, split), i32),
        ] + forward_scratch(pairs, split, cols),
        compiler_params=pltpu.CompilerParams(vmem_limit_bytes=VMEM_CAP),
        cost_estimate=pl.CostEstimate(flops=4 * 10**10, bytes_accessed=25000000, transcendentals=0),
        name="attention_head",
    )(used, qkv, pos_key, pos_query, buckets)


def attention_rest(qkv, pos_key, bucket_rest, far_rest, inverse, used, scale, split, span):
    rows, cols = sizes(span)
    width = pos_key.shape[1]
    pairs = width // 128
    whole = pl.BlockSpec(memory_space=pltpu.VMEM)

    def kernel(used_ref, qkv_ref, pk_ref, b_ref, far_ref, inv_ref, p_ref, ctx_ref, *scratch):
        forward_rows(
            used_ref, qkv_ref.at[:, 0:width], qkv_ref.at[:, width:2 * width], qkv_ref.at[:, 2 * width:3 * width],
            pk_ref, b_ref, far_ref, inv_ref, p_ref, ctx_ref, *scratch,
            first=split, rows=rows - split, span=span, cols=cols, pairs=pairs, scale=scale,
        )

    return pl.pallas_call(
        kernel,
        out_shape=(
            jax.ShapeDtypeStruct((2 * pairs, rows - split, cols), bf16),
            jax.ShapeDtypeStruct((rows - split, width), bf16),
        ),
        in_specs=[pl.BlockSpec(memory_space=pltpu.SMEM)] + [whole] * 5,
        out_specs=(whole,) * 2,
        scratch_shapes=forward_scratch(pairs, rows - split, cols),
        compiler_params=pltpu.CompilerParams(vmem_limit_bytes=VMEM_CAP),
        cost_estimate=pl.CostEstimate(flops=2 * 10**10, bytes_accessed=12000000, transcendentals=0),
        name="attention_rest",
    )(used, qkv, pos_key, bucket_rest, far_rest, inverse)


def attention_draw(share, upstream, qkv, scale, first, rows, adds=()):
    heads, tall, cols = share.shape
    width = upstream.shape[1]
    pairs = heads // 2
    lanes = -(-tall // 128) * 128

    def column(n):
        return pl.BlockSpec((n, 128), lambda p: (0, p))

    return pl.pallas_call(
        functools.partial(draw_kernel, first=first, tall=tall, rows=rows, cols=cols, scale=scale, adds=len(adds)),
        grid=(pairs,),
        in_specs=[
            pl.BlockSpec((2, tall, cols), lambda p: (p, 0, 0)),
            column(tall),
            pl.BlockSpec((cols, 128), lambda p: (0, p)),
            pl.BlockSpec((cols, 128), lambda p: (0, p + pairs)),
            pl.BlockSpec((cols, 128), lambda p: (0, p + 2 * pairs)),
        ] + [column(rows)] * len(adds),
        out_specs=(
            pl.BlockSpec((tall // 8, 16, cols), lambda p: (0, p, 0)),
            pl.BlockSpec((rows // 8, 16, lanes), lambda p: (0, p, 0)),
            column(tall), column(rows), column(rows),
        ),
        out_shape=(
            jax.ShapeDtypeStruct((tall // 8, 8 * heads, cols), bf16),
            jax.ShapeDtypeStruct((rows // 8, 8 * heads, lanes), bf16),
            jax.ShapeDtypeStruct((tall, width), f32),
            jax.ShapeDtypeStruct((rows, width), f32),
            jax.ShapeDtypeStruct((rows, width), bf16 if adds else f32),
        ),
        scratch_shapes=[
            pltpu.VMEM((2, tall, cols), f32),
            pltpu.VMEM((2, tall, cols), bf16),
            pltpu.VMEM((2, rows, lanes), bf16),
        ],
        compiler_params=pltpu.CompilerParams(vmem_limit_bytes=VMEM_CAP),
        cost_estimate=pl.CostEstimate(flops=10**10, bytes_accessed=12000000, transcendentals=0),
        name="attention_draw",
    )(share, upstream, qkv, qkv, qkv, *adds)


def attention_scatter(backs, buckets, merge, part, count):
    groups, high, _ = backs[0].shape
    cols = buckets.shape[2]
    groups = groups // count
    whole = pl.BlockSpec(memory_space=pltpu.VMEM)
    return pl.pallas_call(
        functools.partial(scatter_kernel, groups=groups, cols=cols),
        grid=(1,),
        out_shape=jax.ShapeDtypeStruct((groups, high, 3 * REL), bf16),
        in_specs=[pl.BlockSpec((groups, high, b.shape[2]), lambda g: (part, 0, 0)) for b in backs] + [
            pl.BlockSpec((3, groups * 8, cols), lambda g: (0, part, 0)),
            whole,
        ],
        out_specs=pl.BlockSpec((groups, high, 3 * REL), lambda g: (0, 0, 0)),
        compiler_params=pltpu.CompilerParams(vmem_limit_bytes=VMEM_CAP),
        cost_estimate=pl.CostEstimate(flops=10**9 * groups, bytes_accessed=2 * 10**5 * groups, transcendentals=0),
        name="attention_scatter",
    )(*backs, buckets, merge)


def attention_close(sums, base, pos, qkv, side):
    rows, width = base.shape
    pairs = width // 128
    return pl.pallas_call(
        functools.partial(close_kernel, rows=rows, count=len(sums)),
        grid=(pairs,),
        in_specs=[pl.BlockSpec((part.shape[0], 16, 3 * REL), lambda p: (0, p, 0)) for part in sums] + [
            pl.BlockSpec((rows, 128), lambda p: (0, p)),
            pl.BlockSpec((3 * REL, 128), lambda p: (0, p)),
            pl.BlockSpec((qkv.shape[0], 128), lambda p: (0, p + side * pairs)),
        ],
        out_specs=(
            pl.BlockSpec((rows, 128), lambda p: (0, p)),
            pl.BlockSpec((3 * REL, 128), lambda p: (0, p)),
        ),
        out_shape=(
            jax.ShapeDtypeStruct((rows, width), f32),
            jax.ShapeDtypeStruct((3 * REL, width), bf16),
        ),
        compiler_params=pltpu.CompilerParams(vmem_limit_bytes=VMEM_CAP),
        cost_estimate=pl.CostEstimate(flops=5000000000, bytes_accessed=10000000, transcendentals=0),
        name="attention_close",
    )(*sums, base, pos, qkv)


def fill_turned(x_ref, turned, rows):
    depth = x_ref.shape[1]
    for a in range(0, rows, 128):
        tall = min(128, rows - a)
        for b in range(0, depth, 128):
            block = x_ref[a:a + tall, b:b + 128]
            if tall < 128:
                block = jnp.concatenate([block, jnp.zeros((128 - tall, 128), block.dtype)], axis=0)
            turned[b:b + 128, a:a + tall] = block.T[:, :tall]


def each_block(pick_ref, blocks, keeps, bit, slot):
    if not keeps:
        return [(0, d, d) for d in range(blocks)]
    shift = bit - 1
    listed = []
    for out in range(2):
        value = pick_ref[slot] if out == 1 else 1 - pick_ref[slot]
        for e in range(blocks // 2):
            low = e & ((1 << shift) - 1)
            listed.append((out, e, ((e >> shift) << (shift + 1)) + low + value * (1 << shift)))
    return listed


def weight_kernel(pick_ref, *refs, count, blocks, deep, keeps, bit):
    xs, ys, rest = refs[:count], refs[count:2 * count], refs[2 * count:]
    add_ref = rest[0] if keeps else None
    outs = rest[1:3] if keeps else rest[0:1]
    turned = rest[-count:]

    @pl.when(pl.program_id(0) == 0)
    def _():
        for x_ref, wide in zip(xs, turned):
            fill_turned(x_ref, wide, x_ref.shape[0])

    for out, place, d in each_block(pick_ref, blocks, keeps, bit, 1):
        at = pl.ds(pl.multiple_of((2 * d + pick_ref[0]) * deep, deep), deep)
        part = add_ref[d] if keeps else None
        for wide, y_ref in zip(turned, ys):
            term = nn(wide[at, :], y_ref[...])
            part = term if part is None else part + term
        outs[out][place] = part


def weight_half(pick, xs, ys, add=None, *, parts, bits, tile=512):
    depth = xs[0].shape[1]
    wide = ys[0].shape[1]
    deep = depth // parts
    blocks = parts // 2
    keeps = add is not None

    def tiled(n):
        return pl.BlockSpec((n, deep, tile), lambda c: (0, 0, c))

    ins = [pl.BlockSpec(memory_space=pltpu.SMEM)]
    ins += [pl.BlockSpec(x.shape, lambda c: (0, 0)) for x in xs]
    ins += [pl.BlockSpec((y.shape[0], tile), lambda c: (0, c)) for y in ys]
    args = [pick, *xs, *ys]
    shape = (jax.ShapeDtypeStruct((blocks, deep, wide), f32),)
    specs = (tiled(blocks),)
    if keeps:
        ins.append(tiled(blocks))
        args += add
        shape = (jax.ShapeDtypeStruct((blocks // 2, deep, wide), f32),) * 2
        specs = (tiled(blocks // 2),) * 2
    rows = sum(x.shape[0] for x in xs)
    return pl.pallas_call(
        functools.partial(weight_kernel, count=len(xs), blocks=blocks, deep=deep, keeps=keeps, bit=bits[0]),
        grid=(wide // tile,),
        in_specs=ins,
        out_specs=specs,
        out_shape=shape,
        scratch_shapes=[pltpu.VMEM((depth, x.shape[0]), bf16) for x in xs],
        compiler_params=pltpu.CompilerParams(vmem_limit_bytes=VMEM_CAP),
        cost_estimate=pl.CostEstimate(
            flops=rows * depth * wide, bytes_accessed=4 * depth * wide, transcendentals=0
        ),
        name="weight_half",
    )(*args)


def many_kernel(pick_ref, *refs, plan, widths, turns, blocks, deep, keeps, bits):
    n_in = 2 * len(plan)
    ins = refs[:n_in]
    n_out = len(widths)
    adds = refs[n_in:n_in + n_out] if keeps else None
    outs = refs[n_in + n_out:n_in + 3 * n_out] if keeps else refs[n_in:n_in + n_out]
    scratch = refs[len(refs) - sum(turns):]
    left = []
    used = 0
    for n, turn in enumerate(turns):
        if turn:
            fill_turned(ins[2 * n], scratch[used], ins[2 * n].shape[0])
            left.append(scratch[used])
            used += 1
        else:
            left.append(ins[2 * n])
    right = [ins[2 * n + 1][...] for n in range(len(plan))]
    for group in range(n_out):
        for out, place, d in each_block(pick_ref, blocks, keeps, bits[group], 1 + group):
            at = pl.ds(pl.multiple_of((2 * d + pick_ref[0]) * deep, deep), deep)
            target = outs[2 * group + out] if keeps else outs[group]
            for n, (kind, own, start, wide) in enumerate(plan):
                if own != group:
                    continue
                rows = left[n][at, :]
                if kind == "copy":
                    part = rows
                elif kind == "nt":
                    part = nt(rows, right[n])
                else:
                    part = nn(rows, right[n])
                cut = slice(start, start + wide)
                if keeps:
                    part = part + adds[group][d, :, cut]
                target[place, :, cut] = part


def many_half(pick, pairs, plan, widths, add=None, *, parts, bits):
    whole = pl.BlockSpec(memory_space=pltpu.VMEM)
    turns = [kind != "nt" for kind, *_ in plan]
    depth = max(left.shape[1] for (left, _), turn in zip(pairs, turns) if turn)
    deep = depth // parts
    blocks = parts // 2
    keeps = add is not None
    args = [pick] + [operand for pair in pairs for operand in pair] + (list(add) if keeps else [])
    if keeps:
        shape = [jax.ShapeDtypeStruct((blocks // 2, deep, w), f32) for w in widths for _ in range(2)]
    else:
        shape = [jax.ShapeDtypeStruct((blocks, deep, w), f32) for w in widths]
    return pl.pallas_call(
        functools.partial(
            many_kernel, plan=plan, widths=widths, turns=turns, blocks=blocks, deep=deep,
            keeps=keeps, bits=[b[0] for b in bits],
        ),
        in_specs=[pl.BlockSpec(memory_space=pltpu.SMEM)] + [whole] * (len(args) - 1),
        out_specs=[whole] * len(shape),
        out_shape=shape,
        scratch_shapes=[
            pltpu.VMEM((left.shape[1], left.shape[0]), left.dtype)
            for (left, _), turn in zip(pairs, turns) if turn
        ],
        compiler_params=pltpu.CompilerParams(vmem_limit_bytes=VMEM_CAP),
        cost_estimate=pl.CostEstimate(
            flops=600 * depth * sum(widths), bytes_accessed=6 * depth * sum(widths), transcendentals=0
        ),
        name="many_half",
    )(*args)


def flipped(value, bit, size):
    return lax.ppermute(value, "dp", [(i, i ^ (1 << bit)) for i in range(size)])


def bit_of(index, bit):
    return (index >> bit) & 1


class Halving:
    def __init__(self, make, index, size, orders):
        self.make, self.index, self.size, self.orders = make, index, size, orders
        mine = bit_of(index, 0).astype(jnp.int32)
        self.pick = jnp.stack([mine] + [bit_of(index, bits[0]).astype(jnp.int32) for bits in orders])
        self.other = self.pick.at[0].set(1 - mine)
        self.stage = 0

    def work(self):
        if self.stage == 0:
            self.pending = [(sent, None) for sent in self.make(self.other, None)]
        elif self.stage == 1:
            outs = self.make(self.pick, self.extra)
            self.pending = [(outs[2 * g], outs[2 * g + 1]) for g in range(len(self.orders))]
            self.axes = [
                [b for b in range(self.size.bit_length() - 1, 0, -1) if b != bits[0] and b < self.size.bit_length() - 1]
                for bits in self.orders
            ]
        else:
            self.pending = [
                self.split(g, held, extra) for g, (held, extra) in enumerate(zip(self.held, self.extra))
            ]
        return [part for pair in self.pending for part in pair if part is not None]

    def split(self, g, held, extra):
        bits = self.orders[g]
        if self.stage > len(bits):
            return held + extra, None
        bit = bits[self.stage - 1]
        axis = self.axes[g].index(bit)
        shape = (2,) * len(self.axes[g]) + held.shape[-2:]
        self.axes[g].remove(bit)
        own = bit_of(self.index, bit)
        held, extra = held.reshape(shape), extra.reshape(shape)

        def half(value, at):
            return lax.dynamic_index_in_dim(value, at, axis, keepdims=False)

        return half(held, 1 - own) + half(extra, 1 - own), half(held, own) + half(extra, own)

    def go(self, parts):
        parts = list(parts)
        pairs = [
            tuple(None if part is None else parts.pop(0) for part in pair) for pair in self.pending
        ]
        self.held = [home for _, home in pairs]
        last = self.stage > len(self.orders[0])
        if last:
            self.result = [away for away, _ in pairs]
        else:
            bit = lambda g: 0 if self.stage == 0 else self.orders[g][self.stage - 1]
            self.extra = [flipped(away, bit(g), self.size) for g, (away, _) in enumerate(pairs)]
        self.stage += 1

    def step(self):
        self.go(self.work())

    def finish(self):
        while self.stage <= len(self.orders[0]) + 1:
            self.step()
        return self.result


def tie(values, *chains):
    works = [chain.work() for chain in chains]
    values, works = lax.optimization_barrier((values, works))
    for chain, parts in zip(chains, works):
        chain.go(parts)
    return values


def swap(value):
    return lax.ppermute(value.astype(f32), "mp", [(0, 1), (1, 0)])


def join_kernel(head_ref, rest_ref, early_ref, early_other_ref, mine_ref, w_ref, other_ref, ow_ref, out_ref, *, span):
    weight = ow_ref[...].astype(bf16)
    split = head_ref.shape[0]
    for start in range(0, span, 64):
        tall = min(64, span - start)
        at = slice(start, start + 64)
        base = head_ref[at, :] if start < split else rest_ref[start - split:start - split + 64, :]
        total = base + early_ref[at, :] + early_other_ref[at, :] + nt(mine_ref[at, :], w_ref[...])
        total = total + nt(other_ref[at, :].astype(bf16), weight)
        out_ref[start:start + tall, :] = total.astype(bf16)[:tall]


def join(bases, early, early_other, mine, weight, other, other_weight, span):
    whole = pl.BlockSpec(memory_space=pltpu.VMEM)
    return pl.pallas_call(
        functools.partial(join_kernel, span=span),
        in_specs=[whole] * 8,
        out_specs=whole,
        out_shape=jax.ShapeDtypeStruct((span, early.shape[1]), bf16),
        compiler_params=pltpu.CompilerParams(vmem_limit_bytes=VMEM_CAP),
        cost_estimate=pl.CostEstimate(flops=3 * 10**9, bytes_accessed=12 * 10**6, transcendentals=0),
        name="join",
    )(*bases, early, early_other, mine, weight, other, other_weight)


def attend_kernel(
    t_ref, c_ref, o_ref, w_ref, ow_ref, gain_ref, shift_ref, first_ref, low_ref, normal_ref, inverse_ref,
):
    weight = ow_ref[...].astype(bf16)

    def body(step, carry):
        at = pl.ds(pl.multiple_of(step * 64, 64), 64)
        summed = t_ref[at, :].astype(f32) + nn(c_ref[at, :], w_ref[...])
        summed = summed + nn(o_ref[at, :].astype(bf16), weight)
        first, normal, inverse = norm_forward(summed, gain_ref[...], shift_ref[...])
        first_ref[at, :] = first
        low_ref[at, :] = first.astype(bf16)
        normal_ref[at, :] = normal
        inverse_ref[at, :] = inverse
        return carry

    lax.fori_loop(0, t_ref.shape[0] // 64, body, 0)


def attend(tokens, context, other, weight, other_weight, gain, shift):
    tall, depth = tokens.shape
    whole = pl.BlockSpec(memory_space=pltpu.VMEM)
    return pl.pallas_call(
        attend_kernel,
        in_specs=[whole] * 7,
        out_specs=(whole,) * 4,
        out_shape=(
            jax.ShapeDtypeStruct((tall, depth), f32),
            jax.ShapeDtypeStruct((tall, depth), bf16),
            jax.ShapeDtypeStruct((tall, depth), f32),
            jax.ShapeDtypeStruct((tall, 1), f32),
        ),
        compiler_params=pltpu.CompilerParams(vmem_limit_bytes=VMEM_CAP),
        cost_estimate=pl.CostEstimate(flops=2 * 10**9, bytes_accessed=8 * 10**6, transcendentals=0),
        name="attend",
    )(tokens, context, other, weight, other_weight, gain[None], shift[None])


def norm_forward(summed, gain, shift):
    centred = summed - jnp.mean(summed, axis=1, keepdims=True)
    inverse = lax.rsqrt(jnp.mean(centred * centred, axis=1, keepdims=True) + epsilon)
    normal = centred * inverse
    return (normal * gain + shift, normal, inverse)


def norm_backward(upstream, normal, inverse, gain):
    scaled = upstream * gain
    inner = jnp.mean(scaled, axis=1, keepdims=True)
    aligned = jnp.mean(scaled * normal, axis=1, keepdims=True)
    return (
        inverse * (scaled - inner - normal * aligned),
        jnp.sum(upstream * normal, axis=0),
        jnp.sum(upstream, axis=0),
    )


def shards(
    tokens,
    query_weight,
    key_weight,
    value_weight,
    output_weight,
    query_position,
    key_position,
    position_tables,
    gain_one,
    shift_one,
    up_weight,
    down_weight,
    gain_two,
    shift_two,
    buckets,
    text_length,
    cotangent,
):
    span = buckets.shape[2]
    rows, cols = sizes(span)
    size = lax.axis_size("dp")
    index = lax.axis_index("dp")
    bits = list(range(1, size.bit_length() - 1))
    low_first, high_first = bits, bits[1:] + bits[:1]
    score_scale = (7.0 * HEAD) ** (-0.5)
    tables_flat = position_tables.reshape(3 * REL, D)
    width = query_weight.shape[1]
    spare = ((0, rows - span), (0, 0))

    def chain(make, *orders):
        return Halving(make, index, size, list(orders))

    split = rows // 2 // 128 * 128
    other_output = swap(output_weight)
    qkv, pos_key, pos_query = project(
        tokens, query_weight, key_weight, value_weight, position_tables, key_position, query_position, span
    )
    tokens = jnp.pad(tokens, spare)
    cotangent = jnp.pad(cotangent, spare)
    edges = [(0, split), (split, rows)]

    share_head, context_head, bucket_head, bucket_rest, bucket_cols, far_rest, far_inverse = attention_head(
        qkv, pos_key, pos_query, buckets, text_length, score_scale, split
    )
    other_head = swap(context_head)
    far_rest, other_output = lax.optimization_barrier((far_rest, other_output))
    share_rest, context_rest = attention_rest(
        qkv, pos_key, bucket_rest, far_rest, far_inverse, text_length, score_scale, split, span
    )
    other_rest = swap(context_rest)
    shares = [share_head, share_rest]
    contexts = [context_head, context_rest]
    contexts_other = [other_head, other_rest]

    def gelu(value):
        return jax.nn.gelu(value, approximate=False)

    firsts, firsts_low, normals_one, inverses_one, upwards, hiddens, feeds, feeds_other = ([] for _ in range(8))
    for (low, high), context, other in zip(edges, contexts, contexts_other):
        first, first_low, normal_one, inverse_one = attend(
            tokens[low:high], context, other, output_weight, other_output, gain_one, shift_one
        )
        firsts.append(first)
        normals_one.append(normal_one)
        inverses_one.append(inverse_one)
        firsts_low.append(first_low)
        upwards.append(nn(firsts_low[-1], up_weight))
        hiddens.append(gelu(upwards[-1]).astype(bf16))
        feeds.append(nn(hiddens[-1], down_weight))
        feeds_other.append(swap(feeds[-1]))

    finals, seconds_back, seconds_low, upwards_back, backs_part, backs_other, two_sums = ([] for _ in range(7))
    for n, (low, high) in enumerate(edges):
        final, normal_two, inverse_two = norm_forward(
            firsts[n] + feeds[n] + feeds_other[n], gain_two, shift_two
        )
        finals.append(final.astype(bf16))
        second_back, *sums = norm_backward(
            cotangent[low:high].astype(f32), normal_two, inverse_two, gain_two
        )
        two_sums.append(sums)
        seconds_back.append(second_back)
        seconds_low.append(second_back.astype(bf16))
        hidden_back = nt(seconds_low[n], down_weight)
        upwards_back.append(jax.vjp(gelu, upwards[n])[1](hidden_back)[0].astype(bf16))
        backs_part.append(nt(upwards_back[n], up_weight))
        backs_other.append(swap(backs_part[n]))
    layer_output = jnp.concatenate(finals, axis=0)[:span]
    gain_two_grad, shift_two_grad = (two_sums[0][n] + two_sums[1][n] for n in range(2))

    backs_part, down_pair, up_pair = lax.optimization_barrier(
        (backs_part, (seconds_low, hiddens), (firsts_low, upwards_back))
    )
    down_chain = chain(
        lambda pick, add: weight_half(pick, *down_pair, add, parts=size, bits=high_first), high_first
    )
    up_chain = chain(
        lambda pick, add: weight_half(pick, *up_pair, add, parts=size, bits=low_first), low_first
    )
    down_chain.step()
    up_chain.step()
    down_chain.step()
    backs_other[1] = tie(backs_other[1], up_chain)
    residuals_back, residuals_low, contexts_back, one_sums = ([] for _ in range(4))
    for n in range(2):
        residual_back, *sums = norm_backward(
            seconds_back[n] + backs_part[n] + backs_other[n], normals_one[n], inverses_one[n], gain_one
        )
        one_sums.append(sums)
        residuals_back.append(residual_back)
        residuals_low.append(residual_back.astype(bf16))
        contexts_back.append(nt(residuals_low[n], output_weight).astype(bf16))
    gain_one_grad, shift_one_grad = (one_sums[0][n] + one_sums[1][n] for n in range(2))

    merge = merge_table()
    back_head, turned_head, query_head, key_head, value_head = attention_draw(
        shares[0], contexts_back[0], qkv, score_scale, 0, rows
    )
    back_rest, turned_rest, query_rest, key_base, value_back = attention_draw(
        shares[1], contexts_back[1], qkv, score_scale, split, rows, (key_head, value_head)
    )
    query_base = jnp.concatenate([query_head, query_rest], axis=0)
    residual_low = jnp.concatenate(residuals_low, axis=0)
    context = jnp.concatenate(contexts, axis=0)
    nothing = jnp.zeros_like(gain_one)
    gains = jnp.stack(
        [gain_one_grad, shift_one_grad, gain_two_grad, shift_two_grad] + [nothing] * 4
    )
    gains = jnp.concatenate([gains, jnp.zeros((120, gains.shape[1]), f32)], axis=0)
    dummy = jnp.zeros((8, 128), bf16)
    outer_chain = chain(
        lambda pick, add: many_half(
            pick,
            [(residual_low, context), (tokens, value_back), (gains, dummy)],
            [("nn", 0, 0, width), ("nn", 0, width, width), ("copy", 0, 2 * width, 128)],
            [2 * width + 128],
            add, parts=size, bits=[low_first],
        ),
        low_first,
    )
    outer_chain.step()

    def tail(rows_back, sums, position, orders):
        return chain(
            lambda pick, add: many_half(
                pick,
                [(tokens, rows_back), (tables_flat, sums), (position, sums)],
                [("nn", 0, 0, width), ("nn", 1, 0, width), ("nt", 0, width, 3 * REL)],
                [width + 3 * REL, width],
                add, parts=size, bits=orders,
            ),
            *orders,
        )

    near = []
    near.append(attention_scatter([back_head], bucket_head, merge, 0, 1))
    back_rest, near, key_wide = tie((back_rest, near, key_weight.astype(f32)), outer_chain, down_chain)
    other_key_weight = swap(key_wide)
    near.append(attention_scatter([back_rest], bucket_rest, merge, 0, 1))
    near, backs, other_key_weight = tie((near, [turned_head, turned_rest], other_key_weight), up_chain)
    query_back, key_table_sum = attention_close(near, query_base, pos_key, qkv, 0)
    query_low = query_back.astype(bf16)
    early = nt(query_low, query_weight) + nt(value_back, value_weight)
    early_other = swap(early)
    near_chain = tail(query_low, key_table_sum, key_position, [high_first, low_first])
    backs = tie(backs, near_chain, down_chain)
    far = []
    far.append(attention_scatter(backs, bucket_cols, merge, 0, 2))
    backs, far, early_other = tie((backs, far, early_other), near_chain, up_chain, outer_chain)
    far.append(attention_scatter(backs, bucket_cols, merge, 1, 2))
    far = tie(far, near_chain, outer_chain, up_chain, down_chain)
    key_back, query_table_sum = attention_close(far, key_base, pos_query, qkv, 1)
    key_other = swap(key_back)
    key_low = key_back.astype(bf16)
    far_chain = tail(key_low, query_table_sum, query_position, [low_first, high_first])
    far_chain.step()
    far_chain.step()
    input_gradient = join(
        residuals_back, early, early_other, key_low, key_weight, key_other, other_key_weight, span
    )
    (down_share,) = down_chain.finish()
    (up_share,) = up_chain.finish()
    (outer_share,) = outer_chain.finish()
    near_main, key_position_grad = near_chain.finish()
    far_main, query_position_grad = far_chain.finish()

    table_rows = near_main[:, width:] + far_main[:, width:]
    table_rows = table_rows.reshape(2, table_rows.shape[0] // 2, 3 * REL)
    side = lax.axis_index("mp")
    table_mine = lax.dynamic_index_in_dim(table_rows, side, 0, keepdims=False) + lax.ppermute(
        lax.dynamic_index_in_dim(table_rows, 1 - side, 0, keepdims=False), "mp", [(0, 1), (1, 0)]
    )
    table_gradient = table_mine.T.reshape(3, REL, table_mine.shape[0])
    gains_mine = outer_share[:, 2 * width:]
    return (
        layer_output,
        input_gradient,
        near_main[:, 0:width],
        far_main[:, 0:width],
        outer_share[:, width:2 * width],
        outer_share[:, 0:width].T,
        query_position_grad,
        key_position_grad,
        table_gradient,
        gains_mine[:, 0],
        gains_mine[:, 1],
        up_share,
        down_share.T,
        gains_mine[:, 2],
        gains_mine[:, 3],
    )


def solution(mesh):
    return jax.shard_map(
        shards,
        mesh=mesh,
        in_specs=(
            P("dp", None),
            P(None, "mp"),
            P(None, "mp"),
            P(None, "mp"),
            P("mp", None),
            P(None, "mp"),
            P(None, "mp"),
            P(),
            P(),
            P(),
            P(None, "mp"),
            P("mp", None),
            P(),
            P(),
            P("dp", None, None, None),
            P("dp"),
            P("dp", None),
        ),
        out_specs=(
            P("dp", None),
            P("dp", None),
            P("dp", "mp"),
            P("dp", "mp"),
            P("dp", "mp"),
            P("mp", "dp"),
            P("dp", "mp"),
            P("dp", "mp"),
            P(None, None, ("dp", "mp")),
            P("dp"),
            P("dp"),
            P("dp", "mp"),
            P("mp", "dp"),
            P("dp"),
            P("dp"),
        ),
        check_vma=False,
    )
```

```python
import functools

import jax
import jax.numpy as jnp
from jax import lax
from jax.experimental import pallas as pl
from jax.experimental.pallas import tpu as pltpu
from jax.sharding import PartitionSpec as P

D = 1024
epsilon = 1e-05
HEAD = 64
REL = 128
TEXT = 512
bf16 = jnp.bfloat16
f32 = jnp.float32
LIMIT = 10900.0
VMEM_CAP = 62 * 2**20


def lane_gather(table, index):
    numbers = lax.GatherDimensionNumbers(
        offset_dims=(),
        collapsed_slice_dims=(1,),
        start_index_map=(1,),
        operand_batching_dims=(0,),
        start_indices_batching_dims=(0,),
    )
    return lax.gather(
        table, index[..., None], numbers, (1, 1), mode=lax.GatherScatterMode.PROMISE_IN_BOUNDS
    )


def nt(left, right):
    return lax.dot_general(left, right, (((1,), (1,)), ((), ())), preferred_element_type=f32)


def nn(left, right):
    return jnp.dot(left, right, preferred_element_type=f32)


def tn(left, right):
    return lax.dot_general(left, right, (((0,), (0,)), ((), ())), preferred_element_type=f32)


def lane_half(shape):
    return lax.broadcasted_iota(jnp.int32, shape, len(shape) - 1) < HEAD


def unpack_pair(packed):
    low = (packed << 16) >> 16
    high = (packed - low) >> 16
    return high.astype(f32), low.astype(f32)


def fill_tables(src_ref, first, tall, pos_ref, tab, inv, p):
    half = lane_half((64, 128))
    cut = slice(p * 128, (p + 1) * 128)

    def body(step, carry):
        at = pl.ds(pl.multiple_of(step * 64, 64), 64)
        block = src_ref[pl.ds(pl.multiple_of(first + step * 64, 64), 64), cut]
        zero = jnp.zeros_like(block)
        first_head = nt(jnp.where(half, block, zero), pos_ref[:, cut]).astype(bf16).astype(f32)
        second_head = nt(jnp.where(half, zero, block), pos_ref[:, cut]).astype(bf16).astype(f32)
        top0 = jnp.maximum(jnp.max(jnp.abs(first_head), axis=1, keepdims=True), 1e-30)
        top1 = jnp.maximum(jnp.max(jnp.abs(second_head), axis=1, keepdims=True), 1e-30)
        whole0 = jnp.round(first_head * (LIMIT / top0)).astype(jnp.int32)
        whole1 = jnp.round(second_head * (LIMIT / top1)).astype(jnp.int32)
        tab[p, at, :] = whole0 * 65536 + whole1
        inv[2 * p, at, :] = jnp.broadcast_to(top0 * (1.0 / LIMIT), (64, 128))
        inv[2 * p + 1, at, :] = jnp.broadcast_to(top1 * (1.0 / LIMIT), (64, 128))
        return carry

    lax.fori_loop(0, tall // 64, body, 0)


def look_up(tab, index_ref, at, store, *, pairs, cols):
    for c in range(cols // 128):
        total = [None] * pairs
        for r in range(3):
            index = index_ref[r, at, c * 128:(c + 1) * 128]
            for p in range(pairs):
                got = lane_gather(tab[p, at, r * 128:(r + 1) * 128], index)
                total[p] = got if total[p] is None else total[p] + got
        for p in range(pairs):
            store(p, c, total[p])


def prepare_rows(
    k_ref, pq_ref, b_ref, head_ref, rest_ref, bt_ref, far_head, far_rest, inv_ref,
    far_tab, far_inv, *, span, rows, cols, pairs, split,
):
    edge = span - span % 8 - split
    for r in range(3):
        head_ref[r, :, span - span % 128:cols] = jnp.zeros((split, cols - span + span % 128), jnp.int32)
        rest_ref[r, edge:rows - split, :] = jnp.zeros((rows - split - edge, cols), jnp.int32)
        rest_ref[r, :, span - span % 128:cols] = jnp.zeros((rows - split, cols - span + span % 128), jnp.int32)
        head_ref[r, :, 0:span] = b_ref[0, r, 0:split]
        rest_ref[r, 0:span - split, 0:span] = b_ref[0, r, split:span]
    for r in range(3):
        for jb in range(cols // 128):
            high = min(128, rows - jb * 128)
            for ib in range(cols // 128):
                tall = min(128, rows - ib * 128)
                here = slice(jb * 128, (jb + 1) * 128)
                if ib * 128 < split:
                    block = head_ref[r, ib * 128:ib * 128 + tall, here]
                else:
                    block = rest_ref[r, ib * 128 - split:ib * 128 - split + tall, here]
                if tall < 128:
                    block = jnp.concatenate([block, jnp.zeros((128 - tall, 128), jnp.int32)], axis=0)
                bt_ref[r, jb * 128:jb * 128 + high, ib * 128:(ib + 1) * 128] = block.T[:high]
    for p in range(pairs):
        fill_tables(k_ref, 0, rows, pq_ref, far_tab, far_inv, p)

    def far_body(step, carry):
        at = pl.ds(pl.multiple_of(step * 8, 8), 8)

        def store(p, c, total):
            if c * 128 < split:
                far_head[p, at, c * 128:(c + 1) * 128] = total
            else:
                far_rest[p, at, c * 128 - split:(c + 1) * 128 - split] = total

        look_up(far_tab, bt_ref, at, store, pairs=pairs, cols=cols)
        return carry

    lax.fori_loop(0, rows // 8, far_body, 0)
    for p in range(pairs):
        far_head[p, rows:, :] = jnp.zeros((cols - rows, split), jnp.int32)
        far_rest[p, rows:, :] = jnp.zeros((cols - rows, cols - split), jnp.int32)
    for h in range(2 * pairs):
        inv_ref[h:h + 1, :] = jnp.concatenate(
            [far_inv[h, j * 128:min(rows, (j + 1) * 128), :].T[0:1] for j in range(cols // 128 - 1)]
            + [jnp.concatenate([far_inv[h, cols - 128:rows, :],
                                jnp.zeros((cols - rows, 128), f32)], axis=0).T[0:1]], axis=1)


def forward_rows(
    used_ref, q_ref, k_ref, v_ref, pk_ref, b_ref, far_sum, inv_ref, p_ref, ctx_ref,
    near_tab, near_inv, near_sum, score, *, first, rows, span, cols, pairs, scale,
):
    for p in range(pairs):
        fill_tables(q_ref, first, rows, pk_ref, near_tab, near_inv, p)
    used = used_ref[0]
    place = lax.broadcasted_iota(jnp.int32, (1, cols), 1)
    valid = ((place >= TEXT) & (place < span)) | (place < used)

    def block_body(start, tall):
        def near_body(step, carry):
            at = pl.ds(pl.multiple_of(start + step * 8, 8), 8)
            out_at = pl.ds(pl.multiple_of(step * 8, 8), 8)

            def store(p, c, total):
                near_sum[p, out_at, c * 128:(c + 1) * 128] = total

            look_up(near_tab, b_ref, at, store, pairs=pairs, cols=cols)
            return carry

        lax.fori_loop(0, tall // 8, near_body, 0)
        at = pl.ds(start, tall)
        for p in range(pairs):
            cut = slice(p * 128, (p + 1) * 128)
            block = q_ref[pl.ds(pl.multiple_of(first + start, 64), tall), cut]
            zero = jnp.zeros_like(block)
            mask = lane_half((tall, 128))
            score[0, 0:tall, :] = nt(jnp.where(mask, block, zero), k_ref[:, cut])
            score[1, 0:tall, :] = nt(jnp.where(mask, zero, block), k_ref[:, cut])
            for c in range(cols // 128):
                turned = far_sum[p, c * 128:(c + 1) * 128, pl.ds(start, 128)].T[0:tall]
                here = slice(c * 128, (c + 1) * 128)
                f0, f1 = unpack_pair(turned)
                n0, n1 = unpack_pair(near_sum[p, 0:tall, here])
                score[0, 0:tall, here] += (
                    f0 * inv_ref[2 * p:2 * p + 1, here] + n0 * near_inv[2 * p, at, :]
                )
                score[1, 0:tall, here] += (
                    f1 * inv_ref[2 * p + 1:2 * p + 2, here] + n1 * near_inv[2 * p + 1, at, :]
                )
            for h in range(2):
                for s in range(tall // 16):
                    raw = score[h, s * 16:(s + 1) * 16, :]
                    logits = jnp.where(valid, raw * scale, -1e30)
                    top = jnp.max(logits, axis=1, keepdims=True)
                    grown = jnp.exp(logits - top)
                    share = grown * (1.0 / jnp.sum(grown, axis=1, keepdims=True))
                    p_ref[2 * p + h, pl.ds(pl.multiple_of(start + s * 16, 16), 16), :] = share.astype(bf16)
            c0 = nn(p_ref[2 * p, at, :], v_ref[:, cut])
            c1 = nn(p_ref[2 * p + 1, at, :], v_ref[:, cut])
            ctx_ref[at, cut] = jnp.where(mask, c0, c1).astype(bf16)

    def outer(step, carry):
        block_body(pl.multiple_of(step * 128, 128), 128)
        return carry

    lax.fori_loop(0, rows // 128, outer, 0)
    if rows % 128:
        block_body(rows - rows % 128, rows % 128)


def project_kernel(x_ref, wq_ref, wk_ref, wv_ref, t_ref, kp_ref, qp_ref, qkv_ref, pk_ref, pq_ref, *, span, cols, width):
    tail = span - span % 128
    qkv_ref[span - span % 16:cols, :] = jnp.zeros((cols - span + span % 16, 3 * width), bf16)
    for n, w_ref in enumerate((wq_ref, wk_ref, wv_ref)):
        cut = slice(n * width, (n + 1) * width)

        def body(step, carry, cut=cut, w_ref=w_ref):
            at = pl.ds(pl.multiple_of(step * 128, 128), 128)
            qkv_ref[at, cut] = nn(x_ref[at, :], w_ref[...]).astype(bf16)
            return carry

        lax.fori_loop(0, span // 128, body, 0)
        if tail < span:
            qkv_ref[tail:span, cut] = nn(x_ref[tail:span, :], w_ref[...]).astype(bf16)
    for r in range(3):
        at = slice(r * REL, (r + 1) * REL)
        pk_ref[at, :] = nn(t_ref[r], kp_ref[...]).astype(bf16)
        pq_ref[at, :] = nn(t_ref[r], qp_ref[...]).astype(bf16)


def project(tokens, query_weight, key_weight, value_weight, tables, key_position, query_position, span):
    width = query_weight.shape[1]
    rows, cols = sizes(span)
    whole = pl.BlockSpec(memory_space=pltpu.VMEM)
    return pl.pallas_call(
        functools.partial(project_kernel, span=span, cols=cols, width=width),
        out_shape=(
            jax.ShapeDtypeStruct((cols, 3 * width), bf16),
            jax.ShapeDtypeStruct((3 * REL, width), bf16),
            jax.ShapeDtypeStruct((3 * REL, width), bf16),
        ),
        in_specs=[whole] * 7,
        out_specs=(whole,) * 3,
        compiler_params=pltpu.CompilerParams(vmem_limit_bytes=VMEM_CAP),
        cost_estimate=pl.CostEstimate(flops=4 * 10**9, bytes_accessed=9 * 10**6, transcendentals=0),
        name="project",
    )(tokens, query_weight, key_weight, value_weight, tables, key_position, query_position)


def pick(half, block, h):
    zero = jnp.zeros_like(block)
    return jnp.where(half, block, zero) if h == 0 else jnp.where(half, zero, block)


def draw_kernel(
    p_ref, up_ref, q_ref, k_ref, v_ref, *refs, first, tall, rows, cols, scale, adds,
):
    extra = refs[:adds]
    d_ref, dt_ref, dq_ref, dk_ref, dv_ref, wide, flat, turned = refs[adds:]
    lanes = turned.shape[2]
    half = lane_half((64, 128))

    def body(step, carry):
        at = pl.ds(pl.multiple_of(step * 64, 64), 64)
        pair = []
        for h in range(2):
            reach = nt(pick(half, up_ref[at, :], h), v_ref[...])
            share = p_ref[h, at, :].astype(f32)
            inner = jnp.sum(reach * share, axis=1, keepdims=True)
            back = share * (reach - inner) * scale
            wide[h, at, :] = back
            flat[h, at, :] = back.astype(bf16)
            pair.append(back.reshape(8, 8, cols))
        d_ref[pl.ds(pl.multiple_of(step * 8, 8), 8), :, :] = jnp.concatenate(pair, axis=1).astype(bf16)
        return carry

    lax.fori_loop(0, tall // 64, body, 0)
    for jb in range(cols // 128):
        high = min(128, rows - jb * 128)
        for ib in range(lanes // 128):
            wide_rows = min(128, tall - ib * 128)
            pair = []
            for h in range(2):
                block = wide[h, ib * 128:ib * 128 + wide_rows, jb * 128:(jb + 1) * 128]
                if wide_rows < 128:
                    block = jnp.concatenate([block, jnp.zeros((128 - wide_rows, 128), f32)], axis=0)
                other = block.T[:high]
                turned[h, jb * 128:jb * 128 + high, ib * 128:(ib + 1) * 128] = other.astype(bf16)
                pair.append(other.reshape(high // 8, 8, 128))
            dt_ref[jb * 16:jb * 16 + high // 8, :, ib * 128:(ib + 1) * 128] = jnp.concatenate(
                pair, axis=1
            ).astype(bf16)
    keys, queries, ups = k_ref[...], q_ref[first:first + lanes, :], up_ref[...]
    cols_half, lanes_half, tall_half = (lane_half((n, 128)) for n in (cols, lanes, tall))
    dq_ref[...] = nn(flat[0], pick(cols_half, keys, 0)) + nn(flat[1], pick(cols_half, keys, 1))
    dk = nn(turned[0], pick(lanes_half, queries, 0)) + nn(turned[1], pick(lanes_half, queries, 1))
    dv = tn(p_ref[0], pick(tall_half, ups, 0)) + tn(p_ref[1], pick(tall_half, ups, 1))
    dv = dv[:rows]
    if adds:
        dk, dv = dk + extra[0][...], dv + extra[1][...]
    dk_ref[...] = dk
    dv_ref[...] = dv.astype(dv_ref.dtype)


def scatter_kernel(*refs, groups, cols):
    *d_refs, b_ref, merge_ref, out_ref = refs
    base = jnp.where(lax.broadcasted_iota(jnp.int32, (16, cols), 0) >= 8, 1.0, 0.0).astype(bf16)
    own = (lax.broadcasted_iota(jnp.int32, (256, 256), 0) % 8) == (
        lax.broadcasted_iota(jnp.int32, (256, 256), 1) % 8
    )
    zero = jnp.asarray(0.0, bf16)
    one = jnp.asarray(1.0, bf16)

    def sieve(g, r, back):
        bucket = b_ref[r, pl.ds(pl.multiple_of(g * 8, 8), 8), :]
        low = (bucket & 31).astype(f32)
        high = (bucket >> 5).astype(f32)
        low = jnp.concatenate([low, low], axis=0).astype(bf16) - base
        high = jnp.concatenate([high, high], axis=0).astype(bf16)
        hot = jnp.concatenate(
            [jnp.where(low == jnp.asarray(2.0 * k, bf16), one, zero) for k in range(16)], axis=0
        )
        sieved = []
        for l in range(4):
            mask = high == jnp.asarray(float(l), bf16)
            for p in range(4):
                sieved.append(jnp.where(mask, back[p * 16:(p + 1) * 16], zero))
        sums = nt(jnp.concatenate(sieved, axis=0), hot)
        return jnp.where(own, sums, 0.0).astype(bf16)

    def body(step, carry):
        got = []
        for g in (2 * step, 2 * step + 1):
            back = jnp.concatenate([d_ref[g] for d_ref in d_refs], axis=1) if len(d_refs) > 1 else d_refs[0][g]
            for r in range(3):
                got.append((g, r, sieve(g, r, back)))
        for g, r, sums in got:
            total = None
            for l in range(4):
                term = nn(sums[l * 64:(l + 1) * 64], merge_ref[l])
                total = term if total is None else total + term
            out_ref[g, :, r * 128:(r + 1) * 128] = total.astype(bf16)
        return carry

    lax.fori_loop(0, groups // 2, body, 0)


def close_kernel(*refs, rows, count):
    base_ref, pos_ref, side_ref, out_ref, table_ref = refs[count:]
    rows2 = 2 * rows
    half3 = lane_half((rows // 8, 8, 128))
    flat = jnp.concatenate([ref[...] for ref in refs[:count]], axis=0).reshape(rows2, 3 * REL)
    both = nn(flat, pos_ref[...]).reshape(rows // 8, 16, 128)
    mine = jnp.where(half3, both[:, 0:8, :], both[:, 8:16, :]).reshape(rows, 128)
    out_ref[...] = base_ref[...] + mine
    side = side_ref[0:rows, :].astype(f32).reshape(rows // 8, 8, 128)
    zero = jnp.zeros_like(side)
    spread = jnp.concatenate([jnp.where(half3, side, zero), jnp.where(half3, zero, side)], axis=1)
    table_ref[...] = tn(flat, spread.reshape(rows2, 128).astype(bf16)).astype(bf16)


def merge_table():
    l = lax.broadcasted_iota(jnp.int32, (4, 256, 128), 0)
    a = lax.broadcasted_iota(jnp.int32, (4, 256, 128), 1) // 8
    c = lax.broadcasted_iota(jnp.int32, (4, 256, 128), 2)
    return (c == l * 32 + a).astype(bf16)


def sizes(span):
    return -(-span // 64) * 64, -(-span // 128) * 128


def forward_scratch(pairs, tall, cols):
    return [
        pltpu.VMEM((pairs, tall, 3 * REL), jnp.int32),
        pltpu.VMEM((2 * pairs, tall, 128), f32),
        pltpu.VMEM((pairs, 128, cols), jnp.int32),
        pltpu.VMEM((2, 128, cols), f32),
    ]


def attention_head(qkv, pos_key, pos_query, buckets, used, scale, split):
    span = buckets.shape[2]
    rows, cols = sizes(span)
    width = pos_key.shape[1]
    pairs = width // 128
    whole = pl.BlockSpec(memory_space=pltpu.VMEM)
    i32 = jnp.int32

    def kernel(
        used_ref, qkv_ref, pk_ref, pq_ref, b_ref, p_ref, ctx_ref, head_ref, rest_ref, bt_ref, far_rest, inv_ref,
        far_tab, far_inv, far_head, *scratch,
    ):
        k_ref = qkv_ref.at[:, width:2 * width]
        prepare_rows(
            k_ref, pq_ref, b_ref, head_ref, rest_ref, bt_ref, far_head, far_rest, inv_ref, far_tab, far_inv,
            span=span, rows=rows, cols=cols, pairs=pairs, split=split,
        )
        forward_rows(
            used_ref, qkv_ref.at[:, 0:width], k_ref, qkv_ref.at[:, 2 * width:3 * width], pk_ref, head_ref,
            far_head, inv_ref, p_ref, ctx_ref, *scratch,
            first=0, rows=split, span=span, cols=cols, pairs=pairs, scale=scale,
        )

    return pl.pallas_call(
        kernel,
        out_shape=(
            jax.ShapeDtypeStruct((2 * pairs, split, cols), bf16),
            jax.ShapeDtypeStruct((split, width), bf16),
            jax.ShapeDtypeStruct((3, split, cols), i32),
            jax.ShapeDtypeStruct((3, rows - split, cols), i32),
            jax.ShapeDtypeStruct((3, rows, cols), i32),
            jax.ShapeDtypeStruct((pairs, cols, cols - split), i32),
            jax.ShapeDtypeStruct((2 * pairs, cols), f32),
        ),
        in_specs=[pl.BlockSpec(memory_space=pltpu.SMEM)] + [whole] * 4,
        out_specs=(whole,) * 7,
        scratch_shapes=[
            pltpu.VMEM((pairs, rows, 3 * REL), i32),
            pltpu.VMEM((2 * pairs, rows, 128), f32),
            pltpu.VMEM((pairs, cols, split), i32),
        ] + forward_scratch(pairs, split, cols),
        compiler_params=pltpu.CompilerParams(vmem_limit_bytes=VMEM_CAP),
        cost_estimate=pl.CostEstimate(flops=4 * 10**10, bytes_accessed=25000000, transcendentals=0),
        name="attention_head",
    )(used, qkv, pos_key, pos_query, buckets)


def attention_rest(qkv, pos_key, bucket_rest, far_rest, inverse, used, scale, split, span):
    rows, cols = sizes(span)
    width = pos_key.shape[1]
    pairs = width // 128
    whole = pl.BlockSpec(memory_space=pltpu.VMEM)

    def kernel(used_ref, qkv_ref, pk_ref, b_ref, far_ref, inv_ref, p_ref, ctx_ref, *scratch):
        forward_rows(
            used_ref, qkv_ref.at[:, 0:width], qkv_ref.at[:, width:2 * width], qkv_ref.at[:, 2 * width:3 * width],
            pk_ref, b_ref, far_ref, inv_ref, p_ref, ctx_ref, *scratch,
            first=split, rows=rows - split, span=span, cols=cols, pairs=pairs, scale=scale,
        )

    return pl.pallas_call(
        kernel,
        out_shape=(
            jax.ShapeDtypeStruct((2 * pairs, rows - split, cols), bf16),
            jax.ShapeDtypeStruct((rows - split, width), bf16),
        ),
        in_specs=[pl.BlockSpec(memory_space=pltpu.SMEM)] + [whole] * 5,
        out_specs=(whole,) * 2,
        scratch_shapes=forward_scratch(pairs, rows - split, cols),
        compiler_params=pltpu.CompilerParams(vmem_limit_bytes=VMEM_CAP),
        cost_estimate=pl.CostEstimate(flops=2 * 10**10, bytes_accessed=12000000, transcendentals=0),
        name="attention_rest",
    )(used, qkv, pos_key, bucket_rest, far_rest, inverse)


def attention_draw(share, upstream, qkv, scale, first, rows, adds=()):
    heads, tall, cols = share.shape
    width = upstream.shape[1]
    pairs = heads // 2
    lanes = -(-tall // 128) * 128

    def column(n):
        return pl.BlockSpec((n, 128), lambda p: (0, p))

    return pl.pallas_call(
        functools.partial(draw_kernel, first=first, tall=tall, rows=rows, cols=cols, scale=scale, adds=len(adds)),
        grid=(pairs,),
        in_specs=[
            pl.BlockSpec((2, tall, cols), lambda p: (p, 0, 0)),
            column(tall),
            pl.BlockSpec((cols, 128), lambda p: (0, p)),
            pl.BlockSpec((cols, 128), lambda p: (0, p + pairs)),
            pl.BlockSpec((cols, 128), lambda p: (0, p + 2 * pairs)),
        ] + [column(rows)] * len(adds),
        out_specs=(
            pl.BlockSpec((tall // 8, 16, cols), lambda p: (0, p, 0)),
            pl.BlockSpec((rows // 8, 16, lanes), lambda p: (0, p, 0)),
            column(tall), column(rows), column(rows),
        ),
        out_shape=(
            jax.ShapeDtypeStruct((tall // 8, 8 * heads, cols), bf16),
            jax.ShapeDtypeStruct((rows // 8, 8 * heads, lanes), bf16),
            jax.ShapeDtypeStruct((tall, width), f32),
            jax.ShapeDtypeStruct((rows, width), f32),
            jax.ShapeDtypeStruct((rows, width), bf16 if adds else f32),
        ),
        scratch_shapes=[
            pltpu.VMEM((2, tall, cols), f32),
            pltpu.VMEM((2, tall, cols), bf16),
            pltpu.VMEM((2, rows, lanes), bf16),
        ],
        compiler_params=pltpu.CompilerParams(vmem_limit_bytes=VMEM_CAP),
        cost_estimate=pl.CostEstimate(flops=10**10, bytes_accessed=12000000, transcendentals=0),
        name="attention_draw",
    )(share, upstream, qkv, qkv, qkv, *adds)


def attention_scatter(backs, buckets, merge, first, count):
    high = backs[0].shape[1]
    cols = buckets.shape[2]
    return pl.pallas_call(
        functools.partial(scatter_kernel, groups=8, cols=cols),
        grid=(count,),
        out_shape=jax.ShapeDtypeStruct((8 * count, high, 3 * REL), bf16),
        in_specs=[pl.BlockSpec((8, high, b.shape[2]), lambda g: (first + g, 0, 0)) for b in backs] + [
            pl.BlockSpec((3, 64, cols), lambda g: (0, first + g, 0)),
            pl.BlockSpec(merge.shape, lambda g: (0, 0, 0)),
        ],
        out_specs=pl.BlockSpec((8, high, 3 * REL), lambda g: (g, 0, 0)),
        compiler_params=pltpu.CompilerParams(vmem_limit_bytes=VMEM_CAP),
        cost_estimate=pl.CostEstimate(flops=5 * 10**9 * count, bytes_accessed=10**6 * count, transcendentals=0),
        name="attention_scatter",
    )(*backs, buckets, merge)


def attention_close(sums, base, pos, qkv, side):
    rows, width = base.shape
    pairs = width // 128
    return pl.pallas_call(
        functools.partial(close_kernel, rows=rows, count=len(sums)),
        grid=(pairs,),
        in_specs=[pl.BlockSpec((part.shape[0], 16, 3 * REL), lambda p: (0, p, 0)) for part in sums] + [
            pl.BlockSpec((rows, 128), lambda p: (0, p)),
            pl.BlockSpec((3 * REL, 128), lambda p: (0, p)),
            pl.BlockSpec((qkv.shape[0], 128), lambda p: (0, p + side * pairs)),
        ],
        out_specs=(
            pl.BlockSpec((rows, 128), lambda p: (0, p)),
            pl.BlockSpec((3 * REL, 128), lambda p: (0, p)),
        ),
        out_shape=(
            jax.ShapeDtypeStruct((rows, width), f32),
            jax.ShapeDtypeStruct((3 * REL, width), bf16),
        ),
        compiler_params=pltpu.CompilerParams(vmem_limit_bytes=VMEM_CAP),
        cost_estimate=pl.CostEstimate(flops=5000000000, bytes_accessed=10000000, transcendentals=0),
        name="attention_close",
    )(*sums, base, pos, qkv)


def fill_turned(x_ref, turned, rows):
    depth = x_ref.shape[1]
    for a in range(0, rows, 128):
        tall = min(128, rows - a)
        for b in range(0, depth, 128):
            block = x_ref[a:a + tall, b:b + 128]
            if tall < 128:
                block = jnp.concatenate([block, jnp.zeros((128 - tall, 128), block.dtype)], axis=0)
            turned[b:b + 128, a:a + tall] = block.T[:, :tall]


def each_block(pick_ref, blocks, keeps, bit, slot):
    if not keeps:
        return [(0, d, d) for d in range(blocks)]
    shift = bit - 1
    listed = []
    for out in range(2):
        value = pick_ref[slot] if out == 1 else 1 - pick_ref[slot]
        for e in range(blocks // 2):
            low = e & ((1 << shift) - 1)
            listed.append((out, e, ((e >> shift) << (shift + 1)) + low + value * (1 << shift)))
    return listed


def weight_kernel(pick_ref, *refs, count, blocks, deep, keeps, bit):
    xs, ys, rest = refs[:count], refs[count:2 * count], refs[2 * count:]
    add_ref = rest[0] if keeps else None
    outs = rest[1:3] if keeps else rest[0:1]
    turned = rest[-count:]

    @pl.when(pl.program_id(0) == 0)
    def _():
        for x_ref, wide in zip(xs, turned):
            fill_turned(x_ref, wide, x_ref.shape[0])

    for out, place, d in each_block(pick_ref, blocks, keeps, bit, 1):
        at = pl.ds(pl.multiple_of((2 * d + pick_ref[0]) * deep, deep), deep)
        part = add_ref[d] if keeps else None
        for wide, y_ref in zip(turned, ys):
            term = nn(wide[at, :], y_ref[...])
            part = term if part is None else part + term
        outs[out][place] = part


def weight_half(pick, xs, ys, add=None, *, parts, bits, tile=512):
    depth = xs[0].shape[1]
    wide = ys[0].shape[1]
    deep = depth // parts
    blocks = parts // 2
    keeps = add is not None

    def tiled(n):
        return pl.BlockSpec((n, deep, tile), lambda c: (0, 0, c))

    ins = [pl.BlockSpec(memory_space=pltpu.SMEM)]
    ins += [pl.BlockSpec(x.shape, lambda c: (0, 0)) for x in xs]
    ins += [pl.BlockSpec((y.shape[0], tile), lambda c: (0, c)) for y in ys]
    args = [pick, *xs, *ys]
    shape = (jax.ShapeDtypeStruct((blocks, deep, wide), f32),)
    specs = (tiled(blocks),)
    if keeps:
        ins.append(tiled(blocks))
        args += add
        shape = (jax.ShapeDtypeStruct((blocks // 2, deep, wide), f32),) * 2
        specs = (tiled(blocks // 2),) * 2
    rows = sum(x.shape[0] for x in xs)
    return pl.pallas_call(
        functools.partial(weight_kernel, count=len(xs), blocks=blocks, deep=deep, keeps=keeps, bit=bits[0]),
        grid=(wide // tile,),
        in_specs=ins,
        out_specs=specs,
        out_shape=shape,
        scratch_shapes=[pltpu.VMEM((depth, x.shape[0]), bf16) for x in xs],
        compiler_params=pltpu.CompilerParams(vmem_limit_bytes=VMEM_CAP),
        cost_estimate=pl.CostEstimate(
            flops=rows * depth * wide, bytes_accessed=4 * depth * wide, transcendentals=0
        ),
        name="weight_half",
    )(*args)


def many_kernel(pick_ref, *refs, plan, widths, turns, blocks, deep, keeps, bits):
    n_in = 2 * len(plan)
    ins = refs[:n_in]
    n_out = len(widths)
    adds = refs[n_in:n_in + n_out] if keeps else None
    outs = refs[n_in + n_out:n_in + 3 * n_out] if keeps else refs[n_in:n_in + n_out]
    scratch = refs[len(refs) - sum(turns):]
    left = []
    used = 0
    for n, turn in enumerate(turns):
        if turn:
            fill_turned(ins[2 * n], scratch[used], ins[2 * n].shape[0])
            left.append(scratch[used])
            used += 1
        else:
            left.append(ins[2 * n])
    right = [ins[2 * n + 1][...] for n in range(len(plan))]
    for group in range(n_out):
        for out, place, d in each_block(pick_ref, blocks, keeps, bits[group], 1 + group):
            at = pl.ds(pl.multiple_of((2 * d + pick_ref[0]) * deep, deep), deep)
            target = outs[2 * group + out] if keeps else outs[group]
            for n, (kind, own, start, wide) in enumerate(plan):
                if own != group:
                    continue
                rows = left[n][at, :]
                if kind == "copy":
                    part = rows
                elif kind == "nt":
                    part = nt(rows, right[n])
                else:
                    part = nn(rows, right[n])
                cut = slice(start, start + wide)
                if keeps:
                    part = part + adds[group][d, :, cut]
                target[place, :, cut] = part


def many_half(pick, pairs, plan, widths, add=None, *, parts, bits):
    whole = pl.BlockSpec(memory_space=pltpu.VMEM)
    turns = [kind in ("turn", "copy") for kind, *_ in plan]
    depth = max(left.shape[1 if turn else 0] for (left, _), turn in zip(pairs, turns))
    deep = depth // parts
    blocks = parts // 2
    keeps = add is not None
    args = [pick] + [operand for pair in pairs for operand in pair] + (list(add) if keeps else [])
    if keeps:
        shape = [jax.ShapeDtypeStruct((blocks // 2, deep, w), f32) for w in widths for _ in range(2)]
    else:
        shape = [jax.ShapeDtypeStruct((blocks, deep, w), f32) for w in widths]
    return pl.pallas_call(
        functools.partial(
            many_kernel, plan=plan, widths=widths, turns=turns, blocks=blocks, deep=deep,
            keeps=keeps, bits=[b[0] for b in bits],
        ),
        in_specs=[pl.BlockSpec(memory_space=pltpu.SMEM)] + [whole] * (len(args) - 1),
        out_specs=[whole] * len(shape),
        out_shape=shape,
        scratch_shapes=[
            pltpu.VMEM((left.shape[1], left.shape[0]), left.dtype)
            for (left, _), turn in zip(pairs, turns) if turn
        ],
        compiler_params=pltpu.CompilerParams(vmem_limit_bytes=VMEM_CAP),
        cost_estimate=pl.CostEstimate(
            flops=600 * depth * sum(widths), bytes_accessed=6 * depth * sum(widths), transcendentals=0
        ),
        name="many_half",
    )(*args)


def flipped(value, bit, size):
    return lax.ppermute(value, "dp", [(i, i ^ (1 << bit)) for i in range(size)])


def bit_of(index, bit):
    return (index >> bit) & 1


class Halving:
    def __init__(self, make, index, size, orders):
        self.make, self.index, self.size, self.orders = make, index, size, orders
        mine = bit_of(index, 0).astype(jnp.int32)
        self.pick = jnp.stack([mine] + [bit_of(index, bits[0]).astype(jnp.int32) for bits in orders])
        self.other = self.pick.at[0].set(1 - mine)
        self.stage = 0

    def work(self):
        if self.stage == 0:
            self.pending = [(sent, None) for sent in self.make(self.other, None)]
        elif self.stage == 1:
            outs = self.make(self.pick, self.extra)
            self.pending = [(outs[2 * g], outs[2 * g + 1]) for g in range(len(self.orders))]
            self.axes = [
                [b for b in range(self.size.bit_length() - 1, 0, -1) if b != bits[0] and b < self.size.bit_length() - 1]
                for bits in self.orders
            ]
        else:
            self.pending = [
                self.split(g, held, extra) for g, (held, extra) in enumerate(zip(self.held, self.extra))
            ]
        return [part for pair in self.pending for part in pair if part is not None]

    def split(self, g, held, extra):
        bits = self.orders[g]
        if self.stage > len(bits):
            return held + extra, None
        bit = bits[self.stage - 1]
        axis = self.axes[g].index(bit)
        shape = (2,) * len(self.axes[g]) + held.shape[-2:]
        self.axes[g].remove(bit)
        own = bit_of(self.index, bit)
        held, extra = held.reshape(shape), extra.reshape(shape)

        def half(value, at):
            return lax.dynamic_index_in_dim(value, at, axis, keepdims=False)

        return half(held, 1 - own) + half(extra, 1 - own), half(held, own) + half(extra, own)

    def go(self, parts):
        parts = list(parts)
        pairs = [
            tuple(None if part is None else parts.pop(0) for part in pair) for pair in self.pending
        ]
        self.held = [home for _, home in pairs]
        last = self.stage > len(self.orders[0])
        if last:
            self.result = [away for away, _ in pairs]
        else:
            bit = lambda g: 0 if self.stage == 0 else self.orders[g][self.stage - 1]
            self.extra = [flipped(away, bit(g), self.size) for g, (away, _) in enumerate(pairs)]
        self.stage += 1

    def step(self):
        self.go(self.work())

    def over(self):
        return self.stage > len(self.orders[0]) + 1

    def finish(self):
        while not self.over():
            self.step()
        return self.result


def tie(values, *chains):
    works = [chain.work() for chain in chains]
    values, works = lax.optimization_barrier((values, works))
    for chain, parts in zip(chains, works):
        chain.go(parts)
    return values


def swap(value):
    return lax.ppermute(value.astype(f32), "mp", [(0, 1), (1, 0)])


def join_kernel(head_ref, rest_ref, early_ref, early_other_ref, mine_ref, w_ref, other_ref, ow_ref, out_ref, *, span):
    weight = ow_ref[...].astype(bf16)
    split = head_ref.shape[0]
    for start in range(0, span, 64):
        tall = min(64, span - start)
        at = slice(start, start + 64)
        base = head_ref[at, :] if start < split else rest_ref[start - split:start - split + 64, :]
        total = base + early_ref[at, :] + early_other_ref[at, :] + nt(mine_ref[at, :], w_ref[...])
        total = total + nt(other_ref[at, :].astype(bf16), weight)
        out_ref[start:start + tall, :] = total.astype(bf16)[:tall]


def join(bases, early, early_other, mine, weight, other, other_weight, span):
    whole = pl.BlockSpec(memory_space=pltpu.VMEM)
    return pl.pallas_call(
        functools.partial(join_kernel, span=span),
        in_specs=[whole] * 8,
        out_specs=whole,
        out_shape=jax.ShapeDtypeStruct((span, early.shape[1]), bf16),
        compiler_params=pltpu.CompilerParams(vmem_limit_bytes=VMEM_CAP),
        cost_estimate=pl.CostEstimate(flops=3 * 10**9, bytes_accessed=12 * 10**6, transcendentals=0),
        name="join",
    )(*bases, early, early_other, mine, weight, other, other_weight)


def attend_kernel(
    t_ref, c_ref, o_ref, w_ref, ow_ref, gain_ref, shift_ref, first_ref, low_ref, normal_ref, inverse_ref,
):
    weight = ow_ref[...].astype(bf16)

    def body(step, carry):
        at = pl.ds(pl.multiple_of(step * 64, 64), 64)
        summed = t_ref[at, :].astype(f32) + nn(c_ref[at, :], w_ref[...])
        summed = summed + nn(o_ref[at, :].astype(bf16), weight)
        first, normal, inverse = norm_forward(summed, gain_ref[...], shift_ref[...])
        first_ref[at, :] = first
        low_ref[at, :] = first.astype(bf16)
        normal_ref[at, :] = normal
        inverse_ref[at, :] = inverse
        return carry

    lax.fori_loop(0, t_ref.shape[0] // 64, body, 0)


def attend(tokens, context, other, weight, other_weight, gain, shift):
    tall, depth = tokens.shape
    whole = pl.BlockSpec(memory_space=pltpu.VMEM)
    return pl.pallas_call(
        attend_kernel,
        in_specs=[whole] * 7,
        out_specs=(whole,) * 4,
        out_shape=(
            jax.ShapeDtypeStruct((tall, depth), f32),
            jax.ShapeDtypeStruct((tall, depth), bf16),
            jax.ShapeDtypeStruct((tall, depth), f32),
            jax.ShapeDtypeStruct((tall, 1), f32),
        ),
        compiler_params=pltpu.CompilerParams(vmem_limit_bytes=VMEM_CAP),
        cost_estimate=pl.CostEstimate(flops=2 * 10**9, bytes_accessed=8 * 10**6, transcendentals=0),
        name="attend",
    )(tokens, context, other, weight, other_weight, gain[None], shift[None])


def norm_forward(summed, gain, shift):
    centred = summed - jnp.mean(summed, axis=1, keepdims=True)
    inverse = lax.rsqrt(jnp.mean(centred * centred, axis=1, keepdims=True) + epsilon)
    normal = centred * inverse
    return (normal * gain + shift, normal, inverse)


def norm_backward(upstream, normal, inverse, gain):
    scaled = upstream * gain
    inner = jnp.mean(scaled, axis=1, keepdims=True)
    aligned = jnp.mean(scaled * normal, axis=1, keepdims=True)
    return (
        inverse * (scaled - inner - normal * aligned),
        jnp.sum(upstream * normal, axis=0),
        jnp.sum(upstream, axis=0),
    )


def shards(
    tokens,
    query_weight,
    key_weight,
    value_weight,
    output_weight,
    query_position,
    key_position,
    position_tables,
    gain_one,
    shift_one,
    up_weight,
    down_weight,
    gain_two,
    shift_two,
    buckets,
    text_length,
    cotangent,
):
    span = buckets.shape[2]
    rows, cols = sizes(span)
    size = lax.axis_size("dp")
    index = lax.axis_index("dp")
    bits = list(range(1, size.bit_length() - 1))
    low_first, high_first = bits, bits[1:2] + bits[:1] + bits[2:]
    score_scale = (7.0 * HEAD) ** (-0.5)
    tables_flat = position_tables.reshape(3 * REL, D)
    width = query_weight.shape[1]
    spare = ((0, rows - span), (0, 0))

    def chain(make, *orders):
        return Halving(make, index, size, list(orders))

    split = rows // 2 // 128 * 128
    other_output = swap(output_weight)
    qkv, pos_key, pos_query = project(
        tokens, query_weight, key_weight, value_weight, position_tables, key_position, query_position, span
    )
    tokens = jnp.pad(tokens, spare)
    cotangent = jnp.pad(cotangent, spare)
    tokens_turned, tables_turned = tokens.T, tables_flat.T
    edges = [(0, split), (split, rows)]

    share_head, context_head, bucket_head, bucket_rest, bucket_cols, far_rest, far_inverse = attention_head(
        qkv, pos_key, pos_query, buckets, text_length, score_scale, split
    )
    other_head = swap(context_head)
    far_rest, other_output = lax.optimization_barrier((far_rest, other_output))
    share_rest, context_rest = attention_rest(
        qkv, pos_key, bucket_rest, far_rest, far_inverse, text_length, score_scale, split, span
    )
    other_rest = swap(context_rest)
    shares = [share_head, share_rest]
    contexts = [context_head, context_rest]
    contexts_other = [other_head, other_rest]

    def gelu(value):
        return jax.nn.gelu(value, approximate=False)

    firsts, firsts_low, normals_one, inverses_one, upwards, hiddens, feeds, feeds_other = ([] for _ in range(8))
    for (low, high), context, other in zip(edges, contexts, contexts_other):
        first, first_low, normal_one, inverse_one = attend(
            tokens[low:high], context, other, output_weight, other_output, gain_one, shift_one
        )
        firsts.append(first)
        normals_one.append(normal_one)
        inverses_one.append(inverse_one)
        firsts_low.append(first_low)
        upwards.append(nn(firsts_low[-1], up_weight))
        hiddens.append(gelu(upwards[-1]).astype(bf16))
        feeds.append(nn(hiddens[-1], down_weight))
        feeds_other.append(swap(feeds[-1]))

    finals, seconds_back, seconds_low, upwards_back, backs_part, backs_other, two_sums = ([] for _ in range(7))
    for n, (low, high) in enumerate(edges):
        final, normal_two, inverse_two = norm_forward(
            firsts[n] + feeds[n] + feeds_other[n], gain_two, shift_two
        )
        finals.append(final.astype(bf16))
        second_back, *sums = norm_backward(
            cotangent[low:high].astype(f32), normal_two, inverse_two, gain_two
        )
        two_sums.append(sums)
        seconds_back.append(second_back)
        seconds_low.append(second_back.astype(bf16))
        hidden_back = nt(seconds_low[n], down_weight)
        upwards_back.append(jax.vjp(gelu, upwards[n])[1](hidden_back)[0].astype(bf16))
        backs_part.append(nt(upwards_back[n], up_weight))
        backs_other.append(swap(backs_part[n]))
    layer_output = jnp.concatenate(finals, axis=0)[:span]
    gain_two_grad, shift_two_grad = (two_sums[0][n] + two_sums[1][n] for n in range(2))

    backs_part, down_pair, up_pair = lax.optimization_barrier(
        (backs_part, (seconds_low, hiddens), (firsts_low, upwards_back))
    )
    down_chain = chain(
        lambda pick, add: weight_half(pick, *down_pair, add, parts=size, bits=high_first), high_first
    )
    up_chain = chain(
        lambda pick, add: weight_half(pick, *up_pair, add, parts=size, bits=low_first), low_first
    )
    down_chain.step()
    up_chain.step()
    down_chain.step()
    backs_other[1] = tie(backs_other[1], up_chain)
    residuals_back, residuals_low, contexts_back, one_sums = ([] for _ in range(4))
    for n in range(2):
        residual_back, *sums = norm_backward(
            seconds_back[n] + backs_part[n] + backs_other[n], normals_one[n], inverses_one[n], gain_one
        )
        one_sums.append(sums)
        residuals_back.append(residual_back)
        residuals_low.append(residual_back.astype(bf16))
        contexts_back.append(nt(residuals_low[n], output_weight).astype(bf16))
    gain_one_grad, shift_one_grad = (one_sums[0][n] + one_sums[1][n] for n in range(2))

    merge = merge_table()
    back_head, turned_head, query_head, key_head, value_head = attention_draw(
        shares[0], contexts_back[0], qkv, score_scale, 0, rows
    )
    back_rest, turned_rest, query_rest, key_base, value_back = attention_draw(
        shares[1], contexts_back[1], qkv, score_scale, split, rows, (key_head, value_head)
    )
    query_base = jnp.concatenate([query_head, query_rest], axis=0)
    residual_low = jnp.concatenate(residuals_low, axis=0)
    context = jnp.concatenate(contexts, axis=0)
    nothing = jnp.zeros_like(gain_one)
    gains = jnp.stack(
        [gain_one_grad, shift_one_grad, gain_two_grad, shift_two_grad] + [nothing] * 4
    )
    gains = jnp.concatenate([gains, jnp.zeros((120, gains.shape[1]), f32)], axis=0)
    dummy = jnp.zeros((8, 128), bf16)
    outer_chain = chain(
        lambda pick, add: many_half(
            pick,
            [(residual_low, context), (tokens_turned, value_back), (gains, dummy)],
            [("turn", 0, 0, width), ("nn", 0, width, width), ("copy", 0, 2 * width, 128)],
            [2 * width + 128],
            add, parts=size, bits=[low_first],
        ),
        low_first,
    )
    outer_chain.step()

    def tail(rows_back, sums, position, orders):
        return chain(
            lambda pick, add: many_half(
                pick,
                [(tokens_turned, rows_back), (tables_turned, sums), (position, sums)],
                [("nn", 0, 0, width), ("nn", 1, 0, width), ("nt", 0, width, 3 * REL)],
                [width + 3 * REL, width],
                add, parts=size, bits=orders,
            ),
            *orders,
        )

    near = []
    near.append(attention_scatter([back_head], bucket_head, merge, 0, split // 64))
    back_rest, near, key_wide = tie((back_rest, near, key_weight.astype(f32)), outer_chain, down_chain)
    other_key_weight = swap(key_wide)
    near.append(attention_scatter([back_rest], bucket_rest, merge, 0, (rows - split) // 64))
    near, backs, other_key_weight = tie((near, [turned_head, turned_rest], other_key_weight), up_chain)
    query_back, key_table_sum = attention_close(near, query_base, pos_key, qkv, 0)
    query_low = query_back.astype(bf16)
    early = nt(query_low, query_weight) + nt(value_back, value_weight)
    early_other = swap(early)
    near_chain = tail(query_low, key_table_sum, key_position, [high_first, low_first])
    backs = tie(backs, near_chain, down_chain)
    far = []
    blocks = rows // 64
    cuts = [n * blocks // 3 for n in range(4)]
    for part, chains in enumerate((
        (near_chain, up_chain, outer_chain), (near_chain, down_chain), (near_chain, outer_chain, up_chain, down_chain),
    )):
        far.append(attention_scatter(backs, bucket_cols, merge, cuts[part], cuts[part + 1] - cuts[part]))
        backs, far, early_other = tie((backs, far, early_other), *[c for c in chains if not c.over()])
    key_back, query_table_sum = attention_close(far, key_base, pos_query, qkv, 1)
    key_other = swap(key_back)
    key_low = key_back.astype(bf16)
    far_chain = tail(key_low, query_table_sum, query_position, [low_first, high_first])
    far_chain.step()
    far_chain.step()
    input_gradient = join(
        residuals_back, early, early_other, key_low, key_weight, key_other, other_key_weight, span
    )
    (down_share,) = down_chain.finish()
    (up_share,) = up_chain.finish()
    (outer_share,) = outer_chain.finish()
    near_main, key_position_grad = near_chain.finish()
    far_main, query_position_grad = far_chain.finish()

    table_rows = near_main[:, width:] + far_main[:, width:]
    table_rows = table_rows.reshape(2, table_rows.shape[0] // 2, 3 * REL)
    side = lax.axis_index("mp")
    table_mine = lax.dynamic_index_in_dim(table_rows, side, 0, keepdims=False) + lax.ppermute(
        lax.dynamic_index_in_dim(table_rows, 1 - side, 0, keepdims=False), "mp", [(0, 1), (1, 0)]
    )
    table_gradient = table_mine.T.reshape(3, REL, table_mine.shape[0])
    gains_mine = outer_share[:, 2 * width:]
    return (
        layer_output,
        input_gradient,
        near_main[:, 0:width],
        far_main[:, 0:width],
        outer_share[:, width:2 * width],
        outer_share[:, 0:width].T,
        query_position_grad,
        key_position_grad,
        table_gradient,
        gains_mine[:, 0],
        gains_mine[:, 1],
        up_share,
        down_share.T,
        gains_mine[:, 2],
        gains_mine[:, 3],
    )


def solution(mesh):
    return jax.shard_map(
        shards,
        mesh=mesh,
        in_specs=(
            P("dp", None),
            P(None, "mp"),
            P(None, "mp"),
            P(None, "mp"),
            P("mp", None),
            P(None, "mp"),
            P(None, "mp"),
            P(),
            P(),
            P(),
            P(None, "mp"),
            P("mp", None),
            P(),
            P(),
            P("dp", None, None, None),
            P("dp"),
            P("dp", None),
        ),
        out_specs=(
            P("dp", None),
            P("dp", None),
            P("dp", "mp"),
            P("dp", "mp"),
            P("dp", "mp"),
            P("mp", "dp"),
            P("dp", "mp"),
            P("dp", "mp"),
            P(None, None, ("dp", "mp")),
            P("dp"),
            P("dp"),
            P("dp", "mp"),
            P("mp", "dp"),
            P("dp"),
            P("dp"),
        ),
        check_vma=False,
    )
```

```python
import functools

import jax
import jax.numpy as jnp
from jax import lax
from jax.experimental import pallas as pl
from jax.experimental.pallas import tpu as pltpu
from jax.sharding import PartitionSpec as P

D = 1024
epsilon = 1e-05
HEAD = 64
REL = 128
TEXT = 512
bf16 = jnp.bfloat16
f32 = jnp.float32
LIMIT = 10900.0
VMEM_CAP = 62 * 2**20


def lane_gather(table, index):
    numbers = lax.GatherDimensionNumbers(
        offset_dims=(),
        collapsed_slice_dims=(1,),
        start_index_map=(1,),
        operand_batching_dims=(0,),
        start_indices_batching_dims=(0,),
    )
    return lax.gather(
        table, index[..., None], numbers, (1, 1), mode=lax.GatherScatterMode.PROMISE_IN_BOUNDS
    )


def nt(left, right):
    return lax.dot_general(left, right, (((1,), (1,)), ((), ())), preferred_element_type=f32)


def nn(left, right):
    return jnp.dot(left, right, preferred_element_type=f32)


def tn(left, right):
    return lax.dot_general(left, right, (((0,), (0,)), ((), ())), preferred_element_type=f32)


def lane_half(shape):
    return lax.broadcasted_iota(jnp.int32, shape, len(shape) - 1) < HEAD


def unpack_pair(packed):
    low = (packed << 16) >> 16
    high = (packed - low) >> 16
    return high.astype(f32), low.astype(f32)


def fill_tables(src_ref, first, tall, pos_ref, tab, inv, p):
    half = lane_half((64, 128))
    cut = slice(p * 128, (p + 1) * 128)

    def body(step, carry):
        at = pl.ds(pl.multiple_of(step * 64, 64), 64)
        block = src_ref[pl.ds(pl.multiple_of(first + step * 64, 64), 64), cut]
        zero = jnp.zeros_like(block)
        first_head = nt(jnp.where(half, block, zero), pos_ref[:, cut]).astype(bf16).astype(f32)
        second_head = nt(jnp.where(half, zero, block), pos_ref[:, cut]).astype(bf16).astype(f32)
        top0 = jnp.maximum(jnp.max(jnp.abs(first_head), axis=1, keepdims=True), 1e-30)
        top1 = jnp.maximum(jnp.max(jnp.abs(second_head), axis=1, keepdims=True), 1e-30)
        whole0 = jnp.round(first_head * (LIMIT / top0)).astype(jnp.int32)
        whole1 = jnp.round(second_head * (LIMIT / top1)).astype(jnp.int32)
        tab[p, at, :] = whole0 * 65536 + whole1
        inv[2 * p, at, :] = jnp.broadcast_to(top0 * (1.0 / LIMIT), (64, 128))
        inv[2 * p + 1, at, :] = jnp.broadcast_to(top1 * (1.0 / LIMIT), (64, 128))
        return carry

    lax.fori_loop(0, tall // 64, body, 0)


def look_up(tab, index_ref, at, store, *, pairs, cols):
    for c in range(cols // 128):
        total = [None] * pairs
        for r in range(3):
            index = index_ref[r, at, c * 128:(c + 1) * 128]
            for p in range(pairs):
                got = lane_gather(tab[p, at, r * 128:(r + 1) * 128], index)
                total[p] = got if total[p] is None else total[p] + got
        for p in range(pairs):
            store(p, c, total[p])


def prepare_rows(
    k_ref, pq_ref, b_ref, head_ref, rest_ref, bt_ref, far_head, far_rest, inv_ref,
    far_tab, far_inv, *, span, rows, cols, pairs, split,
):
    edge = span - span % 8 - split
    for r in range(3):
        head_ref[r, :, span - span % 128:cols] = jnp.zeros((split, cols - span + span % 128), jnp.int32)
        rest_ref[r, edge:rows - split, :] = jnp.zeros((rows - split - edge, cols), jnp.int32)
        rest_ref[r, :, span - span % 128:cols] = jnp.zeros((rows - split, cols - span + span % 128), jnp.int32)
        head_ref[r, :, 0:span] = b_ref[0, r, 0:split]
        rest_ref[r, 0:span - split, 0:span] = b_ref[0, r, split:span]
    for r in range(3):
        for jb in range(cols // 128):
            high = min(128, rows - jb * 128)
            for ib in range(cols // 128):
                tall = min(128, rows - ib * 128)
                here = slice(jb * 128, (jb + 1) * 128)
                if ib * 128 < split:
                    block = head_ref[r, ib * 128:ib * 128 + tall, here]
                else:
                    block = rest_ref[r, ib * 128 - split:ib * 128 - split + tall, here]
                if tall < 128:
                    block = jnp.concatenate([block, jnp.zeros((128 - tall, 128), jnp.int32)], axis=0)
                bt_ref[r, jb * 128:jb * 128 + high, ib * 128:(ib + 1) * 128] = block.T[:high]
    for p in range(pairs):
        fill_tables(k_ref, 0, rows, pq_ref, far_tab, far_inv, p)

    def far_body(step, carry):
        at = pl.ds(pl.multiple_of(step * 8, 8), 8)

        def store(p, c, total):
            if c * 128 < split:
                far_head[p, at, c * 128:(c + 1) * 128] = total
            else:
                far_rest[p, at, c * 128 - split:(c + 1) * 128 - split] = total

        look_up(far_tab, bt_ref, at, store, pairs=pairs, cols=cols)
        return carry

    lax.fori_loop(0, rows // 8, far_body, 0)
    for p in range(pairs):
        far_head[p, rows:, :] = jnp.zeros((cols - rows, split), jnp.int32)
        far_rest[p, rows:, :] = jnp.zeros((cols - rows, cols - split), jnp.int32)
    for h in range(2 * pairs):
        inv_ref[h:h + 1, :] = jnp.concatenate(
            [far_inv[h, j * 128:min(rows, (j + 1) * 128), :].T[0:1] for j in range(cols // 128 - 1)]
            + [jnp.concatenate([far_inv[h, cols - 128:rows, :],
                                jnp.zeros((cols - rows, 128), f32)], axis=0).T[0:1]], axis=1)


def forward_rows(
    used_ref, q_ref, k_ref, v_ref, pk_ref, b_ref, far_sum, inv_ref, p_ref, ctx_ref,
    near_tab, near_inv, near_sum, score, *, first, rows, span, cols, pairs, scale,
):
    for p in range(pairs):
        fill_tables(q_ref, first, rows, pk_ref, near_tab, near_inv, p)
    used = used_ref[0]
    place = lax.broadcasted_iota(jnp.int32, (1, cols), 1)
    valid = ((place >= TEXT) & (place < span)) | (place < used)

    def block_body(start, tall):
        def near_body(step, carry):
            at = pl.ds(pl.multiple_of(start + step * 8, 8), 8)
            out_at = pl.ds(pl.multiple_of(step * 8, 8), 8)

            def store(p, c, total):
                near_sum[p, out_at, c * 128:(c + 1) * 128] = total

            look_up(near_tab, b_ref, at, store, pairs=pairs, cols=cols)
            return carry

        lax.fori_loop(0, tall // 8, near_body, 0)
        at = pl.ds(start, tall)
        for p in range(pairs):
            cut = slice(p * 128, (p + 1) * 128)
            block = q_ref[pl.ds(pl.multiple_of(first + start, 64), tall), cut]
            zero = jnp.zeros_like(block)
            mask = lane_half((tall, 128))
            score[0, 0:tall, :] = nt(jnp.where(mask, block, zero), k_ref[:, cut])
            score[1, 0:tall, :] = nt(jnp.where(mask, zero, block), k_ref[:, cut])
            for c in range(cols // 128):
                turned = far_sum[p, c * 128:(c + 1) * 128, pl.ds(start, 128)].T[0:tall]
                here = slice(c * 128, (c + 1) * 128)
                f0, f1 = unpack_pair(turned)
                n0, n1 = unpack_pair(near_sum[p, 0:tall, here])
                score[0, 0:tall, here] += (
                    f0 * inv_ref[2 * p:2 * p + 1, here] + n0 * near_inv[2 * p, at, :]
                )
                score[1, 0:tall, here] += (
                    f1 * inv_ref[2 * p + 1:2 * p + 2, here] + n1 * near_inv[2 * p + 1, at, :]
                )
            for h in range(2):
                for s in range(tall // 16):
                    raw = score[h, s * 16:(s + 1) * 16, :]
                    logits = jnp.where(valid, raw * scale, -1e30)
                    top = jnp.max(logits, axis=1, keepdims=True)
                    grown = jnp.exp(logits - top)
                    share = grown * (1.0 / jnp.sum(grown, axis=1, keepdims=True))
                    p_ref[2 * p + h, pl.ds(pl.multiple_of(start + s * 16, 16), 16), :] = share.astype(bf16)
            c0 = nn(p_ref[2 * p, at, :], v_ref[:, cut])
            c1 = nn(p_ref[2 * p + 1, at, :], v_ref[:, cut])
            ctx_ref[at, cut] = jnp.where(mask, c0, c1).astype(bf16)

    def outer(step, carry):
        block_body(pl.multiple_of(step * 128, 128), 128)
        return carry

    lax.fori_loop(0, rows // 128, outer, 0)
    if rows % 128:
        block_body(rows - rows % 128, rows % 128)


def project_kernel(x_ref, wq_ref, wk_ref, wv_ref, t_ref, kp_ref, qp_ref, qkv_ref, pk_ref, pq_ref, *, span, cols, width):
    tail = span - span % 128
    qkv_ref[span - span % 16:cols, :] = jnp.zeros((cols - span + span % 16, 3 * width), bf16)
    for n, w_ref in enumerate((wq_ref, wk_ref, wv_ref)):
        cut = slice(n * width, (n + 1) * width)

        def body(step, carry, cut=cut, w_ref=w_ref):
            at = pl.ds(pl.multiple_of(step * 128, 128), 128)
            qkv_ref[at, cut] = nn(x_ref[at, :], w_ref[...]).astype(bf16)
            return carry

        lax.fori_loop(0, span // 128, body, 0)
        if tail < span:
            qkv_ref[tail:span, cut] = nn(x_ref[tail:span, :], w_ref[...]).astype(bf16)
    for r in range(3):
        at = slice(r * REL, (r + 1) * REL)
        pk_ref[at, :] = nn(t_ref[r], kp_ref[...]).astype(bf16)
        pq_ref[at, :] = nn(t_ref[r], qp_ref[...]).astype(bf16)


def project(tokens, query_weight, key_weight, value_weight, tables, key_position, query_position, span):
    width = query_weight.shape[1]
    rows, cols = sizes(span)
    whole = pl.BlockSpec(memory_space=pltpu.VMEM)
    return pl.pallas_call(
        functools.partial(project_kernel, span=span, cols=cols, width=width),
        out_shape=(
            jax.ShapeDtypeStruct((cols, 3 * width), bf16),
            jax.ShapeDtypeStruct((3 * REL, width), bf16),
            jax.ShapeDtypeStruct((3 * REL, width), bf16),
        ),
        in_specs=[whole] * 7,
        out_specs=(whole,) * 3,
        compiler_params=pltpu.CompilerParams(vmem_limit_bytes=VMEM_CAP),
        cost_estimate=pl.CostEstimate(flops=4 * 10**9, bytes_accessed=9 * 10**6, transcendentals=0),
        name="project",
    )(tokens, query_weight, key_weight, value_weight, tables, key_position, query_position)


def pick(half, block, h):
    zero = jnp.zeros_like(block)
    return jnp.where(half, block, zero) if h == 0 else jnp.where(half, zero, block)


def draw_kernel(
    p_ref, up_ref, q_ref, k_ref, v_ref, *refs, first, tall, rows, cols, scale, adds,
):
    extra = refs[:adds]
    d_ref, dt_ref, dq_ref, dk_ref, dv_ref, wide, flat, turned = refs[adds:]
    lanes = turned.shape[2]
    half = lane_half((64, 128))

    def body(step, carry):
        at = pl.ds(pl.multiple_of(step * 64, 64), 64)
        pair = []
        for h in range(2):
            reach = nt(pick(half, up_ref[at, :], h), v_ref[...])
            share = p_ref[h, at, :].astype(f32)
            inner = jnp.sum(reach * share, axis=1, keepdims=True)
            back = share * (reach - inner) * scale
            wide[h, at, :] = back
            flat[h, at, :] = back.astype(bf16)
            pair.append(back.reshape(8, 8, cols))
        d_ref[pl.ds(pl.multiple_of(step * 8, 8), 8), :, :] = jnp.concatenate(pair, axis=1).astype(bf16)
        return carry

    lax.fori_loop(0, tall // 64, body, 0)
    for jb in range(cols // 128):
        high = min(128, rows - jb * 128)
        for ib in range(lanes // 128):
            wide_rows = min(128, tall - ib * 128)
            pair = []
            for h in range(2):
                block = wide[h, ib * 128:ib * 128 + wide_rows, jb * 128:(jb + 1) * 128]
                if wide_rows < 128:
                    block = jnp.concatenate([block, jnp.zeros((128 - wide_rows, 128), f32)], axis=0)
                other = block.T[:high]
                turned[h, jb * 128:jb * 128 + high, ib * 128:(ib + 1) * 128] = other.astype(bf16)
                pair.append(other.reshape(high // 8, 8, 128))
            dt_ref[jb * 16:jb * 16 + high // 8, :, ib * 128:(ib + 1) * 128] = jnp.concatenate(
                pair, axis=1
            ).astype(bf16)
    keys, queries, ups = k_ref[...], q_ref[first:first + lanes, :], up_ref[...]
    cols_half, lanes_half, tall_half = (lane_half((n, 128)) for n in (cols, lanes, tall))
    dq_ref[...] = nn(flat[0], pick(cols_half, keys, 0)) + nn(flat[1], pick(cols_half, keys, 1))
    dk = nn(turned[0], pick(lanes_half, queries, 0)) + nn(turned[1], pick(lanes_half, queries, 1))
    dv = tn(p_ref[0], pick(tall_half, ups, 0)) + tn(p_ref[1], pick(tall_half, ups, 1))
    dv = dv[:rows]
    if adds:
        dk, dv = dk + extra[0][...], dv + extra[1][...]
    dk_ref[...] = dk
    dv_ref[...] = dv.astype(dv_ref.dtype)


def scatter_kernel(*refs, groups, cols):
    *d_refs, b_ref, merge_ref, out_ref = refs
    base = jnp.where(lax.broadcasted_iota(jnp.int32, (16, cols), 0) >= 8, 1.0, 0.0).astype(bf16)
    own = (lax.broadcasted_iota(jnp.int32, (256, 256), 0) % 8) == (
        lax.broadcasted_iota(jnp.int32, (256, 256), 1) % 8
    )
    zero = jnp.asarray(0.0, bf16)
    one = jnp.asarray(1.0, bf16)

    def sieve(g, r, back):
        bucket = b_ref[r, pl.ds(pl.multiple_of(g * 8, 8), 8), :]
        low = (bucket & 31).astype(f32)
        high = (bucket >> 5).astype(f32)
        low = jnp.concatenate([low, low], axis=0).astype(bf16) - base
        high = jnp.concatenate([high, high], axis=0).astype(bf16)
        hot = jnp.concatenate(
            [jnp.where(low == jnp.asarray(2.0 * k, bf16), one, zero) for k in range(16)], axis=0
        )
        sieved = []
        for l in range(4):
            mask = high == jnp.asarray(float(l), bf16)
            for p in range(4):
                sieved.append(jnp.where(mask, back[p * 16:(p + 1) * 16], zero))
        sums = nt(jnp.concatenate(sieved, axis=0), hot)
        return jnp.where(own, sums, 0.0).astype(bf16)

    def body(step, carry):
        got = []
        for g in (2 * step, 2 * step + 1):
            back = jnp.concatenate([d_ref[g] for d_ref in d_refs], axis=1) if len(d_refs) > 1 else d_refs[0][g]
            for r in range(3):
                got.append((g, r, sieve(g, r, back)))
        for g, r, sums in got:
            total = None
            for l in range(4):
                term = nn(sums[l * 64:(l + 1) * 64], merge_ref[l])
                total = term if total is None else total + term
            out_ref[g, :, r * 128:(r + 1) * 128] = total.astype(bf16)
        return carry

    lax.fori_loop(0, groups // 2, body, 0)


def close_kernel(*refs, rows, count):
    base_ref, pos_ref, side_ref, out_ref, table_ref = refs[count:]
    rows2 = 2 * rows
    half3 = lane_half((rows // 8, 8, 128))
    flat = jnp.concatenate([ref[...] for ref in refs[:count]], axis=0).reshape(rows2, 3 * REL)
    both = nn(flat, pos_ref[...]).reshape(rows // 8, 16, 128)
    mine = jnp.where(half3, both[:, 0:8, :], both[:, 8:16, :]).reshape(rows, 128)
    out_ref[...] = base_ref[...] + mine
    side = side_ref[0:rows, :].astype(f32).reshape(rows // 8, 8, 128)
    zero = jnp.zeros_like(side)
    spread = jnp.concatenate([jnp.where(half3, side, zero), jnp.where(half3, zero, side)], axis=1)
    table_ref[...] = tn(flat, spread.reshape(rows2, 128).astype(bf16)).astype(bf16)


def merge_table():
    l = lax.broadcasted_iota(jnp.int32, (4, 256, 128), 0)
    a = lax.broadcasted_iota(jnp.int32, (4, 256, 128), 1) // 8
    c = lax.broadcasted_iota(jnp.int32, (4, 256, 128), 2)
    return (c == l * 32 + a).astype(bf16)


def sizes(span):
    return -(-span // 64) * 64, -(-span // 128) * 128


def forward_scratch(pairs, tall, cols):
    return [
        pltpu.VMEM((pairs, tall, 3 * REL), jnp.int32),
        pltpu.VMEM((2 * pairs, tall, 128), f32),
        pltpu.VMEM((pairs, 128, cols), jnp.int32),
        pltpu.VMEM((2, 128, cols), f32),
    ]


def attention_head(qkv, pos_key, pos_query, buckets, used, scale, split):
    span = buckets.shape[2]
    rows, cols = sizes(span)
    width = pos_key.shape[1]
    pairs = width // 128
    whole = pl.BlockSpec(memory_space=pltpu.VMEM)
    i32 = jnp.int32

    def kernel(
        used_ref, qkv_ref, pk_ref, pq_ref, b_ref, p_ref, ctx_ref, head_ref, rest_ref, bt_ref, far_rest, inv_ref,
        far_tab, far_inv, far_head, *scratch,
    ):
        k_ref = qkv_ref.at[:, width:2 * width]
        prepare_rows(
            k_ref, pq_ref, b_ref, head_ref, rest_ref, bt_ref, far_head, far_rest, inv_ref, far_tab, far_inv,
            span=span, rows=rows, cols=cols, pairs=pairs, split=split,
        )
        forward_rows(
            used_ref, qkv_ref.at[:, 0:width], k_ref, qkv_ref.at[:, 2 * width:3 * width], pk_ref, head_ref,
            far_head, inv_ref, p_ref, ctx_ref, *scratch,
            first=0, rows=split, span=span, cols=cols, pairs=pairs, scale=scale,
        )

    return pl.pallas_call(
        kernel,
        out_shape=(
            jax.ShapeDtypeStruct((2 * pairs, split, cols), bf16),
            jax.ShapeDtypeStruct((split, width), bf16),
            jax.ShapeDtypeStruct((3, split, cols), i32),
            jax.ShapeDtypeStruct((3, rows - split, cols), i32),
            jax.ShapeDtypeStruct((3, rows, cols), i32),
            jax.ShapeDtypeStruct((pairs, cols, cols - split), i32),
            jax.ShapeDtypeStruct((2 * pairs, cols), f32),
        ),
        in_specs=[pl.BlockSpec(memory_space=pltpu.SMEM)] + [whole] * 4,
        out_specs=(whole,) * 7,
        scratch_shapes=[
            pltpu.VMEM((pairs, rows, 3 * REL), i32),
            pltpu.VMEM((2 * pairs, rows, 128), f32),
            pltpu.VMEM((pairs, cols, split), i32),
        ] + forward_scratch(pairs, split, cols),
        compiler_params=pltpu.CompilerParams(vmem_limit_bytes=VMEM_CAP),
        cost_estimate=pl.CostEstimate(flops=4 * 10**10, bytes_accessed=25000000, transcendentals=0),
        name="attention_head",
    )(used, qkv, pos_key, pos_query, buckets)


def attention_rest(qkv, pos_key, bucket_rest, far_rest, inverse, used, scale, split, span):
    rows, cols = sizes(span)
    width = pos_key.shape[1]
    pairs = width // 128
    whole = pl.BlockSpec(memory_space=pltpu.VMEM)

    def kernel(used_ref, qkv_ref, pk_ref, b_ref, far_ref, inv_ref, p_ref, ctx_ref, *scratch):
        forward_rows(
            used_ref, qkv_ref.at[:, 0:width], qkv_ref.at[:, width:2 * width], qkv_ref.at[:, 2 * width:3 * width],
            pk_ref, b_ref, far_ref, inv_ref, p_ref, ctx_ref, *scratch,
            first=split, rows=rows - split, span=span, cols=cols, pairs=pairs, scale=scale,
        )

    return pl.pallas_call(
        kernel,
        out_shape=(
            jax.ShapeDtypeStruct((2 * pairs, rows - split, cols), bf16),
            jax.ShapeDtypeStruct((rows - split, width), bf16),
        ),
        in_specs=[pl.BlockSpec(memory_space=pltpu.SMEM)] + [whole] * 5,
        out_specs=(whole,) * 2,
        scratch_shapes=forward_scratch(pairs, rows - split, cols),
        compiler_params=pltpu.CompilerParams(vmem_limit_bytes=VMEM_CAP),
        cost_estimate=pl.CostEstimate(flops=2 * 10**10, bytes_accessed=12000000, transcendentals=0),
        name="attention_rest",
    )(used, qkv, pos_key, bucket_rest, far_rest, inverse)


def attention_draw(share, upstream, qkv, scale, first, rows, adds=()):
    heads, tall, cols = share.shape
    width = upstream.shape[1]
    pairs = heads // 2
    lanes = -(-tall // 128) * 128

    def column(n):
        return pl.BlockSpec((n, 128), lambda p: (0, p))

    return pl.pallas_call(
        functools.partial(draw_kernel, first=first, tall=tall, rows=rows, cols=cols, scale=scale, adds=len(adds)),
        grid=(pairs,),
        in_specs=[
            pl.BlockSpec((2, tall, cols), lambda p: (p, 0, 0)),
            column(tall),
            pl.BlockSpec((cols, 128), lambda p: (0, p)),
            pl.BlockSpec((cols, 128), lambda p: (0, p + pairs)),
            pl.BlockSpec((cols, 128), lambda p: (0, p + 2 * pairs)),
        ] + [column(rows)] * len(adds),
        out_specs=(
            pl.BlockSpec((tall // 8, 16, cols), lambda p: (0, p, 0)),
            pl.BlockSpec((rows // 8, 16, lanes), lambda p: (0, p, 0)),
            column(tall), column(rows), column(rows),
        ),
        out_shape=(
            jax.ShapeDtypeStruct((tall // 8, 8 * heads, cols), bf16),
            jax.ShapeDtypeStruct((rows // 8, 8 * heads, lanes), bf16),
            jax.ShapeDtypeStruct((tall, width), f32),
            jax.ShapeDtypeStruct((rows, width), f32),
            jax.ShapeDtypeStruct((rows, width), bf16 if adds else f32),
        ),
        scratch_shapes=[
            pltpu.VMEM((2, tall, cols), f32),
            pltpu.VMEM((2, tall, cols), bf16),
            pltpu.VMEM((2, rows, lanes), bf16),
        ],
        compiler_params=pltpu.CompilerParams(vmem_limit_bytes=VMEM_CAP),
        cost_estimate=pl.CostEstimate(flops=10**6, bytes_accessed=10**4, transcendentals=0),
        name="attention_draw",
    )(share, upstream, qkv, qkv, qkv, *adds)


def attention_scatter(backs, buckets, merge, first, count):
    high = backs[0].shape[1]
    cols = buckets.shape[2]
    return pl.pallas_call(
        functools.partial(scatter_kernel, groups=8, cols=cols),
        grid=(count,),
        out_shape=jax.ShapeDtypeStruct((8 * count, high, 3 * REL), bf16),
        in_specs=[pl.BlockSpec((8, high, b.shape[2]), lambda g: (first + g, 0, 0)) for b in backs] + [
            pl.BlockSpec((3, 64, cols), lambda g: (0, first + g, 0)),
            pl.BlockSpec(merge.shape, lambda g: (0, 0, 0)),
        ],
        out_specs=pl.BlockSpec((8, high, 3 * REL), lambda g: (g, 0, 0)),
        compiler_params=pltpu.CompilerParams(vmem_limit_bytes=VMEM_CAP),
        cost_estimate=pl.CostEstimate(flops=10**6, bytes_accessed=10**4, transcendentals=0),
        name="attention_scatter",
    )(*backs, buckets, merge)


def attention_close(sums, base, pos, qkv, side):
    rows, width = base.shape
    pairs = width // 128
    return pl.pallas_call(
        functools.partial(close_kernel, rows=rows, count=len(sums)),
        grid=(pairs,),
        in_specs=[pl.BlockSpec((part.shape[0], 16, 3 * REL), lambda p: (0, p, 0)) for part in sums] + [
            pl.BlockSpec((rows, 128), lambda p: (0, p)),
            pl.BlockSpec((3 * REL, 128), lambda p: (0, p)),
            pl.BlockSpec((qkv.shape[0], 128), lambda p: (0, p + side * pairs)),
        ],
        out_specs=(
            pl.BlockSpec((rows, 128), lambda p: (0, p)),
            pl.BlockSpec((3 * REL, 128), lambda p: (0, p)),
        ),
        out_shape=(
            jax.ShapeDtypeStruct((rows, width), f32),
            jax.ShapeDtypeStruct((3 * REL, width), bf16),
        ),
        compiler_params=pltpu.CompilerParams(vmem_limit_bytes=VMEM_CAP),
        cost_estimate=pl.CostEstimate(flops=5000000000, bytes_accessed=10000000, transcendentals=0),
        name="attention_close",
    )(*sums, base, pos, qkv)


def fill_turned(x_ref, turned, rows):
    depth = x_ref.shape[1]
    for a in range(0, rows, 128):
        tall = min(128, rows - a)
        for b in range(0, depth, 128):
            block = x_ref[a:a + tall, b:b + 128]
            if tall < 128:
                block = jnp.concatenate([block, jnp.zeros((128 - tall, 128), block.dtype)], axis=0)
            turned[b:b + 128, a:a + tall] = block.T[:, :tall]


def each_block(pick_ref, blocks, keeps, bit, slot):
    if not keeps:
        return [(0, d, d) for d in range(blocks)]
    shift = bit - 1
    listed = []
    for out in range(2):
        value = pick_ref[slot] if out == 1 else 1 - pick_ref[slot]
        for e in range(blocks // 2):
            low = e & ((1 << shift) - 1)
            listed.append((out, e, ((e >> shift) << (shift + 1)) + low + value * (1 << shift)))
    return listed


def weight_kernel(pick_ref, *refs, count, blocks, deep, keeps, bit):
    xs, ys, rest = refs[:count], refs[count:2 * count], refs[2 * count:]
    add_ref = rest[0] if keeps else None
    outs = rest[1:3] if keeps else rest[0:1]
    turned = rest[-count:]

    @pl.when(pl.program_id(0) == 0)
    def _():
        for x_ref, wide in zip(xs, turned):
            fill_turned(x_ref, wide, x_ref.shape[0])

    for out, place, d in each_block(pick_ref, blocks, keeps, bit, 1):
        at = pl.ds(pl.multiple_of((2 * d + pick_ref[0]) * deep, deep), deep)
        part = add_ref[d] if keeps else None
        for wide, y_ref in zip(turned, ys):
            term = nn(wide[at, :], y_ref[...])
            part = term if part is None else part + term
        outs[out][place] = part


def weight_half(pick, xs, ys, add=None, *, parts, bits, tile=512):
    depth = xs[0].shape[1]
    wide = ys[0].shape[1]
    deep = depth // parts
    blocks = parts // 2
    keeps = add is not None

    def tiled(n):
        return pl.BlockSpec((n, deep, tile), lambda c: (0, 0, c))

    ins = [pl.BlockSpec(memory_space=pltpu.SMEM)]
    ins += [pl.BlockSpec(x.shape, lambda c: (0, 0)) for x in xs]
    ins += [pl.BlockSpec((y.shape[0], tile), lambda c: (0, c)) for y in ys]
    args = [pick, *xs, *ys]
    shape = (jax.ShapeDtypeStruct((blocks, deep, wide), f32),)
    specs = (tiled(blocks),)
    if keeps:
        ins.append(tiled(blocks))
        args += add
        shape = (jax.ShapeDtypeStruct((blocks // 2, deep, wide), f32),) * 2
        specs = (tiled(blocks // 2),) * 2
    rows = sum(x.shape[0] for x in xs)
    return pl.pallas_call(
        functools.partial(weight_kernel, count=len(xs), blocks=blocks, deep=deep, keeps=keeps, bit=bits[0]),
        grid=(wide // tile,),
        in_specs=ins,
        out_specs=specs,
        out_shape=shape,
        scratch_shapes=[pltpu.VMEM((depth, x.shape[0]), bf16) for x in xs],
        compiler_params=pltpu.CompilerParams(vmem_limit_bytes=VMEM_CAP),
        cost_estimate=pl.CostEstimate(
            flops=rows * depth * wide, bytes_accessed=4 * depth * wide, transcendentals=0
        ),
        name="weight_half",
    )(*args)


def many_kernel(pick_ref, *refs, plan, widths, turns, blocks, deep, keeps, bits):
    n_in = 2 * len(plan)
    ins = refs[:n_in]
    n_out = len(widths)
    adds = refs[n_in:n_in + n_out] if keeps else None
    outs = refs[n_in + n_out:n_in + 3 * n_out] if keeps else refs[n_in:n_in + n_out]
    scratch = refs[len(refs) - sum(turns):]
    left = []
    used = 0
    for n, turn in enumerate(turns):
        if turn:
            fill_turned(ins[2 * n], scratch[used], ins[2 * n].shape[0])
            left.append(scratch[used])
            used += 1
        else:
            left.append(ins[2 * n])
    right = [ins[2 * n + 1][...] for n in range(len(plan))]
    for group in range(n_out):
        for out, place, d in each_block(pick_ref, blocks, keeps, bits[group], 1 + group):
            at = pl.ds(pl.multiple_of((2 * d + pick_ref[0]) * deep, deep), deep)
            target = outs[2 * group + out] if keeps else outs[group]
            for n, (kind, own, start, wide) in enumerate(plan):
                if own != group:
                    continue
                rows = left[n][at, :]
                if kind == "copy":
                    part = rows
                elif kind == "nt":
                    part = nt(rows, right[n])
                else:
                    part = nn(rows, right[n])
                cut = slice(start, start + wide)
                if keeps:
                    part = part + adds[group][d, :, cut]
                target[place, :, cut] = part


def many_half(pick, pairs, plan, widths, add=None, *, parts, bits):
    whole = pl.BlockSpec(memory_space=pltpu.VMEM)
    turns = [kind in ("turn", "copy") for kind, *_ in plan]
    depth = max(left.shape[1 if turn else 0] for (left, _), turn in zip(pairs, turns))
    deep = depth // parts
    blocks = parts // 2
    keeps = add is not None
    args = [pick] + [operand for pair in pairs for operand in pair] + (list(add) if keeps else [])
    if keeps:
        shape = [jax.ShapeDtypeStruct((blocks // 2, deep, w), f32) for w in widths for _ in range(2)]
    else:
        shape = [jax.ShapeDtypeStruct((blocks, deep, w), f32) for w in widths]
    return pl.pallas_call(
        functools.partial(
            many_kernel, plan=plan, widths=widths, turns=turns, blocks=blocks, deep=deep,
            keeps=keeps, bits=[b[0] for b in bits],
        ),
        in_specs=[pl.BlockSpec(memory_space=pltpu.SMEM)] + [whole] * (len(args) - 1),
        out_specs=[whole] * len(shape),
        out_shape=shape,
        scratch_shapes=[
            pltpu.VMEM((left.shape[1], left.shape[0]), left.dtype)
            for (left, _), turn in zip(pairs, turns) if turn
        ],
        compiler_params=pltpu.CompilerParams(vmem_limit_bytes=VMEM_CAP),
        cost_estimate=pl.CostEstimate(
            flops=600 * depth * sum(widths), bytes_accessed=6 * depth * sum(widths), transcendentals=0
        ),
        name="many_half",
    )(*args)


def flipped(value, bit, size):
    return lax.ppermute(value, "dp", [(i, i ^ (1 << bit)) for i in range(size)])


def bit_of(index, bit):
    return (index >> bit) & 1


class Halving:
    def __init__(self, make, index, size, orders):
        self.make, self.index, self.size, self.orders = make, index, size, orders
        mine = bit_of(index, 0).astype(jnp.int32)
        self.pick = jnp.stack([mine] + [bit_of(index, bits[0]).astype(jnp.int32) for bits in orders])
        self.other = self.pick.at[0].set(1 - mine)
        self.stage = 0
        self.extra = None

    def work(self):
        if self.stage == 0:
            self.pending = [(sent, None) for sent in self.make(self.other, None)]
        elif self.stage == 1:
            outs = self.make(self.pick, self.extra)
            self.pending = [(outs[2 * g], outs[2 * g + 1]) for g in range(len(self.orders))]
            self.axes = [
                [b for b in range(self.size.bit_length() - 1, 0, -1) if b != bits[0] and b < self.size.bit_length() - 1]
                for bits in self.orders
            ]
        else:
            self.pending = [
                self.split(g, held, extra) for g, (held, extra) in enumerate(zip(self.held, self.extra))
            ]
        return [part for pair in self.pending for part in pair if part is not None]

    def split(self, g, held, extra):
        bits = self.orders[g]
        if self.stage > len(bits):
            return held + extra, None
        bit = bits[self.stage - 1]
        axis = self.axes[g].index(bit)
        shape = (2,) * len(self.axes[g]) + held.shape[-2:]
        self.axes[g].remove(bit)
        own = bit_of(self.index, bit)
        held, extra = held.reshape(shape), extra.reshape(shape)

        def half(value, at):
            return lax.dynamic_index_in_dim(value, at, axis, keepdims=False)

        return half(held, 1 - own) + half(extra, 1 - own), half(held, own) + half(extra, own)

    def go(self, parts):
        parts = list(parts)
        pairs = [
            tuple(None if part is None else parts.pop(0) for part in pair) for pair in self.pending
        ]
        self.held = [home for _, home in pairs]
        last = self.stage > len(self.orders[0])
        if last:
            self.result = [away for away, _ in pairs]
        else:
            bit = lambda g: 0 if self.stage == 0 else self.orders[g][self.stage - 1]
            self.extra = [flipped(away, bit(g), self.size) for g, (away, _) in enumerate(pairs)]
        self.stage += 1

    def step(self):
        self.go(self.work())

    def over(self):
        return self.stage > len(self.orders[0]) + 1

    def finish(self):
        while not self.over():
            self.step()
        return self.result


def tie(values, *chains):
    chains = [chain for chain in chains if not chain.over()]
    values, extras = lax.optimization_barrier((values, [chain.extra for chain in chains]))
    for chain, extra in zip(chains, extras):
        chain.extra = extra
    works = [chain.work() for chain in chains]
    values, works = lax.optimization_barrier((values, works))
    for chain, parts in zip(chains, works):
        chain.go(parts)
    return values


def swap(value):
    return lax.ppermute(value.astype(f32), "mp", [(0, 1), (1, 0)])


def attend_kernel(
    t_ref, c_ref, o_ref, w_ref, ow_ref, gain_ref, shift_ref, first_ref, low_ref, normal_ref, inverse_ref,
):
    weight = ow_ref[...].astype(bf16)

    def body(step, carry):
        at = pl.ds(pl.multiple_of(step * 64, 64), 64)
        summed = t_ref[at, :].astype(f32) + nn(c_ref[at, :], w_ref[...])
        summed = summed + nn(o_ref[at, :].astype(bf16), weight)
        first, normal, inverse = norm_forward(summed, gain_ref[...], shift_ref[...])
        first_ref[at, :] = first
        low_ref[at, :] = first.astype(bf16)
        normal_ref[at, :] = normal
        inverse_ref[at, :] = inverse
        return carry

    lax.fori_loop(0, t_ref.shape[0] // 64, body, 0)


def attend(tokens, context, other, weight, other_weight, gain, shift):
    tall, depth = tokens.shape
    whole = pl.BlockSpec(memory_space=pltpu.VMEM)
    return pl.pallas_call(
        attend_kernel,
        in_specs=[whole] * 7,
        out_specs=(whole,) * 4,
        out_shape=(
            jax.ShapeDtypeStruct((tall, depth), f32),
            jax.ShapeDtypeStruct((tall, depth), bf16),
            jax.ShapeDtypeStruct((tall, depth), f32),
            jax.ShapeDtypeStruct((tall, 1), f32),
        ),
        compiler_params=pltpu.CompilerParams(vmem_limit_bytes=VMEM_CAP),
        cost_estimate=pl.CostEstimate(flops=2 * 10**9, bytes_accessed=8 * 10**6, transcendentals=0),
        name="attend",
    )(tokens, context, other, weight, other_weight, gain[None], shift[None])


def norm_forward(summed, gain, shift):
    centred = summed - jnp.mean(summed, axis=1, keepdims=True)
    inverse = lax.rsqrt(jnp.mean(centred * centred, axis=1, keepdims=True) + epsilon)
    normal = centred * inverse
    return (normal * gain + shift, normal, inverse)


def norm_backward(upstream, normal, inverse, gain):
    scaled = upstream * gain
    inner = jnp.mean(scaled, axis=1, keepdims=True)
    aligned = jnp.mean(scaled * normal, axis=1, keepdims=True)
    return (
        inverse * (scaled - inner - normal * aligned),
        jnp.sum(upstream * normal, axis=0),
        jnp.sum(upstream, axis=0),
    )


def shards(
    tokens,
    query_weight,
    key_weight,
    value_weight,
    output_weight,
    query_position,
    key_position,
    position_tables,
    gain_one,
    shift_one,
    up_weight,
    down_weight,
    gain_two,
    shift_two,
    buckets,
    text_length,
    cotangent,
):
    span = buckets.shape[2]
    rows, cols = sizes(span)
    size = lax.axis_size("dp")
    index = lax.axis_index("dp")
    bits = list(range(1, size.bit_length() - 1))
    low_first, high_first = bits, bits[1:2] + bits[:1] + bits[2:]
    score_scale = (7.0 * HEAD) ** (-0.5)
    tables_flat = position_tables.reshape(3 * REL, D)
    width = query_weight.shape[1]
    spare = ((0, rows - span), (0, 0))

    def chain(make, *orders):
        return Halving(make, index, size, list(orders))

    split = rows // 2 // 128 * 128
    other_output = swap(output_weight)
    qkv, pos_key, pos_query = project(
        tokens, query_weight, key_weight, value_weight, position_tables, key_position, query_position, span
    )
    tokens = jnp.pad(tokens, spare)
    cotangent = jnp.pad(cotangent, spare)
    tokens_turned, tables_turned = tokens.T, tables_flat.T
    edges = [(0, split), (split, rows)]

    share_head, context_head, bucket_head, bucket_rest, bucket_cols, far_rest, far_inverse = attention_head(
        qkv, pos_key, pos_query, buckets, text_length, score_scale, split
    )
    other_head = swap(context_head)
    far_rest, other_output = lax.optimization_barrier((far_rest, other_output))
    share_rest, context_rest = attention_rest(
        qkv, pos_key, bucket_rest, far_rest, far_inverse, text_length, score_scale, split, span
    )
    other_rest = swap(context_rest)
    shares = [share_head, share_rest]
    contexts = [context_head, context_rest]
    contexts_other = [other_head, other_rest]

    def gelu(value):
        return jax.nn.gelu(value, approximate=False)

    firsts, firsts_low, normals_one, inverses_one, upwards, hiddens, feeds, feeds_other = ([] for _ in range(8))
    for (low, high), context, other in zip(edges, contexts, contexts_other):
        first, first_low, normal_one, inverse_one = attend(
            tokens[low:high], context, other, output_weight, other_output, gain_one, shift_one
        )
        firsts.append(first)
        normals_one.append(normal_one)
        inverses_one.append(inverse_one)
        firsts_low.append(first_low)
        upwards.append(nn(firsts_low[-1], up_weight))
        hiddens.append(gelu(upwards[-1]).astype(bf16))
        feeds.append(nn(hiddens[-1], down_weight))
        feeds_other.append(swap(feeds[-1]))

    finals, seconds_back, seconds_low, upwards_back, backs_part, backs_other, two_sums = ([] for _ in range(7))
    for n, (low, high) in enumerate(edges):
        final, normal_two, inverse_two = norm_forward(
            firsts[n] + feeds[n] + feeds_other[n], gain_two, shift_two
        )
        finals.append(final.astype(bf16))
        second_back, *sums = norm_backward(
            cotangent[low:high].astype(f32), normal_two, inverse_two, gain_two
        )
        two_sums.append(sums)
        seconds_back.append(second_back)
        seconds_low.append(second_back.astype(bf16))
        hidden_back = nt(seconds_low[n], down_weight)
        upwards_back.append(jax.vjp(gelu, upwards[n])[1](hidden_back)[0].astype(bf16))
        backs_part.append(nt(upwards_back[n], up_weight))
        backs_other.append(swap(backs_part[n]))
    layer_output = jnp.concatenate(finals, axis=0)[:span]
    gain_two_grad, shift_two_grad = (two_sums[0][n] + two_sums[1][n] for n in range(2))

    backs_part, down_pair, up_pair = lax.optimization_barrier(
        (backs_part, (seconds_low, hiddens), (firsts_low, upwards_back))
    )
    up_pair, backs_other[0] = lax.optimization_barrier((up_pair, backs_other[0]))
    down_chain = chain(
        lambda pick, add: weight_half(pick, *down_pair, add, parts=size, bits=high_first), high_first
    )
    up_chain = chain(
        lambda pick, add: weight_half(pick, *up_pair, add, parts=size, bits=low_first), low_first
    )
    down_chain.step()
    up_chain.step()
    backs_other[0] = tie(backs_other[0], down_chain)
    backs_other[0] = tie(backs_other[0], up_chain)
    merge = merge_table()
    residuals_back, residuals_low, one_sums = [], [], []

    def draw(n, adds=()):
        residual_back, *sums = norm_backward(
            seconds_back[n] + backs_part[n] + backs_other[n], normals_one[n], inverses_one[n], gain_one
        )
        one_sums.append(sums)
        residuals_back.append(residual_back)
        residuals_low.append(residual_back.astype(bf16))
        context_back = nt(residuals_low[n], output_weight).astype(bf16)
        return attention_draw(shares[n], context_back, qkv, score_scale, edges[n][0], rows, adds)

    back_head, turned_head, query_head, key_head, value_head = draw(0)
    back_head, key_head, backs_other[1] = lax.optimization_barrier((back_head, key_head, backs_other[1]))
    back_rest, turned_rest, query_rest, key_base, value_back = draw(1, (key_head, value_head))
    gain_one_grad, shift_one_grad = (one_sums[0][n] + one_sums[1][n] for n in range(2))
    back_rest, value_back = tie((back_rest, value_back), down_chain)
    query_base = jnp.concatenate([query_head, query_rest], axis=0)
    residual_low = jnp.concatenate(residuals_low, axis=0)
    context = jnp.concatenate(contexts, axis=0)
    nothing = jnp.zeros_like(gain_one)
    gains = jnp.stack(
        [gain_one_grad, shift_one_grad, gain_two_grad, shift_two_grad] + [nothing] * 4
    )
    gains = jnp.concatenate([gains, jnp.zeros((120, gains.shape[1]), f32)], axis=0)
    dummy = jnp.zeros((8, 128), bf16)
    outer_chain = chain(
        lambda pick, add: many_half(
            pick,
            [(residual_low, context), (tokens_turned, value_back), (gains, dummy)],
            [("turn", 0, 0, width), ("nn", 0, width, width), ("copy", 0, 2 * width, 128)],
            [2 * width + 128],
            add, parts=size, bits=[low_first],
        ),
        low_first,
    )
    outer_chain.step()

    def tail(rows_back, sums, position, orders):
        return chain(
            lambda pick, add: many_half(
                pick,
                [(tokens_turned, rows_back), (tables_turned, sums), (position, sums)],
                [("nn", 0, 0, width), ("nn", 1, 0, width), ("nt", 0, width, 3 * REL)],
                [width + 3 * REL, width],
                add, parts=size, bits=orders,
            ),
            *orders,
        )

    near = []
    blocks = rows // 64
    back_head, back_rest = tie((back_head, back_rest), up_chain)
    near.append(attention_scatter([back_head], bucket_head, merge, 0, split // 64))
    back_rest, near = tie((back_rest, near), down_chain)
    back_rest, near = tie((back_rest, near), outer_chain)
    near.append(attention_scatter([back_rest], bucket_rest, merge, 0, blocks - split // 64))
    near, backs = tie((near, [turned_head, turned_rest]), up_chain)
    query_back, key_table_sum = attention_close(near, query_base, pos_key, qkv, 0)
    query_low = query_back.astype(bf16)
    early = nt(query_low, query_weight) + nt(value_back, value_weight)
    near_chain = tail(query_low, key_table_sum, key_position, [high_first, low_first])
    backs, key_table_sum = tie((backs, key_table_sum), near_chain, outer_chain, down_chain)
    far = []
    cuts = [n * blocks // 3 for n in range(4)]
    for part, chains in enumerate(((near_chain,), (outer_chain, up_chain), (near_chain, outer_chain))):
        far.append(attention_scatter(backs, bucket_cols, merge, cuts[part], cuts[part + 1] - cuts[part]))
        backs, far = tie((backs, far), *chains)
    key_back, query_table_sum = attention_close(far, key_base, pos_query, qkv, 1)
    key_low = key_back.astype(bf16)
    input_part = early + nt(key_low, key_weight)
    input_other = swap(input_part)
    far_chain = tail(key_low, query_table_sum, query_position, [low_first, high_first])
    far_chain.step()
    far_chain.step()
    input_gradient = (jnp.concatenate(residuals_back, axis=0) + input_part + input_other)[:span].astype(bf16)
    (down_share,) = down_chain.finish()
    (up_share,) = up_chain.finish()
    (outer_share,) = outer_chain.finish()
    near_main, key_position_grad = near_chain.finish()
    far_main, query_position_grad = far_chain.finish()

    table_rows = near_main[:, width:] + far_main[:, width:]
    table_rows = table_rows.reshape(2, table_rows.shape[0] // 2, 3 * REL)
    side = lax.axis_index("mp")
    table_mine = lax.dynamic_index_in_dim(table_rows, side, 0, keepdims=False) + lax.ppermute(
        lax.dynamic_index_in_dim(table_rows, 1 - side, 0, keepdims=False), "mp", [(0, 1), (1, 0)]
    )
    table_gradient = table_mine.T.reshape(3, REL, table_mine.shape[0])
    gains_mine = outer_share[:, 2 * width:]
    return (
        layer_output,
        input_gradient,
        near_main[:, 0:width],
        far_main[:, 0:width],
        outer_share[:, width:2 * width],
        outer_share[:, 0:width].T,
        query_position_grad,
        key_position_grad,
        table_gradient,
        gains_mine[:, 0],
        gains_mine[:, 1],
        up_share,
        down_share.T,
        gains_mine[:, 2],
        gains_mine[:, 3],
    )


def solution(mesh):
    return jax.shard_map(
        shards,
        mesh=mesh,
        in_specs=(
            P("dp", None),
            P(None, "mp"),
            P(None, "mp"),
            P(None, "mp"),
            P("mp", None),
            P(None, "mp"),
            P(None, "mp"),
            P(),
            P(),
            P(),
            P(None, "mp"),
            P("mp", None),
            P(),
            P(),
            P("dp", None, None, None),
            P("dp"),
            P("dp", None),
        ),
        out_specs=(
            P("dp", None),
            P("dp", None),
            P("dp", "mp"),
            P("dp", "mp"),
            P("dp", "mp"),
            P("mp", "dp"),
            P("dp", "mp"),
            P("dp", "mp"),
            P(None, None, ("dp", "mp")),
            P("dp"),
            P("dp"),
            P("dp", "mp"),
            P("mp", "dp"),
            P("dp"),
            P("dp"),
        ),
        check_vma=False,
    )
```

```python
import functools

import jax
import jax.numpy as jnp
from jax import lax
from jax.experimental import pallas as pl
from jax.experimental.pallas import tpu as pltpu
from jax.sharding import PartitionSpec as P

D = 1024
epsilon = 1e-05
HEAD = 64
REL = 128
TEXT = 512
bf16 = jnp.bfloat16
f32 = jnp.float32
LIMIT = 10900.0
VMEM_CAP = 62 * 2**20


def lane_gather(table, index):
    numbers = lax.GatherDimensionNumbers(
        offset_dims=(),
        collapsed_slice_dims=(1,),
        start_index_map=(1,),
        operand_batching_dims=(0,),
        start_indices_batching_dims=(0,),
    )
    return lax.gather(
        table, index[..., None], numbers, (1, 1), mode=lax.GatherScatterMode.PROMISE_IN_BOUNDS
    )


def nt(left, right):
    return lax.dot_general(left, right, (((1,), (1,)), ((), ())), preferred_element_type=f32)


def nn(left, right):
    return jnp.dot(left, right, preferred_element_type=f32)


def tn(left, right):
    return lax.dot_general(left, right, (((0,), (0,)), ((), ())), preferred_element_type=f32)


def lane_half(shape):
    return lax.broadcasted_iota(jnp.int32, shape, len(shape) - 1) < HEAD


def unpack_pair(packed):
    low = (packed << 16) >> 16
    high = (packed - low) >> 16
    return high.astype(f32), low.astype(f32)


def fill_tables(src_ref, first, tall, pos_ref, tab, inv, p):
    half = lane_half((64, 128))
    cut = slice(p * 128, (p + 1) * 128)

    def body(step, carry):
        at = pl.ds(pl.multiple_of(step * 64, 64), 64)
        block = src_ref[pl.ds(pl.multiple_of(first + step * 64, 64), 64), cut]
        zero = jnp.zeros_like(block)
        first_head = nt(jnp.where(half, block, zero), pos_ref[:, cut]).astype(bf16).astype(f32)
        second_head = nt(jnp.where(half, zero, block), pos_ref[:, cut]).astype(bf16).astype(f32)
        top0 = jnp.maximum(jnp.max(jnp.abs(first_head), axis=1, keepdims=True), 1e-30)
        top1 = jnp.maximum(jnp.max(jnp.abs(second_head), axis=1, keepdims=True), 1e-30)
        whole0 = jnp.round(first_head * (LIMIT / top0)).astype(jnp.int32)
        whole1 = jnp.round(second_head * (LIMIT / top1)).astype(jnp.int32)
        tab[p, at, :] = whole0 * 65536 + whole1
        inv[2 * p, at, :] = jnp.broadcast_to(top0 * (1.0 / LIMIT), (64, 128))
        inv[2 * p + 1, at, :] = jnp.broadcast_to(top1 * (1.0 / LIMIT), (64, 128))
        return carry

    lax.fori_loop(0, tall // 64, body, 0)


def look_up(tab, index_ref, at, store, *, pairs, cols):
    for c in range(cols // 128):
        total = [None] * pairs
        for r in range(3):
            index = index_ref[r, at, c * 128:(c + 1) * 128]
            for p in range(pairs):
                got = lane_gather(tab[p, at, r * 128:(r + 1) * 128], index)
                total[p] = got if total[p] is None else total[p] + got
        for p in range(pairs):
            store(p, c, total[p])


def prepare_rows(
    k_ref, pq_ref, b_ref, head_ref, rest_ref, bt_ref, far_head, far_rest, inv_ref,
    far_tab, far_inv, *, span, rows, cols, pairs, split,
):
    edge = span - span % 8 - split
    for r in range(3):
        head_ref[r, :, span - span % 128:cols] = jnp.zeros((split, cols - span + span % 128), jnp.int32)
        rest_ref[r, edge:rows - split, :] = jnp.zeros((rows - split - edge, cols), jnp.int32)
        rest_ref[r, :, span - span % 128:cols] = jnp.zeros((rows - split, cols - span + span % 128), jnp.int32)
        head_ref[r, :, 0:span] = b_ref[0, r, 0:split]
        rest_ref[r, 0:span - split, 0:span] = b_ref[0, r, split:span]
    for r in range(3):
        for jb in range(cols // 128):
            high = min(128, rows - jb * 128)
            for ib in range(cols // 128):
                tall = min(128, rows - ib * 128)
                here = slice(jb * 128, (jb + 1) * 128)
                if ib * 128 < split:
                    block = head_ref[r, ib * 128:ib * 128 + tall, here]
                else:
                    block = rest_ref[r, ib * 128 - split:ib * 128 - split + tall, here]
                if tall < 128:
                    block = jnp.concatenate([block, jnp.zeros((128 - tall, 128), jnp.int32)], axis=0)
                bt_ref[r, jb * 128:jb * 128 + high, ib * 128:(ib + 1) * 128] = block.T[:high]
    for p in range(pairs):
        fill_tables(k_ref, 0, rows, pq_ref, far_tab, far_inv, p)

    def far_body(step, carry):
        at = pl.ds(pl.multiple_of(step * 8, 8), 8)

        def store(p, c, total):
            if c * 128 < split:
                far_head[p, at, c * 128:(c + 1) * 128] = total
            else:
                far_rest[p, at, c * 128 - split:(c + 1) * 128 - split] = total

        look_up(far_tab, bt_ref, at, store, pairs=pairs, cols=cols)
        return carry

    lax.fori_loop(0, rows // 8, far_body, 0)
    for p in range(pairs):
        far_head[p, rows:, :] = jnp.zeros((cols - rows, split), jnp.int32)
        far_rest[p, rows:, :] = jnp.zeros((cols - rows, cols - split), jnp.int32)
    for h in range(2 * pairs):
        inv_ref[h:h + 1, :] = jnp.concatenate(
            [far_inv[h, j * 128:min(rows, (j + 1) * 128), :].T[0:1] for j in range(cols // 128 - 1)]
            + [jnp.concatenate([far_inv[h, cols - 128:rows, :],
                                jnp.zeros((cols - rows, 128), f32)], axis=0).T[0:1]], axis=1)


def forward_rows(
    used_ref, q_ref, k_ref, v_ref, pk_ref, b_ref, far_sum, inv_ref, p_ref, ctx_ref,
    near_tab, near_inv, near_sum, score, *, first, rows, span, cols, pairs, scale,
):
    for p in range(pairs):
        fill_tables(q_ref, first, rows, pk_ref, near_tab, near_inv, p)
    used = used_ref[0]
    place = lax.broadcasted_iota(jnp.int32, (1, cols), 1)
    valid = ((place >= TEXT) & (place < span)) | (place < used)

    def block_body(start, tall):
        def near_body(step, carry):
            at = pl.ds(pl.multiple_of(start + step * 8, 8), 8)
            out_at = pl.ds(pl.multiple_of(step * 8, 8), 8)

            def store(p, c, total):
                near_sum[p, out_at, c * 128:(c + 1) * 128] = total

            look_up(near_tab, b_ref, at, store, pairs=pairs, cols=cols)
            return carry

        lax.fori_loop(0, tall // 8, near_body, 0)
        at = pl.ds(start, tall)
        for p in range(pairs):
            cut = slice(p * 128, (p + 1) * 128)
            block = q_ref[pl.ds(pl.multiple_of(first + start, 64), tall), cut]
            zero = jnp.zeros_like(block)
            mask = lane_half((tall, 128))
            score[0, 0:tall, :] = nt(jnp.where(mask, block, zero), k_ref[:, cut])
            score[1, 0:tall, :] = nt(jnp.where(mask, zero, block), k_ref[:, cut])
            for c in range(cols // 128):
                turned = far_sum[p, c * 128:(c + 1) * 128, pl.ds(start, 128)].T[0:tall]
                here = slice(c * 128, (c + 1) * 128)
                f0, f1 = unpack_pair(turned)
                n0, n1 = unpack_pair(near_sum[p, 0:tall, here])
                score[0, 0:tall, here] += (
                    f0 * inv_ref[2 * p:2 * p + 1, here] + n0 * near_inv[2 * p, at, :]
                )
                score[1, 0:tall, here] += (
                    f1 * inv_ref[2 * p + 1:2 * p + 2, here] + n1 * near_inv[2 * p + 1, at, :]
                )
            for h in range(2):
                for s in range(tall // 16):
                    raw = score[h, s * 16:(s + 1) * 16, :]
                    logits = jnp.where(valid, raw * scale, -1e30)
                    top = jnp.max(logits, axis=1, keepdims=True)
                    grown = jnp.exp(logits - top)
                    share = grown * (1.0 / jnp.sum(grown, axis=1, keepdims=True))
                    p_ref[2 * p + h, pl.ds(pl.multiple_of(start + s * 16, 16), 16), :] = share.astype(bf16)
            c0 = nn(p_ref[2 * p, at, :], v_ref[:, cut])
            c1 = nn(p_ref[2 * p + 1, at, :], v_ref[:, cut])
            ctx_ref[at, cut] = jnp.where(mask, c0, c1).astype(bf16)

    def outer(step, carry):
        block_body(pl.multiple_of(step * 128, 128), 128)
        return carry

    lax.fori_loop(0, rows // 128, outer, 0)
    if rows % 128:
        block_body(rows - rows % 128, rows % 128)


def project_kernel(x_ref, wq_ref, wk_ref, wv_ref, t_ref, kp_ref, qp_ref, qkv_ref, pk_ref, pq_ref, *, span, cols, width):
    tail = span - span % 128
    qkv_ref[span - span % 16:cols, :] = jnp.zeros((cols - span + span % 16, 3 * width), bf16)
    for n, w_ref in enumerate((wq_ref, wk_ref, wv_ref)):
        cut = slice(n * width, (n + 1) * width)

        def body(step, carry, cut=cut, w_ref=w_ref):
            at = pl.ds(pl.multiple_of(step * 128, 128), 128)
            qkv_ref[at, cut] = nn(x_ref[at, :], w_ref[...]).astype(bf16)
            return carry

        lax.fori_loop(0, span // 128, body, 0)
        if tail < span:
            qkv_ref[tail:span, cut] = nn(x_ref[tail:span, :], w_ref[...]).astype(bf16)
    for r in range(3):
        at = slice(r * REL, (r + 1) * REL)
        pk_ref[at, :] = nn(t_ref[r], kp_ref[...]).astype(bf16)
        pq_ref[at, :] = nn(t_ref[r], qp_ref[...]).astype(bf16)


def project(tokens, query_weight, key_weight, value_weight, tables, key_position, query_position, span):
    width = query_weight.shape[1]
    rows, cols = sizes(span)
    whole = pl.BlockSpec(memory_space=pltpu.VMEM)
    return pl.pallas_call(
        functools.partial(project_kernel, span=span, cols=cols, width=width),
        out_shape=(
            jax.ShapeDtypeStruct((cols, 3 * width), bf16),
            jax.ShapeDtypeStruct((3 * REL, width), bf16),
            jax.ShapeDtypeStruct((3 * REL, width), bf16),
        ),
        in_specs=[whole] * 7,
        out_specs=(whole,) * 3,
        compiler_params=pltpu.CompilerParams(vmem_limit_bytes=VMEM_CAP),
        cost_estimate=pl.CostEstimate(flops=4 * 10**9, bytes_accessed=9 * 10**6, transcendentals=0),
        name="project",
    )(tokens, query_weight, key_weight, value_weight, tables, key_position, query_position)


def pick(half, block, h):
    zero = jnp.zeros_like(block)
    return jnp.where(half, block, zero) if h == 0 else jnp.where(half, zero, block)


def draw_kernel(
    p_ref, up_ref, q_ref, k_ref, v_ref, *refs, first, tall, rows, cols, scale, adds,
):
    extra = refs[:adds]
    d_ref, dt_ref, dq_ref, dk_ref, dv_ref, wide, flat, turned = refs[adds:]
    lanes = turned.shape[2]
    half = lane_half((64, 128))

    def body(step, carry):
        at = pl.ds(pl.multiple_of(step * 64, 64), 64)
        pair = []
        for h in range(2):
            reach = nt(pick(half, up_ref[at, :], h), v_ref[...])
            share = p_ref[h, at, :].astype(f32)
            inner = jnp.sum(reach * share, axis=1, keepdims=True)
            back = share * (reach - inner) * scale
            wide[h, at, :] = back
            flat[h, at, :] = back.astype(bf16)
            pair.append(back.reshape(8, 8, cols))
        d_ref[pl.ds(pl.multiple_of(step * 8, 8), 8), :, :] = jnp.concatenate(pair, axis=1).astype(bf16)
        return carry

    lax.fori_loop(0, tall // 64, body, 0)
    for jb in range(cols // 128):
        high = min(128, rows - jb * 128)
        for ib in range(lanes // 128):
            wide_rows = min(128, tall - ib * 128)
            pair = []
            for h in range(2):
                block = wide[h, ib * 128:ib * 128 + wide_rows, jb * 128:(jb + 1) * 128]
                if wide_rows < 128:
                    block = jnp.concatenate([block, jnp.zeros((128 - wide_rows, 128), f32)], axis=0)
                other = block.T[:high]
                turned[h, jb * 128:jb * 128 + high, ib * 128:(ib + 1) * 128] = other.astype(bf16)
                pair.append(other.reshape(high // 8, 8, 128))
            dt_ref[jb * 16:jb * 16 + high // 8, :, ib * 128:(ib + 1) * 128] = jnp.concatenate(
                pair, axis=1
            ).astype(bf16)
    keys, queries, ups = k_ref[...], q_ref[first:first + lanes, :], up_ref[...]
    cols_half, lanes_half, tall_half = (lane_half((n, 128)) for n in (cols, lanes, tall))
    dq_ref[...] = nn(flat[0], pick(cols_half, keys, 0)) + nn(flat[1], pick(cols_half, keys, 1))
    dk = nn(turned[0], pick(lanes_half, queries, 0)) + nn(turned[1], pick(lanes_half, queries, 1))
    dv = tn(p_ref[0], pick(tall_half, ups, 0)) + tn(p_ref[1], pick(tall_half, ups, 1))
    dv = dv[:rows]
    if adds:
        dk, dv = dk + extra[0][...], dv + extra[1][...]
    dk_ref[...] = dk
    dv_ref[...] = dv.astype(dv_ref.dtype)


def scatter_kernel(*refs, groups, cols):
    *d_refs, b_ref, merge_ref, out_ref = refs
    base = jnp.where(lax.broadcasted_iota(jnp.int32, (16, cols), 0) >= 8, 1.0, 0.0).astype(bf16)
    own = (lax.broadcasted_iota(jnp.int32, (256, 256), 0) % 8) == (
        lax.broadcasted_iota(jnp.int32, (256, 256), 1) % 8
    )
    zero = jnp.asarray(0.0, bf16)
    one = jnp.asarray(1.0, bf16)

    def sieve(g, r, back):
        bucket = b_ref[r, pl.ds(pl.multiple_of(g * 8, 8), 8), :]
        low = (bucket & 31).astype(f32)
        high = (bucket >> 5).astype(f32)
        low = jnp.concatenate([low, low], axis=0).astype(bf16) - base
        high = jnp.concatenate([high, high], axis=0).astype(bf16)
        hot = jnp.concatenate(
            [jnp.where(low == jnp.asarray(2.0 * k, bf16), one, zero) for k in range(16)], axis=0
        )
        sieved = []
        for l in range(4):
            mask = high == jnp.asarray(float(l), bf16)
            for p in range(4):
                sieved.append(jnp.where(mask, back[p * 16:(p + 1) * 16], zero))
        sums = nt(jnp.concatenate(sieved, axis=0), hot)
        return jnp.where(own, sums, 0.0).astype(bf16)

    def body(step, carry):
        got = []
        for g in (2 * step, 2 * step + 1):
            back = jnp.concatenate([d_ref[g] for d_ref in d_refs], axis=1) if len(d_refs) > 1 else d_refs[0][g]
            for r in range(3):
                got.append((g, r, sieve(g, r, back)))
        for g, r, sums in got:
            total = None
            for l in range(4):
                term = nn(sums[l * 64:(l + 1) * 64], merge_ref[l])
                total = term if total is None else total + term
            out_ref[g, :, r * 128:(r + 1) * 128] = total.astype(bf16)
        return carry

    lax.fori_loop(0, groups // 2, body, 0)


def close_kernel(*refs, rows, count):
    *base_refs, pos_ref, side_ref, out_ref, table_ref = refs[count:]
    rows2 = 2 * rows
    half3 = lane_half((rows // 8, 8, 128))
    flat = jnp.concatenate([ref[...] for ref in refs[:count]], axis=0).reshape(rows2, 3 * REL)
    both = nn(flat, pos_ref[...]).reshape(rows // 8, 16, 128)
    mine = jnp.where(half3, both[:, 0:8, :], both[:, 8:16, :]).reshape(rows, 128)
    first = 0
    for base_ref in base_refs:
        here = slice(first, first + base_ref.shape[0])
        out_ref[here, :] = (base_ref[...] + mine[here]).astype(bf16)
        first += base_ref.shape[0]
    side = side_ref[0:rows, :].astype(f32).reshape(rows // 8, 8, 128)
    zero = jnp.zeros_like(side)
    spread = jnp.concatenate([jnp.where(half3, side, zero), jnp.where(half3, zero, side)], axis=1)
    table_ref[...] = tn(flat, spread.reshape(rows2, 128).astype(bf16)).astype(bf16)


def merge_table():
    l = lax.broadcasted_iota(jnp.int32, (4, 256, 128), 0)
    a = lax.broadcasted_iota(jnp.int32, (4, 256, 128), 1) // 8
    c = lax.broadcasted_iota(jnp.int32, (4, 256, 128), 2)
    return (c == l * 32 + a).astype(bf16)


def sizes(span):
    return -(-span // 64) * 64, -(-span // 128) * 128


def forward_scratch(pairs, tall, cols):
    return [
        pltpu.VMEM((pairs, tall, 3 * REL), jnp.int32),
        pltpu.VMEM((2 * pairs, tall, 128), f32),
        pltpu.VMEM((pairs, 128, cols), jnp.int32),
        pltpu.VMEM((2, 128, cols), f32),
    ]


def attention_head(qkv, pos_key, pos_query, buckets, used, scale, split):
    span = buckets.shape[2]
    rows, cols = sizes(span)
    width = pos_key.shape[1]
    pairs = width // 128
    whole = pl.BlockSpec(memory_space=pltpu.VMEM)
    i32 = jnp.int32

    def kernel(
        used_ref, qkv_ref, pk_ref, pq_ref, b_ref, p_ref, ctx_ref, head_ref, rest_ref, bt_ref, far_rest, inv_ref,
        far_tab, far_inv, far_head, *scratch,
    ):
        k_ref = qkv_ref.at[:, width:2 * width]
        prepare_rows(
            k_ref, pq_ref, b_ref, head_ref, rest_ref, bt_ref, far_head, far_rest, inv_ref, far_tab, far_inv,
            span=span, rows=rows, cols=cols, pairs=pairs, split=split,
        )
        forward_rows(
            used_ref, qkv_ref.at[:, 0:width], k_ref, qkv_ref.at[:, 2 * width:3 * width], pk_ref, head_ref,
            far_head, inv_ref, p_ref, ctx_ref, *scratch,
            first=0, rows=split, span=span, cols=cols, pairs=pairs, scale=scale,
        )

    return pl.pallas_call(
        kernel,
        out_shape=(
            jax.ShapeDtypeStruct((2 * pairs, split, cols), bf16),
            jax.ShapeDtypeStruct((split, width), bf16),
            jax.ShapeDtypeStruct((3, split, cols), i32),
            jax.ShapeDtypeStruct((3, rows - split, cols), i32),
            jax.ShapeDtypeStruct((3, rows, cols), i32),
            jax.ShapeDtypeStruct((pairs, cols, cols - split), i32),
            jax.ShapeDtypeStruct((2 * pairs, cols), f32),
        ),
        in_specs=[pl.BlockSpec(memory_space=pltpu.SMEM)] + [whole] * 4,
        out_specs=(whole,) * 7,
        scratch_shapes=[
            pltpu.VMEM((pairs, rows, 3 * REL), i32),
            pltpu.VMEM((2 * pairs, rows, 128), f32),
            pltpu.VMEM((pairs, cols, split), i32),
        ] + forward_scratch(pairs, split, cols),
        compiler_params=pltpu.CompilerParams(vmem_limit_bytes=VMEM_CAP),
        cost_estimate=pl.CostEstimate(flops=4 * 10**10, bytes_accessed=25000000, transcendentals=0),
        name="attention_head",
    )(used, qkv, pos_key, pos_query, buckets)


def attention_rest(qkv, pos_key, bucket_rest, far_rest, inverse, used, scale, split, span):
    rows, cols = sizes(span)
    width = pos_key.shape[1]
    pairs = width // 128
    whole = pl.BlockSpec(memory_space=pltpu.VMEM)

    def kernel(used_ref, qkv_ref, pk_ref, b_ref, far_ref, inv_ref, p_ref, ctx_ref, *scratch):
        forward_rows(
            used_ref, qkv_ref.at[:, 0:width], qkv_ref.at[:, width:2 * width], qkv_ref.at[:, 2 * width:3 * width],
            pk_ref, b_ref, far_ref, inv_ref, p_ref, ctx_ref, *scratch,
            first=split, rows=rows - split, span=span, cols=cols, pairs=pairs, scale=scale,
        )

    return pl.pallas_call(
        kernel,
        out_shape=(
            jax.ShapeDtypeStruct((2 * pairs, rows - split, cols), bf16),
            jax.ShapeDtypeStruct((rows - split, width), bf16),
        ),
        in_specs=[pl.BlockSpec(memory_space=pltpu.SMEM)] + [whole] * 5,
        out_specs=(whole,) * 2,
        scratch_shapes=forward_scratch(pairs, rows - split, cols),
        compiler_params=pltpu.CompilerParams(vmem_limit_bytes=VMEM_CAP),
        cost_estimate=pl.CostEstimate(flops=2 * 10**10, bytes_accessed=12000000, transcendentals=0),
        name="attention_rest",
    )(used, qkv, pos_key, bucket_rest, far_rest, inverse)


def attention_draw(share, upstream, qkv, scale, first, rows, adds=()):
    heads, tall, cols = share.shape
    width = upstream.shape[1]
    pairs = heads // 2
    lanes = -(-tall // 128) * 128

    def column(n):
        return pl.BlockSpec((n, 128), lambda p: (0, p))

    return pl.pallas_call(
        functools.partial(draw_kernel, first=first, tall=tall, rows=rows, cols=cols, scale=scale, adds=len(adds)),
        grid=(pairs,),
        in_specs=[
            pl.BlockSpec((2, tall, cols), lambda p: (p, 0, 0)),
            column(tall),
            pl.BlockSpec((cols, 128), lambda p: (0, p)),
            pl.BlockSpec((cols, 128), lambda p: (0, p + pairs)),
            pl.BlockSpec((cols, 128), lambda p: (0, p + 2 * pairs)),
        ] + [column(rows)] * len(adds),
        out_specs=(
            pl.BlockSpec((tall // 8, 16, cols), lambda p: (0, p, 0)),
            pl.BlockSpec((rows // 8, 16, lanes), lambda p: (0, p, 0)),
            column(tall), column(rows), column(rows),
        ),
        out_shape=(
            jax.ShapeDtypeStruct((tall // 8, 8 * heads, cols), bf16),
            jax.ShapeDtypeStruct((rows // 8, 8 * heads, lanes), bf16),
            jax.ShapeDtypeStruct((tall, width), f32),
            jax.ShapeDtypeStruct((rows, width), f32),
            jax.ShapeDtypeStruct((rows, width), bf16 if adds else f32),
        ),
        scratch_shapes=[
            pltpu.VMEM((2, tall, cols), f32),
            pltpu.VMEM((2, tall, cols), bf16),
            pltpu.VMEM((2, rows, lanes), bf16),
        ],
        compiler_params=pltpu.CompilerParams(vmem_limit_bytes=VMEM_CAP),
        cost_estimate=pl.CostEstimate(flops=10**6, bytes_accessed=10**4, transcendentals=0),
        name="attention_draw",
    )(share, upstream, qkv, qkv, qkv, *adds)


def attention_scatter(backs, buckets, merge, first, count):
    high = backs[0].shape[1]
    cols = buckets.shape[2]
    return pl.pallas_call(
        functools.partial(scatter_kernel, groups=8, cols=cols),
        grid=(count,),
        out_shape=jax.ShapeDtypeStruct((8 * count, high, 3 * REL), bf16),
        in_specs=[pl.BlockSpec((8, high, b.shape[2]), lambda g: (first + g, 0, 0)) for b in backs] + [
            pl.BlockSpec((3, 64, cols), lambda g: (0, first + g, 0)),
            pl.BlockSpec(merge.shape, lambda g: (0, 0, 0)),
        ],
        out_specs=pl.BlockSpec((8, high, 3 * REL), lambda g: (g, 0, 0)),
        compiler_params=pltpu.CompilerParams(vmem_limit_bytes=VMEM_CAP),
        cost_estimate=pl.CostEstimate(flops=10**6, bytes_accessed=10**4, transcendentals=0),
        name="attention_scatter",
    )(*backs, buckets, merge)


def attention_close(sums, bases, pos, qkv, side):
    rows, width = sum(base.shape[0] for base in bases), bases[0].shape[1]
    pairs = width // 128
    return pl.pallas_call(
        functools.partial(close_kernel, rows=rows, count=len(sums)),
        grid=(pairs,),
        in_specs=[pl.BlockSpec((part.shape[0], 16, 3 * REL), lambda p: (0, p, 0)) for part in sums] + [
            pl.BlockSpec((base.shape[0], 128), lambda p: (0, p)) for base in bases
        ] + [
            pl.BlockSpec((3 * REL, 128), lambda p: (0, p)),
            pl.BlockSpec((qkv.shape[0], 128), lambda p: (0, p + side * pairs)),
        ],
        out_specs=(
            pl.BlockSpec((rows, 128), lambda p: (0, p)),
            pl.BlockSpec((3 * REL, 128), lambda p: (0, p)),
        ),
        out_shape=(
            jax.ShapeDtypeStruct((rows, width), bf16),
            jax.ShapeDtypeStruct((3 * REL, width), bf16),
        ),
        compiler_params=pltpu.CompilerParams(vmem_limit_bytes=VMEM_CAP),
        cost_estimate=pl.CostEstimate(flops=10**6, bytes_accessed=10**4, transcendentals=0),
        name="attention_close",
    )(*sums, *bases, pos, qkv)


def fill_turned(x_ref, turned, rows):
    depth = x_ref.shape[1]
    for a in range(0, rows, 128):
        tall = min(128, rows - a)
        for b in range(0, depth, 128):
            block = x_ref[a:a + tall, b:b + 128]
            if tall < 128:
                block = jnp.concatenate([block, jnp.zeros((128 - tall, 128), block.dtype)], axis=0)
            turned[b:b + 128, a:a + tall] = block.T[:, :tall]


def each_block(pick_ref, blocks, keeps, bit, slot):
    if not keeps:
        return [(0, d, d) for d in range(blocks)]
    shift = bit - 1
    listed = []
    for out in range(2):
        value = pick_ref[slot] if out == 1 else 1 - pick_ref[slot]
        for e in range(blocks // 2):
            low = e & ((1 << shift) - 1)
            listed.append((out, e, ((e >> shift) << (shift + 1)) + low + value * (1 << shift)))
    return listed


def weight_kernel(pick_ref, *refs, count, blocks, deep, keeps, bit):
    xs, ys, rest = refs[:count], refs[count:2 * count], refs[2 * count:]
    add_ref = rest[0] if keeps else None
    outs = rest[1:3] if keeps else rest[0:1]
    turned = rest[-count:]

    @pl.when(pl.program_id(0) == 0)
    def _():
        for x_ref, wide in zip(xs, turned):
            fill_turned(x_ref, wide, x_ref.shape[0])

    for out, place, d in each_block(pick_ref, blocks, keeps, bit, 1):
        at = pl.ds(pl.multiple_of((2 * d + pick_ref[0]) * deep, deep), deep)
        part = add_ref[d] if keeps else None
        for wide, y_ref in zip(turned, ys):
            term = nn(wide[at, :], y_ref[...])
            part = term if part is None else part + term
        outs[out][place] = part


def weight_half(pick, xs, ys, add=None, *, parts, bits, tile=512):
    depth = xs[0].shape[1]
    wide = ys[0].shape[1]
    deep = depth // parts
    blocks = parts // 2
    keeps = add is not None

    def tiled(n):
        return pl.BlockSpec((n, deep, tile), lambda c: (0, 0, c))

    ins = [pl.BlockSpec(memory_space=pltpu.SMEM)]
    ins += [pl.BlockSpec(x.shape, lambda c: (0, 0)) for x in xs]
    ins += [pl.BlockSpec((y.shape[0], tile), lambda c: (0, c)) for y in ys]
    args = [pick, *xs, *ys]
    shape = (jax.ShapeDtypeStruct((blocks, deep, wide), f32),)
    specs = (tiled(blocks),)
    if keeps:
        ins.append(tiled(blocks))
        args += add
        shape = (jax.ShapeDtypeStruct((blocks // 2, deep, wide), f32),) * 2
        specs = (tiled(blocks // 2),) * 2
    rows = sum(x.shape[0] for x in xs)
    return pl.pallas_call(
        functools.partial(weight_kernel, count=len(xs), blocks=blocks, deep=deep, keeps=keeps, bit=bits[0]),
        grid=(wide // tile,),
        in_specs=ins,
        out_specs=specs,
        out_shape=shape,
        scratch_shapes=[pltpu.VMEM((depth, x.shape[0]), bf16) for x in xs],
        compiler_params=pltpu.CompilerParams(vmem_limit_bytes=VMEM_CAP),
        cost_estimate=pl.CostEstimate(
            flops=rows * depth * wide, bytes_accessed=4 * depth * wide, transcendentals=0
        ),
        name="weight_half",
    )(*args)


def many_kernel(pick_ref, *refs, plan, widths, turns, blocks, deep, keeps, bits):
    n_in = 2 * len(plan)
    ins = refs[:n_in]
    n_out = len(widths)
    adds = refs[n_in:n_in + n_out] if keeps else None
    outs = refs[n_in + n_out:n_in + 3 * n_out] if keeps else refs[n_in:n_in + n_out]
    scratch = refs[len(refs) - sum(turns):]
    left = []
    used = 0
    for n, turn in enumerate(turns):
        if turn:
            fill_turned(ins[2 * n], scratch[used], ins[2 * n].shape[0])
            left.append(scratch[used])
            used += 1
        else:
            left.append(ins[2 * n])
    right = [ins[2 * n + 1][...] for n in range(len(plan))]
    for group in range(n_out):
        for out, place, d in each_block(pick_ref, blocks, keeps, bits[group], 1 + group):
            at = pl.ds(pl.multiple_of((2 * d + pick_ref[0]) * deep, deep), deep)
            target = outs[2 * group + out] if keeps else outs[group]
            for n, (kind, own, start, wide) in enumerate(plan):
                if own != group:
                    continue
                rows = left[n][at, :]
                if kind == "copy":
                    part = rows
                elif kind == "nt":
                    part = nt(rows, right[n])
                else:
                    part = nn(rows, right[n])
                cut = slice(start, start + wide)
                if keeps:
                    part = part + adds[group][d, :, cut]
                target[place, :, cut] = part


def many_half(pick, pairs, plan, widths, add=None, *, parts, bits):
    whole = pl.BlockSpec(memory_space=pltpu.VMEM)
    turns = [kind in ("turn", "copy") for kind, *_ in plan]
    depth = max(left.shape[1 if turn else 0] for (left, _), turn in zip(pairs, turns))
    deep = depth // parts
    blocks = parts // 2
    keeps = add is not None
    args = [pick] + [operand for pair in pairs for operand in pair] + (list(add) if keeps else [])
    if keeps:
        shape = [jax.ShapeDtypeStruct((blocks // 2, deep, w), f32) for w in widths for _ in range(2)]
    else:
        shape = [jax.ShapeDtypeStruct((blocks, deep, w), f32) for w in widths]
    return pl.pallas_call(
        functools.partial(
            many_kernel, plan=plan, widths=widths, turns=turns, blocks=blocks, deep=deep,
            keeps=keeps, bits=[b[0] for b in bits],
        ),
        in_specs=[pl.BlockSpec(memory_space=pltpu.SMEM)] + [whole] * (len(args) - 1),
        out_specs=[whole] * len(shape),
        out_shape=shape,
        scratch_shapes=[
            pltpu.VMEM((left.shape[1], left.shape[0]), left.dtype)
            for (left, _), turn in zip(pairs, turns) if turn
        ],
        compiler_params=pltpu.CompilerParams(vmem_limit_bytes=VMEM_CAP),
        cost_estimate=pl.CostEstimate(flops=10**6, bytes_accessed=10**4, transcendentals=0),
        name="many_half",
    )(*args)


def flipped(value, bit, size):
    return lax.ppermute(value, "dp", [(i, i ^ (1 << bit)) for i in range(size)])


def bit_of(index, bit):
    return (index >> bit) & 1


class Halving:
    def __init__(self, make, index, size, orders):
        self.make, self.index, self.size, self.orders = make, index, size, orders
        mine = bit_of(index, 0).astype(jnp.int32)
        self.pick = jnp.stack([mine] + [bit_of(index, bits[0]).astype(jnp.int32) for bits in orders])
        self.other = self.pick.at[0].set(1 - mine)
        self.stage = 0
        self.extra = None

    def work(self):
        if self.stage == 0:
            self.pending = [(sent, None) for sent in self.make(self.other, None)]
        elif self.stage == 1:
            outs = self.make(self.pick, self.extra)
            self.pending = [(outs[2 * g], outs[2 * g + 1]) for g in range(len(self.orders))]
            self.axes = [
                [b for b in range(self.size.bit_length() - 1, 0, -1) if b != bits[0] and b < self.size.bit_length() - 1]
                for bits in self.orders
            ]
        else:
            self.pending = [
                self.split(g, held, extra) for g, (held, extra) in enumerate(zip(self.held, self.extra))
            ]
        return [part for pair in self.pending for part in pair if part is not None]

    def split(self, g, held, extra):
        bits = self.orders[g]
        if self.stage > len(bits):
            return held + extra, None
        bit = bits[self.stage - 1]
        axis = self.axes[g].index(bit)
        shape = (2,) * len(self.axes[g]) + held.shape[-2:]
        self.axes[g].remove(bit)
        own = bit_of(self.index, bit)
        held, extra = held.reshape(shape), extra.reshape(shape)

        def half(value, at):
            return lax.dynamic_index_in_dim(value, at, axis, keepdims=False)

        return half(held, 1 - own) + half(extra, 1 - own), half(held, own) + half(extra, own)

    def go(self, parts):
        parts = list(parts)
        pairs = [
            tuple(None if part is None else parts.pop(0) for part in pair) for pair in self.pending
        ]
        self.held = [home for _, home in pairs]
        last = self.stage > len(self.orders[0])
        if last:
            self.result = [away for away, _ in pairs]
        else:
            bit = lambda g: 0 if self.stage == 0 else self.orders[g][self.stage - 1]
            self.extra = [flipped(away, bit(g), self.size) for g, (away, _) in enumerate(pairs)]
        self.stage += 1

    def step(self):
        self.go(self.work())

    def over(self):
        return self.stage > len(self.orders[0]) + 1

    def finish(self):
        while not self.over():
            self.step()
        return self.result


def tie(values, *chains):
    chains = [chain for chain in chains if not chain.over()]
    values, extras = lax.optimization_barrier((values, [chain.extra for chain in chains]))
    for chain, extra in zip(chains, extras):
        chain.extra = extra
    works = [chain.work() for chain in chains]
    values, works = lax.optimization_barrier((values, works))
    for chain, parts in zip(chains, works):
        chain.go(parts)
    return values


def swap(value):
    return lax.ppermute(value.astype(f32), "mp", [(0, 1), (1, 0)])


def attend_kernel(
    t_ref, c_ref, o_ref, w_ref, ow_ref, gain_ref, shift_ref, first_ref, low_ref, normal_ref, inverse_ref,
):
    weight = ow_ref[...].astype(bf16)

    def body(step, carry):
        at = pl.ds(pl.multiple_of(step * 64, 64), 64)
        summed = t_ref[at, :].astype(f32) + nn(c_ref[at, :], w_ref[...])
        summed = summed + nn(o_ref[at, :].astype(bf16), weight)
        first, normal, inverse = norm_forward(summed, gain_ref[...], shift_ref[...])
        first_ref[at, :] = first
        low_ref[at, :] = first.astype(bf16)
        normal_ref[at, :] = normal
        inverse_ref[at, :] = inverse
        return carry

    lax.fori_loop(0, t_ref.shape[0] // 64, body, 0)


def attend(tokens, context, other, weight, other_weight, gain, shift):
    tall, depth = tokens.shape
    whole = pl.BlockSpec(memory_space=pltpu.VMEM)
    return pl.pallas_call(
        attend_kernel,
        in_specs=[whole] * 7,
        out_specs=(whole,) * 4,
        out_shape=(
            jax.ShapeDtypeStruct((tall, depth), f32),
            jax.ShapeDtypeStruct((tall, depth), bf16),
            jax.ShapeDtypeStruct((tall, depth), f32),
            jax.ShapeDtypeStruct((tall, 1), f32),
        ),
        compiler_params=pltpu.CompilerParams(vmem_limit_bytes=VMEM_CAP),
        cost_estimate=pl.CostEstimate(flops=2 * 10**9, bytes_accessed=8 * 10**6, transcendentals=0),
        name="attend",
    )(tokens, context, other, weight, other_weight, gain[None], shift[None])


def norm_forward(summed, gain, shift):
    centred = summed - jnp.mean(summed, axis=1, keepdims=True)
    inverse = lax.rsqrt(jnp.mean(centred * centred, axis=1, keepdims=True) + epsilon)
    normal = centred * inverse
    return (normal * gain + shift, normal, inverse)


def norm_backward(upstream, normal, inverse, gain):
    scaled = upstream * gain
    inner = jnp.mean(scaled, axis=1, keepdims=True)
    aligned = jnp.mean(scaled * normal, axis=1, keepdims=True)
    return (
        inverse * (scaled - inner - normal * aligned),
        jnp.sum(upstream * normal, axis=0),
        jnp.sum(upstream, axis=0),
    )


def shards(
    tokens,
    query_weight,
    key_weight,
    value_weight,
    output_weight,
    query_position,
    key_position,
    position_tables,
    gain_one,
    shift_one,
    up_weight,
    down_weight,
    gain_two,
    shift_two,
    buckets,
    text_length,
    cotangent,
):
    span = buckets.shape[2]
    rows, cols = sizes(span)
    size = lax.axis_size("dp")
    index = lax.axis_index("dp")
    bits = list(range(1, size.bit_length() - 1))
    low_first, high_first = bits, bits[1:2] + bits[:1] + bits[2:]
    score_scale = (7.0 * HEAD) ** (-0.5)
    tables_flat = position_tables.reshape(3 * REL, D)
    width = query_weight.shape[1]
    spare = ((0, rows - span), (0, 0))

    def chain(make, *orders):
        return Halving(make, index, size, list(orders))

    split = rows // 2 // 128 * 128
    other_output = swap(output_weight)
    qkv, pos_key, pos_query = project(
        tokens, query_weight, key_weight, value_weight, position_tables, key_position, query_position, span
    )
    tokens = jnp.pad(tokens, spare)
    cotangent = jnp.pad(cotangent, spare)
    tokens_turned, tables_turned = tokens.T, tables_flat.T
    edges = [(0, split), (split, rows)]

    share_head, context_head, bucket_head, bucket_rest, bucket_cols, far_rest, far_inverse = attention_head(
        qkv, pos_key, pos_query, buckets, text_length, score_scale, split
    )
    other_head = swap(context_head)
    far_rest, other_output = lax.optimization_barrier((far_rest, other_output))
    share_rest, context_rest = attention_rest(
        qkv, pos_key, bucket_rest, far_rest, far_inverse, text_length, score_scale, split, span
    )
    other_rest = swap(context_rest)
    shares = [share_head, share_rest]
    contexts = [context_head, context_rest]
    contexts_other = [other_head, other_rest]

    def gelu(value):
        return jax.nn.gelu(value, approximate=False)

    firsts, firsts_low, normals_one, inverses_one, upwards, hiddens, feeds, feeds_other = ([] for _ in range(8))
    for (low, high), context, other in zip(edges, contexts, contexts_other):
        first, first_low, normal_one, inverse_one = attend(
            tokens[low:high], context, other, output_weight, other_output, gain_one, shift_one
        )
        firsts.append(first)
        normals_one.append(normal_one)
        inverses_one.append(inverse_one)
        firsts_low.append(first_low)
        upwards.append(nn(firsts_low[-1], up_weight))
        hiddens.append(gelu(upwards[-1]).astype(bf16))
        feeds.append(nn(hiddens[-1], down_weight))
        feeds_other.append(swap(feeds[-1]))

    finals, seconds_back, seconds_low, upwards_back, backs_part, backs_other, two_sums = ([] for _ in range(7))
    for n, (low, high) in enumerate(edges):
        final, normal_two, inverse_two = norm_forward(
            firsts[n] + feeds[n] + feeds_other[n], gain_two, shift_two
        )
        finals.append(final.astype(bf16))
        second_back, *sums = norm_backward(
            cotangent[low:high].astype(f32), normal_two, inverse_two, gain_two
        )
        two_sums.append(sums)
        seconds_back.append(second_back)
        seconds_low.append(second_back.astype(bf16))
        hidden_back = nt(seconds_low[n], down_weight)
        upwards_back.append(jax.vjp(gelu, upwards[n])[1](hidden_back)[0].astype(bf16))
        backs_part.append(nt(upwards_back[n], up_weight))
        backs_other.append(swap(backs_part[n]))
    layer_output = jnp.concatenate(finals, axis=0)[:span]
    gain_two_grad, shift_two_grad = (two_sums[0][n] + two_sums[1][n] for n in range(2))

    backs_part, down_pair, up_pair = lax.optimization_barrier(
        (backs_part, (seconds_low, hiddens), (firsts_low, upwards_back))
    )
    up_pair, backs_other[0] = lax.optimization_barrier((up_pair, backs_other[0]))
    down_chain = chain(
        lambda pick, add: weight_half(pick, *down_pair, add, parts=size, bits=high_first), high_first
    )
    up_chain = chain(
        lambda pick, add: weight_half(pick, *up_pair, add, parts=size, bits=low_first), low_first
    )
    down_chain.step()
    up_chain.step()
    backs_other[0] = tie(backs_other[0], down_chain)
    backs_other[0] = tie(backs_other[0], up_chain)
    merge = merge_table()
    residuals_back, residuals_low, one_sums = [], [], []

    def draw(n, adds=()):
        residual_back, *sums = norm_backward(
            seconds_back[n] + backs_part[n] + backs_other[n], normals_one[n], inverses_one[n], gain_one
        )
        one_sums.append(sums)
        residuals_back.append(residual_back)
        residuals_low.append(residual_back.astype(bf16))
        context_back = nt(residuals_low[n], output_weight).astype(bf16)
        return attention_draw(shares[n], context_back, qkv, score_scale, edges[n][0], rows, adds)

    back_head, turned_head, query_head, key_head, value_head = draw(0)
    back_head, key_head, backs_other[1] = lax.optimization_barrier((back_head, key_head, backs_other[1]))
    back_rest, turned_rest, query_rest, key_base, value_back = draw(1, (key_head, value_head))
    gain_one_grad, shift_one_grad = (one_sums[0][n] + one_sums[1][n] for n in range(2))
    back_rest, value_back = tie((back_rest, value_back), down_chain)
    residual_low = jnp.concatenate(residuals_low, axis=0)
    context = jnp.concatenate(contexts, axis=0)
    nothing = jnp.zeros_like(gain_one)
    gains = jnp.stack(
        [gain_one_grad, shift_one_grad, gain_two_grad, shift_two_grad] + [nothing] * 4
    )
    gains = jnp.concatenate([gains, jnp.zeros((120, gains.shape[1]), f32)], axis=0)
    dummy = jnp.zeros((8, 128), bf16)
    outer_chain = chain(
        lambda pick, add: many_half(
            pick,
            [(residual_low, context), (tokens_turned, value_back), (gains, dummy)],
            [("turn", 0, 0, width), ("nn", 0, width, width), ("copy", 0, 2 * width, 128)],
            [2 * width + 128],
            add, parts=size, bits=[low_first],
        ),
        low_first,
    )
    outer_chain.step()

    def tail(rows_back, sums, position, orders):
        return chain(
            lambda pick, add: many_half(
                pick,
                [(tokens_turned, rows_back), (tables_turned, sums), (position, sums)],
                [("nn", 0, 0, width), ("nn", 1, 0, width), ("nt", 0, width, 3 * REL)],
                [width + 3 * REL, width],
                add, parts=size, bits=orders,
            ),
            *orders,
        )

    near = []
    blocks = rows // 64
    back_head, back_rest = tie((back_head, back_rest), up_chain)
    near.append(attention_scatter([back_head], bucket_head, merge, 0, split // 64))
    back_rest, near = tie((back_rest, near), down_chain)
    back_rest, near = tie((back_rest, near), outer_chain)
    near.append(attention_scatter([back_rest], bucket_rest, merge, 0, blocks - split // 64))
    near, backs = tie((near, [turned_head, turned_rest]), up_chain)
    query_low, key_table_sum = attention_close(near, [query_head, query_rest], pos_key, qkv, 0)
    early = nt(query_low, query_weight) + nt(value_back, value_weight)
    near_chain = tail(query_low, key_table_sum, key_position, [high_first, low_first])
    backs, key_table_sum = tie((backs, key_table_sum), near_chain, outer_chain, down_chain)
    far = []
    cuts = [n * blocks // 3 for n in range(4)]
    for part, chains in enumerate(((near_chain,), (outer_chain, up_chain), (near_chain, outer_chain))):
        far.append(attention_scatter(backs, bucket_cols, merge, cuts[part], cuts[part + 1] - cuts[part]))
        backs, far = tie((backs, far), *chains)
    key_low, query_table_sum = attention_close(far, [key_base], pos_query, qkv, 1)
    far_chain = tail(key_low, query_table_sum, query_position, [low_first, high_first])
    parts, others = [], []
    for low, high in ((0, rows // 2), (rows // 2, rows)):
        parts.append(early[low:high] + nt(key_low[low:high], key_weight))
        others.append(swap(parts[-1]))
    far_chain.step()
    far_chain.step()
    far_chain.extra, others[0] = lax.optimization_barrier((far_chain.extra, others[0]))
    far_main, query_position_grad = far_chain.finish()
    far_main, others[1] = lax.optimization_barrier((far_main, others[1]))
    input_gradient = (
        jnp.concatenate(residuals_back, axis=0) + jnp.concatenate(parts, axis=0) + jnp.concatenate(others, axis=0)
    )[:span].astype(bf16)
    (down_share,) = down_chain.finish()
    (up_share,) = up_chain.finish()
    (outer_share,) = outer_chain.finish()
    near_main, key_position_grad = near_chain.finish()

    table_rows = near_main[:, width:] + far_main[:, width:]
    table_rows = table_rows.reshape(2, table_rows.shape[0] // 2, 3 * REL)
    side = lax.axis_index("mp")
    table_mine = lax.dynamic_index_in_dim(table_rows, side, 0, keepdims=False) + lax.ppermute(
        lax.dynamic_index_in_dim(table_rows, 1 - side, 0, keepdims=False), "mp", [(0, 1), (1, 0)]
    )
    table_gradient = table_mine.T.reshape(3, REL, table_mine.shape[0])
    gains_mine = outer_share[:, 2 * width:]
    return (
        layer_output,
        input_gradient,
        near_main[:, 0:width],
        far_main[:, 0:width],
        outer_share[:, width:2 * width],
        outer_share[:, 0:width].T,
        query_position_grad,
        key_position_grad,
        table_gradient,
        gains_mine[:, 0],
        gains_mine[:, 1],
        up_share,
        down_share.T,
        gains_mine[:, 2],
        gains_mine[:, 3],
    )


def solution(mesh):
    return jax.shard_map(
        shards,
        mesh=mesh,
        in_specs=(
            P("dp", None),
            P(None, "mp"),
            P(None, "mp"),
            P(None, "mp"),
            P("mp", None),
            P(None, "mp"),
            P(None, "mp"),
            P(),
            P(),
            P(),
            P(None, "mp"),
            P("mp", None),
            P(),
            P(),
            P("dp", None, None, None),
            P("dp"),
            P("dp", None),
        ),
        out_specs=(
            P("dp", None),
            P("dp", None),
            P("dp", "mp"),
            P("dp", "mp"),
            P("dp", "mp"),
            P("mp", "dp"),
            P("dp", "mp"),
            P("dp", "mp"),
            P(None, None, ("dp", "mp")),
            P("dp"),
            P("dp"),
            P("dp", "mp"),
            P("mp", "dp"),
            P("dp"),
            P("dp"),
        ),
        check_vma=False,
    )
```

```python
import functools

import jax
import jax.numpy as jnp
from jax import lax
from jax.experimental import pallas as pl
from jax.experimental.pallas import tpu as pltpu
from jax.sharding import PartitionSpec as P

D = 1024
epsilon = 1e-05
HEAD = 64
REL = 128
TEXT = 512
bf16 = jnp.bfloat16
f32 = jnp.float32
LIMIT = 10900.0
VMEM_CAP = 62 * 2**20
STEPS = 4


def lane_gather(table, index):
    numbers = lax.GatherDimensionNumbers(
        offset_dims=(),
        collapsed_slice_dims=(1,),
        start_index_map=(1,),
        operand_batching_dims=(0,),
        start_indices_batching_dims=(0,),
    )
    return lax.gather(
        table, index[..., None], numbers, (1, 1), mode=lax.GatherScatterMode.PROMISE_IN_BOUNDS
    )


def nt(left, right):
    return lax.dot_general(left, right, (((1,), (1,)), ((), ())), preferred_element_type=f32)


def nn(left, right):
    return jnp.dot(left, right, preferred_element_type=f32)


def tn(left, right):
    return lax.dot_general(left, right, (((0,), (0,)), ((), ())), preferred_element_type=f32)


def lane_half(shape):
    return lax.broadcasted_iota(jnp.int32, shape, len(shape) - 1) < HEAD


def unpack_pair(packed):
    low = (packed << 16) >> 16
    high = (packed - low) >> 16
    return high.astype(f32), low.astype(f32)


def fill_tables(src_ref, first, tall, pos_ref, tab, inv, p):
    half = lane_half((64, 128))
    cut = slice(p * 128, (p + 1) * 128)

    def body(step, carry):
        at = pl.ds(pl.multiple_of(step * 64, 64), 64)
        block = src_ref[pl.ds(pl.multiple_of(first + step * 64, 64), 64), cut]
        zero = jnp.zeros_like(block)
        first_head = nt(jnp.where(half, block, zero), pos_ref[:, cut]).astype(bf16).astype(f32)
        second_head = nt(jnp.where(half, zero, block), pos_ref[:, cut]).astype(bf16).astype(f32)
        top0 = jnp.maximum(jnp.max(jnp.abs(first_head), axis=1, keepdims=True), 1e-30)
        top1 = jnp.maximum(jnp.max(jnp.abs(second_head), axis=1, keepdims=True), 1e-30)
        whole0 = jnp.round(first_head * (LIMIT / top0)).astype(jnp.int32)
        whole1 = jnp.round(second_head * (LIMIT / top1)).astype(jnp.int32)
        tab[p, at, :] = whole0 * 65536 + whole1
        inv[2 * p, at, :] = jnp.broadcast_to(top0 * (1.0 / LIMIT), (64, 128))
        inv[2 * p + 1, at, :] = jnp.broadcast_to(top1 * (1.0 / LIMIT), (64, 128))
        return carry

    lax.fori_loop(0, tall // 64, body, 0)


def look_up(tab, index_ref, at, store, *, pairs, cols):
    for c in range(cols // 128):
        total = [None] * pairs
        for r in range(3):
            index = index_ref[r, at, c * 128:(c + 1) * 128]
            for p in range(pairs):
                got = lane_gather(tab[p, at, r * 128:(r + 1) * 128], index)
                total[p] = got if total[p] is None else total[p] + got
        for p in range(pairs):
            store(p, c, total[p])


def prepare_rows(
    k_ref, pq_ref, b_ref, head_ref, rest_ref, bt_ref, far_head, far_rest, inv_ref,
    far_tab, far_inv, *, span, rows, cols, pairs, split,
):
    edge = span - span % 8 - split
    for r in range(3):
        head_ref[r, :, span - span % 128:cols] = jnp.zeros((split, cols - span + span % 128), jnp.int32)
        rest_ref[r, edge:rows - split, :] = jnp.zeros((rows - split - edge, cols), jnp.int32)
        rest_ref[r, :, span - span % 128:cols] = jnp.zeros((rows - split, cols - span + span % 128), jnp.int32)
        head_ref[r, :, 0:span] = b_ref[0, r, 0:split]
        rest_ref[r, 0:span - split, 0:span] = b_ref[0, r, split:span]
    for r in range(3):
        for jb in range(cols // 128):
            high = min(128, rows - jb * 128)
            for ib in range(cols // 128):
                tall = min(128, rows - ib * 128)
                here = slice(jb * 128, (jb + 1) * 128)
                if ib * 128 < split:
                    block = head_ref[r, ib * 128:ib * 128 + tall, here]
                else:
                    block = rest_ref[r, ib * 128 - split:ib * 128 - split + tall, here]
                if tall < 128:
                    block = jnp.concatenate([block, jnp.zeros((128 - tall, 128), jnp.int32)], axis=0)
                bt_ref[r, jb * 128:jb * 128 + high, ib * 128:(ib + 1) * 128] = block.T[:high]
    for p in range(pairs):
        fill_tables(k_ref, 0, rows, pq_ref, far_tab, far_inv, p)

    def far_body(step, carry):
        for turn in range(STEPS):
            at = pl.ds(pl.multiple_of(step * 8 * STEPS + turn * 8, 8), 8)

            def store(p, c, total, at=at):
                if c * 128 < split:
                    far_head[p, at, c * 128:(c + 1) * 128] = total
                else:
                    far_rest[p, at, c * 128 - split:(c + 1) * 128 - split] = total

            look_up(far_tab, bt_ref, at, store, pairs=pairs, cols=cols)
        return carry

    lax.fori_loop(0, rows // (8 * STEPS), far_body, 0)
    for p in range(pairs):
        far_head[p, rows:, :] = jnp.zeros((cols - rows, split), jnp.int32)
        far_rest[p, rows:, :] = jnp.zeros((cols - rows, cols - split), jnp.int32)
    for h in range(2 * pairs):
        inv_ref[h:h + 1, :] = jnp.concatenate(
            [far_inv[h, j * 128:min(rows, (j + 1) * 128), :].T[0:1] for j in range(cols // 128 - 1)]
            + [jnp.concatenate([far_inv[h, cols - 128:rows, :],
                                jnp.zeros((cols - rows, 128), f32)], axis=0).T[0:1]], axis=1)


def forward_rows(
    used_ref, q_ref, k_ref, v_ref, pk_ref, b_ref, far_sum, inv_ref, p_ref, ctx_ref,
    near_tab, near_inv, near_sum, score, *, first, rows, span, cols, pairs, scale,
):
    for p in range(pairs):
        fill_tables(q_ref, first, rows, pk_ref, near_tab, near_inv, p)
    used = used_ref[0]
    place = lax.broadcasted_iota(jnp.int32, (1, cols), 1)
    valid = ((place >= TEXT) & (place < span)) | (place < used)

    def block_body(start, tall):
        def near_body(step, carry):
            for turn in range(STEPS):
                at = pl.ds(pl.multiple_of(start + step * 8 * STEPS + turn * 8, 8), 8)
                out_at = pl.ds(pl.multiple_of(step * 8 * STEPS + turn * 8, 8), 8)

                def store(p, c, total, out_at=out_at):
                    near_sum[p, out_at, c * 128:(c + 1) * 128] = total

                look_up(near_tab, b_ref, at, store, pairs=pairs, cols=cols)
            return carry

        lax.fori_loop(0, tall // (8 * STEPS), near_body, 0)
        at = pl.ds(start, tall)
        for p in range(pairs):
            cut = slice(p * 128, (p + 1) * 128)
            block = q_ref[pl.ds(pl.multiple_of(first + start, 64), tall), cut]
            zero = jnp.zeros_like(block)
            mask = lane_half((tall, 128))
            score[0, 0:tall, :] = nt(jnp.where(mask, block, zero), k_ref[:, cut])
            score[1, 0:tall, :] = nt(jnp.where(mask, zero, block), k_ref[:, cut])
            for c in range(cols // 128):
                turned = far_sum[p, c * 128:(c + 1) * 128, pl.ds(start, 128)].T[0:tall]
                here = slice(c * 128, (c + 1) * 128)
                f0, f1 = unpack_pair(turned)
                n0, n1 = unpack_pair(near_sum[p, 0:tall, here])
                score[0, 0:tall, here] += (
                    f0 * inv_ref[2 * p:2 * p + 1, here] + n0 * near_inv[2 * p, at, :]
                )
                score[1, 0:tall, here] += (
                    f1 * inv_ref[2 * p + 1:2 * p + 2, here] + n1 * near_inv[2 * p + 1, at, :]
                )
            for h in range(2):
                for s in range(tall // 16):
                    raw = score[h, s * 16:(s + 1) * 16, :]
                    logits = jnp.where(valid, raw * scale, -1e30)
                    top = jnp.max(logits, axis=1, keepdims=True)
                    grown = jnp.exp(logits - top)
                    share = grown * (1.0 / jnp.sum(grown, axis=1, keepdims=True))
                    p_ref[2 * p + h, pl.ds(pl.multiple_of(start + s * 16, 16), 16), :] = share.astype(bf16)
            c0 = nn(p_ref[2 * p, at, :], v_ref[:, cut])
            c1 = nn(p_ref[2 * p + 1, at, :], v_ref[:, cut])
            ctx_ref[at, cut] = jnp.where(mask, c0, c1).astype(bf16)

    def outer(step, carry):
        block_body(pl.multiple_of(step * 128, 128), 128)
        return carry

    lax.fori_loop(0, rows // 128, outer, 0)
    if rows % 128:
        block_body(rows - rows % 128, rows % 128)


def project_kernel(x_ref, wq_ref, wk_ref, wv_ref, t_ref, kp_ref, qp_ref, qkv_ref, pk_ref, pq_ref, *, span, cols, width):
    tail = span - span % 128
    qkv_ref[span - span % 16:cols, :] = jnp.zeros((cols - span + span % 16, 3 * width), bf16)
    for n, w_ref in enumerate((wq_ref, wk_ref, wv_ref)):
        cut = slice(n * width, (n + 1) * width)

        def body(step, carry, cut=cut, w_ref=w_ref):
            at = pl.ds(pl.multiple_of(step * 128, 128), 128)
            qkv_ref[at, cut] = nn(x_ref[at, :], w_ref[...]).astype(bf16)
            return carry

        lax.fori_loop(0, span // 128, body, 0)
        if tail < span:
            qkv_ref[tail:span, cut] = nn(x_ref[tail:span, :], w_ref[...]).astype(bf16)
    for r in range(3):
        at = slice(r * REL, (r + 1) * REL)
        pk_ref[at, :] = nn(t_ref[r], kp_ref[...]).astype(bf16)
        pq_ref[at, :] = nn(t_ref[r], qp_ref[...]).astype(bf16)


def project(tokens, query_weight, key_weight, value_weight, tables, key_position, query_position, span):
    width = query_weight.shape[1]
    rows, cols = sizes(span)
    whole = pl.BlockSpec(memory_space=pltpu.VMEM)
    return pl.pallas_call(
        functools.partial(project_kernel, span=span, cols=cols, width=width),
        out_shape=(
            jax.ShapeDtypeStruct((cols, 3 * width), bf16),
            jax.ShapeDtypeStruct((3 * REL, width), bf16),
            jax.ShapeDtypeStruct((3 * REL, width), bf16),
        ),
        in_specs=[whole] * 7,
        out_specs=(whole,) * 3,
        compiler_params=pltpu.CompilerParams(vmem_limit_bytes=VMEM_CAP),
        cost_estimate=pl.CostEstimate(flops=4 * 10**9, bytes_accessed=9 * 10**6, transcendentals=0),
        name="project",
    )(tokens, query_weight, key_weight, value_weight, tables, key_position, query_position)


def pick(half, block, h):
    zero = jnp.zeros_like(block)
    return jnp.where(half, block, zero) if h == 0 else jnp.where(half, zero, block)


def draw_kernel(
    p_ref, up_ref, q_ref, k_ref, v_ref, *refs, first, tall, rows, cols, scale, adds,
):
    extra = refs[:adds]
    d_ref, dt_ref, dq_ref, dk_ref, dv_ref, wide, flat, turned = refs[adds:]
    lanes = turned.shape[2]
    half = lane_half((64, 128))

    def body(step, carry):
        at = pl.ds(pl.multiple_of(step * 64, 64), 64)
        pair = []
        for h in range(2):
            reach = nt(pick(half, up_ref[at, :], h), v_ref[...])
            share = p_ref[h, at, :].astype(f32)
            inner = jnp.sum(reach * share, axis=1, keepdims=True)
            back = share * (reach - inner) * scale
            wide[h, at, :] = back
            flat[h, at, :] = back.astype(bf16)
            pair.append(back.reshape(8, 8, cols))
        d_ref[pl.ds(pl.multiple_of(step * 8, 8), 8), :, :] = jnp.concatenate(pair, axis=1).astype(bf16)
        return carry

    lax.fori_loop(0, tall // 64, body, 0)
    for jb in range(cols // 128):
        high = min(128, rows - jb * 128)
        for ib in range(lanes // 128):
            wide_rows = min(128, tall - ib * 128)
            pair = []
            for h in range(2):
                block = wide[h, ib * 128:ib * 128 + wide_rows, jb * 128:(jb + 1) * 128]
                if wide_rows < 128:
                    block = jnp.concatenate([block, jnp.zeros((128 - wide_rows, 128), f32)], axis=0)
                other = block.T[:high]
                turned[h, jb * 128:jb * 128 + high, ib * 128:(ib + 1) * 128] = other.astype(bf16)
                pair.append(other.reshape(high // 8, 8, 128))
            dt_ref[jb * 16:jb * 16 + high // 8, :, ib * 128:(ib + 1) * 128] = jnp.concatenate(
                pair, axis=1
            ).astype(bf16)
    keys, queries, ups = k_ref[...], q_ref[first:first + lanes, :], up_ref[...]
    cols_half, lanes_half, tall_half = (lane_half((n, 128)) for n in (cols, lanes, tall))
    dq_ref[...] = nn(flat[0], pick(cols_half, keys, 0)) + nn(flat[1], pick(cols_half, keys, 1))
    dk = nn(turned[0], pick(lanes_half, queries, 0)) + nn(turned[1], pick(lanes_half, queries, 1))
    dv = tn(p_ref[0], pick(tall_half, ups, 0)) + tn(p_ref[1], pick(tall_half, ups, 1))
    dv = dv[:rows]
    if adds:
        dk, dv = dk + extra[0][...], dv + extra[1][...]
    dk_ref[...] = dk
    dv_ref[...] = dv.astype(dv_ref.dtype)


def scatter_kernel(*refs, groups, cols):
    *d_refs, b_ref, merge_ref, out_ref = refs
    base = jnp.where(lax.broadcasted_iota(jnp.int32, (16, cols), 0) >= 8, 1.0, 0.0).astype(bf16)
    own = (lax.broadcasted_iota(jnp.int32, (256, 256), 0) % 8) == (
        lax.broadcasted_iota(jnp.int32, (256, 256), 1) % 8
    )
    zero = jnp.asarray(0.0, bf16)
    one = jnp.asarray(1.0, bf16)

    def sieve(g, r, back):
        bucket = b_ref[r, pl.ds(pl.multiple_of(g * 8, 8), 8), :]
        low = (bucket & 31).astype(f32)
        high = (bucket >> 5).astype(f32)
        low = jnp.concatenate([low, low], axis=0).astype(bf16) - base
        high = jnp.concatenate([high, high], axis=0).astype(bf16)
        hot = jnp.concatenate(
            [jnp.where(low == jnp.asarray(2.0 * k, bf16), one, zero) for k in range(16)], axis=0
        )
        sieved = []
        for l in range(4):
            mask = high == jnp.asarray(float(l), bf16)
            for p in range(4):
                sieved.append(jnp.where(mask, back[p * 16:(p + 1) * 16], zero))
        sums = nt(jnp.concatenate(sieved, axis=0), hot)
        return jnp.where(own, sums, 0.0).astype(bf16)

    def body(step, carry):
        got = []
        for g in (2 * step, 2 * step + 1):
            back = jnp.concatenate([d_ref[g] for d_ref in d_refs], axis=1) if len(d_refs) > 1 else d_refs[0][g]
            for r in range(3):
                got.append((g, r, sieve(g, r, back)))
        for g, r, sums in got:
            total = None
            for l in range(4):
                term = nn(sums[l * 64:(l + 1) * 64], merge_ref[l])
                total = term if total is None else total + term
            out_ref[g, :, r * 128:(r + 1) * 128] = total.astype(bf16)
        return carry

    lax.fori_loop(0, groups // 2, body, 0)


def close_kernel(*refs, rows, count):
    *base_refs, pos_ref, side_ref, out_ref, table_ref = refs[count:]
    rows2 = 2 * rows
    half3 = lane_half((rows // 8, 8, 128))
    flat = jnp.concatenate([ref[...] for ref in refs[:count]], axis=0).reshape(rows2, 3 * REL)
    both = nn(flat, pos_ref[...]).reshape(rows // 8, 16, 128)
    mine = jnp.where(half3, both[:, 0:8, :], both[:, 8:16, :]).reshape(rows, 128)
    first = 0
    for base_ref in base_refs:
        here = slice(first, first + base_ref.shape[0])
        out_ref[here, :] = (base_ref[...] + mine[here]).astype(bf16)
        first += base_ref.shape[0]
    side = side_ref[0:rows, :].astype(f32).reshape(rows // 8, 8, 128)
    zero = jnp.zeros_like(side)
    spread = jnp.concatenate([jnp.where(half3, side, zero), jnp.where(half3, zero, side)], axis=1)
    table_ref[...] = tn(flat, spread.reshape(rows2, 128).astype(bf16)).astype(bf16)


def merge_table():
    l = lax.broadcasted_iota(jnp.int32, (4, 256, 128), 0)
    a = lax.broadcasted_iota(jnp.int32, (4, 256, 128), 1) // 8
    c = lax.broadcasted_iota(jnp.int32, (4, 256, 128), 2)
    return (c == l * 32 + a).astype(bf16)


def sizes(span):
    return -(-span // 64) * 64, -(-span // 128) * 128


def forward_scratch(pairs, tall, cols):
    return [
        pltpu.VMEM((pairs, tall, 3 * REL), jnp.int32),
        pltpu.VMEM((2 * pairs, tall, 128), f32),
        pltpu.VMEM((pairs, 128, cols), jnp.int32),
        pltpu.VMEM((2, 128, cols), f32),
    ]


def attention_head(qkv, pos_key, pos_query, buckets, used, scale, split):
    span = buckets.shape[2]
    rows, cols = sizes(span)
    width = pos_key.shape[1]
    pairs = width // 128
    whole = pl.BlockSpec(memory_space=pltpu.VMEM)
    i32 = jnp.int32

    def kernel(
        used_ref, qkv_ref, pk_ref, pq_ref, b_ref, p_ref, ctx_ref, head_ref, rest_ref, bt_ref, far_rest, inv_ref,
        far_tab, far_inv, far_head, *scratch,
    ):
        k_ref = qkv_ref.at[:, width:2 * width]
        prepare_rows(
            k_ref, pq_ref, b_ref, head_ref, rest_ref, bt_ref, far_head, far_rest, inv_ref, far_tab, far_inv,
            span=span, rows=rows, cols=cols, pairs=pairs, split=split,
        )
        forward_rows(
            used_ref, qkv_ref.at[:, 0:width], k_ref, qkv_ref.at[:, 2 * width:3 * width], pk_ref, head_ref,
            far_head, inv_ref, p_ref, ctx_ref, *scratch,
            first=0, rows=split, span=span, cols=cols, pairs=pairs, scale=scale,
        )

    return pl.pallas_call(
        kernel,
        out_shape=(
            jax.ShapeDtypeStruct((2 * pairs, split, cols), bf16),
            jax.ShapeDtypeStruct((split, width), bf16),
            jax.ShapeDtypeStruct((3, split, cols), i32),
            jax.ShapeDtypeStruct((3, rows - split, cols), i32),
            jax.ShapeDtypeStruct((3, rows, cols), i32),
            jax.ShapeDtypeStruct((pairs, cols, cols - split), i32),
            jax.ShapeDtypeStruct((2 * pairs, cols), f32),
        ),
        in_specs=[pl.BlockSpec(memory_space=pltpu.SMEM)] + [whole] * 4,
        out_specs=(whole,) * 7,
        scratch_shapes=[
            pltpu.VMEM((pairs, rows, 3 * REL), i32),
            pltpu.VMEM((2 * pairs, rows, 128), f32),
            pltpu.VMEM((pairs, cols, split), i32),
        ] + forward_scratch(pairs, split, cols),
        compiler_params=pltpu.CompilerParams(vmem_limit_bytes=VMEM_CAP),
        cost_estimate=pl.CostEstimate(flops=4 * 10**10, bytes_accessed=25000000, transcendentals=0),
        name="attention_head",
    )(used, qkv, pos_key, pos_query, buckets)


def attention_rest(qkv, pos_key, bucket_rest, far_rest, inverse, used, scale, split, span):
    rows, cols = sizes(span)
    width = pos_key.shape[1]
    pairs = width // 128
    whole = pl.BlockSpec(memory_space=pltpu.VMEM)

    def kernel(used_ref, qkv_ref, pk_ref, b_ref, far_ref, inv_ref, p_ref, ctx_ref, *scratch):
        forward_rows(
            used_ref, qkv_ref.at[:, 0:width], qkv_ref.at[:, width:2 * width], qkv_ref.at[:, 2 * width:3 * width],
            pk_ref, b_ref, far_ref, inv_ref, p_ref, ctx_ref, *scratch,
            first=split, rows=rows - split, span=span, cols=cols, pairs=pairs, scale=scale,
        )

    return pl.pallas_call(
        kernel,
        out_shape=(
            jax.ShapeDtypeStruct((2 * pairs, rows - split, cols), bf16),
            jax.ShapeDtypeStruct((rows - split, width), bf16),
        ),
        in_specs=[pl.BlockSpec(memory_space=pltpu.SMEM)] + [whole] * 5,
        out_specs=(whole,) * 2,
        scratch_shapes=forward_scratch(pairs, rows - split, cols),
        compiler_params=pltpu.CompilerParams(vmem_limit_bytes=VMEM_CAP),
        cost_estimate=pl.CostEstimate(flops=2 * 10**10, bytes_accessed=12000000, transcendentals=0),
        name="attention_rest",
    )(used, qkv, pos_key, bucket_rest, far_rest, inverse)


def attention_draw(share, upstream, qkv, scale, first, rows, adds=()):
    heads, tall, cols = share.shape
    width = upstream.shape[1]
    pairs = heads // 2
    lanes = -(-tall // 128) * 128

    def column(n):
        return pl.BlockSpec((n, 128), lambda p: (0, p))

    return pl.pallas_call(
        functools.partial(draw_kernel, first=first, tall=tall, rows=rows, cols=cols, scale=scale, adds=len(adds)),
        grid=(pairs,),
        in_specs=[
            pl.BlockSpec((2, tall, cols), lambda p: (p, 0, 0)),
            column(tall),
            pl.BlockSpec((cols, 128), lambda p: (0, p)),
            pl.BlockSpec((cols, 128), lambda p: (0, p + pairs)),
            pl.BlockSpec((cols, 128), lambda p: (0, p + 2 * pairs)),
        ] + [column(rows)] * len(adds),
        out_specs=(
            pl.BlockSpec((tall // 8, 16, cols), lambda p: (0, p, 0)),
            pl.BlockSpec((rows // 8, 16, lanes), lambda p: (0, p, 0)),
            column(tall), column(rows), column(rows),
        ),
        out_shape=(
            jax.ShapeDtypeStruct((tall // 8, 8 * heads, cols), bf16),
            jax.ShapeDtypeStruct((rows // 8, 8 * heads, lanes), bf16),
            jax.ShapeDtypeStruct((tall, width), f32),
            jax.ShapeDtypeStruct((rows, width), f32),
            jax.ShapeDtypeStruct((rows, width), bf16 if adds else f32),
        ),
        scratch_shapes=[
            pltpu.VMEM((2, tall, cols), f32),
            pltpu.VMEM((2, tall, cols), bf16),
            pltpu.VMEM((2, rows, lanes), bf16),
        ],
        compiler_params=pltpu.CompilerParams(vmem_limit_bytes=VMEM_CAP),
        cost_estimate=pl.CostEstimate(flops=10**6, bytes_accessed=10**4, transcendentals=0),
        name="attention_draw",
    )(share, upstream, qkv, qkv, qkv, *adds)


def attention_scatter(backs, buckets, merge, first, count):
    high = backs[0].shape[1]
    cols = buckets.shape[2]
    return pl.pallas_call(
        functools.partial(scatter_kernel, groups=8, cols=cols),
        grid=(count,),
        out_shape=jax.ShapeDtypeStruct((8 * count, high, 3 * REL), bf16),
        in_specs=[pl.BlockSpec((8, high, b.shape[2]), lambda g: (first + g, 0, 0)) for b in backs] + [
            pl.BlockSpec((3, 64, cols), lambda g: (0, first + g, 0)),
            pl.BlockSpec(merge.shape, lambda g: (0, 0, 0)),
        ],
        out_specs=pl.BlockSpec((8, high, 3 * REL), lambda g: (g, 0, 0)),
        compiler_params=pltpu.CompilerParams(vmem_limit_bytes=VMEM_CAP),
        cost_estimate=pl.CostEstimate(flops=10**6, bytes_accessed=10**4, transcendentals=0),
        name="attention_scatter",
    )(*backs, buckets, merge)


def attention_close(sums, bases, pos, qkv, side):
    rows, width = sum(base.shape[0] for base in bases), bases[0].shape[1]
    pairs = width // 128
    return pl.pallas_call(
        functools.partial(close_kernel, rows=rows, count=len(sums)),
        grid=(pairs,),
        in_specs=[pl.BlockSpec((part.shape[0], 16, 3 * REL), lambda p: (0, p, 0)) for part in sums] + [
            pl.BlockSpec((base.shape[0], 128), lambda p: (0, p)) for base in bases
        ] + [
            pl.BlockSpec((3 * REL, 128), lambda p: (0, p)),
            pl.BlockSpec((qkv.shape[0], 128), lambda p: (0, p + side * pairs)),
        ],
        out_specs=(
            pl.BlockSpec((rows, 128), lambda p: (0, p)),
            pl.BlockSpec((3 * REL, 128), lambda p: (0, p)),
        ),
        out_shape=(
            jax.ShapeDtypeStruct((rows, width), bf16),
            jax.ShapeDtypeStruct((3 * REL, width), bf16),
        ),
        compiler_params=pltpu.CompilerParams(vmem_limit_bytes=VMEM_CAP),
        cost_estimate=pl.CostEstimate(flops=10**6, bytes_accessed=10**4, transcendentals=0),
        name="attention_close",
    )(*sums, *bases, pos, qkv)


def fill_turned(x_ref, turned, rows):
    depth = x_ref.shape[1]
    for a in range(0, rows, 128):
        tall = min(128, rows - a)
        for b in range(0, depth, 128):
            block = x_ref[a:a + tall, b:b + 128]
            if tall < 128:
                block = jnp.concatenate([block, jnp.zeros((128 - tall, 128), block.dtype)], axis=0)
            turned[b:b + 128, a:a + tall] = block.T[:, :tall]


def each_block(pick_ref, blocks, keeps, bit, slot):
    if not keeps:
        return [(0, d, d) for d in range(blocks)]
    shift = bit - 1
    listed = []
    for out in range(2):
        value = pick_ref[slot] if out == 1 else 1 - pick_ref[slot]
        for e in range(blocks // 2):
            low = e & ((1 << shift) - 1)
            listed.append((out, e, ((e >> shift) << (shift + 1)) + low + value * (1 << shift)))
    return listed


def weight_kernel(pick_ref, *refs, count, blocks, deep, keeps, bit):
    xs, ys, rest = refs[:count], refs[count:2 * count], refs[2 * count:]
    add_ref = rest[0] if keeps else None
    outs = rest[1:3] if keeps else rest[0:1]
    turned = rest[-count:]

    @pl.when(pl.program_id(0) == 0)
    def _():
        for x_ref, wide in zip(xs, turned):
            fill_turned(x_ref, wide, x_ref.shape[0])

    for out, place, d in each_block(pick_ref, blocks, keeps, bit, 1):
        at = pl.ds(pl.multiple_of((2 * d + pick_ref[0]) * deep, deep), deep)
        part = add_ref[d] if keeps else None
        for wide, y_ref in zip(turned, ys):
            term = nn(wide[at, :], y_ref[...])
            part = term if part is None else part + term
        outs[out][place] = part


def weight_half(pick, xs, ys, add=None, *, parts, bits, tile=512):
    depth = xs[0].shape[1]
    wide = ys[0].shape[1]
    deep = depth // parts
    blocks = parts // 2
    keeps = add is not None

    def tiled(n):
        return pl.BlockSpec((n, deep, tile), lambda c: (0, 0, c))

    ins = [pl.BlockSpec(memory_space=pltpu.SMEM)]
    ins += [pl.BlockSpec(x.shape, lambda c: (0, 0)) for x in xs]
    ins += [pl.BlockSpec((y.shape[0], tile), lambda c: (0, c)) for y in ys]
    args = [pick, *xs, *ys]
    shape = (jax.ShapeDtypeStruct((blocks, deep, wide), f32),)
    specs = (tiled(blocks),)
    if keeps:
        ins.append(tiled(blocks))
        args += add
        shape = (jax.ShapeDtypeStruct((blocks // 2, deep, wide), f32),) * 2
        specs = (tiled(blocks // 2),) * 2
    rows = sum(x.shape[0] for x in xs)
    return pl.pallas_call(
        functools.partial(weight_kernel, count=len(xs), blocks=blocks, deep=deep, keeps=keeps, bit=bits[0]),
        grid=(wide // tile,),
        in_specs=ins,
        out_specs=specs,
        out_shape=shape,
        scratch_shapes=[pltpu.VMEM((depth, x.shape[0]), bf16) for x in xs],
        compiler_params=pltpu.CompilerParams(vmem_limit_bytes=VMEM_CAP),
        cost_estimate=pl.CostEstimate(
            flops=rows * depth * wide, bytes_accessed=4 * depth * wide, transcendentals=0
        ),
        name="weight_half",
    )(*args)


def many_kernel(pick_ref, *refs, plan, widths, turns, blocks, deep, keeps, bits):
    n_in = 2 * len(plan)
    ins = refs[:n_in]
    n_out = len(widths)
    adds = refs[n_in:n_in + n_out] if keeps else None
    outs = refs[n_in + n_out:n_in + 3 * n_out] if keeps else refs[n_in:n_in + n_out]
    scratch = refs[len(refs) - sum(turns):]
    left = []
    used = 0
    for n, turn in enumerate(turns):
        if turn:
            fill_turned(ins[2 * n], scratch[used], ins[2 * n].shape[0])
            left.append(scratch[used])
            used += 1
        else:
            left.append(ins[2 * n])
    right = [ins[2 * n + 1][...] for n in range(len(plan))]
    for group in range(n_out):
        for out, place, d in each_block(pick_ref, blocks, keeps, bits[group], 1 + group):
            at = pl.ds(pl.multiple_of((2 * d + pick_ref[0]) * deep, deep), deep)
            target = outs[2 * group + out] if keeps else outs[group]
            for n, (kind, own, start, wide) in enumerate(plan):
                if own != group:
                    continue
                rows = left[n][at, :]
                if kind == "copy":
                    part = rows
                elif kind == "nt":
                    part = nt(rows, right[n])
                else:
                    part = nn(rows, right[n])
                cut = slice(start, start + wide)
                if keeps:
                    part = part + adds[group][d, :, cut]
                target[place, :, cut] = part


def many_half(pick, pairs, plan, widths, add=None, *, parts, bits):
    whole = pl.BlockSpec(memory_space=pltpu.VMEM)
    turns = [kind in ("turn", "copy") for kind, *_ in plan]
    depth = max(left.shape[1 if turn else 0] for (left, _), turn in zip(pairs, turns))
    deep = depth // parts
    blocks = parts // 2
    keeps = add is not None
    args = [pick] + [operand for pair in pairs for operand in pair] + (list(add) if keeps else [])
    if keeps:
        shape = [jax.ShapeDtypeStruct((blocks // 2, deep, w), f32) for w in widths for _ in range(2)]
    else:
        shape = [jax.ShapeDtypeStruct((blocks, deep, w), f32) for w in widths]
    return pl.pallas_call(
        functools.partial(
            many_kernel, plan=plan, widths=widths, turns=turns, blocks=blocks, deep=deep,
            keeps=keeps, bits=[b[0] for b in bits],
        ),
        in_specs=[pl.BlockSpec(memory_space=pltpu.SMEM)] + [whole] * (len(args) - 1),
        out_specs=[whole] * len(shape),
        out_shape=shape,
        scratch_shapes=[
            pltpu.VMEM((left.shape[1], left.shape[0]), left.dtype)
            for (left, _), turn in zip(pairs, turns) if turn
        ],
        compiler_params=pltpu.CompilerParams(vmem_limit_bytes=VMEM_CAP),
        cost_estimate=pl.CostEstimate(flops=10**6, bytes_accessed=10**4, transcendentals=0),
        name="many_half",
    )(*args)


def flipped(value, bit, size):
    return lax.ppermute(value, "dp", [(i, i ^ (1 << bit)) for i in range(size)])


def bit_of(index, bit):
    return (index >> bit) & 1


class Halving:
    def __init__(self, make, index, size, orders):
        self.make, self.index, self.size, self.orders = make, index, size, orders
        mine = bit_of(index, 0).astype(jnp.int32)
        self.pick = jnp.stack([mine] + [bit_of(index, bits[0]).astype(jnp.int32) for bits in orders])
        self.other = self.pick.at[0].set(1 - mine)
        self.stage = 0
        self.extra = None

    def work(self):
        if self.stage == 0:
            self.pending = [(sent, None) for sent in self.make(self.other, None)]
        elif self.stage == 1:
            outs = self.make(self.pick, self.extra)
            self.pending = [(outs[2 * g], outs[2 * g + 1]) for g in range(len(self.orders))]
            self.axes = [
                [b for b in range(self.size.bit_length() - 1, 0, -1) if b != bits[0] and b < self.size.bit_length() - 1]
                for bits in self.orders
            ]
        else:
            self.pending = [
                self.split(g, held, extra) for g, (held, extra) in enumerate(zip(self.held, self.extra))
            ]
        return [part for pair in self.pending for part in pair if part is not None]

    def split(self, g, held, extra):
        bits = self.orders[g]
        if self.stage > len(bits):
            return held + extra, None
        bit = bits[self.stage - 1]
        axis = self.axes[g].index(bit)
        shape = (2,) * len(self.axes[g]) + held.shape[-2:]
        self.axes[g].remove(bit)
        own = bit_of(self.index, bit)
        held, extra = held.reshape(shape), extra.reshape(shape)

        def half(value, at):
            return lax.dynamic_index_in_dim(value, at, axis, keepdims=False)

        return half(held, 1 - own) + half(extra, 1 - own), half(held, own) + half(extra, own)

    def go(self, parts):
        parts = list(parts)
        pairs = [
            tuple(None if part is None else parts.pop(0) for part in pair) for pair in self.pending
        ]
        self.held = [home for _, home in pairs]
        last = self.stage > len(self.orders[0])
        if last:
            self.result = [away for away, _ in pairs]
        else:
            bit = lambda g: 0 if self.stage == 0 else self.orders[g][self.stage - 1]
            self.extra = [flipped(away, bit(g), self.size) for g, (away, _) in enumerate(pairs)]
        self.stage += 1

    def step(self):
        self.go(self.work())

    def over(self):
        return self.stage > len(self.orders[0]) + 1

    def finish(self):
        while not self.over():
            self.step()
        return self.result


def tie(values, *chains):
    chains = [chain for chain in chains if not chain.over()]
    values, extras = lax.optimization_barrier((values, [chain.extra for chain in chains]))
    for chain, extra in zip(chains, extras):
        chain.extra = extra
    works = [chain.work() for chain in chains]
    values, works = lax.optimization_barrier((values, works))
    for chain, parts in zip(chains, works):
        chain.go(parts)
    return values


def swap(value):
    return lax.ppermute(value.astype(f32), "mp", [(0, 1), (1, 0)])


def attend_kernel(
    t_ref, c_ref, o_ref, w_ref, ow_ref, gain_ref, shift_ref, first_ref, low_ref, normal_ref, inverse_ref,
):
    weight = ow_ref[...].astype(bf16)

    def body(step, carry):
        at = pl.ds(pl.multiple_of(step * 64, 64), 64)
        summed = t_ref[at, :].astype(f32) + nn(c_ref[at, :], w_ref[...])
        summed = summed + nn(o_ref[at, :].astype(bf16), weight)
        first, normal, inverse = norm_forward(summed, gain_ref[...], shift_ref[...])
        first_ref[at, :] = first
        low_ref[at, :] = first.astype(bf16)
        normal_ref[at, :] = normal
        inverse_ref[at, :] = inverse
        return carry

    lax.fori_loop(0, t_ref.shape[0] // 64, body, 0)


def attend(tokens, context, other, weight, other_weight, gain, shift):
    tall, depth = tokens.shape
    whole = pl.BlockSpec(memory_space=pltpu.VMEM)
    return pl.pallas_call(
        attend_kernel,
        in_specs=[whole] * 7,
        out_specs=(whole,) * 4,
        out_shape=(
            jax.ShapeDtypeStruct((tall, depth), f32),
            jax.ShapeDtypeStruct((tall, depth), bf16),
            jax.ShapeDtypeStruct((tall, depth), f32),
            jax.ShapeDtypeStruct((tall, 1), f32),
        ),
        compiler_params=pltpu.CompilerParams(vmem_limit_bytes=VMEM_CAP),
        cost_estimate=pl.CostEstimate(flops=2 * 10**9, bytes_accessed=8 * 10**6, transcendentals=0),
        name="attend",
    )(tokens, context, other, weight, other_weight, gain[None], shift[None])


def norm_forward(summed, gain, shift):
    centred = summed - jnp.mean(summed, axis=1, keepdims=True)
    inverse = lax.rsqrt(jnp.mean(centred * centred, axis=1, keepdims=True) + epsilon)
    normal = centred * inverse
    return (normal * gain + shift, normal, inverse)


def norm_backward(upstream, normal, inverse, gain):
    scaled = upstream * gain
    inner = jnp.mean(scaled, axis=1, keepdims=True)
    aligned = jnp.mean(scaled * normal, axis=1, keepdims=True)
    return (
        inverse * (scaled - inner - normal * aligned),
        jnp.sum(upstream * normal, axis=0),
        jnp.sum(upstream, axis=0),
    )


def shards(
    tokens,
    query_weight,
    key_weight,
    value_weight,
    output_weight,
    query_position,
    key_position,
    position_tables,
    gain_one,
    shift_one,
    up_weight,
    down_weight,
    gain_two,
    shift_two,
    buckets,
    text_length,
    cotangent,
):
    span = buckets.shape[2]
    rows, cols = sizes(span)
    size = lax.axis_size("dp")
    index = lax.axis_index("dp")
    bits = list(range(1, size.bit_length() - 1))
    low_first, high_first = bits, bits[1:2] + bits[:1] + bits[2:]
    score_scale = (7.0 * HEAD) ** (-0.5)
    tables_flat = position_tables.reshape(3 * REL, D)
    width = query_weight.shape[1]
    spare = ((0, rows - span), (0, 0))

    def chain(make, *orders):
        return Halving(make, index, size, list(orders))

    split = rows // 2 // 128 * 128
    other_output = swap(output_weight)
    qkv, pos_key, pos_query = project(
        tokens, query_weight, key_weight, value_weight, position_tables, key_position, query_position, span
    )
    tokens = jnp.pad(tokens, spare)
    cotangent = jnp.pad(cotangent, spare)
    tokens_turned, tables_turned = tokens.T, tables_flat.T
    edges = [(0, split), (split, rows)]

    share_head, context_head, bucket_head, bucket_rest, bucket_cols, far_rest, far_inverse = attention_head(
        qkv, pos_key, pos_query, buckets, text_length, score_scale, split
    )
    other_head = swap(context_head)
    far_rest, other_output = lax.optimization_barrier((far_rest, other_output))
    share_rest, context_rest = attention_rest(
        qkv, pos_key, bucket_rest, far_rest, far_inverse, text_length, score_scale, split, span
    )
    other_rest = swap(context_rest)
    shares = [share_head, share_rest]
    contexts = [context_head, context_rest]
    contexts_other = [other_head, other_rest]

    def gelu(value):
        return jax.nn.gelu(value, approximate=False)

    firsts, firsts_low, normals_one, inverses_one, upwards, hiddens, feeds, feeds_other = ([] for _ in range(8))
    for (low, high), context, other in zip(edges, contexts, contexts_other):
        first, first_low, normal_one, inverse_one = attend(
            tokens[low:high], context, other, output_weight, other_output, gain_one, shift_one
        )
        firsts.append(first)
        normals_one.append(normal_one)
        inverses_one.append(inverse_one)
        firsts_low.append(first_low)
        upwards.append(nn(firsts_low[-1], up_weight))
        hiddens.append(gelu(upwards[-1]).astype(bf16))
        feeds.append(nn(hiddens[-1], down_weight))
        feeds_other.append(swap(feeds[-1]))

    finals, seconds_back, seconds_low, upwards_back, backs_part, backs_other, two_sums = ([] for _ in range(7))
    for n, (low, high) in enumerate(edges):
        final, normal_two, inverse_two = norm_forward(
            firsts[n] + feeds[n] + feeds_other[n], gain_two, shift_two
        )
        finals.append(final.astype(bf16))
        second_back, *sums = norm_backward(
            cotangent[low:high].astype(f32), normal_two, inverse_two, gain_two
        )
        two_sums.append(sums)
        seconds_back.append(second_back)
        seconds_low.append(second_back.astype(bf16))
        hidden_back = nt(seconds_low[n], down_weight)
        upwards_back.append(jax.vjp(gelu, upwards[n])[1](hidden_back)[0].astype(bf16))
        backs_part.append(nt(upwards_back[n], up_weight))
        backs_other.append(swap(backs_part[n]))
    layer_output = jnp.concatenate(finals, axis=0)[:span]
    gain_two_grad, shift_two_grad = (two_sums[0][n] + two_sums[1][n] for n in range(2))

    backs_part, down_pair, up_pair = lax.optimization_barrier(
        (backs_part, (seconds_low, hiddens), (firsts_low, upwards_back))
    )
    up_pair, backs_other[0] = lax.optimization_barrier((up_pair, backs_other[0]))
    down_chain = chain(
        lambda pick, add: weight_half(pick, *down_pair, add, parts=size, bits=high_first), high_first
    )
    up_chain = chain(
        lambda pick, add: weight_half(pick, *up_pair, add, parts=size, bits=low_first), low_first
    )
    down_chain.step()
    up_chain.step()
    backs_other[0] = tie(backs_other[0], down_chain)
    backs_other[0] = tie(backs_other[0], up_chain)
    merge = merge_table()
    residuals_back, residuals_low, one_sums = [], [], []

    def draw(n, adds=()):
        residual_back, *sums = norm_backward(
            seconds_back[n] + backs_part[n] + backs_other[n], normals_one[n], inverses_one[n], gain_one
        )
        one_sums.append(sums)
        residuals_back.append(residual_back)
        residuals_low.append(residual_back.astype(bf16))
        context_back = nt(residuals_low[n], output_weight).astype(bf16)
        return attention_draw(shares[n], context_back, qkv, score_scale, edges[n][0], rows, adds)

    back_head, turned_head, query_head, key_head, value_head = draw(0)
    back_head, key_head, backs_other[1] = lax.optimization_barrier((back_head, key_head, backs_other[1]))
    back_rest, turned_rest, query_rest, key_base, value_back = draw(1, (key_head, value_head))
    gain_one_grad, shift_one_grad = (one_sums[0][n] + one_sums[1][n] for n in range(2))
    back_rest, value_back = tie((back_rest, value_back), down_chain)
    residual_low = jnp.concatenate(residuals_low, axis=0)
    context = jnp.concatenate(contexts, axis=0)
    nothing = jnp.zeros_like(gain_one)
    gains = jnp.stack(
        [gain_one_grad, shift_one_grad, gain_two_grad, shift_two_grad] + [nothing] * 4
    )
    gains = jnp.concatenate([gains, jnp.zeros((120, gains.shape[1]), f32)], axis=0)
    dummy = jnp.zeros((8, 128), bf16)
    outer_chain = chain(
        lambda pick, add: many_half(
            pick,
            [(residual_low, context), (tokens_turned, value_back), (gains, dummy)],
            [("turn", 0, 0, width), ("nn", 0, width, width), ("copy", 0, 2 * width, 128)],
            [2 * width + 128],
            add, parts=size, bits=[low_first],
        ),
        low_first,
    )
    outer_chain.step()

    def tail(rows_back, sums, position, orders):
        return chain(
            lambda pick, add: many_half(
                pick,
                [(tokens_turned, rows_back), (tables_turned, sums), (position, sums)],
                [("nn", 0, 0, width), ("nn", 1, 0, width), ("nt", 0, width, 3 * REL)],
                [width + 3 * REL, width],
                add, parts=size, bits=orders,
            ),
            *orders,
        )

    near = []
    blocks = rows // 64
    near.append(attention_scatter([back_head], bucket_head, merge, 0, split // 64))
    back_rest, near = tie((back_rest, near), up_chain)
    back_rest, near = tie((back_rest, near), down_chain)
    back_rest, near = tie((back_rest, near), outer_chain)
    near.append(attention_scatter([back_rest], bucket_rest, merge, 0, blocks - split // 64))
    near, backs = tie((near, [turned_head, turned_rest]), up_chain)
    query_low, key_table_sum = attention_close(near, [query_head, query_rest], pos_key, qkv, 0)
    early = nt(query_low, query_weight) + nt(value_back, value_weight)
    near_chain = tail(query_low, key_table_sum, key_position, [high_first, low_first])
    backs, key_table_sum = tie((backs, key_table_sum), near_chain, outer_chain, down_chain)
    far = []
    cuts = [n * blocks // 3 for n in range(4)]
    for part, chains in enumerate(((near_chain,), (outer_chain, up_chain), (near_chain, outer_chain))):
        far.append(attention_scatter(backs, bucket_cols, merge, cuts[part], cuts[part + 1] - cuts[part]))
        backs, far = tie((backs, far), *chains)
    key_low, query_table_sum = attention_close(far, [key_base], pos_query, qkv, 1)
    key_low, query_table_sum = tie((key_low, query_table_sum), near_chain)
    far_chain = tail(key_low, query_table_sum, query_position, [low_first, high_first])
    parts, others = [], []
    for low, high in ((0, rows // 2), (rows // 2, rows)):
        parts.append(early[low:high] + nt(key_low[low:high], key_weight))
        others.append(swap(parts[-1]))
    far_chain.step()
    far_chain.step()
    far_chain.extra, others[0] = lax.optimization_barrier((far_chain.extra, others[0]))
    far_chain.extra = tie(far_chain.extra, near_chain)
    far_main, query_position_grad = far_chain.finish()
    far_main, others[1] = lax.optimization_barrier((far_main, others[1]))
    input_gradient = (
        jnp.concatenate(residuals_back, axis=0) + jnp.concatenate(parts, axis=0) + jnp.concatenate(others, axis=0)
    )[:span].astype(bf16)
    (down_share,) = down_chain.finish()
    (up_share,) = up_chain.finish()
    (outer_share,) = outer_chain.finish()
    near_main, key_position_grad = near_chain.finish()

    table_rows = near_main[:, width:] + far_main[:, width:]
    table_rows = table_rows.reshape(2, table_rows.shape[0] // 2, 3 * REL)
    side = lax.axis_index("mp")
    table_mine = lax.dynamic_index_in_dim(table_rows, side, 0, keepdims=False) + lax.ppermute(
        lax.dynamic_index_in_dim(table_rows, 1 - side, 0, keepdims=False), "mp", [(0, 1), (1, 0)]
    )
    table_gradient = table_mine.T.reshape(3, REL, table_mine.shape[0])
    gains_mine = outer_share[:, 2 * width:]
    return (
        layer_output,
        input_gradient,
        near_main[:, 0:width],
        far_main[:, 0:width],
        outer_share[:, width:2 * width],
        outer_share[:, 0:width].T,
        query_position_grad,
        key_position_grad,
        table_gradient,
        gains_mine[:, 0],
        gains_mine[:, 1],
        up_share,
        down_share.T,
        gains_mine[:, 2],
        gains_mine[:, 3],
    )


def solution(mesh):
    return jax.shard_map(
        shards,
        mesh=mesh,
        in_specs=(
            P("dp", None),
            P(None, "mp"),
            P(None, "mp"),
            P(None, "mp"),
            P("mp", None),
            P(None, "mp"),
            P(None, "mp"),
            P(),
            P(),
            P(),
            P(None, "mp"),
            P("mp", None),
            P(),
            P(),
            P("dp", None, None, None),
            P("dp"),
            P("dp", None),
        ),
        out_specs=(
            P("dp", None),
            P("dp", None),
            P("dp", "mp"),
            P("dp", "mp"),
            P("dp", "mp"),
            P("mp", "dp"),
            P("dp", "mp"),
            P("dp", "mp"),
            P(None, None, ("dp", "mp")),
            P("dp"),
            P("dp"),
            P("dp", "mp"),
            P("mp", "dp"),
            P("dp"),
            P("dp"),
        ),
        check_vma=False,
    )
```

```python
import functools

import jax
import jax.numpy as jnp
from jax import lax
from jax.experimental import pallas as pl
from jax.experimental.pallas import tpu as pltpu
from jax.sharding import PartitionSpec as P

D = 1024
epsilon = 1e-05
HEAD = 64
REL = 128
TEXT = 512
bf16 = jnp.bfloat16
f32 = jnp.float32
LIMIT = 10900.0
VMEM_CAP = 62 * 2**20
STEPS = 4


def lane_gather(table, index):
    numbers = lax.GatherDimensionNumbers(
        offset_dims=(),
        collapsed_slice_dims=(1,),
        start_index_map=(1,),
        operand_batching_dims=(0,),
        start_indices_batching_dims=(0,),
    )
    return lax.gather(
        table, index[..., None], numbers, (1, 1), mode=lax.GatherScatterMode.PROMISE_IN_BOUNDS
    )


def nt(left, right):
    return lax.dot_general(left, right, (((1,), (1,)), ((), ())), preferred_element_type=f32)


def nn(left, right):
    return jnp.dot(left, right, preferred_element_type=f32)


def tn(left, right):
    return lax.dot_general(left, right, (((0,), (0,)), ((), ())), preferred_element_type=f32)


def lane_half(shape):
    return lax.broadcasted_iota(jnp.int32, shape, len(shape) - 1) < HEAD


def unpack_pair(packed):
    low = (packed << 16) >> 16
    high = (packed - low) >> 16
    return high.astype(f32), low.astype(f32)


def fill_tables(src_ref, first, tall, pos_ref, tab, inv, p):
    half = lane_half((64, 128))
    cut = slice(p * 128, (p + 1) * 128)

    def body(step, carry):
        at = pl.ds(pl.multiple_of(step * 64, 64), 64)
        block = src_ref[pl.ds(pl.multiple_of(first + step * 64, 64), 64), cut]
        zero = jnp.zeros_like(block)
        first_head = nt(jnp.where(half, block, zero), pos_ref[:, cut]).astype(bf16).astype(f32)
        second_head = nt(jnp.where(half, zero, block), pos_ref[:, cut]).astype(bf16).astype(f32)
        top0 = jnp.maximum(jnp.max(jnp.abs(first_head), axis=1, keepdims=True), 1e-30)
        top1 = jnp.maximum(jnp.max(jnp.abs(second_head), axis=1, keepdims=True), 1e-30)
        whole0 = jnp.round(first_head * (LIMIT / top0)).astype(jnp.int32)
        whole1 = jnp.round(second_head * (LIMIT / top1)).astype(jnp.int32)
        tab[p, at, :] = whole0 * 65536 + whole1
        inv[2 * p, at, :] = jnp.broadcast_to(top0 * (1.0 / LIMIT), (64, 128))
        inv[2 * p + 1, at, :] = jnp.broadcast_to(top1 * (1.0 / LIMIT), (64, 128))
        return carry

    lax.fori_loop(0, tall // 64, body, 0)


def look_up(tab, index_ref, at, store, *, pairs, cols):
    for c in range(cols // 128):
        total = [None] * pairs
        for r in range(3):
            index = index_ref[r, at, c * 128:(c + 1) * 128]
            for p in range(pairs):
                got = lane_gather(tab[p, at, r * 128:(r + 1) * 128], index)
                total[p] = got if total[p] is None else total[p] + got
        for p in range(pairs):
            store(p, c, total[p])


def prepare_rows(
    k_ref, pq_ref, b_ref, head_ref, rest_ref, bt_ref, far_head, far_rest, inv_ref,
    far_tab, far_inv, *, span, rows, cols, pairs, split,
):
    edge = span - span % 8 - split
    for r in range(3):
        head_ref[r, :, span - span % 128:cols] = jnp.zeros((split, cols - span + span % 128), jnp.int32)
        rest_ref[r, edge:rows - split, :] = jnp.zeros((rows - split - edge, cols), jnp.int32)
        rest_ref[r, :, span - span % 128:cols] = jnp.zeros((rows - split, cols - span + span % 128), jnp.int32)
        head_ref[r, :, 0:span] = b_ref[0, r, 0:split]
        rest_ref[r, 0:span - split, 0:span] = b_ref[0, r, split:span]
    for r in range(3):
        for jb in range(cols // 128):
            high = min(128, rows - jb * 128)
            for ib in range(cols // 128):
                tall = min(128, rows - ib * 128)
                here = slice(jb * 128, (jb + 1) * 128)
                if ib * 128 < split:
                    block = head_ref[r, ib * 128:ib * 128 + tall, here]
                else:
                    block = rest_ref[r, ib * 128 - split:ib * 128 - split + tall, here]
                if tall < 128:
                    block = jnp.concatenate([block, jnp.zeros((128 - tall, 128), jnp.int32)], axis=0)
                bt_ref[r, jb * 128:jb * 128 + high, ib * 128:(ib + 1) * 128] = block.T[:high]
    for p in range(pairs):
        fill_tables(k_ref, 0, rows, pq_ref, far_tab, far_inv, p)

    def far_body(step, carry):
        for turn in range(STEPS):
            at = pl.ds(pl.multiple_of(step * 8 * STEPS + turn * 8, 8), 8)

            def store(p, c, total, at=at):
                if c * 128 < split:
                    far_head[p, at, c * 128:(c + 1) * 128] = total
                else:
                    far_rest[p, at, c * 128 - split:(c + 1) * 128 - split] = total

            look_up(far_tab, bt_ref, at, store, pairs=pairs, cols=cols)
        return carry

    lax.fori_loop(0, rows // (8 * STEPS), far_body, 0)
    for p in range(pairs):
        far_head[p, rows:, :] = jnp.zeros((cols - rows, split), jnp.int32)
        far_rest[p, rows:, :] = jnp.zeros((cols - rows, cols - split), jnp.int32)
    for h in range(2 * pairs):
        inv_ref[h:h + 1, :] = jnp.concatenate(
            [far_inv[h, j * 128:min(rows, (j + 1) * 128), :].T[0:1] for j in range(cols // 128 - 1)]
            + [jnp.concatenate([far_inv[h, cols - 128:rows, :],
                                jnp.zeros((cols - rows, 128), f32)], axis=0).T[0:1]], axis=1)


def forward_rows(
    used_ref, q_ref, k_ref, v_ref, pk_ref, b_ref, far_sum, inv_ref, p_ref, ctx_ref, wide_ref,
    near_tab, near_inv, near_sum, score, *, first, rows, span, cols, pairs, scale,
):
    for p in range(pairs):
        fill_tables(q_ref, first, rows, pk_ref, near_tab, near_inv, p)
    used = used_ref[0]
    place = lax.broadcasted_iota(jnp.int32, (1, cols), 1)
    valid = ((place >= TEXT) & (place < span)) | (place < used)

    def block_body(start, tall):
        def near_body(step, carry):
            for turn in range(STEPS):
                at = pl.ds(pl.multiple_of(start + step * 8 * STEPS + turn * 8, 8), 8)
                out_at = pl.ds(pl.multiple_of(step * 8 * STEPS + turn * 8, 8), 8)

                def store(p, c, total, out_at=out_at):
                    near_sum[p, out_at, c * 128:(c + 1) * 128] = total

                look_up(near_tab, b_ref, at, store, pairs=pairs, cols=cols)
            return carry

        lax.fori_loop(0, tall // (8 * STEPS), near_body, 0)
        at = pl.ds(start, tall)
        for p in range(pairs):
            cut = slice(p * 128, (p + 1) * 128)
            block = q_ref[pl.ds(pl.multiple_of(first + start, 64), tall), cut]
            zero = jnp.zeros_like(block)
            mask = lane_half((tall, 128))
            score[0, 0:tall, :] = nt(jnp.where(mask, block, zero), k_ref[:, cut])
            score[1, 0:tall, :] = nt(jnp.where(mask, zero, block), k_ref[:, cut])
            for c in range(cols // 128):
                turned = far_sum[p, c * 128:(c + 1) * 128, pl.ds(start, 128)].T[0:tall]
                here = slice(c * 128, (c + 1) * 128)
                f0, f1 = unpack_pair(turned)
                n0, n1 = unpack_pair(near_sum[p, 0:tall, here])
                score[0, 0:tall, here] += (
                    f0 * inv_ref[2 * p:2 * p + 1, here] + n0 * near_inv[2 * p, at, :]
                )
                score[1, 0:tall, here] += (
                    f1 * inv_ref[2 * p + 1:2 * p + 2, here] + n1 * near_inv[2 * p + 1, at, :]
                )
            for h in range(2):
                for s in range(tall // 16):
                    raw = score[h, s * 16:(s + 1) * 16, :]
                    logits = jnp.where(valid, raw * scale, -1e30)
                    top = jnp.max(logits, axis=1, keepdims=True)
                    grown = jnp.exp(logits - top)
                    share = grown * (1.0 / jnp.sum(grown, axis=1, keepdims=True))
                    p_ref[2 * p + h, pl.ds(pl.multiple_of(start + s * 16, 16), 16), :] = share.astype(bf16)
            c0 = nn(p_ref[2 * p, at, :], v_ref[:, cut])
            c1 = nn(p_ref[2 * p + 1, at, :], v_ref[:, cut])
            context = jnp.where(mask, c0, c1).astype(bf16)
            ctx_ref[at, cut] = context
            wide_ref[at, cut] = context.astype(f32)

    def outer(step, carry):
        block_body(pl.multiple_of(step * 128, 128), 128)
        return carry

    lax.fori_loop(0, rows // 128, outer, 0)
    if rows % 128:
        block_body(rows - rows % 128, rows % 128)


def project_kernel(x_ref, wq_ref, wk_ref, wv_ref, t_ref, kp_ref, qp_ref, qkv_ref, pk_ref, pq_ref, *, span, cols, width):
    tail = span - span % 128
    qkv_ref[span - span % 16:cols, :] = jnp.zeros((cols - span + span % 16, 3 * width), bf16)
    for n, w_ref in enumerate((wq_ref, wk_ref, wv_ref)):
        cut = slice(n * width, (n + 1) * width)

        def body(step, carry, cut=cut, w_ref=w_ref):
            at = pl.ds(pl.multiple_of(step * 128, 128), 128)
            qkv_ref[at, cut] = nn(x_ref[at, :], w_ref[...]).astype(bf16)
            return carry

        lax.fori_loop(0, span // 128, body, 0)
        if tail < span:
            qkv_ref[tail:span, cut] = nn(x_ref[tail:span, :], w_ref[...]).astype(bf16)
    for r in range(3):
        at = slice(r * REL, (r + 1) * REL)
        pk_ref[at, :] = nn(t_ref[r], kp_ref[...]).astype(bf16)
        pq_ref[at, :] = nn(t_ref[r], qp_ref[...]).astype(bf16)


def project(tokens, query_weight, key_weight, value_weight, tables, key_position, query_position, span):
    width = query_weight.shape[1]
    rows, cols = sizes(span)
    whole = pl.BlockSpec(memory_space=pltpu.VMEM)
    return pl.pallas_call(
        functools.partial(project_kernel, span=span, cols=cols, width=width),
        out_shape=(
            jax.ShapeDtypeStruct((cols, 3 * width), bf16),
            jax.ShapeDtypeStruct((3 * REL, width), bf16),
            jax.ShapeDtypeStruct((3 * REL, width), bf16),
        ),
        in_specs=[whole] * 7,
        out_specs=(whole,) * 3,
        compiler_params=pltpu.CompilerParams(vmem_limit_bytes=VMEM_CAP),
        cost_estimate=pl.CostEstimate(flops=4 * 10**9, bytes_accessed=9 * 10**6, transcendentals=0),
        name="project",
    )(tokens, query_weight, key_weight, value_weight, tables, key_position, query_position)


def pick(half, block, h):
    zero = jnp.zeros_like(block)
    return jnp.where(half, block, zero) if h == 0 else jnp.where(half, zero, block)


def draw_kernel(
    p_ref, up_ref, q_ref, k_ref, v_ref, *refs, first, tall, rows, cols, scale, adds,
):
    extra = refs[:adds]
    d_ref, dt_ref, dq_ref, dk_ref, dv_ref, wide, flat, turned = refs[adds:]
    lanes = turned.shape[2]
    half = lane_half((64, 128))

    def body(step, carry):
        at = pl.ds(pl.multiple_of(step * 64, 64), 64)
        pair = []
        for h in range(2):
            reach = nt(pick(half, up_ref[at, :], h), v_ref[...])
            share = p_ref[h, at, :].astype(f32)
            inner = jnp.sum(reach * share, axis=1, keepdims=True)
            back = share * (reach - inner) * scale
            wide[h, at, :] = back
            flat[h, at, :] = back.astype(bf16)
            pair.append(back.reshape(8, 8, cols))
        d_ref[pl.ds(pl.multiple_of(step * 8, 8), 8), :, :] = jnp.concatenate(pair, axis=1).astype(bf16)
        return carry

    lax.fori_loop(0, tall // 64, body, 0)
    for jb in range(cols // 128):
        high = min(128, rows - jb * 128)
        for ib in range(lanes // 128):
            wide_rows = min(128, tall - ib * 128)
            pair = []
            for h in range(2):
                block = wide[h, ib * 128:ib * 128 + wide_rows, jb * 128:(jb + 1) * 128]
                if wide_rows < 128:
                    block = jnp.concatenate([block, jnp.zeros((128 - wide_rows, 128), f32)], axis=0)
                other = block.T[:high]
                turned[h, jb * 128:jb * 128 + high, ib * 128:(ib + 1) * 128] = other.astype(bf16)
                pair.append(other.reshape(high // 8, 8, 128))
            dt_ref[jb * 16:jb * 16 + high // 8, :, ib * 128:(ib + 1) * 128] = jnp.concatenate(
                pair, axis=1
            ).astype(bf16)
    keys, queries, ups = k_ref[...], q_ref[first:first + lanes, :], up_ref[...]
    cols_half, lanes_half, tall_half = (lane_half((n, 128)) for n in (cols, lanes, tall))
    dq_ref[...] = nn(flat[0], pick(cols_half, keys, 0)) + nn(flat[1], pick(cols_half, keys, 1))
    dk = nn(turned[0], pick(lanes_half, queries, 0)) + nn(turned[1], pick(lanes_half, queries, 1))
    dv = tn(p_ref[0], pick(tall_half, ups, 0)) + tn(p_ref[1], pick(tall_half, ups, 1))
    dv = dv[:rows]
    if adds:
        dk, dv = dk + extra[0][...], dv + extra[1][...]
    dk_ref[...] = dk
    dv_ref[...] = dv.astype(dv_ref.dtype)


def scatter_kernel(*refs, groups, cols):
    *d_refs, b_ref, merge_ref, out_ref = refs
    base = jnp.where(lax.broadcasted_iota(jnp.int32, (16, cols), 0) >= 8, 1.0, 0.0).astype(bf16)
    own = (lax.broadcasted_iota(jnp.int32, (256, 256), 0) % 8) == (
        lax.broadcasted_iota(jnp.int32, (256, 256), 1) % 8
    )
    zero = jnp.asarray(0.0, bf16)
    one = jnp.asarray(1.0, bf16)

    def sieve(g, r, back):
        bucket = b_ref[r, pl.ds(pl.multiple_of(g * 8, 8), 8), :]
        low = (bucket & 31).astype(f32)
        high = (bucket >> 5).astype(f32)
        low = jnp.concatenate([low, low], axis=0).astype(bf16) - base
        high = jnp.concatenate([high, high], axis=0).astype(bf16)
        hot = jnp.concatenate(
            [jnp.where(low == jnp.asarray(2.0 * k, bf16), one, zero) for k in range(16)], axis=0
        )
        sieved = []
        for l in range(4):
            mask = high == jnp.asarray(float(l), bf16)
            for p in range(4):
                sieved.append(jnp.where(mask, back[p * 16:(p + 1) * 16], zero))
        sums = nt(jnp.concatenate(sieved, axis=0), hot)
        return jnp.where(own, sums, 0.0).astype(bf16)

    def body(step, carry):
        got = []
        for g in (2 * step, 2 * step + 1):
            back = jnp.concatenate([d_ref[g] for d_ref in d_refs], axis=1) if len(d_refs) > 1 else d_refs[0][g]
            for r in range(3):
                got.append((g, r, sieve(g, r, back)))
        for g, r, sums in got:
            total = None
            for l in range(4):
                term = nn(sums[l * 64:(l + 1) * 64], merge_ref[l])
                total = term if total is None else total + term
            out_ref[g, :, r * 128:(r + 1) * 128] = total.astype(bf16)
        return carry

    lax.fori_loop(0, groups // 2, body, 0)


def close_kernel(*refs, rows, count):
    *base_refs, pos_ref, side_ref, out_ref, table_ref = refs[count:]
    rows2 = 2 * rows
    half3 = lane_half((rows // 8, 8, 128))
    flat = jnp.concatenate([ref[...] for ref in refs[:count]], axis=0).reshape(rows2, 3 * REL)
    both = nn(flat, pos_ref[...]).reshape(rows // 8, 16, 128)
    mine = jnp.where(half3, both[:, 0:8, :], both[:, 8:16, :]).reshape(rows, 128)
    first = 0
    for base_ref in base_refs:
        here = slice(first, first + base_ref.shape[0])
        out_ref[here, :] = (base_ref[...] + mine[here]).astype(bf16)
        first += base_ref.shape[0]
    side = side_ref[0:rows, :].astype(f32).reshape(rows // 8, 8, 128)
    zero = jnp.zeros_like(side)
    spread = jnp.concatenate([jnp.where(half3, side, zero), jnp.where(half3, zero, side)], axis=1)
    table_ref[...] = tn(flat, spread.reshape(rows2, 128).astype(bf16)).astype(bf16)


def merge_table():
    l = lax.broadcasted_iota(jnp.int32, (4, 256, 128), 0)
    a = lax.broadcasted_iota(jnp.int32, (4, 256, 128), 1) // 8
    c = lax.broadcasted_iota(jnp.int32, (4, 256, 128), 2)
    return (c == l * 32 + a).astype(bf16)


def sizes(span):
    return -(-span // 64) * 64, -(-span // 128) * 128


def forward_scratch(pairs, tall, cols):
    return [
        pltpu.VMEM((pairs, tall, 3 * REL), jnp.int32),
        pltpu.VMEM((2 * pairs, tall, 128), f32),
        pltpu.VMEM((pairs, 128, cols), jnp.int32),
        pltpu.VMEM((2, 128, cols), f32),
    ]


def attention_head(qkv, pos_key, pos_query, buckets, used, scale, split):
    span = buckets.shape[2]
    rows, cols = sizes(span)
    width = pos_key.shape[1]
    pairs = width // 128
    whole = pl.BlockSpec(memory_space=pltpu.VMEM)
    i32 = jnp.int32

    def kernel(
        used_ref, qkv_ref, pk_ref, pq_ref, b_ref, p_ref, ctx_ref, wide_ref, head_ref, rest_ref, bt_ref, far_rest,
        inv_ref, far_tab, far_inv, far_head, *scratch,
    ):
        k_ref = qkv_ref.at[:, width:2 * width]
        prepare_rows(
            k_ref, pq_ref, b_ref, head_ref, rest_ref, bt_ref, far_head, far_rest, inv_ref, far_tab, far_inv,
            span=span, rows=rows, cols=cols, pairs=pairs, split=split,
        )
        forward_rows(
            used_ref, qkv_ref.at[:, 0:width], k_ref, qkv_ref.at[:, 2 * width:3 * width], pk_ref, head_ref,
            far_head, inv_ref, p_ref, ctx_ref, wide_ref, *scratch,
            first=0, rows=split, span=span, cols=cols, pairs=pairs, scale=scale,
        )

    return pl.pallas_call(
        kernel,
        out_shape=(
            jax.ShapeDtypeStruct((2 * pairs, split, cols), bf16),
            jax.ShapeDtypeStruct((split, width), bf16),
            jax.ShapeDtypeStruct((split, width), f32),
            jax.ShapeDtypeStruct((3, split, cols), i32),
            jax.ShapeDtypeStruct((3, rows - split, cols), i32),
            jax.ShapeDtypeStruct((3, rows, cols), i32),
            jax.ShapeDtypeStruct((pairs, cols, cols - split), i32),
            jax.ShapeDtypeStruct((2 * pairs, cols), f32),
        ),
        in_specs=[pl.BlockSpec(memory_space=pltpu.SMEM)] + [whole] * 4,
        out_specs=(whole,) * 8,
        scratch_shapes=[
            pltpu.VMEM((pairs, rows, 3 * REL), i32),
            pltpu.VMEM((2 * pairs, rows, 128), f32),
            pltpu.VMEM((pairs, cols, split), i32),
        ] + forward_scratch(pairs, split, cols),
        compiler_params=pltpu.CompilerParams(vmem_limit_bytes=VMEM_CAP),
        cost_estimate=pl.CostEstimate(flops=4 * 10**10, bytes_accessed=25000000, transcendentals=0),
        name="attention_head",
    )(used, qkv, pos_key, pos_query, buckets)


def attention_rest(qkv, pos_key, bucket_rest, far_rest, inverse, used, scale, split, span):
    rows, cols = sizes(span)
    width = pos_key.shape[1]
    pairs = width // 128
    whole = pl.BlockSpec(memory_space=pltpu.VMEM)

    def kernel(used_ref, qkv_ref, pk_ref, b_ref, far_ref, inv_ref, p_ref, ctx_ref, wide_ref, *scratch):
        forward_rows(
            used_ref, qkv_ref.at[:, 0:width], qkv_ref.at[:, width:2 * width], qkv_ref.at[:, 2 * width:3 * width],
            pk_ref, b_ref, far_ref, inv_ref, p_ref, ctx_ref, wide_ref, *scratch,
            first=split, rows=rows - split, span=span, cols=cols, pairs=pairs, scale=scale,
        )

    return pl.pallas_call(
        kernel,
        out_shape=(
            jax.ShapeDtypeStruct((2 * pairs, rows - split, cols), bf16),
            jax.ShapeDtypeStruct((rows - split, width), bf16),
            jax.ShapeDtypeStruct((rows - split, width), f32),
        ),
        in_specs=[pl.BlockSpec(memory_space=pltpu.SMEM)] + [whole] * 5,
        out_specs=(whole,) * 3,
        scratch_shapes=forward_scratch(pairs, rows - split, cols),
        compiler_params=pltpu.CompilerParams(vmem_limit_bytes=VMEM_CAP),
        cost_estimate=pl.CostEstimate(flops=2 * 10**10, bytes_accessed=12000000, transcendentals=0),
        name="attention_rest",
    )(used, qkv, pos_key, bucket_rest, far_rest, inverse)


def attention_draw(share, upstream, qkv, scale, first, rows, adds=()):
    heads, tall, cols = share.shape
    width = upstream.shape[1]
    pairs = heads // 2
    lanes = -(-tall // 128) * 128

    def column(n):
        return pl.BlockSpec((n, 128), lambda p: (0, p))

    return pl.pallas_call(
        functools.partial(draw_kernel, first=first, tall=tall, rows=rows, cols=cols, scale=scale, adds=len(adds)),
        grid=(pairs,),
        in_specs=[
            pl.BlockSpec((2, tall, cols), lambda p: (p, 0, 0)),
            column(tall),
            pl.BlockSpec((cols, 128), lambda p: (0, p)),
            pl.BlockSpec((cols, 128), lambda p: (0, p + pairs)),
            pl.BlockSpec((cols, 128), lambda p: (0, p + 2 * pairs)),
        ] + [column(rows)] * len(adds),
        out_specs=(
            pl.BlockSpec((tall // 8, 16, cols), lambda p: (0, p, 0)),
            pl.BlockSpec((rows // 8, 16, lanes), lambda p: (0, p, 0)),
            column(tall), column(rows), column(rows),
        ),
        out_shape=(
            jax.ShapeDtypeStruct((tall // 8, 8 * heads, cols), bf16),
            jax.ShapeDtypeStruct((rows // 8, 8 * heads, lanes), bf16),
            jax.ShapeDtypeStruct((tall, width), f32),
            jax.ShapeDtypeStruct((rows, width), f32),
            jax.ShapeDtypeStruct((rows, width), bf16 if adds else f32),
        ),
        scratch_shapes=[
            pltpu.VMEM((2, tall, cols), f32),
            pltpu.VMEM((2, tall, cols), bf16),
            pltpu.VMEM((2, rows, lanes), bf16),
        ],
        compiler_params=pltpu.CompilerParams(vmem_limit_bytes=VMEM_CAP),
        cost_estimate=pl.CostEstimate(flops=10**6, bytes_accessed=10**4, transcendentals=0),
        name="attention_draw",
    )(share, upstream, qkv, qkv, qkv, *adds)


def attention_scatter(backs, buckets, merge, first, count):
    high = backs[0].shape[1]
    cols = buckets.shape[2]
    return pl.pallas_call(
        functools.partial(scatter_kernel, groups=8, cols=cols),
        grid=(count,),
        out_shape=jax.ShapeDtypeStruct((8 * count, high, 3 * REL), bf16),
        in_specs=[pl.BlockSpec((8, high, b.shape[2]), lambda g: (first + g, 0, 0)) for b in backs] + [
            pl.BlockSpec((3, 64, cols), lambda g: (0, first + g, 0)),
            pl.BlockSpec(merge.shape, lambda g: (0, 0, 0)),
        ],
        out_specs=pl.BlockSpec((8, high, 3 * REL), lambda g: (g, 0, 0)),
        compiler_params=pltpu.CompilerParams(vmem_limit_bytes=VMEM_CAP),
        cost_estimate=pl.CostEstimate(flops=10**6, bytes_accessed=10**4, transcendentals=0),
        name="attention_scatter",
    )(*backs, buckets, merge)


def attention_close(sums, bases, pos, qkv, side):
    rows, width = sum(base.shape[0] for base in bases), bases[0].shape[1]
    pairs = width // 128
    return pl.pallas_call(
        functools.partial(close_kernel, rows=rows, count=len(sums)),
        grid=(pairs,),
        in_specs=[pl.BlockSpec((part.shape[0], 16, 3 * REL), lambda p: (0, p, 0)) for part in sums] + [
            pl.BlockSpec((base.shape[0], 128), lambda p: (0, p)) for base in bases
        ] + [
            pl.BlockSpec((3 * REL, 128), lambda p: (0, p)),
            pl.BlockSpec((qkv.shape[0], 128), lambda p: (0, p + side * pairs)),
        ],
        out_specs=(
            pl.BlockSpec((rows, 128), lambda p: (0, p)),
            pl.BlockSpec((3 * REL, 128), lambda p: (0, p)),
        ),
        out_shape=(
            jax.ShapeDtypeStruct((rows, width), bf16),
            jax.ShapeDtypeStruct((3 * REL, width), bf16),
        ),
        compiler_params=pltpu.CompilerParams(vmem_limit_bytes=VMEM_CAP),
        cost_estimate=pl.CostEstimate(flops=10**6, bytes_accessed=10**4, transcendentals=0),
        name="attention_close",
    )(*sums, *bases, pos, qkv)


def fill_turned(x_ref, turned, rows):
    depth = x_ref.shape[1]
    for a in range(0, rows, 128):
        tall = min(128, rows - a)
        for b in range(0, depth, 128):
            block = x_ref[a:a + tall, b:b + 128]
            if tall < 128:
                block = jnp.concatenate([block, jnp.zeros((128 - tall, 128), block.dtype)], axis=0)
            turned[b:b + 128, a:a + tall] = block.T[:, :tall]


def each_block(pick_ref, blocks, keeps, bit, slot):
    if not keeps:
        return [(0, d, d) for d in range(blocks)]
    shift = bit - 1
    listed = []
    for out in range(2):
        value = pick_ref[slot] if out == 1 else 1 - pick_ref[slot]
        for e in range(blocks // 2):
            low = e & ((1 << shift) - 1)
            listed.append((out, e, ((e >> shift) << (shift + 1)) + low + value * (1 << shift)))
    return listed


def weight_kernel(pick_ref, *refs, count, blocks, deep, keeps, bit):
    xs, ys, rest = refs[:count], refs[count:2 * count], refs[2 * count:]
    add_ref = rest[0] if keeps else None
    outs = rest[1:3] if keeps else rest[0:1]
    turned = rest[-count:]

    @pl.when(pl.program_id(0) == 0)
    def _():
        for x_ref, wide in zip(xs, turned):
            fill_turned(x_ref, wide, x_ref.shape[0])

    for out, place, d in each_block(pick_ref, blocks, keeps, bit, 1):
        at = pl.ds(pl.multiple_of((2 * d + pick_ref[0]) * deep, deep), deep)
        part = add_ref[d] if keeps else None
        for wide, y_ref in zip(turned, ys):
            term = nn(wide[at, :], y_ref[...])
            part = term if part is None else part + term
        outs[out][place] = part


def weight_half(pick, xs, ys, add=None, *, parts, bits, tile=512):
    depth = xs[0].shape[1]
    wide = ys[0].shape[1]
    deep = depth // parts
    blocks = parts // 2
    keeps = add is not None

    def tiled(n):
        return pl.BlockSpec((n, deep, tile), lambda c: (0, 0, c))

    ins = [pl.BlockSpec(memory_space=pltpu.SMEM)]
    ins += [pl.BlockSpec(x.shape, lambda c: (0, 0)) for x in xs]
    ins += [pl.BlockSpec((y.shape[0], tile), lambda c: (0, c)) for y in ys]
    args = [pick, *xs, *ys]
    shape = (jax.ShapeDtypeStruct((blocks, deep, wide), f32),)
    specs = (tiled(blocks),)
    if keeps:
        ins.append(tiled(blocks))
        args += add
        shape = (jax.ShapeDtypeStruct((blocks // 2, deep, wide), f32),) * 2
        specs = (tiled(blocks // 2),) * 2
    rows = sum(x.shape[0] for x in xs)
    return pl.pallas_call(
        functools.partial(weight_kernel, count=len(xs), blocks=blocks, deep=deep, keeps=keeps, bit=bits[0]),
        grid=(wide // tile,),
        in_specs=ins,
        out_specs=specs,
        out_shape=shape,
        scratch_shapes=[pltpu.VMEM((depth, x.shape[0]), bf16) for x in xs],
        compiler_params=pltpu.CompilerParams(vmem_limit_bytes=VMEM_CAP),
        cost_estimate=pl.CostEstimate(
            flops=rows * depth * wide, bytes_accessed=4 * depth * wide, transcendentals=0
        ),
        name="weight_half",
    )(*args)


def many_kernel(pick_ref, *refs, plan, widths, turns, blocks, deep, keeps, bits):
    n_in = 2 * len(plan)
    ins = refs[:n_in]
    n_out = len(widths)
    adds = refs[n_in:n_in + n_out] if keeps else None
    outs = refs[n_in + n_out:n_in + 3 * n_out] if keeps else refs[n_in:n_in + n_out]
    scratch = refs[len(refs) - sum(turns):]
    left = []
    used = 0
    for n, turn in enumerate(turns):
        if turn:
            fill_turned(ins[2 * n], scratch[used], ins[2 * n].shape[0])
            left.append(scratch[used])
            used += 1
        else:
            left.append(ins[2 * n])
    right = [ins[2 * n + 1][...] for n in range(len(plan))]
    for group in range(n_out):
        for out, place, d in each_block(pick_ref, blocks, keeps, bits[group], 1 + group):
            at = pl.ds(pl.multiple_of((2 * d + pick_ref[0]) * deep, deep), deep)
            target = outs[2 * group + out] if keeps else outs[group]
            for n, (kind, own, start, wide) in enumerate(plan):
                if own != group:
                    continue
                rows = left[n][at, :]
                if kind == "copy":
                    part = rows
                elif kind == "nt":
                    part = nt(rows, right[n])
                else:
                    part = nn(rows, right[n])
                cut = slice(start, start + wide)
                if keeps:
                    part = part + adds[group][d, :, cut]
                target[place, :, cut] = part


def many_half(pick, pairs, plan, widths, add=None, *, parts, bits):
    whole = pl.BlockSpec(memory_space=pltpu.VMEM)
    turns = [kind in ("turn", "copy") for kind, *_ in plan]
    depth = max(left.shape[1 if turn else 0] for (left, _), turn in zip(pairs, turns))
    deep = depth // parts
    blocks = parts // 2
    keeps = add is not None
    args = [pick] + [operand for pair in pairs for operand in pair] + (list(add) if keeps else [])
    if keeps:
        shape = [jax.ShapeDtypeStruct((blocks // 2, deep, w), f32) for w in widths for _ in range(2)]
    else:
        shape = [jax.ShapeDtypeStruct((blocks, deep, w), f32) for w in widths]
    return pl.pallas_call(
        functools.partial(
            many_kernel, plan=plan, widths=widths, turns=turns, blocks=blocks, deep=deep,
            keeps=keeps, bits=[b[0] for b in bits],
        ),
        in_specs=[pl.BlockSpec(memory_space=pltpu.SMEM)] + [whole] * (len(args) - 1),
        out_specs=[whole] * len(shape),
        out_shape=shape,
        scratch_shapes=[
            pltpu.VMEM((left.shape[1], left.shape[0]), left.dtype)
            for (left, _), turn in zip(pairs, turns) if turn
        ],
        compiler_params=pltpu.CompilerParams(vmem_limit_bytes=VMEM_CAP),
        cost_estimate=pl.CostEstimate(flops=10**6, bytes_accessed=10**4, transcendentals=0),
        name="many_half",
    )(*args)


def flipped(value, bit, size):
    return lax.ppermute(value, "dp", [(i, i ^ (1 << bit)) for i in range(size)])


def bit_of(index, bit):
    return (index >> bit) & 1


class Halving:
    def __init__(self, make, index, size, orders):
        self.make, self.index, self.size, self.orders = make, index, size, orders
        mine = bit_of(index, 0).astype(jnp.int32)
        self.pick = jnp.stack([mine] + [bit_of(index, bits[0]).astype(jnp.int32) for bits in orders])
        self.other = self.pick.at[0].set(1 - mine)
        self.stage = 0
        self.extra = None

    def work(self):
        if self.stage == 0:
            self.pending = [(sent, None) for sent in self.make(self.other, None)]
        elif self.stage == 1:
            outs = self.make(self.pick, self.extra)
            self.pending = [(outs[2 * g], outs[2 * g + 1]) for g in range(len(self.orders))]
            self.axes = [
                [b for b in range(self.size.bit_length() - 1, 0, -1) if b != bits[0] and b < self.size.bit_length() - 1]
                for bits in self.orders
            ]
        else:
            self.pending = [
                self.split(g, held, extra) for g, (held, extra) in enumerate(zip(self.held, self.extra))
            ]
        return [part for pair in self.pending for part in pair if part is not None]

    def split(self, g, held, extra):
        bits = self.orders[g]
        if self.stage > len(bits):
            return held + extra, None
        bit = bits[self.stage - 1]
        axis = self.axes[g].index(bit)
        shape = (2,) * len(self.axes[g]) + held.shape[-2:]
        self.axes[g].remove(bit)
        own = bit_of(self.index, bit)
        held, extra = held.reshape(shape), extra.reshape(shape)

        def half(value, at):
            return lax.dynamic_index_in_dim(value, at, axis, keepdims=False)

        return half(held, 1 - own) + half(extra, 1 - own), half(held, own) + half(extra, own)

    def go(self, parts):
        parts = list(parts)
        pairs = [
            tuple(None if part is None else parts.pop(0) for part in pair) for pair in self.pending
        ]
        self.held = [home for _, home in pairs]
        last = self.stage > len(self.orders[0])
        if last:
            self.result = [away for away, _ in pairs]
        else:
            bit = lambda g: 0 if self.stage == 0 else self.orders[g][self.stage - 1]
            self.extra = [flipped(away, bit(g), self.size) for g, (away, _) in enumerate(pairs)]
        self.stage += 1

    def step(self):
        self.go(self.work())

    def over(self):
        return self.stage > len(self.orders[0]) + 1

    def finish(self):
        while not self.over():
            self.step()
        return self.result


def tie(values, *chains):
    chains = [chain for chain in chains if not chain.over()]
    values, extras = lax.optimization_barrier((values, [chain.extra for chain in chains]))
    for chain, extra in zip(chains, extras):
        chain.extra = extra
    works = [chain.work() for chain in chains]
    values, works = lax.optimization_barrier((values, works))
    for chain, parts in zip(chains, works):
        chain.go(parts)
    return values


def swap(value):
    return lax.ppermute(value.astype(f32), "mp", [(0, 1), (1, 0)])


def attend_kernel(
    t_ref, c_ref, o_ref, w_ref, ow_ref, gain_ref, shift_ref, first_ref, low_ref, normal_ref, inverse_ref,
    *, start,
):
    weight = ow_ref[...].astype(bf16)

    def body(step, carry):
        at = pl.ds(pl.multiple_of(step * 64, 64), 64)
        here = pl.ds(pl.multiple_of(start + step * 64, 64), 64)
        summed = t_ref[here, :].astype(f32) + nn(c_ref[at, :], w_ref[...])
        summed = summed + nn(o_ref[at, :].astype(bf16), weight)
        first, normal, inverse = norm_forward(summed, gain_ref[...], shift_ref[...])
        first_ref[at, :] = first
        low_ref[at, :] = first.astype(bf16)
        normal_ref[at, :] = normal
        inverse_ref[at, :] = inverse
        return carry

    lax.fori_loop(0, c_ref.shape[0] // 64, body, 0)


def attend(tokens, context, other, weight, other_weight, gain, shift, start):
    tall, depth = context.shape[0], tokens.shape[1]
    whole = pl.BlockSpec(memory_space=pltpu.VMEM)
    return pl.pallas_call(
        functools.partial(attend_kernel, start=start),
        in_specs=[whole] * 7,
        out_specs=(whole,) * 4,
        out_shape=(
            jax.ShapeDtypeStruct((tall, depth), f32),
            jax.ShapeDtypeStruct((tall, depth), bf16),
            jax.ShapeDtypeStruct((tall, depth), f32),
            jax.ShapeDtypeStruct((tall, 1), f32),
        ),
        compiler_params=pltpu.CompilerParams(vmem_limit_bytes=VMEM_CAP),
        cost_estimate=pl.CostEstimate(flops=2 * 10**9, bytes_accessed=8 * 10**6, transcendentals=0),
        name="attend",
    )(tokens, context, other, weight, other_weight, gain[None], shift[None])


def norm_forward(summed, gain, shift):
    centred = summed - jnp.mean(summed, axis=1, keepdims=True)
    inverse = lax.rsqrt(jnp.mean(centred * centred, axis=1, keepdims=True) + epsilon)
    normal = centred * inverse
    return (normal * gain + shift, normal, inverse)


def norm_backward(upstream, normal, inverse, gain):
    scaled = upstream * gain
    inner = jnp.mean(scaled, axis=1, keepdims=True)
    aligned = jnp.mean(scaled * normal, axis=1, keepdims=True)
    return (
        inverse * (scaled - inner - normal * aligned),
        jnp.sum(upstream * normal, axis=0),
        jnp.sum(upstream, axis=0),
    )


def shards(
    tokens,
    query_weight,
    key_weight,
    value_weight,
    output_weight,
    query_position,
    key_position,
    position_tables,
    gain_one,
    shift_one,
    up_weight,
    down_weight,
    gain_two,
    shift_two,
    buckets,
    text_length,
    cotangent,
):
    span = buckets.shape[2]
    rows, cols = sizes(span)
    size = lax.axis_size("dp")
    index = lax.axis_index("dp")
    bits = list(range(1, size.bit_length() - 1))
    low_first, high_first = bits, bits[1:2] + bits[:1] + bits[2:]
    score_scale = (7.0 * HEAD) ** (-0.5)
    tables_flat = position_tables.reshape(3 * REL, D)
    width = query_weight.shape[1]
    spare = ((0, rows - span), (0, 0))

    def chain(make, *orders):
        return Halving(make, index, size, list(orders))

    split = rows // 2 // 128 * 128
    other_output = swap(output_weight)
    qkv, pos_key, pos_query = project(
        tokens, query_weight, key_weight, value_weight, position_tables, key_position, query_position, span
    )
    tokens = jnp.pad(tokens, spare)
    cotangent = jnp.pad(cotangent, spare)
    edges = [(0, split), (split, rows)]

    share_head, context_head, wide_head, bucket_head, bucket_rest, bucket_cols, far_rest, far_inverse = attention_head(
        qkv, pos_key, pos_query, buckets, text_length, score_scale, split
    )
    other_head = swap(wide_head)
    far_rest, other_output = lax.optimization_barrier((far_rest, other_output))
    share_rest, context_rest, wide_rest = attention_rest(
        qkv, pos_key, bucket_rest, far_rest, far_inverse, text_length, score_scale, split, span
    )
    other_rest = swap(wide_rest)
    shares = [share_head, share_rest]
    contexts = [context_head, context_rest]
    contexts_other = [other_head, other_rest]

    def gelu(value):
        return jax.nn.gelu(value, approximate=False)

    firsts, firsts_low, normals_one, inverses_one, upwards, hiddens, feeds, feeds_other = ([] for _ in range(8))
    for (low, high), context, other in zip(edges, contexts, contexts_other):
        first, first_low, normal_one, inverse_one = attend(
            tokens, context, other, output_weight, other_output, gain_one, shift_one, low
        )
        firsts.append(first)
        normals_one.append(normal_one)
        inverses_one.append(inverse_one)
        firsts_low.append(first_low)
        upwards.append(nn(firsts_low[-1], up_weight))
        hiddens.append(gelu(upwards[-1]).astype(bf16))
        feeds.append(nn(hiddens[-1], down_weight))
        feeds_other.append(swap(feeds[-1]))

    feeds[1], tokens_late, tables_late = lax.optimization_barrier((feeds[1], tokens, tables_flat))
    tokens_turned, tables_turned = tokens_late.T, tables_late.T
    finals, seconds_back, seconds_low, upwards_back, backs_part, backs_other, two_sums = ([] for _ in range(7))
    for n, (low, high) in enumerate(edges):
        final, normal_two, inverse_two = norm_forward(
            firsts[n] + feeds[n] + feeds_other[n], gain_two, shift_two
        )
        finals.append(final.astype(bf16))
        second_back, *sums = norm_backward(
            cotangent[low:high].astype(f32), normal_two, inverse_two, gain_two
        )
        two_sums.append(sums)
        seconds_back.append(second_back)
        seconds_low.append(second_back.astype(bf16))
        hidden_back = nt(seconds_low[n], down_weight)
        upwards_back.append(jax.vjp(gelu, upwards[n])[1](hidden_back)[0].astype(bf16))
        backs_part.append(nt(upwards_back[n], up_weight))
        backs_other.append(swap(backs_part[n]))
    layer_output = jnp.concatenate(finals, axis=0)[:span]
    gain_two_grad, shift_two_grad = (two_sums[0][n] + two_sums[1][n] for n in range(2))

    backs_part, down_pair, up_pair = lax.optimization_barrier(
        (backs_part, (seconds_low, hiddens), (firsts_low, upwards_back))
    )
    up_pair, backs_other[0] = lax.optimization_barrier((up_pair, backs_other[0]))
    down_chain = chain(
        lambda pick, add: weight_half(pick, *down_pair, add, parts=size, bits=high_first), high_first
    )
    up_chain = chain(
        lambda pick, add: weight_half(pick, *up_pair, add, parts=size, bits=low_first), low_first
    )
    down_chain.step()
    up_chain.step()
    backs_other[0] = tie(backs_other[0], down_chain)
    backs_other[0] = tie(backs_other[0], up_chain)
    merge = merge_table()
    residuals_back, residuals_low, one_sums = [], [], []

    def draw(n, adds=()):
        residual_back, *sums = norm_backward(
            seconds_back[n] + backs_part[n] + backs_other[n], normals_one[n], inverses_one[n], gain_one
        )
        one_sums.append(sums)
        residuals_back.append(residual_back)
        residuals_low.append(residual_back.astype(bf16))
        context_back = nt(residuals_low[n], output_weight).astype(bf16)
        return attention_draw(shares[n], context_back, qkv, score_scale, edges[n][0], rows, adds)

    back_head, turned_head, query_head, key_head, value_head = draw(0)
    back_head, key_head, backs_other[1] = lax.optimization_barrier((back_head, key_head, backs_other[1]))
    back_rest, turned_rest, query_rest, key_base, value_back = draw(1, (key_head, value_head))
    gain_one_grad, shift_one_grad = (one_sums[0][n] + one_sums[1][n] for n in range(2))
    back_rest, value_back = tie((back_rest, value_back), down_chain)
    residual_low = jnp.concatenate(residuals_low, axis=0)
    context = jnp.concatenate(contexts, axis=0)
    nothing = jnp.zeros_like(gain_one)
    gains = jnp.stack(
        [gain_one_grad, shift_one_grad, gain_two_grad, shift_two_grad] + [nothing] * 4
    )
    gains = jnp.concatenate([gains, jnp.zeros((120, gains.shape[1]), f32)], axis=0)
    dummy = jnp.zeros((8, 128), bf16)
    outer_chain = chain(
        lambda pick, add: many_half(
            pick,
            [(residual_low, context), (tokens_turned, value_back), (gains, dummy)],
            [("turn", 0, 0, width), ("nn", 0, width, width), ("copy", 0, 2 * width, 128)],
            [2 * width + 128],
            add, parts=size, bits=[low_first],
        ),
        low_first,
    )
    outer_chain.step()

    def tail(rows_back, sums, position, orders):
        return chain(
            lambda pick, add: many_half(
                pick,
                [(tokens_turned, rows_back), (tables_turned, sums), (position, sums)],
                [("nn", 0, 0, width), ("nn", 1, 0, width), ("nt", 0, width, 3 * REL)],
                [width + 3 * REL, width],
                add, parts=size, bits=orders,
            ),
            *orders,
        )

    near = []
    blocks = rows // 64
    near.append(attention_scatter([back_head], bucket_head, merge, 0, split // 64))
    back_rest, near = tie((back_rest, near), up_chain)
    back_rest, near = tie((back_rest, near), outer_chain)
    back_rest, near = tie((back_rest, near), down_chain)
    near.append(attention_scatter([back_rest], bucket_rest, merge, 0, blocks - split // 64))
    near, backs = tie((near, [turned_head, turned_rest]), up_chain)
    query_low, key_table_sum = attention_close(near, [query_head, query_rest], pos_key, qkv, 0)
    early = nt(query_low, query_weight) + nt(value_back, value_weight)
    near_chain = tail(query_low, key_table_sum, key_position, [high_first, low_first])
    backs, key_table_sum = tie((backs, key_table_sum), near_chain, outer_chain, down_chain)
    far = []
    cuts = [n * blocks // 3 for n in range(4)]
    for part, chains in enumerate(((near_chain,), (outer_chain, up_chain), (near_chain, outer_chain))):
        far.append(attention_scatter(backs, bucket_cols, merge, cuts[part], cuts[part + 1] - cuts[part]))
        backs, far = tie((backs, far), *chains)
    key_low, query_table_sum = attention_close(far, [key_base], pos_query, qkv, 1)
    key_low, query_table_sum = tie((key_low, query_table_sum), near_chain)
    far_chain = tail(key_low, query_table_sum, query_position, [low_first, high_first])
    parts, others = [], []
    for low, high in ((0, rows // 2), (rows // 2, rows)):
        parts.append(early[low:high] + nt(key_low[low:high], key_weight))
        others.append(swap(parts[-1]))
    far_chain.step()
    far_chain.step()
    far_chain.extra, others[0] = lax.optimization_barrier((far_chain.extra, others[0]))
    far_chain.extra = tie(far_chain.extra, near_chain)
    far_main, query_position_grad = far_chain.finish()
    far_main, others[1] = lax.optimization_barrier((far_main, others[1]))
    input_gradient = (
        jnp.concatenate(residuals_back, axis=0) + jnp.concatenate(parts, axis=0) + jnp.concatenate(others, axis=0)
    )[:span].astype(bf16)
    (down_share,) = down_chain.finish()
    (up_share,) = up_chain.finish()
    (outer_share,) = outer_chain.finish()
    near_main, key_position_grad = near_chain.finish()

    table_rows = near_main[:, width:] + far_main[:, width:]
    table_rows = table_rows.reshape(2, table_rows.shape[0] // 2, 3 * REL)
    side = lax.axis_index("mp")
    table_mine = lax.dynamic_index_in_dim(table_rows, side, 0, keepdims=False) + lax.ppermute(
        lax.dynamic_index_in_dim(table_rows, 1 - side, 0, keepdims=False), "mp", [(0, 1), (1, 0)]
    )
    table_gradient = table_mine.T.reshape(3, REL, table_mine.shape[0])
    gains_mine = outer_share[:, 2 * width:]
    return (
        layer_output,
        input_gradient,
        near_main[:, 0:width],
        far_main[:, 0:width],
        outer_share[:, width:2 * width],
        outer_share[:, 0:width].T,
        query_position_grad,
        key_position_grad,
        table_gradient,
        gains_mine[:, 0],
        gains_mine[:, 1],
        up_share,
        down_share.T,
        gains_mine[:, 2],
        gains_mine[:, 3],
    )


def solution(mesh):
    return jax.shard_map(
        shards,
        mesh=mesh,
        in_specs=(
            P("dp", None),
            P(None, "mp"),
            P(None, "mp"),
            P(None, "mp"),
            P("mp", None),
            P(None, "mp"),
            P(None, "mp"),
            P(),
            P(),
            P(),
            P(None, "mp"),
            P("mp", None),
            P(),
            P(),
            P("dp", None, None, None),
            P("dp"),
            P("dp", None),
        ),
        out_specs=(
            P("dp", None),
            P("dp", None),
            P("dp", "mp"),
            P("dp", "mp"),
            P("dp", "mp"),
            P("mp", "dp"),
            P("dp", "mp"),
            P("dp", "mp"),
            P(None, None, ("dp", "mp")),
            P("dp"),
            P("dp"),
            P("dp", "mp"),
            P("mp", "dp"),
            P("dp"),
            P("dp"),
        ),
        check_vma=False,
    )
```

```python
import functools

import jax
import jax.numpy as jnp
from jax import lax
from jax.experimental import pallas as pl
from jax.experimental.pallas import tpu as pltpu
from jax.sharding import PartitionSpec as P

D = 1024
epsilon = 1e-05
HEAD = 64
REL = 128
TEXT = 512
bf16 = jnp.bfloat16
f32 = jnp.float32
LIMIT = 10900.0
VMEM_CAP = 62 * 2**20
STEPS = 4


def lane_gather(table, index):
    numbers = lax.GatherDimensionNumbers(
        offset_dims=(),
        collapsed_slice_dims=(1,),
        start_index_map=(1,),
        operand_batching_dims=(0,),
        start_indices_batching_dims=(0,),
    )
    return lax.gather(
        table, index[..., None], numbers, (1, 1), mode=lax.GatherScatterMode.PROMISE_IN_BOUNDS
    )


def nt(left, right):
    return lax.dot_general(left, right, (((1,), (1,)), ((), ())), preferred_element_type=f32)


def nn(left, right):
    return jnp.dot(left, right, preferred_element_type=f32)


def tn(left, right):
    return lax.dot_general(left, right, (((0,), (0,)), ((), ())), preferred_element_type=f32)


def lane_half(shape):
    return lax.broadcasted_iota(jnp.int32, shape, len(shape) - 1) < HEAD


def unpack_pair(packed):
    low = (packed << 16) >> 16
    high = (packed - low) >> 16
    return high.astype(f32), low.astype(f32)


def fill_tables(src_ref, first, tall, pos_ref, tab, inv, p):
    half = lane_half((64, 128))
    cut = slice(p * 128, (p + 1) * 128)

    def body(step, carry):
        at = pl.ds(pl.multiple_of(step * 64, 64), 64)
        block = src_ref[pl.ds(pl.multiple_of(first + step * 64, 64), 64), cut]
        zero = jnp.zeros_like(block)
        first_head = nt(jnp.where(half, block, zero), pos_ref[:, cut]).astype(bf16).astype(f32)
        second_head = nt(jnp.where(half, zero, block), pos_ref[:, cut]).astype(bf16).astype(f32)
        top0 = jnp.maximum(jnp.max(jnp.abs(first_head), axis=1, keepdims=True), 1e-30)
        top1 = jnp.maximum(jnp.max(jnp.abs(second_head), axis=1, keepdims=True), 1e-30)
        whole0 = jnp.round(first_head * (LIMIT / top0)).astype(jnp.int32)
        whole1 = jnp.round(second_head * (LIMIT / top1)).astype(jnp.int32)
        tab[p, at, :] = whole0 * 65536 + whole1
        inv[2 * p, at, :] = jnp.broadcast_to(top0 * (1.0 / LIMIT), (64, 128))
        inv[2 * p + 1, at, :] = jnp.broadcast_to(top1 * (1.0 / LIMIT), (64, 128))
        return carry

    lax.fori_loop(0, tall // 64, body, 0)


def look_up(tab, index_ref, at, store, *, pairs, cols):
    for c in range(cols // 128):
        total = [None] * pairs
        for r in range(3):
            index = index_ref[r, at, c * 128:(c + 1) * 128]
            for p in range(pairs):
                got = lane_gather(tab[p, at, r * 128:(r + 1) * 128], index)
                total[p] = got if total[p] is None else total[p] + got
        for p in range(pairs):
            store(p, c, total[p])


def prepare_rows(
    k_ref, pq_ref, b_ref, head_ref, rest_ref, bt_ref, far_head, far_rest, inv_ref,
    far_tab, far_inv, *, span, rows, cols, pairs, split,
):
    edge = span - span % 8 - split
    for r in range(3):
        head_ref[r, :, span - span % 128:cols] = jnp.zeros((split, cols - span + span % 128), jnp.int32)
        rest_ref[r, edge:rows - split, :] = jnp.zeros((rows - split - edge, cols), jnp.int32)
        rest_ref[r, :, span - span % 128:cols] = jnp.zeros((rows - split, cols - span + span % 128), jnp.int32)
        head_ref[r, :, 0:span] = b_ref[0, r, 0:split]
        rest_ref[r, 0:span - split, 0:span] = b_ref[0, r, split:span]
    for r in range(3):
        for jb in range(cols // 128):
            high = min(128, rows - jb * 128)
            for ib in range(cols // 128):
                tall = min(128, rows - ib * 128)
                here = slice(jb * 128, (jb + 1) * 128)
                if ib * 128 < split:
                    block = head_ref[r, ib * 128:ib * 128 + tall, here]
                else:
                    block = rest_ref[r, ib * 128 - split:ib * 128 - split + tall, here]
                if tall < 128:
                    block = jnp.concatenate([block, jnp.zeros((128 - tall, 128), jnp.int32)], axis=0)
                bt_ref[r, jb * 128:jb * 128 + high, ib * 128:(ib + 1) * 128] = block.T[:high]
    for p in range(pairs):
        fill_tables(k_ref, 0, rows, pq_ref, far_tab, far_inv, p)

    def far_body(step, carry):
        for turn in range(STEPS):
            at = pl.ds(pl.multiple_of(step * 8 * STEPS + turn * 8, 8), 8)

            def store(p, c, total, at=at):
                if c * 128 < split:
                    far_head[p, at, c * 128:(c + 1) * 128] = total
                else:
                    far_rest[p, at, c * 128 - split:(c + 1) * 128 - split] = total

            look_up(far_tab, bt_ref, at, store, pairs=pairs, cols=cols)
        return carry

    lax.fori_loop(0, rows // (8 * STEPS), far_body, 0)
    for p in range(pairs):
        far_head[p, rows:, :] = jnp.zeros((cols - rows, split), jnp.int32)
        far_rest[p, rows:, :] = jnp.zeros((cols - rows, cols - split), jnp.int32)
    for h in range(2 * pairs):
        inv_ref[h:h + 1, :] = jnp.concatenate(
            [far_inv[h, j * 128:min(rows, (j + 1) * 128), :].T[0:1] for j in range(cols // 128 - 1)]
            + [jnp.concatenate([far_inv[h, cols - 128:rows, :],
                                jnp.zeros((cols - rows, 128), f32)], axis=0).T[0:1]], axis=1)


def forward_rows(
    used_ref, q_ref, k_ref, v_ref, pk_ref, b_ref, far_sum, inv_ref, p_ref, ctx_ref, wide_ref,
    near_tab, near_inv, near_sum, score, *, first, rows, span, cols, pairs, scale,
):
    for p in range(pairs):
        fill_tables(q_ref, first, rows, pk_ref, near_tab, near_inv, p)
    used = used_ref[0]
    place = lax.broadcasted_iota(jnp.int32, (1, cols), 1)
    valid = ((place >= TEXT) & (place < span)) | (place < used)

    def block_body(start, tall):
        def near_body(step, carry):
            for turn in range(STEPS):
                at = pl.ds(pl.multiple_of(start + step * 8 * STEPS + turn * 8, 8), 8)
                out_at = pl.ds(pl.multiple_of(step * 8 * STEPS + turn * 8, 8), 8)

                def store(p, c, total, out_at=out_at):
                    near_sum[p, out_at, c * 128:(c + 1) * 128] = total

                look_up(near_tab, b_ref, at, store, pairs=pairs, cols=cols)
            return carry

        lax.fori_loop(0, tall // (8 * STEPS), near_body, 0)
        at = pl.ds(start, tall)
        for p in range(pairs):
            cut = slice(p * 128, (p + 1) * 128)
            block = q_ref[pl.ds(pl.multiple_of(first + start, 64), tall), cut]
            zero = jnp.zeros_like(block)
            mask = lane_half((tall, 128))
            score[0, 0:tall, :] = nt(jnp.where(mask, block, zero), k_ref[:, cut])
            score[1, 0:tall, :] = nt(jnp.where(mask, zero, block), k_ref[:, cut])
            for c in range(cols // 128):
                turned = far_sum[p, c * 128:(c + 1) * 128, pl.ds(start, 128)].T[0:tall]
                here = slice(c * 128, (c + 1) * 128)
                f0, f1 = unpack_pair(turned)
                n0, n1 = unpack_pair(near_sum[p, 0:tall, here])
                score[0, 0:tall, here] += (
                    f0 * inv_ref[2 * p:2 * p + 1, here] + n0 * near_inv[2 * p, at, :]
                )
                score[1, 0:tall, here] += (
                    f1 * inv_ref[2 * p + 1:2 * p + 2, here] + n1 * near_inv[2 * p + 1, at, :]
                )
            for h in range(2):
                for s in range(tall // 16):
                    raw = score[h, s * 16:(s + 1) * 16, :]
                    logits = jnp.where(valid, raw * scale, -1e30)
                    top = jnp.max(logits, axis=1, keepdims=True)
                    grown = jnp.exp(logits - top)
                    share = grown * (1.0 / jnp.sum(grown, axis=1, keepdims=True))
                    p_ref[2 * p + h, pl.ds(pl.multiple_of(start + s * 16, 16), 16), :] = share.astype(bf16)
            c0 = nn(p_ref[2 * p, at, :], v_ref[:, cut])
            c1 = nn(p_ref[2 * p + 1, at, :], v_ref[:, cut])
            context = jnp.where(mask, c0, c1).astype(bf16)
            ctx_ref[at, cut] = context
            wide_ref[at, cut] = context.astype(f32)

    def outer(step, carry):
        block_body(pl.multiple_of(step * 128, 128), 128)
        return carry

    lax.fori_loop(0, rows // 128, outer, 0)
    if rows % 128:
        block_body(rows - rows % 128, rows % 128)


def project_kernel(x_ref, wq_ref, wk_ref, wv_ref, t_ref, kp_ref, qp_ref, qkv_ref, pk_ref, pq_ref, *, span, cols, width):
    tail = span - span % 128
    qkv_ref[span - span % 16:cols, :] = jnp.zeros((cols - span + span % 16, 3 * width), bf16)
    for n, w_ref in enumerate((wq_ref, wk_ref, wv_ref)):
        cut = slice(n * width, (n + 1) * width)

        def body(step, carry, cut=cut, w_ref=w_ref):
            at = pl.ds(pl.multiple_of(step * 128, 128), 128)
            qkv_ref[at, cut] = nn(x_ref[at, :], w_ref[...]).astype(bf16)
            return carry

        lax.fori_loop(0, span // 128, body, 0)
        if tail < span:
            qkv_ref[tail:span, cut] = nn(x_ref[tail:span, :], w_ref[...]).astype(bf16)
    for r in range(3):
        at = slice(r * REL, (r + 1) * REL)
        pk_ref[at, :] = nn(t_ref[r], kp_ref[...]).astype(bf16)
        pq_ref[at, :] = nn(t_ref[r], qp_ref[...]).astype(bf16)


def project(tokens, query_weight, key_weight, value_weight, tables, key_position, query_position, span):
    width = query_weight.shape[1]
    rows, cols = sizes(span)
    whole = pl.BlockSpec(memory_space=pltpu.VMEM)
    return pl.pallas_call(
        functools.partial(project_kernel, span=span, cols=cols, width=width),
        out_shape=(
            jax.ShapeDtypeStruct((cols, 3 * width), bf16),
            jax.ShapeDtypeStruct((3 * REL, width), bf16),
            jax.ShapeDtypeStruct((3 * REL, width), bf16),
        ),
        in_specs=[whole] * 7,
        out_specs=(whole,) * 3,
        compiler_params=pltpu.CompilerParams(vmem_limit_bytes=VMEM_CAP),
        cost_estimate=pl.CostEstimate(flops=4 * 10**9, bytes_accessed=9 * 10**6, transcendentals=0),
        name="project",
    )(tokens, query_weight, key_weight, value_weight, tables, key_position, query_position)


def pick(half, block, h):
    zero = jnp.zeros_like(block)
    return jnp.where(half, block, zero) if h == 0 else jnp.where(half, zero, block)


def draw_kernel(
    p_ref, up_ref, q_ref, k_ref, v_ref, *refs, first, tall, rows, cols, scale, adds,
):
    extra = refs[:adds]
    d_ref, dt_ref, dq_ref, dk_ref, dv_ref, wide, flat, turned = refs[adds:]
    lanes = turned.shape[2]
    half = lane_half((64, 128))

    def body(step, carry):
        at = pl.ds(pl.multiple_of(step * 64, 64), 64)
        pair = []
        for h in range(2):
            reach = nt(pick(half, up_ref[at, :], h), v_ref[...])
            share = p_ref[h, at, :].astype(f32)
            inner = jnp.sum(reach * share, axis=1, keepdims=True)
            back = share * (reach - inner) * scale
            wide[h, at, :] = back
            flat[h, at, :] = back.astype(bf16)
            pair.append(back.reshape(8, 8, cols))
        d_ref[pl.ds(pl.multiple_of(step * 8, 8), 8), :, :] = jnp.concatenate(pair, axis=1).astype(bf16)
        return carry

    lax.fori_loop(0, tall // 64, body, 0)
    for jb in range(cols // 128):
        high = min(128, rows - jb * 128)
        for ib in range(lanes // 128):
            wide_rows = min(128, tall - ib * 128)
            pair = []
            for h in range(2):
                block = wide[h, ib * 128:ib * 128 + wide_rows, jb * 128:(jb + 1) * 128]
                if wide_rows < 128:
                    block = jnp.concatenate([block, jnp.zeros((128 - wide_rows, 128), f32)], axis=0)
                other = block.T[:high]
                turned[h, jb * 128:jb * 128 + high, ib * 128:(ib + 1) * 128] = other.astype(bf16)
                pair.append(other.reshape(high // 8, 8, 128))
            dt_ref[jb * 16:jb * 16 + high // 8, :, ib * 128:(ib + 1) * 128] = jnp.concatenate(
                pair, axis=1
            ).astype(bf16)
    keys, queries, ups = k_ref[...], q_ref[first:first + lanes, :], up_ref[...]
    cols_half, lanes_half, tall_half = (lane_half((n, 128)) for n in (cols, lanes, tall))
    dq_ref[...] = nn(flat[0], pick(cols_half, keys, 0)) + nn(flat[1], pick(cols_half, keys, 1))
    dk = nn(turned[0], pick(lanes_half, queries, 0)) + nn(turned[1], pick(lanes_half, queries, 1))
    dv = tn(p_ref[0], pick(tall_half, ups, 0)) + tn(p_ref[1], pick(tall_half, ups, 1))
    dv = dv[:rows]
    if adds:
        dk, dv = dk + extra[0][...], dv + extra[1][...]
    dk_ref[...] = dk
    dv_ref[...] = dv.astype(dv_ref.dtype)


def scatter_kernel(*refs, groups, cols):
    *d_refs, b_ref, merge_ref, out_ref = refs
    base = jnp.where(lax.broadcasted_iota(jnp.int32, (16, cols), 0) >= 8, 1.0, 0.0).astype(bf16)
    own = (lax.broadcasted_iota(jnp.int32, (256, 256), 0) % 8) == (
        lax.broadcasted_iota(jnp.int32, (256, 256), 1) % 8
    )
    zero = jnp.asarray(0.0, bf16)
    one = jnp.asarray(1.0, bf16)

    def sieve(g, r, back):
        bucket = b_ref[r, pl.ds(pl.multiple_of(g * 8, 8), 8), :]
        low = (bucket & 31).astype(f32)
        high = (bucket >> 5).astype(f32)
        low = jnp.concatenate([low, low], axis=0).astype(bf16) - base
        high = jnp.concatenate([high, high], axis=0).astype(bf16)
        hot = jnp.concatenate(
            [jnp.where(low == jnp.asarray(2.0 * k, bf16), one, zero) for k in range(16)], axis=0
        )
        sieved = []
        for l in range(4):
            mask = high == jnp.asarray(float(l), bf16)
            for p in range(4):
                sieved.append(jnp.where(mask, back[p * 16:(p + 1) * 16], zero))
        sums = nt(jnp.concatenate(sieved, axis=0), hot)
        return jnp.where(own, sums, 0.0).astype(bf16)

    def body(step, carry):
        got = []
        for g in (2 * step, 2 * step + 1):
            back = jnp.concatenate([d_ref[g] for d_ref in d_refs], axis=1) if len(d_refs) > 1 else d_refs[0][g]
            for r in range(3):
                got.append((g, r, sieve(g, r, back)))
        for g, r, sums in got:
            total = None
            for l in range(4):
                term = nn(sums[l * 64:(l + 1) * 64], merge_ref[l])
                total = term if total is None else total + term
            out_ref[g, :, r * 128:(r + 1) * 128] = total.astype(bf16)
        return carry

    lax.fori_loop(0, groups // 2, body, 0)


def close_kernel(*refs, rows, count):
    *base_refs, pos_ref, side_ref, out_ref, table_ref = refs[count:]
    rows2 = 2 * rows
    half3 = lane_half((rows // 8, 8, 128))
    flat = jnp.concatenate([ref[...] for ref in refs[:count]], axis=0).reshape(rows2, 3 * REL)
    both = nn(flat, pos_ref[...]).reshape(rows // 8, 16, 128)
    mine = jnp.where(half3, both[:, 0:8, :], both[:, 8:16, :]).reshape(rows, 128)
    first = 0
    for base_ref in base_refs:
        here = slice(first, first + base_ref.shape[0])
        out_ref[here, :] = (base_ref[...] + mine[here]).astype(bf16)
        first += base_ref.shape[0]
    side = side_ref[0:rows, :].astype(f32).reshape(rows // 8, 8, 128)
    zero = jnp.zeros_like(side)
    spread = jnp.concatenate([jnp.where(half3, side, zero), jnp.where(half3, zero, side)], axis=1)
    table_ref[...] = tn(flat, spread.reshape(rows2, 128).astype(bf16)).astype(bf16)


def merge_table():
    l = lax.broadcasted_iota(jnp.int32, (4, 256, 128), 0)
    a = lax.broadcasted_iota(jnp.int32, (4, 256, 128), 1) // 8
    c = lax.broadcasted_iota(jnp.int32, (4, 256, 128), 2)
    return (c == l * 32 + a).astype(bf16)


def sizes(span):
    return -(-span // 64) * 64, -(-span // 128) * 128


def forward_scratch(pairs, tall, cols):
    return [
        pltpu.VMEM((pairs, tall, 3 * REL), jnp.int32),
        pltpu.VMEM((2 * pairs, tall, 128), f32),
        pltpu.VMEM((pairs, 128, cols), jnp.int32),
        pltpu.VMEM((2, 128, cols), f32),
    ]


def attention_head(qkv, pos_key, pos_query, buckets, used, scale, split):
    span = buckets.shape[2]
    rows, cols = sizes(span)
    width = pos_key.shape[1]
    pairs = width // 128
    whole = pl.BlockSpec(memory_space=pltpu.VMEM)
    i32 = jnp.int32

    def kernel(
        used_ref, qkv_ref, pk_ref, pq_ref, b_ref, p_ref, ctx_ref, wide_ref, head_ref, rest_ref, bt_ref, far_rest,
        inv_ref, far_tab, far_inv, far_head, *scratch,
    ):
        k_ref = qkv_ref.at[:, width:2 * width]
        prepare_rows(
            k_ref, pq_ref, b_ref, head_ref, rest_ref, bt_ref, far_head, far_rest, inv_ref, far_tab, far_inv,
            span=span, rows=rows, cols=cols, pairs=pairs, split=split,
        )
        forward_rows(
            used_ref, qkv_ref.at[:, 0:width], k_ref, qkv_ref.at[:, 2 * width:3 * width], pk_ref, head_ref,
            far_head, inv_ref, p_ref, ctx_ref, wide_ref, *scratch,
            first=0, rows=split, span=span, cols=cols, pairs=pairs, scale=scale,
        )

    return pl.pallas_call(
        kernel,
        out_shape=(
            jax.ShapeDtypeStruct((2 * pairs, split, cols), bf16),
            jax.ShapeDtypeStruct((split, width), bf16),
            jax.ShapeDtypeStruct((split, width), f32),
            jax.ShapeDtypeStruct((3, split, cols), i32),
            jax.ShapeDtypeStruct((3, rows - split, cols), i32),
            jax.ShapeDtypeStruct((3, rows, cols), i32),
            jax.ShapeDtypeStruct((pairs, cols, cols - split), i32),
            jax.ShapeDtypeStruct((2 * pairs, cols), f32),
        ),
        in_specs=[pl.BlockSpec(memory_space=pltpu.SMEM)] + [whole] * 4,
        out_specs=(whole,) * 8,
        scratch_shapes=[
            pltpu.VMEM((pairs, rows, 3 * REL), i32),
            pltpu.VMEM((2 * pairs, rows, 128), f32),
            pltpu.VMEM((pairs, cols, split), i32),
        ] + forward_scratch(pairs, split, cols),
        compiler_params=pltpu.CompilerParams(vmem_limit_bytes=VMEM_CAP),
        cost_estimate=pl.CostEstimate(flops=4 * 10**10, bytes_accessed=25000000, transcendentals=0),
        name="attention_head",
    )(used, qkv, pos_key, pos_query, buckets)


def attention_rest(qkv, pos_key, bucket_rest, far_rest, inverse, used, scale, split, span):
    rows, cols = sizes(span)
    width = pos_key.shape[1]
    pairs = width // 128
    whole = pl.BlockSpec(memory_space=pltpu.VMEM)

    def kernel(used_ref, qkv_ref, pk_ref, b_ref, far_ref, inv_ref, p_ref, ctx_ref, wide_ref, *scratch):
        forward_rows(
            used_ref, qkv_ref.at[:, 0:width], qkv_ref.at[:, width:2 * width], qkv_ref.at[:, 2 * width:3 * width],
            pk_ref, b_ref, far_ref, inv_ref, p_ref, ctx_ref, wide_ref, *scratch,
            first=split, rows=rows - split, span=span, cols=cols, pairs=pairs, scale=scale,
        )

    return pl.pallas_call(
        kernel,
        out_shape=(
            jax.ShapeDtypeStruct((2 * pairs, rows - split, cols), bf16),
            jax.ShapeDtypeStruct((rows - split, width), bf16),
            jax.ShapeDtypeStruct((rows - split, width), f32),
        ),
        in_specs=[pl.BlockSpec(memory_space=pltpu.SMEM)] + [whole] * 5,
        out_specs=(whole,) * 3,
        scratch_shapes=forward_scratch(pairs, rows - split, cols),
        compiler_params=pltpu.CompilerParams(vmem_limit_bytes=VMEM_CAP),
        cost_estimate=pl.CostEstimate(flops=2 * 10**10, bytes_accessed=12000000, transcendentals=0),
        name="attention_rest",
    )(used, qkv, pos_key, bucket_rest, far_rest, inverse)


def attention_draw(share, upstream, qkv, scale, first, rows, adds=()):
    heads, tall, cols = share.shape
    width = upstream.shape[1]
    pairs = heads // 2
    lanes = -(-tall // 128) * 128

    def column(n):
        return pl.BlockSpec((n, 128), lambda p: (0, p))

    return pl.pallas_call(
        functools.partial(draw_kernel, first=first, tall=tall, rows=rows, cols=cols, scale=scale, adds=len(adds)),
        grid=(pairs,),
        in_specs=[
            pl.BlockSpec((2, tall, cols), lambda p: (p, 0, 0)),
            column(tall),
            pl.BlockSpec((cols, 128), lambda p: (0, p)),
            pl.BlockSpec((cols, 128), lambda p: (0, p + pairs)),
            pl.BlockSpec((cols, 128), lambda p: (0, p + 2 * pairs)),
        ] + [column(rows)] * len(adds),
        out_specs=(
            pl.BlockSpec((tall // 8, 16, cols), lambda p: (0, p, 0)),
            pl.BlockSpec((rows // 8, 16, lanes), lambda p: (0, p, 0)),
            column(tall), column(rows), column(rows),
        ),
        out_shape=(
            jax.ShapeDtypeStruct((tall // 8, 8 * heads, cols), bf16),
            jax.ShapeDtypeStruct((rows // 8, 8 * heads, lanes), bf16),
            jax.ShapeDtypeStruct((tall, width), f32),
            jax.ShapeDtypeStruct((rows, width), f32),
            jax.ShapeDtypeStruct((rows, width), bf16 if adds else f32),
        ),
        scratch_shapes=[
            pltpu.VMEM((2, tall, cols), f32),
            pltpu.VMEM((2, tall, cols), bf16),
            pltpu.VMEM((2, rows, lanes), bf16),
        ],
        compiler_params=pltpu.CompilerParams(vmem_limit_bytes=VMEM_CAP),
        cost_estimate=pl.CostEstimate(flops=10**6, bytes_accessed=10**4, transcendentals=0),
        name="attention_draw",
    )(share, upstream, qkv, qkv, qkv, *adds)


def attention_scatter(backs, buckets, merge, first, count):
    high = backs[0].shape[1]
    cols = buckets.shape[2]
    return pl.pallas_call(
        functools.partial(scatter_kernel, groups=8, cols=cols),
        grid=(count,),
        out_shape=jax.ShapeDtypeStruct((8 * count, high, 3 * REL), bf16),
        in_specs=[pl.BlockSpec((8, high, b.shape[2]), lambda g: (first + g, 0, 0)) for b in backs] + [
            pl.BlockSpec((3, 64, cols), lambda g: (0, first + g, 0)),
            pl.BlockSpec(merge.shape, lambda g: (0, 0, 0)),
        ],
        out_specs=pl.BlockSpec((8, high, 3 * REL), lambda g: (g, 0, 0)),
        compiler_params=pltpu.CompilerParams(vmem_limit_bytes=VMEM_CAP),
        cost_estimate=pl.CostEstimate(flops=10**6, bytes_accessed=10**4, transcendentals=0),
        name="attention_scatter",
    )(*backs, buckets, merge)


def attention_close(sums, bases, pos, qkv, side):
    rows, width = sum(base.shape[0] for base in bases), bases[0].shape[1]
    pairs = width // 128
    return pl.pallas_call(
        functools.partial(close_kernel, rows=rows, count=len(sums)),
        grid=(pairs,),
        in_specs=[pl.BlockSpec((part.shape[0], 16, 3 * REL), lambda p: (0, p, 0)) for part in sums] + [
            pl.BlockSpec((base.shape[0], 128), lambda p: (0, p)) for base in bases
        ] + [
            pl.BlockSpec((3 * REL, 128), lambda p: (0, p)),
            pl.BlockSpec((qkv.shape[0], 128), lambda p: (0, p + side * pairs)),
        ],
        out_specs=(
            pl.BlockSpec((rows, 128), lambda p: (0, p)),
            pl.BlockSpec((3 * REL, 128), lambda p: (0, p)),
        ),
        out_shape=(
            jax.ShapeDtypeStruct((rows, width), bf16),
            jax.ShapeDtypeStruct((3 * REL, width), bf16),
        ),
        compiler_params=pltpu.CompilerParams(vmem_limit_bytes=VMEM_CAP),
        cost_estimate=pl.CostEstimate(flops=10**6, bytes_accessed=10**4, transcendentals=0),
        name="attention_close",
    )(*sums, *bases, pos, qkv)


def fill_turned(x_ref, turned, rows):
    depth = x_ref.shape[1]
    for a in range(0, rows, 128):
        tall = min(128, rows - a)
        for b in range(0, depth, 128):
            block = x_ref[a:a + tall, b:b + 128]
            if tall < 128:
                block = jnp.concatenate([block, jnp.zeros((128 - tall, 128), block.dtype)], axis=0)
            turned[b:b + 128, a:a + tall] = block.T[:, :tall]


def each_block(pick_ref, blocks, keeps, bit, slot):
    if not keeps:
        return [(0, d, d) for d in range(blocks)]
    shift = bit - 1
    listed = []
    for out in range(2):
        value = pick_ref[slot] if out == 1 else 1 - pick_ref[slot]
        for e in range(blocks // 2):
            low = e & ((1 << shift) - 1)
            listed.append((out, e, ((e >> shift) << (shift + 1)) + low + value * (1 << shift)))
    return listed


def weight_kernel(pick_ref, *refs, count, blocks, deep, keeps, bit, turn):
    xs, ys, rest = refs[:count], refs[count:2 * count], refs[2 * count:]
    add_ref = rest[0] if keeps else None
    outs = rest[1:3] if keeps else rest[0:1]
    turned = rest[-count:] if turn else xs

    if turn:
        @pl.when(pl.program_id(0) == 0)
        def _():
            for x_ref, wide in zip(xs, turned):
                fill_turned(x_ref, wide, x_ref.shape[0])

    for out, place, d in each_block(pick_ref, blocks, keeps, bit, 1):
        at = pl.ds(pl.multiple_of((2 * d + pick_ref[0]) * deep, deep), deep)
        part = add_ref[d] if keeps else None
        for wide, y_ref in zip(turned, ys):
            term = nn(wide[at, :], y_ref[...])
            part = term if part is None else part + term
        outs[out][place] = part


def weight_half(pick, xs, ys, add=None, *, parts, bits, tile=512, turn=True):
    depth = xs[0].shape[1 if turn else 0]
    wide = ys[0].shape[1]
    deep = depth // parts
    blocks = parts // 2
    keeps = add is not None

    def tiled(n):
        return pl.BlockSpec((n, deep, tile), lambda c: (0, 0, c))

    ins = [pl.BlockSpec(memory_space=pltpu.SMEM)]
    ins += [pl.BlockSpec(x.shape, lambda c: (0, 0)) for x in xs]
    ins += [pl.BlockSpec((y.shape[0], tile), lambda c: (0, c)) for y in ys]
    args = [pick, *xs, *ys]
    shape = (jax.ShapeDtypeStruct((blocks, deep, wide), f32),)
    specs = (tiled(blocks),)
    if keeps:
        ins.append(tiled(blocks))
        args += add
        shape = (jax.ShapeDtypeStruct((blocks // 2, deep, wide), f32),) * 2
        specs = (tiled(blocks // 2),) * 2
    rows = sum(y.shape[0] for y in ys)
    return pl.pallas_call(
        functools.partial(
            weight_kernel, count=len(xs), blocks=blocks, deep=deep, keeps=keeps, bit=bits[0], turn=turn
        ),
        grid=(wide // tile,),
        in_specs=ins,
        out_specs=specs,
        out_shape=shape,
        scratch_shapes=[pltpu.VMEM((depth, x.shape[0]), bf16) for x in xs] if turn else [],
        compiler_params=pltpu.CompilerParams(vmem_limit_bytes=VMEM_CAP),
        cost_estimate=pl.CostEstimate(
            flops=rows * depth * wide, bytes_accessed=4 * depth * wide, transcendentals=0
        ),
        name="weight_half",
    )(*args)


def many_kernel(pick_ref, *refs, plan, widths, turns, blocks, deep, keeps, bits):
    n_in = 2 * len(plan)
    ins = refs[:n_in]
    n_out = len(widths)
    adds = refs[n_in:n_in + n_out] if keeps else None
    outs = refs[n_in + n_out:n_in + 3 * n_out] if keeps else refs[n_in:n_in + n_out]
    scratch = refs[len(refs) - sum(turns):]
    left = []
    used = 0
    for n, turn in enumerate(turns):
        if turn:
            fill_turned(ins[2 * n], scratch[used], ins[2 * n].shape[0])
            left.append(scratch[used])
            used += 1
        else:
            left.append(ins[2 * n])
    right = [ins[2 * n + 1][...] for n in range(len(plan))]
    for group in range(n_out):
        for out, place, d in each_block(pick_ref, blocks, keeps, bits[group], 1 + group):
            at = pl.ds(pl.multiple_of((2 * d + pick_ref[0]) * deep, deep), deep)
            target = outs[2 * group + out] if keeps else outs[group]
            for n, (kind, own, start, wide) in enumerate(plan):
                if own != group:
                    continue
                rows = left[n][at, :]
                if kind == "copy":
                    part = rows
                elif kind == "nt":
                    part = nt(rows, right[n])
                else:
                    part = nn(rows, right[n])
                cut = slice(start, start + wide)
                if keeps:
                    part = part + adds[group][d, :, cut]
                target[place, :, cut] = part


def many_half(pick, pairs, plan, widths, add=None, *, parts, bits):
    whole = pl.BlockSpec(memory_space=pltpu.VMEM)
    turns = [kind in ("turn", "copy") for kind, *_ in plan]
    depth = max(left.shape[1 if turn else 0] for (left, _), turn in zip(pairs, turns))
    deep = depth // parts
    blocks = parts // 2
    keeps = add is not None
    args = [pick] + [operand for pair in pairs for operand in pair] + (list(add) if keeps else [])
    if keeps:
        shape = [jax.ShapeDtypeStruct((blocks // 2, deep, w), f32) for w in widths for _ in range(2)]
    else:
        shape = [jax.ShapeDtypeStruct((blocks, deep, w), f32) for w in widths]
    return pl.pallas_call(
        functools.partial(
            many_kernel, plan=plan, widths=widths, turns=turns, blocks=blocks, deep=deep,
            keeps=keeps, bits=[b[0] for b in bits],
        ),
        in_specs=[pl.BlockSpec(memory_space=pltpu.SMEM)] + [whole] * (len(args) - 1),
        out_specs=[whole] * len(shape),
        out_shape=shape,
        scratch_shapes=[
            pltpu.VMEM((left.shape[1], left.shape[0]), left.dtype)
            for (left, _), turn in zip(pairs, turns) if turn
        ],
        compiler_params=pltpu.CompilerParams(vmem_limit_bytes=VMEM_CAP),
        cost_estimate=pl.CostEstimate(flops=10**6, bytes_accessed=10**4, transcendentals=0),
        name="many_half",
    )(*args)


def flipped(value, bit, size):
    return lax.ppermute(value, "dp", [(i, i ^ (1 << bit)) for i in range(size)])


def bit_of(index, bit):
    return (index >> bit) & 1


class Halving:
    def __init__(self, make, index, size, orders):
        self.make, self.index, self.size, self.orders = make, index, size, orders
        mine = bit_of(index, 0).astype(jnp.int32)
        self.pick = jnp.stack([mine] + [bit_of(index, bits[0]).astype(jnp.int32) for bits in orders])
        self.other = self.pick.at[0].set(1 - mine)
        self.stage = 0
        self.extra = None

    def work(self):
        if self.stage == 0:
            self.pending = [(sent, None) for sent in self.make(self.other, None)]
        elif self.stage == 1:
            outs = self.make(self.pick, self.extra)
            self.pending = [(outs[2 * g], outs[2 * g + 1]) for g in range(len(self.orders))]
            self.axes = [
                [b for b in range(self.size.bit_length() - 1, 0, -1) if b != bits[0] and b < self.size.bit_length() - 1]
                for bits in self.orders
            ]
        else:
            self.pending = [
                self.split(g, held, extra) for g, (held, extra) in enumerate(zip(self.held, self.extra))
            ]
        return [part for pair in self.pending for part in pair if part is not None]

    def split(self, g, held, extra):
        bits = self.orders[g]
        if self.stage > len(bits):
            return held + extra, None
        bit = bits[self.stage - 1]
        axis = self.axes[g].index(bit)
        shape = (2,) * len(self.axes[g]) + held.shape[-2:]
        self.axes[g].remove(bit)
        own = bit_of(self.index, bit)
        held, extra = held.reshape(shape), extra.reshape(shape)

        def half(value, at):
            return lax.dynamic_index_in_dim(value, at, axis, keepdims=False)

        return half(held, 1 - own) + half(extra, 1 - own), half(held, own) + half(extra, own)

    def go(self, parts):
        parts = list(parts)
        pairs = [
            tuple(None if part is None else parts.pop(0) for part in pair) for pair in self.pending
        ]
        self.held = [home for _, home in pairs]
        last = self.stage > len(self.orders[0])
        if last:
            self.result = [away for away, _ in pairs]
        else:
            bit = lambda g: 0 if self.stage == 0 else self.orders[g][self.stage - 1]
            self.extra = [flipped(away, bit(g), self.size) for g, (away, _) in enumerate(pairs)]
        self.stage += 1

    def step(self):
        self.go(self.work())

    def over(self):
        return self.stage > len(self.orders[0]) + 1

    def finish(self):
        while not self.over():
            self.step()
        return self.result


def tie(values, *chains):
    chains = [chain for chain in chains if not chain.over()]
    values, extras = lax.optimization_barrier((values, [chain.extra for chain in chains]))
    for chain, extra in zip(chains, extras):
        chain.extra = extra
    works = [chain.work() for chain in chains]
    values, works = lax.optimization_barrier((values, works))
    for chain, parts in zip(chains, works):
        chain.go(parts)
    return values


def swap(value):
    return lax.ppermute(value.astype(f32), "mp", [(0, 1), (1, 0)])


def attend_kernel(
    t_ref, c_ref, o_ref, w_ref, ow_ref, gain_ref, shift_ref, first_ref, low_ref, normal_ref, inverse_ref,
    *, start,
):
    weight = ow_ref[...].astype(bf16)

    def body(step, carry):
        at = pl.ds(pl.multiple_of(step * 64, 64), 64)
        here = pl.ds(pl.multiple_of(start + step * 64, 64), 64)
        summed = t_ref[here, :].astype(f32) + nn(c_ref[at, :], w_ref[...])
        summed = summed + nn(o_ref[at, :].astype(bf16), weight)
        first, normal, inverse = norm_forward(summed, gain_ref[...], shift_ref[...])
        first_ref[at, :] = first
        low_ref[at, :] = first.astype(bf16)
        normal_ref[at, :] = normal
        inverse_ref[at, :] = inverse
        return carry

    lax.fori_loop(0, c_ref.shape[0] // 64, body, 0)


def attend(tokens, context, other, weight, other_weight, gain, shift, start):
    tall, depth = context.shape[0], tokens.shape[1]
    whole = pl.BlockSpec(memory_space=pltpu.VMEM)
    return pl.pallas_call(
        functools.partial(attend_kernel, start=start),
        in_specs=[whole] * 7,
        out_specs=(whole,) * 4,
        out_shape=(
            jax.ShapeDtypeStruct((tall, depth), f32),
            jax.ShapeDtypeStruct((tall, depth), bf16),
            jax.ShapeDtypeStruct((tall, depth), f32),
            jax.ShapeDtypeStruct((tall, 1), f32),
        ),
        compiler_params=pltpu.CompilerParams(vmem_limit_bytes=VMEM_CAP),
        cost_estimate=pl.CostEstimate(flops=2 * 10**9, bytes_accessed=8 * 10**6, transcendentals=0),
        name="attend",
    )(tokens, context, other, weight, other_weight, gain[None], shift[None])


def residual_kernel(
    s_ref, normal_ref, inverse_ref, gain_ref, w_ref, back_ref, low_ref, up_ref, sums_ref,
):
    upstream = s_ref[...]
    normal = normal_ref[...]
    scaled = upstream * gain_ref[...]
    inner = jnp.mean(scaled, axis=1, keepdims=True)
    aligned = jnp.mean(scaled * normal, axis=1, keepdims=True)
    back = inverse_ref[...] * (scaled - inner - normal * aligned)
    back_ref[...] = back
    low_ref[...] = back.astype(bf16)
    up_ref[...] = nt(back.astype(bf16), w_ref[...]).astype(bf16)

    @pl.when(pl.program_id(0) == 0)
    def _():
        sums_ref[...] = jnp.zeros_like(sums_ref)

    sums_ref[0:1, :] += jnp.sum(upstream * normal, axis=0, keepdims=True)
    sums_ref[1:2, :] += jnp.sum(upstream, axis=0, keepdims=True)


def residual(upstream, normal, inverse, gain, weight):
    tall, depth = upstream.shape
    width = weight.shape[0]
    row = pl.BlockSpec((64, depth), lambda r: (r, 0))

    def fixed(*shape):
        return pl.BlockSpec(shape, lambda r: (0, 0))

    return pl.pallas_call(
        residual_kernel,
        grid=(tall // 64,),
        in_specs=[row] * 2 + [pl.BlockSpec((64, 1), lambda r: (r, 0)), fixed(1, depth), fixed(width, depth)],
        out_specs=(row, row, pl.BlockSpec((64, width), lambda r: (r, 0)), fixed(8, depth)),
        out_shape=(
            jax.ShapeDtypeStruct((tall, depth), f32),
            jax.ShapeDtypeStruct((tall, depth), bf16),
            jax.ShapeDtypeStruct((tall, width), bf16),
            jax.ShapeDtypeStruct((8, depth), f32),
        ),
        compiler_params=pltpu.CompilerParams(vmem_limit_bytes=VMEM_CAP),
        cost_estimate=pl.CostEstimate(flops=10**6, bytes_accessed=10**4, transcendentals=0),
        name="residual",
    )(upstream, normal, inverse, gain[None], weight)


def norm_forward(summed, gain, shift):
    centred = summed - jnp.mean(summed, axis=1, keepdims=True)
    inverse = lax.rsqrt(jnp.mean(centred * centred, axis=1, keepdims=True) + epsilon)
    normal = centred * inverse
    return (normal * gain + shift, normal, inverse)


def norm_backward(upstream, normal, inverse, gain):
    scaled = upstream * gain
    inner = jnp.mean(scaled, axis=1, keepdims=True)
    aligned = jnp.mean(scaled * normal, axis=1, keepdims=True)
    return (
        inverse * (scaled - inner - normal * aligned),
        jnp.sum(upstream * normal, axis=0),
        jnp.sum(upstream, axis=0),
    )


def shards(
    tokens,
    query_weight,
    key_weight,
    value_weight,
    output_weight,
    query_position,
    key_position,
    position_tables,
    gain_one,
    shift_one,
    up_weight,
    down_weight,
    gain_two,
    shift_two,
    buckets,
    text_length,
    cotangent,
):
    span = buckets.shape[2]
    rows, cols = sizes(span)
    size = lax.axis_size("dp")
    index = lax.axis_index("dp")
    bits = list(range(1, size.bit_length() - 1))
    low_first, high_first = bits, bits[1:2] + bits[:1] + bits[2:]
    score_scale = (7.0 * HEAD) ** (-0.5)
    tables_flat = position_tables.reshape(3 * REL, D)
    width = query_weight.shape[1]
    spare = ((0, rows - span), (0, 0))

    def chain(make, *orders):
        return Halving(make, index, size, list(orders))

    split = rows // 2 // 128 * 128
    other_output = swap(output_weight)
    qkv, pos_key, pos_query = project(
        tokens, query_weight, key_weight, value_weight, position_tables, key_position, query_position, span
    )
    tokens = jnp.pad(tokens, spare)
    cotangent = jnp.pad(cotangent, spare)
    edges = [(0, split), (split, rows)]

    share_head, context_head, wide_head, bucket_head, bucket_rest, bucket_cols, far_rest, far_inverse = attention_head(
        qkv, pos_key, pos_query, buckets, text_length, score_scale, split
    )
    other_head = swap(wide_head)
    far_rest, other_output = lax.optimization_barrier((far_rest, other_output))
    share_rest, context_rest, wide_rest = attention_rest(
        qkv, pos_key, bucket_rest, far_rest, far_inverse, text_length, score_scale, split, span
    )
    other_rest = swap(wide_rest)
    shares = [share_head, share_rest]
    contexts = [context_head, context_rest]
    contexts_other = [other_head, other_rest]

    def gelu(value):
        return jax.nn.gelu(value, approximate=False)

    firsts, firsts_low, normals_one, inverses_one, upwards, hiddens, feeds, feeds_other = ([] for _ in range(8))
    for (low, high), context, other in zip(edges, contexts, contexts_other):
        first, first_low, normal_one, inverse_one = attend(
            tokens, context, other, output_weight, other_output, gain_one, shift_one, low
        )
        firsts.append(first)
        normals_one.append(normal_one)
        inverses_one.append(inverse_one)
        firsts_low.append(first_low)
        upwards.append(nn(firsts_low[-1], up_weight))
        hiddens.append(gelu(upwards[-1]).astype(bf16))
        feeds.append(nn(hiddens[-1], down_weight))
        feeds_other.append(swap(feeds[-1]))

    feeds[1], tokens_late, tables_late, firsts_late = lax.optimization_barrier(
        (feeds[1], tokens, tables_flat, firsts_low)
    )
    tokens_turned, tables_turned = tokens_late.T, tables_late.T
    firsts_turned = [first_low.T for first_low in firsts_late]
    finals, seconds_back, seconds_low, upwards_back, backs_part, backs_other, two_sums = ([] for _ in range(7))
    for n, (low, high) in enumerate(edges):
        final, normal_two, inverse_two = norm_forward(
            firsts[n] + feeds[n] + feeds_other[n], gain_two, shift_two
        )
        finals.append(final.astype(bf16))
        second_back, *sums = norm_backward(
            cotangent[low:high].astype(f32), normal_two, inverse_two, gain_two
        )
        two_sums.append(sums)
        seconds_back.append(second_back)
        seconds_low.append(second_back.astype(bf16))
        hidden_back = nt(seconds_low[n], down_weight)
        upwards_back.append(jax.vjp(gelu, upwards[n])[1](hidden_back)[0].astype(bf16))
        backs_part.append(nt(upwards_back[n], up_weight))
        backs_other.append(swap(backs_part[n]))
    layer_output = jnp.concatenate(finals, axis=0)[:span]
    gain_two_grad, shift_two_grad = (two_sums[0][n] + two_sums[1][n] for n in range(2))

    backs_part, down_pair, up_pair = lax.optimization_barrier(
        (backs_part, (seconds_low, hiddens), (firsts_turned, upwards_back))
    )
    up_pair, backs_other[0] = lax.optimization_barrier((up_pair, backs_other[0]))
    down_chain = chain(
        lambda pick, add: weight_half(pick, *down_pair, add, parts=size, bits=high_first), high_first
    )
    up_chain = chain(
        lambda pick, add: weight_half(pick, *up_pair, add, parts=size, bits=low_first, turn=False), low_first
    )
    down_chain.step()
    up_chain.step()
    backs_other[0] = tie(backs_other[0], down_chain)
    backs_other[0] = tie(backs_other[0], up_chain)
    merge = merge_table()
    residuals_back, residuals_low, one_sums = [], [], []

    def draw(n, adds=()):
        residual_back, residual_low, context_back, sums = residual(
            seconds_back[n] + backs_part[n] + backs_other[n], normals_one[n], inverses_one[n], gain_one, output_weight
        )
        one_sums.append(sums)
        residuals_back.append(residual_back)
        residuals_low.append(residual_low)
        return attention_draw(shares[n], context_back, qkv, score_scale, edges[n][0], rows, adds)

    back_head, turned_head, query_head, key_head, value_head = draw(0)
    back_head, key_head, backs_other[1] = lax.optimization_barrier((back_head, key_head, backs_other[1]))
    back_rest, turned_rest, query_rest, key_base, value_back = draw(1, (key_head, value_head))
    gain_one_grad, shift_one_grad = (one_sums[0][n] + one_sums[1][n] for n in range(2))
    back_rest, value_back = tie((back_rest, value_back), down_chain)
    residual_low = jnp.concatenate(residuals_low, axis=0)
    context = jnp.concatenate(contexts, axis=0)
    nothing = jnp.zeros_like(gain_one)
    gains = jnp.stack(
        [gain_one_grad, shift_one_grad, gain_two_grad, shift_two_grad] + [nothing] * 4
    )
    gains = jnp.concatenate([gains, jnp.zeros((120, gains.shape[1]), f32)], axis=0)
    dummy = jnp.zeros((8, 128), bf16)
    outer_chain = chain(
        lambda pick, add: many_half(
            pick,
            [(residual_low, context), (tokens_turned, value_back), (gains, dummy)],
            [("turn", 0, 0, width), ("nn", 0, width, width), ("copy", 0, 2 * width, 128)],
            [2 * width + 128],
            add, parts=size, bits=[low_first],
        ),
        low_first,
    )
    outer_chain.step()

    def tail(rows_back, sums, position, orders):
        return chain(
            lambda pick, add: many_half(
                pick,
                [(tokens_turned, rows_back), (tables_turned, sums), (position, sums)],
                [("nn", 0, 0, width), ("nn", 1, 0, width), ("nt", 0, width, 3 * REL)],
                [width + 3 * REL, width],
                add, parts=size, bits=orders,
            ),
            *orders,
        )

    near = []
    blocks = rows // 64
    near.append(attention_scatter([back_head], bucket_head, merge, 0, split // 64))
    back_rest, near = tie((back_rest, near), up_chain)
    back_rest, near = tie((back_rest, near), outer_chain)
    back_rest, near = tie((back_rest, near), down_chain)
    near.append(attention_scatter([back_rest], bucket_rest, merge, 0, blocks - split // 64))
    near, backs = tie((near, [turned_head, turned_rest]), up_chain)
    query_low, key_table_sum = attention_close(near, [query_head, query_rest], pos_key, qkv, 0)
    early = nt(query_low, query_weight) + nt(value_back, value_weight)
    near_chain = tail(query_low, key_table_sum, key_position, [high_first, low_first])
    backs, key_table_sum = tie((backs, key_table_sum), near_chain, outer_chain, down_chain)
    far = []
    cuts = [n * blocks // 3 for n in range(4)]
    for part, chains in enumerate(((near_chain,), (outer_chain, up_chain), (near_chain, outer_chain))):
        far.append(attention_scatter(backs, bucket_cols, merge, cuts[part], cuts[part + 1] - cuts[part]))
        backs, far = tie((backs, far), *chains)
    key_low, query_table_sum = attention_close(far, [key_base], pos_query, qkv, 1)
    key_low, query_table_sum = tie((key_low, query_table_sum), near_chain)
    far_chain = tail(key_low, query_table_sum, query_position, [low_first, high_first])
    parts, others = [], []
    for low, high in ((0, rows // 2), (rows // 2, rows)):
        parts.append(early[low:high] + nt(key_low[low:high], key_weight))
        others.append(swap(parts[-1]))
    far_chain.step()
    far_chain.step()
    far_chain.extra, others[0] = lax.optimization_barrier((far_chain.extra, others[0]))
    far_chain.extra = tie(far_chain.extra, near_chain)
    far_main, query_position_grad = far_chain.finish()
    far_main, others[1] = lax.optimization_barrier((far_main, others[1]))
    input_gradient = (
        jnp.concatenate(residuals_back, axis=0) + jnp.concatenate(parts, axis=0) + jnp.concatenate(others, axis=0)
    )[:span].astype(bf16)
    (down_share,) = down_chain.finish()
    (up_share,) = up_chain.finish()
    (outer_share,) = outer_chain.finish()
    near_main, key_position_grad = near_chain.finish()

    table_rows = near_main[:, width:] + far_main[:, width:]
    table_rows = table_rows.reshape(2, table_rows.shape[0] // 2, 3 * REL)
    side = lax.axis_index("mp")
    table_mine = lax.dynamic_index_in_dim(table_rows, side, 0, keepdims=False) + lax.ppermute(
        lax.dynamic_index_in_dim(table_rows, 1 - side, 0, keepdims=False), "mp", [(0, 1), (1, 0)]
    )
    table_gradient = table_mine.T.reshape(3, REL, table_mine.shape[0])
    gains_mine = outer_share[:, 2 * width:]
    return (
        layer_output,
        input_gradient,
        near_main[:, 0:width],
        far_main[:, 0:width],
        outer_share[:, width:2 * width],
        outer_share[:, 0:width].T,
        query_position_grad,
        key_position_grad,
        table_gradient,
        gains_mine[:, 0],
        gains_mine[:, 1],
        up_share,
        down_share.T,
        gains_mine[:, 2],
        gains_mine[:, 3],
    )


def solution(mesh):
    return jax.shard_map(
        shards,
        mesh=mesh,
        in_specs=(
            P("dp", None),
            P(None, "mp"),
            P(None, "mp"),
            P(None, "mp"),
            P("mp", None),
            P(None, "mp"),
            P(None, "mp"),
            P(),
            P(),
            P(),
            P(None, "mp"),
            P("mp", None),
            P(),
            P(),
            P("dp", None, None, None),
            P("dp"),
            P("dp", None),
        ),
        out_specs=(
            P("dp", None),
            P("dp", None),
            P("dp", "mp"),
            P("dp", "mp"),
            P("dp", "mp"),
            P("mp", "dp"),
            P("dp", "mp"),
            P("dp", "mp"),
            P(None, None, ("dp", "mp")),
            P("dp"),
            P("dp"),
            P("dp", "mp"),
            P("mp", "dp"),
            P("dp"),
            P("dp"),
        ),
        check_vma=False,
    )
```

```python
import functools

import jax
import jax.numpy as jnp
from jax import lax
from jax.experimental import pallas as pl
from jax.experimental.pallas import tpu as pltpu
from jax.sharding import PartitionSpec as P

D = 1024
epsilon = 1e-05
HEAD = 64
REL = 128
TEXT = 512
bf16 = jnp.bfloat16
f32 = jnp.float32
LIMIT = 10900.0
VMEM_CAP = 62 * 2**20
STEPS = 4


def lane_gather(table, index):
    numbers = lax.GatherDimensionNumbers(
        offset_dims=(),
        collapsed_slice_dims=(1,),
        start_index_map=(1,),
        operand_batching_dims=(0,),
        start_indices_batching_dims=(0,),
    )
    return lax.gather(
        table, index[..., None], numbers, (1, 1), mode=lax.GatherScatterMode.PROMISE_IN_BOUNDS
    )


def nt(left, right):
    return lax.dot_general(left, right, (((1,), (1,)), ((), ())), preferred_element_type=f32)


def nn(left, right):
    return jnp.dot(left, right, preferred_element_type=f32)


def tn(left, right):
    return lax.dot_general(left, right, (((0,), (0,)), ((), ())), preferred_element_type=f32)


def lane_half(shape):
    return lax.broadcasted_iota(jnp.int32, shape, len(shape) - 1) < HEAD


def unpack_pair(packed):
    low = (packed << 16) >> 16
    high = (packed - low) >> 16
    return high.astype(f32), low.astype(f32)


def fill_tables(src_ref, first, tall, pos_ref, tab, inv, pairs):
    half = lane_half((64, 128))

    def body(step, carry):
        at = pl.ds(pl.multiple_of(step * 64, 64), 64)
        for p in range(pairs):
            cut = slice(p * 128, (p + 1) * 128)
            block = src_ref[pl.ds(pl.multiple_of(first + step * 64, 64), 64), cut]
            zero = jnp.zeros_like(block)
            first_head = nt(jnp.where(half, block, zero), pos_ref[:, cut]).astype(bf16).astype(f32)
            second_head = nt(jnp.where(half, zero, block), pos_ref[:, cut]).astype(bf16).astype(f32)
            top0 = jnp.maximum(jnp.max(jnp.abs(first_head), axis=1, keepdims=True), 1e-30)
            top1 = jnp.maximum(jnp.max(jnp.abs(second_head), axis=1, keepdims=True), 1e-30)
            whole0 = jnp.round(first_head * (LIMIT / top0)).astype(jnp.int32)
            whole1 = jnp.round(second_head * (LIMIT / top1)).astype(jnp.int32)
            tab[p, at, :] = whole0 * 65536 + whole1
            inv[2 * p, at, :] = jnp.broadcast_to(top0 * (1.0 / LIMIT), (64, 128))
            inv[2 * p + 1, at, :] = jnp.broadcast_to(top1 * (1.0 / LIMIT), (64, 128))
        return carry

    lax.fori_loop(0, tall // 64, body, 0)


def look_up(tab, index_ref, at, store, *, pairs, cols):
    for c in range(cols // 128):
        total = [None] * pairs
        for r in range(3):
            index = index_ref[r, at, c * 128:(c + 1) * 128]
            for p in range(pairs):
                got = lane_gather(tab[p, at, r * 128:(r + 1) * 128], index)
                total[p] = got if total[p] is None else total[p] + got
        for p in range(pairs):
            store(p, c, total[p])


def prepare_rows(
    k_ref, pq_ref, b_ref, head_ref, rest_ref, bt_ref, far_head, far_rest, inv_ref,
    far_tab, far_inv, *, span, rows, cols, pairs, split,
):
    edge = span - span % 8 - split
    for r in range(3):
        head_ref[r, :, span - span % 128:cols] = jnp.zeros((split, cols - span + span % 128), jnp.int32)
        rest_ref[r, edge:rows - split, :] = jnp.zeros((rows - split - edge, cols), jnp.int32)
        rest_ref[r, :, span - span % 128:cols] = jnp.zeros((rows - split, cols - span + span % 128), jnp.int32)
        head_ref[r, :, 0:span] = b_ref[0, r, 0:split]
        rest_ref[r, 0:span - split, 0:span] = b_ref[0, r, split:span]
    for r in range(3):
        for jb in range(cols // 128):
            high = min(128, rows - jb * 128)
            for ib in range(cols // 128):
                tall = min(128, rows - ib * 128)
                here = slice(jb * 128, (jb + 1) * 128)
                if ib * 128 < split:
                    block = head_ref[r, ib * 128:ib * 128 + tall, here]
                else:
                    block = rest_ref[r, ib * 128 - split:ib * 128 - split + tall, here]
                if tall < 128:
                    block = jnp.concatenate([block, jnp.zeros((128 - tall, 128), jnp.int32)], axis=0)
                bt_ref[r, jb * 128:jb * 128 + high, ib * 128:(ib + 1) * 128] = block.T[:high]
    fill_tables(k_ref, 0, rows, pq_ref, far_tab, far_inv, pairs)

    def far_body(step, carry):
        for turn in range(STEPS):
            at = pl.ds(pl.multiple_of(step * 8 * STEPS + turn * 8, 8), 8)

            def store(p, c, total, at=at):
                if c * 128 < split:
                    far_head[p, at, c * 128:(c + 1) * 128] = total
                else:
                    far_rest[p, at, c * 128 - split:(c + 1) * 128 - split] = total

            look_up(far_tab, bt_ref, at, store, pairs=pairs, cols=cols)
        return carry

    lax.fori_loop(0, rows // (8 * STEPS), far_body, 0)
    for p in range(pairs):
        far_head[p, rows:, :] = jnp.zeros((cols - rows, split), jnp.int32)
        far_rest[p, rows:, :] = jnp.zeros((cols - rows, cols - split), jnp.int32)
    for h in range(2 * pairs):
        inv_ref[h:h + 1, :] = jnp.concatenate(
            [far_inv[h, j * 128:min(rows, (j + 1) * 128), :].T[0:1] for j in range(cols // 128 - 1)]
            + [jnp.concatenate([far_inv[h, cols - 128:rows, :],
                                jnp.zeros((cols - rows, 128), f32)], axis=0).T[0:1]], axis=1)


def forward_rows(
    used_ref, q_ref, k_ref, v_ref, pk_ref, b_ref, far_sum, inv_ref, p_ref, ctx_ref, wide_ref,
    near_tab, near_inv, near_sum, score, *, first, rows, span, cols, pairs, scale,
):
    fill_tables(q_ref, first, rows, pk_ref, near_tab, near_inv, pairs)
    used = used_ref[0]
    place = lax.broadcasted_iota(jnp.int32, (1, cols), 1)
    valid = ((place >= TEXT) & (place < span)) | (place < used)

    def block_body(start, tall):
        def near_body(step, carry):
            for turn in range(STEPS):
                at = pl.ds(pl.multiple_of(start + step * 8 * STEPS + turn * 8, 8), 8)
                out_at = pl.ds(pl.multiple_of(step * 8 * STEPS + turn * 8, 8), 8)

                def store(p, c, total, out_at=out_at):
                    near_sum[p, out_at, c * 128:(c + 1) * 128] = total

                look_up(near_tab, b_ref, at, store, pairs=pairs, cols=cols)
            return carry

        lax.fori_loop(0, tall // (8 * STEPS), near_body, 0)
        at = pl.ds(start, tall)
        for p in range(pairs):
            cut = slice(p * 128, (p + 1) * 128)
            block = q_ref[pl.ds(pl.multiple_of(first + start, 64), tall), cut]
            zero = jnp.zeros_like(block)
            mask = lane_half((tall, 128))
            score[0, 0:tall, :] = nt(jnp.where(mask, block, zero), k_ref[:, cut])
            score[1, 0:tall, :] = nt(jnp.where(mask, zero, block), k_ref[:, cut])
            for c in range(cols // 128):
                turned = far_sum[p, c * 128:(c + 1) * 128, pl.ds(start, 128)].T[0:tall]
                here = slice(c * 128, (c + 1) * 128)
                f0, f1 = unpack_pair(turned)
                n0, n1 = unpack_pair(near_sum[p, 0:tall, here])
                score[0, 0:tall, here] += (
                    f0 * inv_ref[2 * p:2 * p + 1, here] + n0 * near_inv[2 * p, at, :]
                )
                score[1, 0:tall, here] += (
                    f1 * inv_ref[2 * p + 1:2 * p + 2, here] + n1 * near_inv[2 * p + 1, at, :]
                )
            for h in range(2):
                for s in range(tall // 16):
                    raw = score[h, s * 16:(s + 1) * 16, :]
                    logits = jnp.where(valid, raw * scale, -1e30)
                    top = jnp.max(logits, axis=1, keepdims=True)
                    grown = jnp.exp(logits - top)
                    share = grown * (1.0 / jnp.sum(grown, axis=1, keepdims=True))
                    p_ref[2 * p + h, pl.ds(pl.multiple_of(start + s * 16, 16), 16), :] = share.astype(bf16)
            c0 = nn(p_ref[2 * p, at, :], v_ref[:, cut])
            c1 = nn(p_ref[2 * p + 1, at, :], v_ref[:, cut])
            context = jnp.where(mask, c0, c1).astype(bf16)
            ctx_ref[at, cut] = context
            wide_ref[at, cut] = context.astype(f32)

    def outer(step, carry):
        block_body(pl.multiple_of(step * 128, 128), 128)
        return carry

    lax.fori_loop(0, rows // 128, outer, 0)
    if rows % 128:
        block_body(rows - rows % 128, rows % 128)


def project_kernel(x_ref, wq_ref, wk_ref, wv_ref, t_ref, kp_ref, qp_ref, qkv_ref, pk_ref, pq_ref, *, span, cols, width):
    tail = span - span % 128
    qkv_ref[span - span % 16:cols, :] = jnp.zeros((cols - span + span % 16, 3 * width), bf16)
    for n, w_ref in enumerate((wq_ref, wk_ref, wv_ref)):
        cut = slice(n * width, (n + 1) * width)

        def body(step, carry, cut=cut, w_ref=w_ref):
            at = pl.ds(pl.multiple_of(step * 128, 128), 128)
            qkv_ref[at, cut] = nn(x_ref[at, :], w_ref[...]).astype(bf16)
            return carry

        lax.fori_loop(0, span // 128, body, 0)
        if tail < span:
            qkv_ref[tail:span, cut] = nn(x_ref[tail:span, :], w_ref[...]).astype(bf16)
    for r in range(3):
        at = slice(r * REL, (r + 1) * REL)
        pk_ref[at, :] = nn(t_ref[r], kp_ref[...]).astype(bf16)
        pq_ref[at, :] = nn(t_ref[r], qp_ref[...]).astype(bf16)


def project(tokens, query_weight, key_weight, value_weight, tables, key_position, query_position, span):
    width = query_weight.shape[1]
    rows, cols = sizes(span)
    whole = pl.BlockSpec(memory_space=pltpu.VMEM)
    return pl.pallas_call(
        functools.partial(project_kernel, span=span, cols=cols, width=width),
        out_shape=(
            jax.ShapeDtypeStruct((cols, 3 * width), bf16),
            jax.ShapeDtypeStruct((3 * REL, width), bf16),
            jax.ShapeDtypeStruct((3 * REL, width), bf16),
        ),
        in_specs=[whole] * 7,
        out_specs=(whole,) * 3,
        compiler_params=pltpu.CompilerParams(vmem_limit_bytes=VMEM_CAP),
        cost_estimate=pl.CostEstimate(flops=4 * 10**9, bytes_accessed=9 * 10**6, transcendentals=0),
        name="project",
    )(tokens, query_weight, key_weight, value_weight, tables, key_position, query_position)


def pick(half, block, h):
    zero = jnp.zeros_like(block)
    return jnp.where(half, block, zero) if h == 0 else jnp.where(half, zero, block)


def draw_kernel(
    p_ref, up_ref, q_ref, k_ref, v_ref, *refs, first, tall, rows, cols, scale, adds,
):
    extra = refs[:adds]
    d_ref, dt_ref, dq_ref, dk_ref, dv_ref, wide, flat, turned = refs[adds:]
    lanes = turned.shape[2]
    half = lane_half((64, 128))

    def body(step, carry):
        at = pl.ds(pl.multiple_of(step * 64, 64), 64)
        pair = []
        for h in range(2):
            reach = nt(pick(half, up_ref[at, :], h), v_ref[...])
            share = p_ref[h, at, :].astype(f32)
            inner = jnp.sum(reach * share, axis=1, keepdims=True)
            back = share * (reach - inner) * scale
            wide[h, at, :] = back
            flat[h, at, :] = back.astype(bf16)
            pair.append(back.reshape(8, 8, cols))
        d_ref[pl.ds(pl.multiple_of(step * 8, 8), 8), :, :] = jnp.concatenate(pair, axis=1).astype(bf16)
        return carry

    lax.fori_loop(0, tall // 64, body, 0)
    for jb in range(cols // 128):
        high = min(128, rows - jb * 128)
        for ib in range(lanes // 128):
            wide_rows = min(128, tall - ib * 128)
            pair = []
            for h in range(2):
                block = wide[h, ib * 128:ib * 128 + wide_rows, jb * 128:(jb + 1) * 128]
                if wide_rows < 128:
                    block = jnp.concatenate([block, jnp.zeros((128 - wide_rows, 128), f32)], axis=0)
                other = block.T[:high]
                turned[h, jb * 128:jb * 128 + high, ib * 128:(ib + 1) * 128] = other.astype(bf16)
                pair.append(other.reshape(high // 8, 8, 128))
            dt_ref[jb * 16:jb * 16 + high // 8, :, ib * 128:(ib + 1) * 128] = jnp.concatenate(
                pair, axis=1
            ).astype(bf16)
    keys, queries, ups = k_ref[...], q_ref[first:first + lanes, :], up_ref[...]
    cols_half, lanes_half, tall_half = (lane_half((n, 128)) for n in (cols, lanes, tall))
    dq_ref[...] = nn(flat[0], pick(cols_half, keys, 0)) + nn(flat[1], pick(cols_half, keys, 1))
    dk = nn(turned[0], pick(lanes_half, queries, 0)) + nn(turned[1], pick(lanes_half, queries, 1))
    dv = tn(p_ref[0], pick(tall_half, ups, 0)) + tn(p_ref[1], pick(tall_half, ups, 1))
    dv = dv[:rows]
    if adds:
        dk, dv = dk + extra[0][...], dv + extra[1][...]
    dk_ref[...] = dk
    dv_ref[...] = dv.astype(dv_ref.dtype)


def scatter_kernel(*refs, groups, cols):
    *d_refs, b_ref, merge_ref, out_ref = refs
    base = jnp.where(lax.broadcasted_iota(jnp.int32, (16, cols), 0) >= 8, 1.0, 0.0).astype(bf16)
    own = (lax.broadcasted_iota(jnp.int32, (256, 256), 0) % 8) == (
        lax.broadcasted_iota(jnp.int32, (256, 256), 1) % 8
    )
    zero = jnp.asarray(0.0, bf16)
    one = jnp.asarray(1.0, bf16)

    def sieve(g, r, back):
        bucket = b_ref[r, pl.ds(pl.multiple_of(g * 8, 8), 8), :]
        low = (bucket & 31).astype(f32)
        high = (bucket >> 5).astype(f32)
        low = jnp.concatenate([low, low], axis=0).astype(bf16) - base
        high = jnp.concatenate([high, high], axis=0).astype(bf16)
        hot = jnp.concatenate(
            [jnp.where(low == jnp.asarray(2.0 * k, bf16), one, zero) for k in range(16)], axis=0
        )
        sieved = []
        for l in range(4):
            mask = high == jnp.asarray(float(l), bf16)
            for p in range(4):
                sieved.append(jnp.where(mask, back[p * 16:(p + 1) * 16], zero))
        sums = nt(jnp.concatenate(sieved, axis=0), hot)
        return jnp.where(own, sums, 0.0).astype(bf16)

    def body(step, carry):
        got = []
        for g in (2 * step, 2 * step + 1):
            back = jnp.concatenate([d_ref[g] for d_ref in d_refs], axis=1) if len(d_refs) > 1 else d_refs[0][g]
            for r in range(3):
                got.append((g, r, sieve(g, r, back)))
        for g, r, sums in got:
            total = None
            for l in range(4):
                term = nn(sums[l * 64:(l + 1) * 64], merge_ref[l])
                total = term if total is None else total + term
            out_ref[g, :, r * 128:(r + 1) * 128] = total.astype(bf16)
        return carry

    lax.fori_loop(0, groups // 2, body, 0)


def close_kernel(*refs, rows, count):
    *base_refs, pos_ref, side_ref, out_ref, table_ref = refs[count:]
    rows2 = 2 * rows
    half3 = lane_half((rows // 8, 8, 128))
    flat = jnp.concatenate([ref[...] for ref in refs[:count]], axis=0).reshape(rows2, 3 * REL)
    both = nn(flat, pos_ref[...]).reshape(rows // 8, 16, 128)
    mine = jnp.where(half3, both[:, 0:8, :], both[:, 8:16, :]).reshape(rows, 128)
    first = 0
    for base_ref in base_refs:
        here = slice(first, first + base_ref.shape[0])
        out_ref[here, :] = (base_ref[...] + mine[here]).astype(bf16)
        first += base_ref.shape[0]
    side = side_ref[0:rows, :].astype(f32).reshape(rows // 8, 8, 128)
    zero = jnp.zeros_like(side)
    spread = jnp.concatenate([jnp.where(half3, side, zero), jnp.where(half3, zero, side)], axis=1)
    table_ref[...] = tn(flat, spread.reshape(rows2, 128).astype(bf16)).astype(bf16)


def merge_table():
    l = lax.broadcasted_iota(jnp.int32, (4, 256, 128), 0)
    a = lax.broadcasted_iota(jnp.int32, (4, 256, 128), 1) // 8
    c = lax.broadcasted_iota(jnp.int32, (4, 256, 128), 2)
    return (c == l * 32 + a).astype(bf16)


def sizes(span):
    return -(-span // 64) * 64, -(-span // 128) * 128


def forward_scratch(pairs, tall, cols):
    return [
        pltpu.VMEM((pairs, tall, 3 * REL), jnp.int32),
        pltpu.VMEM((2 * pairs, tall, 128), f32),
        pltpu.VMEM((pairs, 128, cols), jnp.int32),
        pltpu.VMEM((2, 128, cols), f32),
    ]


def attention_head(qkv, pos_key, pos_query, buckets, used, scale, split):
    span = buckets.shape[2]
    rows, cols = sizes(span)
    width = pos_key.shape[1]
    pairs = width // 128
    whole = pl.BlockSpec(memory_space=pltpu.VMEM)
    i32 = jnp.int32

    def kernel(
        used_ref, qkv_ref, pk_ref, pq_ref, b_ref, p_ref, ctx_ref, wide_ref, head_ref, rest_ref, bt_ref, far_rest,
        inv_ref, far_tab, far_inv, far_head, *scratch,
    ):
        k_ref = qkv_ref.at[:, width:2 * width]
        prepare_rows(
            k_ref, pq_ref, b_ref, head_ref, rest_ref, bt_ref, far_head, far_rest, inv_ref, far_tab, far_inv,
            span=span, rows=rows, cols=cols, pairs=pairs, split=split,
        )
        forward_rows(
            used_ref, qkv_ref.at[:, 0:width], k_ref, qkv_ref.at[:, 2 * width:3 * width], pk_ref, head_ref,
            far_head, inv_ref, p_ref, ctx_ref, wide_ref, *scratch,
            first=0, rows=split, span=span, cols=cols, pairs=pairs, scale=scale,
        )

    return pl.pallas_call(
        kernel,
        out_shape=(
            jax.ShapeDtypeStruct((2 * pairs, split, cols), bf16),
            jax.ShapeDtypeStruct((split, width), bf16),
            jax.ShapeDtypeStruct((split, width), f32),
            jax.ShapeDtypeStruct((3, split, cols), i32),
            jax.ShapeDtypeStruct((3, rows - split, cols), i32),
            jax.ShapeDtypeStruct((3, rows, cols), i32),
            jax.ShapeDtypeStruct((pairs, cols, cols - split), i32),
            jax.ShapeDtypeStruct((2 * pairs, cols), f32),
        ),
        in_specs=[pl.BlockSpec(memory_space=pltpu.SMEM)] + [whole] * 4,
        out_specs=(whole,) * 8,
        scratch_shapes=[
            pltpu.VMEM((pairs, rows, 3 * REL), i32),
            pltpu.VMEM((2 * pairs, rows, 128), f32),
            pltpu.VMEM((pairs, cols, split), i32),
        ] + forward_scratch(pairs, split, cols),
        compiler_params=pltpu.CompilerParams(vmem_limit_bytes=VMEM_CAP),
        cost_estimate=pl.CostEstimate(flops=4 * 10**10, bytes_accessed=25000000, transcendentals=0),
        name="attention_head",
    )(used, qkv, pos_key, pos_query, buckets)


def attention_rest(qkv, pos_key, bucket_rest, far_rest, inverse, used, scale, split, span):
    rows, cols = sizes(span)
    width = pos_key.shape[1]
    pairs = width // 128
    whole = pl.BlockSpec(memory_space=pltpu.VMEM)

    def kernel(used_ref, qkv_ref, pk_ref, b_ref, far_ref, inv_ref, p_ref, ctx_ref, wide_ref, *scratch):
        forward_rows(
            used_ref, qkv_ref.at[:, 0:width], qkv_ref.at[:, width:2 * width], qkv_ref.at[:, 2 * width:3 * width],
            pk_ref, b_ref, far_ref, inv_ref, p_ref, ctx_ref, wide_ref, *scratch,
            first=split, rows=rows - split, span=span, cols=cols, pairs=pairs, scale=scale,
        )

    return pl.pallas_call(
        kernel,
        out_shape=(
            jax.ShapeDtypeStruct((2 * pairs, rows - split, cols), bf16),
            jax.ShapeDtypeStruct((rows - split, width), bf16),
            jax.ShapeDtypeStruct((rows - split, width), f32),
        ),
        in_specs=[pl.BlockSpec(memory_space=pltpu.SMEM)] + [whole] * 5,
        out_specs=(whole,) * 3,
        scratch_shapes=forward_scratch(pairs, rows - split, cols),
        compiler_params=pltpu.CompilerParams(vmem_limit_bytes=VMEM_CAP),
        cost_estimate=pl.CostEstimate(flops=2 * 10**10, bytes_accessed=12000000, transcendentals=0),
        name="attention_rest",
    )(used, qkv, pos_key, bucket_rest, far_rest, inverse)


def attention_draw(share, upstream, qkv, scale, first, rows, adds=()):
    heads, tall, cols = share.shape
    width = upstream.shape[1]
    pairs = heads // 2
    lanes = -(-tall // 128) * 128

    def column(n):
        return pl.BlockSpec((n, 128), lambda p: (0, p))

    return pl.pallas_call(
        functools.partial(draw_kernel, first=first, tall=tall, rows=rows, cols=cols, scale=scale, adds=len(adds)),
        grid=(pairs,),
        in_specs=[
            pl.BlockSpec((2, tall, cols), lambda p: (p, 0, 0)),
            column(tall),
            pl.BlockSpec((cols, 128), lambda p: (0, p)),
            pl.BlockSpec((cols, 128), lambda p: (0, p + pairs)),
            pl.BlockSpec((cols, 128), lambda p: (0, p + 2 * pairs)),
        ] + [column(rows)] * len(adds),
        out_specs=(
            pl.BlockSpec((tall // 8, 16, cols), lambda p: (0, p, 0)),
            pl.BlockSpec((rows // 8, 16, lanes), lambda p: (0, p, 0)),
            column(tall), column(rows), column(rows),
        ),
        out_shape=(
            jax.ShapeDtypeStruct((tall // 8, 8 * heads, cols), bf16),
            jax.ShapeDtypeStruct((rows // 8, 8 * heads, lanes), bf16),
            jax.ShapeDtypeStruct((tall, width), f32),
            jax.ShapeDtypeStruct((rows, width), f32),
            jax.ShapeDtypeStruct((rows, width), bf16 if adds else f32),
        ),
        scratch_shapes=[
            pltpu.VMEM((2, tall, cols), f32),
            pltpu.VMEM((2, tall, cols), bf16),
            pltpu.VMEM((2, rows, lanes), bf16),
        ],
        compiler_params=pltpu.CompilerParams(vmem_limit_bytes=VMEM_CAP),
        cost_estimate=pl.CostEstimate(flops=10**6, bytes_accessed=10**4, transcendentals=0),
        name="attention_draw",
    )(share, upstream, qkv, qkv, qkv, *adds)


def attention_scatter(backs, buckets, merge, first, count):
    high = backs[0].shape[1]
    cols = buckets.shape[2]
    return pl.pallas_call(
        functools.partial(scatter_kernel, groups=8, cols=cols),
        grid=(count,),
        out_shape=jax.ShapeDtypeStruct((8 * count, high, 3 * REL), bf16),
        in_specs=[pl.BlockSpec((8, high, b.shape[2]), lambda g: (first + g, 0, 0)) for b in backs] + [
            pl.BlockSpec((3, 64, cols), lambda g: (0, first + g, 0)),
            pl.BlockSpec(merge.shape, lambda g: (0, 0, 0)),
        ],
        out_specs=pl.BlockSpec((8, high, 3 * REL), lambda g: (g, 0, 0)),
        compiler_params=pltpu.CompilerParams(vmem_limit_bytes=VMEM_CAP),
        cost_estimate=pl.CostEstimate(flops=10**6, bytes_accessed=10**4, transcendentals=0),
        name="attention_scatter",
    )(*backs, buckets, merge)


def attention_close(sums, bases, pos, qkv, side):
    rows, width = sum(base.shape[0] for base in bases), bases[0].shape[1]
    pairs = width // 128
    return pl.pallas_call(
        functools.partial(close_kernel, rows=rows, count=len(sums)),
        grid=(pairs,),
        in_specs=[pl.BlockSpec((part.shape[0], 16, 3 * REL), lambda p: (0, p, 0)) for part in sums] + [
            pl.BlockSpec((base.shape[0], 128), lambda p: (0, p)) for base in bases
        ] + [
            pl.BlockSpec((3 * REL, 128), lambda p: (0, p)),
            pl.BlockSpec((qkv.shape[0], 128), lambda p: (0, p + side * pairs)),
        ],
        out_specs=(
            pl.BlockSpec((rows, 128), lambda p: (0, p)),
            pl.BlockSpec((3 * REL, 128), lambda p: (0, p)),
        ),
        out_shape=(
            jax.ShapeDtypeStruct((rows, width), bf16),
            jax.ShapeDtypeStruct((3 * REL, width), bf16),
        ),
        compiler_params=pltpu.CompilerParams(vmem_limit_bytes=VMEM_CAP),
        cost_estimate=pl.CostEstimate(flops=10**6, bytes_accessed=10**4, transcendentals=0),
        name="attention_close",
    )(*sums, *bases, pos, qkv)


def fill_turned(x_ref, turned, rows):
    depth = x_ref.shape[1]
    for a in range(0, rows, 128):
        tall = min(128, rows - a)
        for b in range(0, depth, 128):
            block = x_ref[a:a + tall, b:b + 128]
            if tall < 128:
                block = jnp.concatenate([block, jnp.zeros((128 - tall, 128), block.dtype)], axis=0)
            turned[b:b + 128, a:a + tall] = block.T[:, :tall]


def each_block(pick_ref, blocks, keeps, bit, slot):
    if not keeps:
        return [(0, d, d) for d in range(blocks)]
    shift = bit - 1
    listed = []
    for out in range(2):
        value = pick_ref[slot] if out == 1 else 1 - pick_ref[slot]
        for e in range(blocks // 2):
            low = e & ((1 << shift) - 1)
            listed.append((out, e, ((e >> shift) << (shift + 1)) + low + value * (1 << shift)))
    return listed


def weight_kernel(pick_ref, *refs, count, blocks, deep, keeps, bit):
    xs, ys, rest = refs[:count], refs[count:2 * count], refs[2 * count:]
    add_ref = rest[0] if keeps else None
    outs = rest[1:3] if keeps else rest[0:1]
    turned = rest[-count:]

    @pl.when(pl.program_id(0) == 0)
    def _():
        for x_ref, wide in zip(xs, turned):
            fill_turned(x_ref, wide, x_ref.shape[0])

    for out, place, d in each_block(pick_ref, blocks, keeps, bit, 1):
        at = pl.ds(pl.multiple_of((2 * d + pick_ref[0]) * deep, deep), deep)
        part = add_ref[d] if keeps else None
        for wide, y_ref in zip(turned, ys):
            term = nn(wide[at, :], y_ref[...])
            part = term if part is None else part + term
        outs[out][place] = part


def weight_half(pick, xs, ys, add=None, *, parts, bits, tile=512):
    depth = xs[0].shape[1]
    wide = ys[0].shape[1]
    deep = depth // parts
    blocks = parts // 2
    keeps = add is not None

    def tiled(n):
        return pl.BlockSpec((n, deep, tile), lambda c: (0, 0, c))

    ins = [pl.BlockSpec(memory_space=pltpu.SMEM)]
    ins += [pl.BlockSpec(x.shape, lambda c: (0, 0)) for x in xs]
    ins += [pl.BlockSpec((y.shape[0], tile), lambda c: (0, c)) for y in ys]
    args = [pick, *xs, *ys]
    shape = (jax.ShapeDtypeStruct((blocks, deep, wide), f32),)
    specs = (tiled(blocks),)
    if keeps:
        ins.append(tiled(blocks))
        args += add
        shape = (jax.ShapeDtypeStruct((blocks // 2, deep, wide), f32),) * 2
        specs = (tiled(blocks // 2),) * 2
    rows = sum(x.shape[0] for x in xs)
    return pl.pallas_call(
        functools.partial(weight_kernel, count=len(xs), blocks=blocks, deep=deep, keeps=keeps, bit=bits[0]),
        grid=(wide // tile,),
        in_specs=ins,
        out_specs=specs,
        out_shape=shape,
        scratch_shapes=[pltpu.VMEM((depth, x.shape[0]), bf16) for x in xs],
        compiler_params=pltpu.CompilerParams(vmem_limit_bytes=VMEM_CAP),
        cost_estimate=pl.CostEstimate(
            flops=rows * depth * wide, bytes_accessed=4 * depth * wide, transcendentals=0
        ),
        name="weight_half",
    )(*args)


def many_kernel(pick_ref, *refs, plan, widths, turns, blocks, deep, keeps, bits):
    n_in = 2 * len(plan)
    ins = refs[:n_in]
    n_out = len(widths)
    adds = refs[n_in:n_in + n_out] if keeps else None
    outs = refs[n_in + n_out:n_in + 3 * n_out] if keeps else refs[n_in:n_in + n_out]
    scratch = refs[len(refs) - sum(turns):]
    left = []
    used = 0
    for n, turn in enumerate(turns):
        if turn:
            fill_turned(ins[2 * n], scratch[used], ins[2 * n].shape[0])
            left.append(scratch[used])
            used += 1
        else:
            left.append(ins[2 * n])
    right = [ins[2 * n + 1][...] for n in range(len(plan))]
    for group in range(n_out):
        for out, place, d in each_block(pick_ref, blocks, keeps, bits[group], 1 + group):
            at = pl.ds(pl.multiple_of((2 * d + pick_ref[0]) * deep, deep), deep)
            target = outs[2 * group + out] if keeps else outs[group]
            for n, (kind, own, start, wide) in enumerate(plan):
                if own != group:
                    continue
                rows = left[n][at, :]
                if kind == "copy":
                    part = rows
                elif kind == "nt":
                    part = nt(rows, right[n])
                else:
                    part = nn(rows, right[n])
                cut = slice(start, start + wide)
                if keeps:
                    part = part + adds[group][d, :, cut]
                target[place, :, cut] = part


def many_half(pick, pairs, plan, widths, add=None, *, parts, bits):
    whole = pl.BlockSpec(memory_space=pltpu.VMEM)
    turns = [kind in ("turn", "copy") for kind, *_ in plan]
    depth = max(left.shape[1 if turn else 0] for (left, _), turn in zip(pairs, turns))
    deep = depth // parts
    blocks = parts // 2
    keeps = add is not None
    args = [pick] + [operand for pair in pairs for operand in pair] + (list(add) if keeps else [])
    if keeps:
        shape = [jax.ShapeDtypeStruct((blocks // 2, deep, w), f32) for w in widths for _ in range(2)]
    else:
        shape = [jax.ShapeDtypeStruct((blocks, deep, w), f32) for w in widths]
    return pl.pallas_call(
        functools.partial(
            many_kernel, plan=plan, widths=widths, turns=turns, blocks=blocks, deep=deep,
            keeps=keeps, bits=[b[0] for b in bits],
        ),
        in_specs=[pl.BlockSpec(memory_space=pltpu.SMEM)] + [whole] * (len(args) - 1),
        out_specs=[whole] * len(shape),
        out_shape=shape,
        scratch_shapes=[
            pltpu.VMEM((left.shape[1], left.shape[0]), left.dtype)
            for (left, _), turn in zip(pairs, turns) if turn
        ],
        compiler_params=pltpu.CompilerParams(vmem_limit_bytes=VMEM_CAP),
        cost_estimate=pl.CostEstimate(flops=10**6, bytes_accessed=10**4, transcendentals=0),
        name="many_half",
    )(*args)


def flipped(value, bit, size):
    return lax.ppermute(value, "dp", [(i, i ^ (1 << bit)) for i in range(size)])


def bit_of(index, bit):
    return (index >> bit) & 1


class Halving:
    def __init__(self, make, index, size, orders):
        self.make, self.index, self.size, self.orders = make, index, size, orders
        mine = bit_of(index, 0).astype(jnp.int32)
        self.pick = jnp.stack([mine] + [bit_of(index, bits[0]).astype(jnp.int32) for bits in orders])
        self.other = self.pick.at[0].set(1 - mine)
        self.stage = 0
        self.extra = None

    def work(self):
        if self.stage == 0:
            self.pending = [(sent, None) for sent in self.make(self.other, None)]
        elif self.stage == 1:
            outs = self.make(self.pick, self.extra)
            self.pending = [(outs[2 * g], outs[2 * g + 1]) for g in range(len(self.orders))]
            self.axes = [
                [b for b in range(self.size.bit_length() - 1, 0, -1) if b != bits[0] and b < self.size.bit_length() - 1]
                for bits in self.orders
            ]
        else:
            self.pending = [
                self.split(g, held, extra) for g, (held, extra) in enumerate(zip(self.held, self.extra))
            ]
        return [part for pair in self.pending for part in pair if part is not None]

    def split(self, g, held, extra):
        bits = self.orders[g]
        if self.stage > len(bits):
            return held + extra, None
        bit = bits[self.stage - 1]
        axis = self.axes[g].index(bit)
        shape = (2,) * len(self.axes[g]) + held.shape[-2:]
        self.axes[g].remove(bit)
        own = bit_of(self.index, bit)
        held, extra = held.reshape(shape), extra.reshape(shape)

        def half(value, at):
            return lax.dynamic_index_in_dim(value, at, axis, keepdims=False)

        return half(held, 1 - own) + half(extra, 1 - own), half(held, own) + half(extra, own)

    def go(self, parts):
        parts = list(parts)
        pairs = [
            tuple(None if part is None else parts.pop(0) for part in pair) for pair in self.pending
        ]
        self.held = [home for _, home in pairs]
        last = self.stage > len(self.orders[0])
        if last:
            self.result = [away for away, _ in pairs]
        else:
            bit = lambda g: 0 if self.stage == 0 else self.orders[g][self.stage - 1]
            self.extra = [flipped(away, bit(g), self.size) for g, (away, _) in enumerate(pairs)]
        self.stage += 1

    def step(self):
        self.go(self.work())

    def over(self):
        return self.stage > len(self.orders[0]) + 1

    def finish(self):
        while not self.over():
            self.step()
        return self.result


def tie(values, *chains):
    chains = [chain for chain in chains if not chain.over()]
    values, extras = lax.optimization_barrier((values, [chain.extra for chain in chains]))
    for chain, extra in zip(chains, extras):
        chain.extra = extra
    works = [chain.work() for chain in chains]
    values, works = lax.optimization_barrier((values, works))
    for chain, parts in zip(chains, works):
        chain.go(parts)
    return values


def swap(value):
    return lax.ppermute(value.astype(f32), "mp", [(0, 1), (1, 0)])


def attend_kernel(
    t_ref, c_ref, o_ref, w_ref, ow_ref, gain_ref, shift_ref, first_ref, low_ref, normal_ref, inverse_ref,
    *, start,
):
    weight = ow_ref[...].astype(bf16)

    def body(step, carry):
        at = pl.ds(pl.multiple_of(step * 64, 64), 64)
        here = pl.ds(pl.multiple_of(start + step * 64, 64), 64)
        summed = t_ref[here, :].astype(f32) + nn(c_ref[at, :], w_ref[...])
        summed = summed + nn(o_ref[at, :].astype(bf16), weight)
        first, normal, inverse = norm_forward(summed, gain_ref[...], shift_ref[...])
        first_ref[at, :] = first
        low_ref[at, :] = first.astype(bf16)
        normal_ref[at, :] = normal
        inverse_ref[at, :] = inverse
        return carry

    lax.fori_loop(0, c_ref.shape[0] // 64, body, 0)


def attend(tokens, context, other, weight, other_weight, gain, shift, start):
    tall, depth = context.shape[0], tokens.shape[1]
    whole = pl.BlockSpec(memory_space=pltpu.VMEM)
    return pl.pallas_call(
        functools.partial(attend_kernel, start=start),
        in_specs=[whole] * 7,
        out_specs=(whole,) * 4,
        out_shape=(
            jax.ShapeDtypeStruct((tall, depth), f32),
            jax.ShapeDtypeStruct((tall, depth), bf16),
            jax.ShapeDtypeStruct((tall, depth), f32),
            jax.ShapeDtypeStruct((tall, 1), f32),
        ),
        compiler_params=pltpu.CompilerParams(vmem_limit_bytes=VMEM_CAP),
        cost_estimate=pl.CostEstimate(flops=2 * 10**9, bytes_accessed=8 * 10**6, transcendentals=0),
        name="attend",
    )(tokens, context, other, weight, other_weight, gain[None], shift[None])


def norm_forward(summed, gain, shift):
    centred = summed - jnp.mean(summed, axis=1, keepdims=True)
    inverse = lax.rsqrt(jnp.mean(centred * centred, axis=1, keepdims=True) + epsilon)
    normal = centred * inverse
    return (normal * gain + shift, normal, inverse)


def norm_backward(upstream, normal, inverse, gain):
    scaled = upstream * gain
    inner = jnp.mean(scaled, axis=1, keepdims=True)
    aligned = jnp.mean(scaled * normal, axis=1, keepdims=True)
    return (
        inverse * (scaled - inner - normal * aligned),
        jnp.sum(upstream * normal, axis=0),
        jnp.sum(upstream, axis=0),
    )


def shards(
    tokens,
    query_weight,
    key_weight,
    value_weight,
    output_weight,
    query_position,
    key_position,
    position_tables,
    gain_one,
    shift_one,
    up_weight,
    down_weight,
    gain_two,
    shift_two,
    buckets,
    text_length,
    cotangent,
):
    span = buckets.shape[2]
    rows, cols = sizes(span)
    size = lax.axis_size("dp")
    index = lax.axis_index("dp")
    bits = list(range(1, size.bit_length() - 1))
    low_first, high_first = bits, bits[1:2] + bits[:1] + bits[2:]
    score_scale = (7.0 * HEAD) ** (-0.5)
    tables_flat = position_tables.reshape(3 * REL, D)
    width = query_weight.shape[1]
    spare = ((0, rows - span), (0, 0))

    def chain(make, *orders):
        return Halving(make, index, size, list(orders))

    split = rows // 2 // 128 * 128
    other_output = swap(output_weight)
    qkv, pos_key, pos_query = project(
        tokens, query_weight, key_weight, value_weight, position_tables, key_position, query_position, span
    )
    tokens = jnp.pad(tokens, spare)
    cotangent = jnp.pad(cotangent, spare)
    edges = [(0, split), (split, rows)]

    share_head, context_head, wide_head, bucket_head, bucket_rest, bucket_cols, far_rest, far_inverse = attention_head(
        qkv, pos_key, pos_query, buckets, text_length, score_scale, split
    )
    other_head = swap(wide_head)
    far_rest, other_output = lax.optimization_barrier((far_rest, other_output))
    share_rest, context_rest, wide_rest = attention_rest(
        qkv, pos_key, bucket_rest, far_rest, far_inverse, text_length, score_scale, split, span
    )
    other_rest = swap(wide_rest)
    shares = [share_head, share_rest]
    contexts = [context_head, context_rest]
    contexts_other = [other_head, other_rest]

    def gelu(value):
        return jax.nn.gelu(value, approximate=False)

    firsts, firsts_low, normals_one, inverses_one, upwards, hiddens, feeds, feeds_other = ([] for _ in range(8))
    for (low, high), context, other in zip(edges, contexts, contexts_other):
        first, first_low, normal_one, inverse_one = attend(
            tokens, context, other, output_weight, other_output, gain_one, shift_one, low
        )
        firsts.append(first)
        normals_one.append(normal_one)
        inverses_one.append(inverse_one)
        firsts_low.append(first_low)
        upwards.append(nn(firsts_low[-1], up_weight))
        hiddens.append(gelu(upwards[-1]).astype(bf16))
        feeds.append(nn(hiddens[-1], down_weight))
        feeds_other.append(swap(feeds[-1]))

    feeds[1], tokens_late, tables_late = lax.optimization_barrier((feeds[1], tokens, tables_flat))
    tokens_turned, tables_turned = tokens_late.T, tables_late.T
    finals, seconds_back, seconds_low, upwards_back, backs_part, backs_other, two_sums = ([] for _ in range(7))
    for n, (low, high) in enumerate(edges):
        final, normal_two, inverse_two = norm_forward(
            firsts[n] + feeds[n] + feeds_other[n], gain_two, shift_two
        )
        finals.append(final.astype(bf16))
        second_back, *sums = norm_backward(
            cotangent[low:high].astype(f32), normal_two, inverse_two, gain_two
        )
        two_sums.append(sums)
        seconds_back.append(second_back)
        seconds_low.append(second_back.astype(bf16))
        hidden_back = nt(seconds_low[n], down_weight)
        upwards_back.append(jax.vjp(gelu, upwards[n])[1](hidden_back)[0].astype(bf16))
        backs_part.append(nt(upwards_back[n], up_weight))
        backs_other.append(swap(backs_part[n]))
    layer_output = jnp.concatenate(finals, axis=0)[:span]
    gain_two_grad, shift_two_grad = (two_sums[0][n] + two_sums[1][n] for n in range(2))

    backs_part, down_pair, up_pair = lax.optimization_barrier(
        (backs_part, (seconds_low, hiddens), (firsts_low, upwards_back))
    )
    up_pair, backs_other[0] = lax.optimization_barrier((up_pair, backs_other[0]))
    down_chain = chain(
        lambda pick, add: weight_half(pick, *down_pair, add, parts=size, bits=high_first), high_first
    )
    up_chain = chain(
        lambda pick, add: weight_half(pick, *up_pair, add, parts=size, bits=low_first), low_first
    )
    down_chain.step()
    up_chain.step()
    backs_other[0] = tie(backs_other[0], down_chain)
    backs_other[0] = tie(backs_other[0], up_chain)
    merge = merge_table()
    residuals_back, residuals_low, one_sums = [], [], []

    def draw(n, adds=()):
        residual_back, *sums = norm_backward(
            seconds_back[n] + backs_part[n] + backs_other[n], normals_one[n], inverses_one[n], gain_one
        )
        one_sums.append(sums)
        residuals_back.append(residual_back)
        residuals_low.append(residual_back.astype(bf16))
        context_back = nt(residuals_low[n], output_weight).astype(bf16)
        return attention_draw(shares[n], context_back, qkv, score_scale, edges[n][0], rows, adds)

    back_head, turned_head, query_head, key_head, value_head = draw(0)
    back_head, key_head, backs_other[1] = lax.optimization_barrier((back_head, key_head, backs_other[1]))
    back_rest, turned_rest, query_rest, key_base, value_back = draw(1, (key_head, value_head))
    gain_one_grad, shift_one_grad = (one_sums[0][n] + one_sums[1][n] for n in range(2))
    back_rest, value_back = tie((back_rest, value_back), down_chain)
    residual_low = jnp.concatenate(residuals_low, axis=0)
    context = jnp.concatenate(contexts, axis=0)
    nothing = jnp.zeros_like(gain_one)
    gains = jnp.stack(
        [gain_one_grad, shift_one_grad, gain_two_grad, shift_two_grad] + [nothing] * 4
    )
    gains = jnp.concatenate([gains, jnp.zeros((120, gains.shape[1]), f32)], axis=0)
    dummy = jnp.zeros((8, 128), bf16)
    outer_chain = chain(
        lambda pick, add: many_half(
            pick,
            [(residual_low, context), (tokens_turned, value_back), (gains, dummy)],
            [("turn", 0, 0, width), ("nn", 0, width, width), ("copy", 0, 2 * width, 128)],
            [2 * width + 128],
            add, parts=size, bits=[low_first],
        ),
        low_first,
    )
    outer_chain.step()

    def tail(rows_back, sums, position, orders):
        return chain(
            lambda pick, add: many_half(
                pick,
                [(tokens_turned, rows_back), (tables_turned, sums), (position, sums)],
                [("nn", 0, 0, width), ("nn", 1, 0, width), ("nt", 0, width, 3 * REL)],
                [width + 3 * REL, width],
                add, parts=size, bits=orders,
            ),
            *orders,
        )

    near = []
    blocks = rows // 64
    near.append(attention_scatter([back_head], bucket_head, merge, 0, split // 64))
    back_rest, near = tie((back_rest, near), up_chain)
    back_rest, near = tie((back_rest, near), outer_chain)
    back_rest, near = tie((back_rest, near), down_chain)
    near.append(attention_scatter([back_rest], bucket_rest, merge, 0, blocks - split // 64))
    near, backs = tie((near, [turned_head, turned_rest]), up_chain)
    query_low, key_table_sum = attention_close(near, [query_head, query_rest], pos_key, qkv, 0)
    early = nt(query_low, query_weight) + nt(value_back, value_weight)
    near_chain = tail(query_low, key_table_sum, key_position, [high_first, low_first])
    backs, key_table_sum = tie((backs, key_table_sum), near_chain, outer_chain, down_chain)
    far = []
    cuts = [n * blocks // 3 for n in range(4)]
    for part, chains in enumerate(((near_chain,), (outer_chain, up_chain), (near_chain, outer_chain))):
        far.append(attention_scatter(backs, bucket_cols, merge, cuts[part], cuts[part + 1] - cuts[part]))
        backs, far = tie((backs, far), *chains)
    key_low, query_table_sum = attention_close(far, [key_base], pos_query, qkv, 1)
    key_low, query_table_sum = tie((key_low, query_table_sum), near_chain)
    far_chain = tail(key_low, query_table_sum, query_position, [low_first, high_first])
    parts, others = [], []
    for low, high in ((0, rows // 2), (rows // 2, rows)):
        parts.append(early[low:high] + nt(key_low[low:high], key_weight))
        others.append(swap(parts[-1]))
    far_chain.step()
    far_chain.step()
    far_chain.extra, others[0] = lax.optimization_barrier((far_chain.extra, others[0]))
    far_chain.extra = tie(far_chain.extra, near_chain)
    far_main, query_position_grad = far_chain.finish()
    far_main, others[1] = lax.optimization_barrier((far_main, others[1]))
    input_gradient = (
        jnp.concatenate(residuals_back, axis=0) + jnp.concatenate(parts, axis=0) + jnp.concatenate(others, axis=0)
    )[:span].astype(bf16)
    (down_share,) = down_chain.finish()
    (up_share,) = up_chain.finish()
    (outer_share,) = outer_chain.finish()
    near_main, key_position_grad = near_chain.finish()

    table_rows = near_main[:, width:] + far_main[:, width:]
    table_rows = table_rows.reshape(2, table_rows.shape[0] // 2, 3 * REL)
    side = lax.axis_index("mp")
    table_mine = lax.dynamic_index_in_dim(table_rows, side, 0, keepdims=False) + lax.ppermute(
        lax.dynamic_index_in_dim(table_rows, 1 - side, 0, keepdims=False), "mp", [(0, 1), (1, 0)]
    )
    table_gradient = table_mine.T.reshape(3, REL, table_mine.shape[0])
    gains_mine = outer_share[:, 2 * width:]
    return (
        layer_output,
        input_gradient,
        near_main[:, 0:width],
        far_main[:, 0:width],
        outer_share[:, width:2 * width],
        outer_share[:, 0:width].T,
        query_position_grad,
        key_position_grad,
        table_gradient,
        gains_mine[:, 0],
        gains_mine[:, 1],
        up_share,
        down_share.T,
        gains_mine[:, 2],
        gains_mine[:, 3],
    )


def solution(mesh):
    return jax.shard_map(
        shards,
        mesh=mesh,
        in_specs=(
            P("dp", None),
            P(None, "mp"),
            P(None, "mp"),
            P(None, "mp"),
            P("mp", None),
            P(None, "mp"),
            P(None, "mp"),
            P(),
            P(),
            P(),
            P(None, "mp"),
            P("mp", None),
            P(),
            P(),
            P("dp", None, None, None),
            P("dp"),
            P("dp", None),
        ),
        out_specs=(
            P("dp", None),
            P("dp", None),
            P("dp", "mp"),
            P("dp", "mp"),
            P("dp", "mp"),
            P("mp", "dp"),
            P("dp", "mp"),
            P("dp", "mp"),
            P(None, None, ("dp", "mp")),
            P("dp"),
            P("dp"),
            P("dp", "mp"),
            P("mp", "dp"),
            P("dp"),
            P("dp"),
        ),
        check_vma=False,
    )
```
